32 devices in a mesh: sp: 8 (over z, y), tp: 4 (over x, core).
Axes of the slice: x: 2, y: 2, z: 4, core: 2. Of those that a mesh axis runs over, the one named last changes fastest.
Arguments:
- patches: float32 [160, 240, 256], P('sp', None, 'tp'), may hold values from -6 to 6
- merge_gain: float32 [4, 256], P(None, 'tp'), may hold values from 0.25 to 1.75
- merge_shift: float32 [4, 256], P(None, 'tp'), may hold values from -1.75 to 1.75
- merge_weight: float32 [4, 256, 512], P(None, 'tp'), may hold values from -0.1875 to 0.1875
- first_gain: float32 [2, 512], replicated, may hold values from 0.25 to 1.75
- first_shift: float32 [2, 512], replicated, may hold values from -1.75 to 1.75
- input_weight: float32 [2, 512, 3, 512], P(None, None, None, 'tp'), may hold values from -0.375 to 0.375
- input_bias: float32 [2, 2, 512], P(None, None, 'tp'), may hold values from -1.75 to 1.75
- position_table: float32 [2, 361, 16], P(None, None, 'tp'), may hold values from -6 to 6
- output_weight: float32 [2, 512, 512], P(None, 'tp'), may hold values from -0.75 to 0.75
- output_bias: float32 [2, 512], replicated, may hold values from -1.75 to 1.75
- second_gain: float32 [2, 512], replicated, may hold values from 0.25 to 1.75
- second_shift: float32 [2, 512], replicated, may hold values from -1.75 to 1.75
- expand_weight: float32 [2, 512, 2048], P(None, None, 'tp'), may hold values from -0.25 to 0.25
- expand_bias: float32 [2, 2048], P(None, 'tp'), may hold values from -1.75 to 1.75
- shrink_weight: float32 [2, 2048, 512], P(None, 'tp'), may hold values from -0.1875 to 0.1875
- shrink_bias: float32 [2, 512], replicated, may hold values from -1.75 to 1.75
- page_map: int32 [8, 12], replicated, may hold values from 0 to 58, as said below
- valid_flags: int32 [80, 120], P('sp'), may hold values from 0 to 1, as said below
- cotangent: float32 [80, 120, 512], P('sp', None, 'tp'), may hold values from -6 to 6
Outputs:
- output: float32 [80, 120, 512], P('sp', None, 'tp')
- patches_grad: float32 [160, 240, 256], P('sp', None, 'tp')
- merge_gain_grad: float32 [4, 256], P(None, 'tp')
- merge_shift_grad: float32 [4, 256], P(None, 'tp')
- merge_weight_grad: float32 [4, 256, 512], P(None, 'tp')
- first_gain_grad: float32 [2, 512], replicated
- first_shift_grad: float32 [2, 512], replicated
- input_weight_grad: float32 [2, 512, 3, 512], P(None, None, None, 'tp')
- input_bias_grad: float32 [2, 2, 512], P(None, None, 'tp')
- position_table_grad: float32 [2, 361, 16], P(None, None, 'tp')
- output_weight_grad: float32 [2, 512, 512], P(None, 'tp')
- output_bias_grad: float32 [2, 512], replicated
- second_gain_grad: float32 [2, 512], replicated
- second_shift_grad: float32 [2, 512], replicated
- expand_weight_grad: float32 [2, 512, 2048], P(None, None, 'tp')
- expand_bias_grad: float32 [2, 2048], P(None, 'tp')
- shrink_weight_grad: float32 [2, 2048, 512], P(None, 'tp')
- shrink_bias_grad: float32 [2, 512], replicated
- rms: float32 [5], replicated
The draws below stay inside these ranges and needn't reach their ends.
Inputs may be any that keep to these rules, and one draw needn't show every extreme that they name: `page_map`: the windows of one page form a rectangle of whole windows; pages are numbered row_page * 13 + column_page, both never falling along their axis, starting at 0 in the first window, with exactly 4 row breaks and 6 column breaks, so the last window holds the largest number. `valid_flags`: the first patch of every window is valid.
All inputs are finite; a program needn't handle non-finite values.
Results may differ from the reference program's by a relative error of at most 0.0003.
Values sent between devices are 32-bit elements; how exact they have to be, the bound alone decides.
A program may use at most 192 MiB of HBM per device.

```python
import jax
import jax.numpy as jnp
from jax import lax

C = 512
HEADS = 16
HD = 32
FF = 2048
C2 = 256
WIN = 10
SHIFT = 5
WCOLS = 12
WROWS = 8
H3 = 80
W3 = 120
H2 = 160
W2 = 240
TABLE = 361


def fixed_breaks(key, count):
    scores = jax.random.randint(key, (count,), 0, 1 << 20) * count + jnp.arange(count, dtype=jnp.int32)
    scores = jnp.where(jnp.arange(count, dtype=jnp.int32) == 0, (1 << 21) * count, scores)
    order = jnp.argsort(scores, stable=True)
    ranks = jnp.argsort(order, stable=True).astype(jnp.int32)
    return (ranks < count // 2).astype(jnp.int32)


def draw_page_map(key, part):
    row_breaks = fixed_breaks(jax.random.fold_in(key, 11), WROWS)
    column_breaks = fixed_breaks(jax.random.fold_in(key, 23), WCOLS)
    row_pages = jnp.cumsum(row_breaks).astype(jnp.int32)
    column_pages = jnp.cumsum(column_breaks).astype(jnp.int32)
    return (row_pages[:, None] * (WCOLS + 1) + column_pages[None, :]).astype(jnp.int32)


def draw_valid_flags(key, part):
    row_index = jnp.arange(H3, dtype=jnp.int32)[:, None]
    column_index = jnp.arange(W3, dtype=jnp.int32)[None, :]
    threshold = 300 + 650 * row_index // H3
    ticket = jax.random.randint(jax.random.fold_in(key, 5), (H3, W3), 0, 1000)
    anchor = (row_index % WIN == 0) & (column_index % WIN == 0)
    return ((ticket < threshold) | anchor).astype(jnp.int32)


def shard_levels(stream_key, dims, cuts, smallest, high):
    def one(dim, blocks):
        steps = jax.random.uniform(jax.random.fold_in(jax.random.fold_in(stream_key, 6), dim), (blocks,), jnp.float32, smallest / len(cuts), high / len(cuts))
        return jnp.repeat(jnp.exp(steps), dims[dim] // blocks).reshape((-1,) + (1,) * (len(dims) - dim - 1))

    loudness = one(*cuts[0])
    for cut in cuts[1:]:
        loudness = loudness * one(*cut)
    return loudness


def normal_values(own_key, shape, width, reach, cuts=(), kind=jnp.bfloat16):
    factor_of = shard_levels(own_key, shape, cuts, -0.22, 0.18) if cuts else 1.0
    values = jax.random.normal(own_key, shape, jnp.float32) * width * factor_of
    return jnp.minimum(jnp.maximum(values, -reach), reach).astype(kind)


def setup_inputs(seed: int = 0) -> dict:
    streams_of = jax.random.split(jax.random.key(seed), 21)
    patches = normal_values(streams_of[0], (H2, W2, C2), 1.0, 6.0, ((0, 8), (2, 4)), jnp.float32)
    merge_gain = jnp.clip(1.0 + 0.15 * jax.random.normal(streams_of[1], (4, C2), jnp.float32), 0.25, 1.75)
    merge_shift = normal_values(streams_of[2], (4, C2), 0.3, 1.75, ((1, 4),), jnp.float32)
    merge_weight = normal_values(streams_of[3], (4, C2, C), (4 * C2) ** -0.5, 0.1875, ((1, 4),), jnp.float32)
    first_gain = jnp.clip(1.0 + 0.15 * jax.random.normal(streams_of[4], (2, C), jnp.float32), 0.25, 1.75)
    first_shift = normal_values(streams_of[5], (2, C), 0.3, 1.75, (), jnp.float32)
    input_weight = normal_values(streams_of[6], (2, C, 3, C), (C // 2) ** -0.5, 0.375, ((3, 4),), jnp.float32)
    input_bias = normal_values(streams_of[7], (2, 2, C), 0.3, 1.75, ((2, 4),), jnp.float32)
    position_table = normal_values(streams_of[8], (2, TABLE, HEADS), 1.0, 6.0, ((2, 4),), jnp.float32)
    output_weight = normal_values(streams_of[9], (2, C, C), (C // 8) ** -0.5, 0.75, ((1, 4),), jnp.float32)
    output_bias = normal_values(streams_of[10], (2, C), 0.3, 1.75, (), jnp.float32)
    second_gain = jnp.clip(1.0 + 0.15 * jax.random.normal(streams_of[11], (2, C), jnp.float32), 0.25, 1.75)
    second_shift = normal_values(streams_of[12], (2, C), 0.3, 1.75, (), jnp.float32)
    expand_weight = normal_values(streams_of[13], (2, C, FF), C ** -0.5, 0.25, ((2, 4),), jnp.float32)
    expand_bias = normal_values(streams_of[14], (2, FF), 0.3, 1.75, ((1, 4),), jnp.float32)
    shrink_weight = normal_values(streams_of[15], (2, FF, C), (FF // 2) ** -0.5, 0.1875, ((1, 4),), jnp.float32)
    shrink_bias = normal_values(streams_of[16], (2, C), 0.3, 1.75, (), jnp.float32)
    page_map = draw_page_map(jax.random.fold_in(streams_of[20], 71), 0)
    valid_flags = draw_valid_flags(jax.random.fold_in(streams_of[20], 71), 0)
    cotangent = normal_values(streams_of[19], (H3, W3, C), 1.0, 6.0, ((0, 8), (2, 4)), jnp.float32)
    return dict(patches=patches, merge_gain=merge_gain, merge_shift=merge_shift, merge_weight=merge_weight, first_gain=first_gain, first_shift=first_shift, input_weight=input_weight, input_bias=input_bias, position_table=position_table, output_weight=output_weight, output_bias=output_bias, second_gain=second_gain, second_shift=second_shift, expand_weight=expand_weight, expand_bias=expand_bias, shrink_weight=shrink_weight, shrink_bias=shrink_bias, page_map=page_map, valid_flags=valid_flags, cotangent=cotangent)


@jax.custom_vjp
def low(v):
    return lax.optimization_barrier(v.astype(jnp.bfloat16)).astype(jnp.float32)

@jax.custom_vjp
def low_back(v):
    return v

def low_keep(v):
    return (low(v), None)

def low_pass(kept, grad):
    return (grad,)

def back_keep(v):
    return (v, None)

def back_low(kept, grad):
    return (low(grad),)
low.defvjp(low_keep, low_pass)
low_back.defvjp(back_keep, back_low)
highest = lax.Precision.HIGHEST
epsilon = 1e-05
masked = -1000000000.0

def layer_norm(values, gain_row, offset):
    center = values - lax.optimization_barrier(jnp.mean(values, axis=-1, keepdims=True))
    spread = lax.optimization_barrier(jnp.mean(center * center, axis=-1, keepdims=True))
    return center * lax.rsqrt(spread + epsilon) * gain_row + offset

def relative_index():
    positions = jnp.arange(WIN * WIN, dtype=jnp.int32)
    row_of = positions // WIN
    column_of = positions % WIN
    row_offset = row_of[:, None] - row_of[None, :] + (WIN - 1)
    column_offset = column_of[:, None] - column_of[None, :] + (WIN - 1)
    return (row_offset * (2 * WIN - 1) + column_offset).astype(jnp.int32)

def window_attention(queries, key_rows, value_rows, bias_grid, region, validity):
    scores = jnp.einsum('wqhd,wkhd->whqk', queries, key_rows, precision=highest) * HD ** (-0.5) + bias_grid[None]
    same_region = region[:, :, None] == region[:, None, :]
    diagonal = jnp.eye(WIN * WIN, dtype=bool)[None]
    allowed = same_region & (validity[:, None, :] > 0) | diagonal
    scores = jnp.where(allowed[:, None], scores, masked)
    row_max = lax.optimization_barrier(jnp.max(scores, axis=-1, keepdims=True))
    weights = jnp.exp(scores - row_max)
    weights = weights / lax.optimization_barrier(jnp.sum(weights, axis=-1, keepdims=True))
    return jnp.einsum('whqk,wkhd->wqhd', weights, value_rows, precision=highest)

def to_windows(values):
    row_count, column_count = (values.shape[0], values.shape[1])
    trailing = values.shape[2:]
    windowed = values.reshape((row_count // WIN, WIN, column_count // WIN, WIN) + trailing)
    windowed = jnp.moveaxis(windowed, 2, 1)
    return windowed.reshape((row_count // WIN, column_count // WIN, WIN * WIN) + trailing)

def from_windows(windowed, row_count, column_count):
    trailing = windowed.shape[3:]
    values = windowed.reshape((row_count // WIN, column_count // WIN, WIN, WIN) + trailing)
    values = jnp.moveaxis(values, 1, 2)
    return values.reshape((row_count, column_count) + trailing)

def shifted_region(page_map):
    row_index = jnp.arange(H3, dtype=jnp.int32)
    column_index = jnp.arange(W3, dtype=jnp.int32)
    page = page_map[row_index[:, None] // WIN, column_index[None, :] // WIN]
    wrap_row = (row_index < SHIFT).astype(jnp.int32)[:, None]
    wrap_column = (column_index < SHIFT).astype(jnp.int32)[None, :]
    region = page * 4 + wrap_row * 2 + wrap_column
    return jnp.roll(region, (-SHIFT, -SHIFT), axis=(0, 1))

def block(field, params, shifted, region, validity):
    first_gain, first_shift, input_weight, input_bias, position_table, output_weight, output_bias, second_gain, second_shift, expand_weight, expand_bias, shrink_weight, shrink_bias = params
    row_count, column_count = (field.shape[0], field.shape[1])
    normed = layer_norm(field, first_gain, first_shift)
    projected = jnp.einsum('rcd,dkf->rckf', normed, input_weight, precision=highest)
    queries = projected[:, :, 0] + input_bias[0]
    key_rows = projected[:, :, 1]
    value_rows = projected[:, :, 2] + input_bias[1]
    if shifted:
        queries = jnp.roll(queries, (-SHIFT, -SHIFT), axis=(0, 1))
        key_rows = jnp.roll(key_rows, (-SHIFT, -SHIFT), axis=(0, 1))
        value_rows = jnp.roll(value_rows, (-SHIFT, -SHIFT), axis=(0, 1))
        validity = jnp.roll(validity, (-SHIFT, -SHIFT), axis=(0, 1))
    bias_grid = jnp.transpose(position_table[relative_index()], (2, 0, 1))

    def heads_split(values):
        windowed = to_windows(values)
        return windowed.reshape(windowed.shape[:3] + (HEADS, HD))

    def one_row(pieces):
        return window_attention(pieces[0], pieces[1], pieces[2], bias_grid, pieces[3], pieces[4])
    attended = lax.map(jax.checkpoint(one_row), (heads_split(queries), heads_split(key_rows), heads_split(value_rows), to_windows(region), to_windows(validity)))
    attended = from_windows(attended.reshape(attended.shape[:3] + (C,)), row_count, column_count)
    if shifted:
        attended = jnp.roll(attended, (SHIFT, SHIFT), axis=(0, 1))
    mixed_out = jnp.einsum('rcf,fd->rcd', attended, output_weight, precision=highest) + output_bias
    middle = field + mixed_out
    normed_two = layer_norm(middle, second_gain, second_shift)
    pre_act = jnp.einsum('rcd,df->rcf', normed_two, expand_weight, precision=highest) + expand_bias
    hidden = jax.nn.gelu(pre_act, approximate=False)
    branch = jnp.einsum('rcf,fd->rcd', hidden, shrink_weight, precision=highest) + shrink_bias
    return (middle + branch, mixed_out, branch)

def reference(patches, merge_gain, merge_shift, merge_weight, first_gain, first_shift, input_weight, input_bias, position_table, output_weight, output_bias, second_gain, second_shift, expand_weight, expand_bias, shrink_weight, shrink_bias, page_map, valid_flags, cotangent):
    floats = (patches, merge_gain, merge_shift, merge_weight, first_gain, first_shift, input_weight, input_bias, position_table, output_weight, output_bias, second_gain, second_shift, expand_weight, expand_bias, shrink_weight, shrink_bias)
    region_moved = shifted_region(page_map)
    region_flat = jnp.zeros_like(region_moved)
    valid_float = valid_flags.astype(jnp.float32)

    def masked_squares(values):
        return jnp.sum(values * values * valid_float[:, :, None])

    def forward(*params):
        section, gain_merge, shift_merge, weight_merge = params[:4]
        stacked = params[4:]
        quads = jnp.concatenate([section[0::2, 0::2], section[1::2, 0::2], section[0::2, 1::2], section[1::2, 1::2]], axis=-1)
        merged = layer_norm(quads, gain_merge.reshape(-1), shift_merge.reshape(-1))
        field = jnp.einsum('rcf,fd->rcd', merged, weight_merge.reshape(-1, C), precision=highest)
        square_sums = []
        for block_index in range(2):
            params_here = [stacked_item[block_index] for stacked_item in stacked]
            region = region_moved if block_index == 1 else region_flat
            field, mixed_out, branch = block(field, params_here, block_index == 1, region, valid_flags)
            square_sums.append(masked_squares(mixed_out))
            square_sums.append(masked_squares(branch))
        square_sums.append(masked_squares(field))
        return (field, jnp.stack(square_sums))
    output, pull_back, square_sums = jax.vjp(forward, *floats, has_aux=True)
    grads = pull_back(cotangent)
    valid_count = jnp.sum(valid_float)
    rms = jnp.sqrt(square_sums / (valid_count * C))
    return (output, grads[0], grads[1], grads[2], grads[3], grads[4], grads[5], grads[6], grads[7], grads[8], grads[9], grads[10], grads[11], grads[12], grads[13], grads[14], grads[15], grads[16], rms)
```

```python
import functools

import jax
import jax.numpy as jnp
import numpy as np
from jax import lax
from jax.experimental import pallas as pl
from jax.experimental.pallas import tpu as pltpu
from jax.sharding import PartitionSpec as P

C = 512
HD = 32
C2 = 256
WIN = 10
SHIFT = 5
SUB = 32
REAL = 25
WT = 128
TOK = 384
NW = 3
GROUP = 4

bf16 = jnp.bfloat16
f32 = jnp.float32
epsilon = 1e-05
masked = -1000000000.0

NN = (((1,), (0,)), ((), ()))
NT = (((1,), (1,)), ((), ()))
TN = (((0,), (0,)), ((), ()))


def split(x):
    high = x.astype(bf16)
    return high, (x - high.astype(f32)).astype(bf16)


def mm(a, b, dims):
    return lax.dot_general(a, b, dims, preferred_element_type=f32)


def mm3(a, b, dims):
    return mm(a[0], b[0], dims) + (mm(a[0], b[1], dims) + mm(a[1], b[0], dims))


def normalized(x):
    center = x - jnp.mean(x, axis=-1, keepdims=True)
    rho = lax.rsqrt(jnp.mean(center * center, axis=-1, keepdims=True) + epsilon)
    return center * rho, rho


def head_masks(dtype):
    lane = lax.broadcasted_iota(jnp.int32, (1, 128), 1) // HD
    return [(lane == h).astype(f32).astype(dtype) for h in range(GROUP)]


def stacked(pair, masks):
    return tuple(jnp.concatenate([part * m for m in masks], axis=0) for part in pair)


def side_by_side(pair):
    return tuple(
        jnp.concatenate([part[h * WT : (h + 1) * WT] for h in range(GROUP)], axis=1)
        for part in pair
    )


def colsum(x):
    return jnp.sum(x, axis=0, keepdims=True)


def attn_fwd_kernel(
    field_ref, gain_ref, shift_ref, wqkv_ref, bqkv_ref, wo_ref, bo_ref, bias_ref,
    regc_ref, regr_ref, valr_ref, valc_ref,
    middle_ref, qkv_ref, p_ref, att_ref, sq_ref,
    nh, nl, mixed,
):
    g = pl.program_id(0)

    @pl.when(g == 0)
    def _():
        xhat, _ = normalized(field_ref[...])
        nh[...], nl[...] = split(xhat * gain_ref[...] + shift_ref[...])
        mixed[...] = jnp.broadcast_to(bo_ref[...], mixed.shape)

    w = jnp.concatenate([wqkv_ref[0, j] for j in range(3)], axis=1)
    qkv = mm3((nh[...], nl[...]), split(w), NN) + bqkv_ref[0]
    lane = lax.broadcasted_iota(jnp.int32, (1, 3 * 128), 1)
    qkv = qkv * jnp.where(lane < 128, HD ** (-0.5), 1.0)
    qkv_ref[0] = qkv
    masks = head_masks(bf16)
    bias = bias_ref[...].reshape(GROUP * WT, WT)
    eye = lax.broadcasted_iota(jnp.int32, (WT, WT), 0) == lax.broadcasted_iota(jnp.int32, (WT, WT), 1)
    for i in range(NW):
        rows = pl.ds(i * WT, WT)
        here = qkv_ref[0, rows, :]
        q4 = stacked(split(here[:, :128]), masks)
        k = split(here[:, 128:256])
        v4 = stacked(split(here[:, 256:]), masks)
        allowed = (regc_ref[rows, :] == regr_ref[i]) & (valr_ref[i] > 0) | eye
        allowed = jnp.concatenate([allowed.astype(f32)] * GROUP, axis=0) > 0
        s = jnp.where(allowed, mm3(q4, k, NT) + bias, masked)
        e = jnp.exp(s - jnp.max(s, axis=-1, keepdims=True))
        p = e / jnp.sum(e, axis=-1, keepdims=True)
        p_ref[0, i] = p
        att_ref[0, rows, :] = mm3(side_by_side(split(p)), v4, NN)
    mixed[...] += mm3(split(att_ref[0]), split(wo_ref[0]), NN)

    @pl.when(g == GROUP - 1)
    def _():
        middle_ref[...] = field_ref[...] + mixed[...]
        sq_ref[...] = colsum(mixed[...] * mixed[...] * valc_ref[...])


def whole(shape):
    return pl.BlockSpec(shape, lambda g: (0,) * len(shape))


def part(shape):
    return pl.BlockSpec((1,) + shape, lambda g: (g,) + (0,) * len(shape))


def sds(*shape):
    return jax.ShapeDtypeStruct(shape, f32)


BIG = pltpu.CompilerParams(vmem_limit_bytes=56 << 20)


def attn_fwd(field, gain, shift, wqkv, bqkv, wo, bo, bias, masks):
    regc, regr, valr, valc = masks
    return pl.pallas_call(
        attn_fwd_kernel,
        grid=(4,),
        in_specs=[
            whole((TOK, C)), whole((1, C)), whole((1, C)), part((3, C, 128)), part((1, 384)),
            part((128, C)), whole((1, C)), pl.BlockSpec((GROUP, WT, WT), lambda g: (g, 0, 0)),
            whole((TOK, 1)), whole((NW, 1, WT)), whole((NW, 1, WT)), whole((TOK, 1)),
        ],
        out_specs=[
            whole((TOK, C)), part((TOK, 384)), part((NW, GROUP * WT, WT)), part((TOK, 128)),
            whole((1, C)),
        ],
        out_shape=[
            sds(TOK, C), sds(4, TOK, 384), sds(4, NW, GROUP * WT, WT), sds(4, TOK, 128), sds(1, C),
        ],
        scratch_shapes=[pltpu.VMEM((TOK, C), bf16), pltpu.VMEM((TOK, C), bf16), pltpu.VMEM((TOK, C), f32)],
        compiler_params=BIG,
        name="attn_fwd",
    )(field, gain, shift, wqkv, bqkv, wo, bo, bias, regc, regr, valr, valc)


def mlp_fwd_kernel(
    mid_ref, gain_ref, shift_ref, we_ref, be_ref, ws_ref, bs_ref, valc_ref,
    out_ref, hid_ref, slope_ref, sq_ref, sqo_ref,
    nh, nl, branch,
):
    g = pl.program_id(0)

    @pl.when(g == 0)
    def _():
        xhat, _ = normalized(mid_ref[...])
        nh[...], nl[...] = split(xhat * gain_ref[...] + shift_ref[...])
        branch[...] = jnp.broadcast_to(bs_ref[...], branch.shape)

    pre = mm3((nh[...], nl[...]), split(we_ref[0]), NN) + be_ref[0]
    phi = 0.5 * (1.0 + lax.erf(pre * (2 ** -0.5)))
    hidden = pre * phi
    hid_ref[0] = hidden
    slope_ref[0] = phi + pre * (jnp.exp(-0.5 * pre * pre) * ((2 * np.pi) ** -0.5))
    branch[...] += mm3(split(hidden), split(ws_ref[0]), NN)

    @pl.when(g == 3)
    def _():
        out = mid_ref[...] + branch[...]
        out_ref[...] = out
        sq_ref[...] = colsum(branch[...] * branch[...] * valc_ref[...])
        sqo_ref[...] = colsum(out * out * valc_ref[...])


def mlp_fwd(mid, gain, shift, we, be, ws, bs, valc):
    return pl.pallas_call(
        mlp_fwd_kernel,
        grid=(4,),
        in_specs=[
            whole((TOK, C)), whole((1, C)), whole((1, C)), part((C, 512)), part((1, 512)),
            part((512, C)), whole((1, C)), whole((TOK, 1)),
        ],
        out_specs=[whole((TOK, C)), part((TOK, 512)), part((TOK, 512)), whole((1, C)), whole((1, C))],
        out_shape=[sds(TOK, C), sds(4, TOK, 512), sds(4, TOK, 512), sds(1, C), sds(1, C)],
        scratch_shapes=[pltpu.VMEM((TOK, C), bf16), pltpu.VMEM((TOK, C), bf16), pltpu.VMEM((TOK, C), f32)],
        compiler_params=BIG,
        name="mlp_fwd",
    )(mid, gain, shift, we, be, ws, bs, valc)


def norm_back(x, gain, grad_y):
    xhat, rho = normalized(x)
    gh = grad_y * gain
    grad_x = rho * (
        gh - jnp.mean(gh, axis=-1, keepdims=True) - xhat * jnp.mean(gh * xhat, axis=-1, keepdims=True)
    )
    return grad_x, colsum(grad_y * xhat), colsum(grad_y)


def mlp_bwd_kernel(
    gf_ref, mid_ref, gain_ref, shift_ref, we_ref, ws_ref, hid_ref, slope_ref,
    gm_ref, pack_ref, dbe_ref, small_ref,
    nth, ntl, gh, gl, acc,
):
    g = pl.program_id(0)

    @pl.when(g == 0)
    def _():
        xhat, _ = normalized(mid_ref[...])
        nth[...], ntl[...] = split((xhat * gain_ref[...] + shift_ref[...]).T)
        gh[...], gl[...] = split(gf_ref[...])
        acc[...] = jnp.zeros_like(acc)

    grad = (gh[...], gl[...])
    dws = mm3(split(hid_ref[0].T), grad, NN)
    for j in range(4):
        pack_ref[0, 2048 + j * 512 : 2560 + j * 512, :] = dws[:, j * 128 : (j + 1) * 128]
    dpre = mm3(grad, split(ws_ref[0]), NT) * slope_ref[0]
    dbe_ref[0] = colsum(dpre)
    pair = split(dpre)
    dwe = mm3((nth[...], ntl[...]), pair, NN)
    for j in range(4):
        pack_ref[0, j * 512 : (j + 1) * 512, :] = dwe[:, j * 128 : (j + 1) * 128]
    acc[...] += mm3(pair, split(we_ref[0]), NT)

    @pl.when(g == 3)
    def _():
        grad_x, dgain, dshift = norm_back(mid_ref[...], gain_ref[...], acc[...])
        gm_ref[...] = gf_ref[...] + grad_x
        small_ref[0:1, :] = dgain
        small_ref[1:2, :] = dshift
        small_ref[2:3, :] = colsum(gf_ref[...])
        small_ref[3:8, :] = jnp.zeros((5, C), f32)


def mlp_bwd(gf, mid, gain, shift, we, ws, hid, slope, pack, place):
    body, more, extra, alias = mlp_bwd_kernel, (), [], {}
    if pack is not None:
        body = lambda *refs: mlp_bwd_kernel(*refs[:8], *refs[9:])
        more, extra, alias = (pack,), [ANY], {8: 1}
    return pl.pallas_call(
        body,
        grid=(4,),
        in_specs=[
            whole((TOK, C)), whole((TOK, C)), whole((1, C)), whole((1, C)), part((C, 512)),
            part((512, C)), part((TOK, 512)), part((TOK, 512)),
        ] + extra,
        out_specs=[
            whole((TOK, C)), pl.BlockSpec((1, 4096, 128), lambda g: (g, place, 0)), part((1, 512)), whole((8, C)),
        ],
        out_shape=[sds(TOK, C), sds(4, 12288, 128), sds(4, 1, 512), sds(8, C)],
        input_output_aliases=alias,
        scratch_shapes=[
            pltpu.VMEM((C, TOK), bf16), pltpu.VMEM((C, TOK), bf16),
            pltpu.VMEM((TOK, C), bf16), pltpu.VMEM((TOK, C), bf16), pltpu.VMEM((TOK, C), f32),
        ],
        compiler_params=BIG,
        name="mlp_bwd",
    )(gf, mid, gain, shift, we, ws, hid, slope, *more)


def attn_bwd_kernel(
    gm_ref, field_ref, gain_ref, shift_ref, wqkv_ref, wo_ref, qkv_ref, p_ref, att_ref, _,
    gf_ref, pack_ref, dbqkv_ref, dbias_ref, small_ref,
    nth, ntl, mh, ml, acc, dqkv,
):
    g = pl.program_id(0)

    @pl.when(g == 0)
    def _():
        xhat, _ = normalized(field_ref[...])
        nth[...], ntl[...] = split((xhat * gain_ref[...] + shift_ref[...]).T)
        mh[...], ml[...] = split(gm_ref[...])
        acc[...] = jnp.zeros_like(acc)

    grad = (mh[...], ml[...])
    dwo = mm3(split(att_ref[0].T), grad, NN)
    for j in range(4):
        pack_ref[0, 1536 + j * 128 : 1664 + j * 128, :] = dwo[:, j * 128 : (j + 1) * 128]
    dout = mm3(grad, split(wo_ref[0]), NT)
    masks = head_masks(bf16)
    dbias = jnp.zeros((GROUP * WT, WT), f32)
    for i in range(NW):
        rows = slice(i * WT, (i + 1) * WT)
        here = qkv_ref[0, pl.ds(i * WT, WT), :]
        q4 = stacked(split(here[:, :128]), masks)
        k4 = stacked(split(here[:, 128:256]), masks)
        v = split(here[:, 256:])
        p = p_ref[0, i]
        do4 = stacked(split(dout[rows]), masks)
        dp = mm3(do4, v, NT)
        ds = p * (dp - jnp.sum(p * dp, axis=-1, keepdims=True))
        dbias = dbias + ds
        dpair = split(ds)
        dqkv[pl.ds(i * WT, WT), 0:128] = mm3(side_by_side(dpair), k4, NN) * HD ** (-0.5)
        dqkv[pl.ds(i * WT, WT), 128:256] = mm3(dpair, q4, TN)
        dqkv[pl.ds(i * WT, WT), 256:384] = mm3(split(p), do4, TN)
    dbias_ref[...] = dbias.reshape(GROUP, WT, WT)
    grads = dqkv[...]
    dbqkv_ref[0] = colsum(grads)
    pair = split(grads)
    dw = mm3((nth[...], ntl[...]), pair, NN)
    for j in range(3):
        pack_ref[0, j * 512 : (j + 1) * 512, :] = dw[:, j * 128 : (j + 1) * 128]
    w = jnp.concatenate([wqkv_ref[0, j] for j in range(3)], axis=1)
    acc[...] += mm3(pair, split(w), NT)

    @pl.when(g == GROUP - 1)
    def _():
        grad_x, dgain, dshift = norm_back(field_ref[...], gain_ref[...], acc[...])
        gf_ref[...] = gm_ref[...] + grad_x
        small_ref[0:1, :] = dgain
        small_ref[1:2, :] = dshift
        small_ref[2:3, :] = colsum(gm_ref[...])
        small_ref[3:8, :] = jnp.zeros((5, C), f32)


def attn_bwd(gm, field, gain, shift, wqkv, wo, qkv, p, att, pack, place):
    return pl.pallas_call(
        attn_bwd_kernel,
        grid=(4,),
        in_specs=[
            whole((TOK, C)), whole((TOK, C)), whole((1, C)), whole((1, C)), part((3, C, 128)),
            part((128, C)), part((TOK, 384)), part((NW, GROUP * WT, WT)), part((TOK, 128)), ANY,
        ],
        out_specs=[
            whole((TOK, C)), pl.BlockSpec((1, 2048, 128), lambda g: (g, place, 0)), part((1, 384)),
            pl.BlockSpec((GROUP, WT, WT), lambda g: (g, 0, 0)), whole((8, C)),
        ],
        out_shape=[sds(TOK, C), sds(4, 12288, 128), sds(4, 1, 384), sds(16, WT, WT), sds(8, C)],
        input_output_aliases={9: 1},
        scratch_shapes=[
            pltpu.VMEM((C, TOK), bf16), pltpu.VMEM((C, TOK), bf16),
            pltpu.VMEM((TOK, C), bf16), pltpu.VMEM((TOK, C), bf16),
            pltpu.VMEM((TOK, C), f32), pltpu.VMEM((TOK, 384), f32),
        ],
        compiler_params=BIG,
        name="attn_bwd",
    )(gm, field, gain, shift, wqkv, wo, qkv, p, att, pack)


MESH = pl.DeviceIdType.MESH
ANY = pl.BlockSpec(memory_space=pl.ANY)
VM = pl.BlockSpec(memory_space=pltpu.VMEM)


def here():
    sp, tp = lax.axis_index("sp"), lax.axis_index("tp")
    return sp, tp, (sp, tp ^ 1), (sp, tp ^ 2), (sp ^ 1, tp)


def meet(peers):
    barrier = pltpu.get_barrier_semaphore()
    for peer in peers:
        pl.semaphore_signal(barrier, inc=1, device_id=peer, device_id_type=MESH)
    pl.semaphore_wait(barrier, len(peers))


def push(src, dst, send, recv, peer):
    return pltpu.make_async_remote_copy(
        src_ref=src, dst_ref=dst, send_sem=send, recv_sem=recv, device_id=peer, device_id_type=MESH
    )


def gather_kernel(axes, count, *refs):
    ins, outs = refs[:count], refs[count : 2 * count]
    send, recv, local = refs[2 * count :]
    sp, tp, sib, across, beside = here()
    par = sp & 1
    meet((sib, across, beside))

    def cut(ref, axis, half):
        if axis is None:
            return ref
        size = ref.shape[axis] // 2
        index = [slice(None)] * len(ref.shape)
        index[axis] = pl.ds(pl.multiple_of(half * size, size), size)
        return ref.at[tuple(index)]

    def own(i):
        return pltpu.make_async_copy(ins[i], outs[i].at[tp], local.at[i])

    def to_sib(i):
        return push(ins[i], outs[i].at[tp], send.at[0, i], recv.at[0, i], sib)

    def to_across(i):
        return push(
            cut(ins[i], axes[i], par), cut(outs[i].at[tp], axes[i], par), send.at[1, i], recv.at[1, i], across
        )

    def far(i, half):
        return cut(outs[i].at[tp ^ 2], axes[i], half)

    def to_beside(i):
        return push(far(i, par), far(i, par), send.at[2, i], recv.at[2, i], beside)

    def on_first(i):
        return push(far(i, par), far(i, par), send.at[3, i], recv.at[3, i], sib)

    def on_second(i):
        return push(far(i, 1 - par), far(i, 1 - par), send.at[4, i], recv.at[4, i], sib)

    for i in range(count):
        to_across(i).start()
        to_sib(i).start()
        own(i).start()
    for i in range(count + 1):
        if i < count:
            to_across(i).wait_recv()
            on_first(i).start()
            if axes[i] is not None:
                to_beside(i).start()
        if i > 0 and axes[i - 1] is not None:
            to_beside(i - 1).wait_recv()
            on_second(i - 1).start()
    for i in range(count):
        own(i).wait()
        to_sib(i).wait()
        to_across(i).wait_send()
        on_first(i).wait()
        if axes[i] is not None:
            to_beside(i).wait_send()
            on_second(i).wait()


def gather_all(arrays, axes, ident):
    count = len(arrays)
    return pl.pallas_call(
        functools.partial(gather_kernel, axes, count),
        in_specs=[ANY] * count,
        out_specs=[ANY] * count,
        out_shape=[jax.ShapeDtypeStruct((4,) + a.shape, a.dtype) for a in arrays],
        scratch_shapes=[
            pltpu.SemaphoreType.DMA((5, count)), pltpu.SemaphoreType.DMA((5, count)),
            pltpu.SemaphoreType.DMA((count,)),
        ],
        compiler_params=pltpu.CompilerParams(collective_id=ident, has_side_effects=True),
        name="gather",
    )(*arrays)


ROWS = 512


def reduce_kernel(n, chunks, tiny_rows, *refs):
    g_ref, t_ref, out_ref, tout_ref = refs[:4]
    loc, pair, xr, yr, zr, fin, ta, tx, tz, ss, rs, zs, zq, fs, fq, ls, os, ts, tq, tzs, tzq = refs[4:]
    sp, tp, sib, across, beside = here()
    par, mine = sp & 1, sp // 2
    m = n // 2
    half = ROWS // 2
    piece = half // m

    barrier = pltpu.get_barrier_semaphore()
    for peer in (sib, across, beside):
        pl.semaphore_signal(barrier, inc=1, device_id=peer, device_id_type=MESH)

    def member(j):
        return (mine + j) % m

    def device(q):
        return (q * 2 + par, tp)

    @pl.loop(1, m)
    def _(j):
        pl.semaphore_signal(barrier, inc=1, device_id=device(member(j)), device_id_type=MESH)

    pl.semaphore_wait(barrier, m + 2)

    def rows(c):
        return pl.ds(pl.multiple_of(c * ROWS, ROWS), ROWS)

    def load(c, k):
        return pltpu.make_async_copy(g_ref.at[tp ^ (2 * k), rows(c)], loc.at[c % 2, k], ls.at[c % 2, k])

    def swap(c, k):
        return push(g_ref.at[tp ^ 1 ^ (2 * k), rows(c)], pair.at[c, k], ss.at[k, c], rs.at[k, c], sib)

    def cross(c):
        return push(pair.at[c, 1], xr.at[c], ss.at[2, c], rs.at[2, c], across)

    def halves(h):
        return pl.ds(pl.multiple_of(h * half, half), half)

    def side(c):
        return push(pair.at[c, 0, halves(1 - par)], yr.at[c], ss.at[3, c], rs.at[3, c], beside)

    def bit(q):
        return pl.ds(pl.multiple_of(q * piece, piece), piece)

    def spread(c, q):
        return push(yr.at[c, bit(q)], zr.at[c, mine], zs.at[c, q], zq.at[c, mine], device(q))

    def spread_in(c, q):
        return push(yr.at[c, bit(q)], zr.at[c, q], zs.at[c, q], zq.at[c, q], device(q))

    def place(q):
        return pl.ds(pl.multiple_of(par * half + q * piece, piece), piece)

    def share(c, q):
        return push(fin.at[c, place(mine)], fin.at[c, place(mine)], fs.at[c, q], fq.at[c, mine], device(q))

    def share_in(c, q):
        return push(fin.at[c, place(q)], fin.at[c, place(q)], fs.at[c, q], fq.at[c, q], device(q))

    def back(c):
        return push(fin.at[c, halves(par)], fin.at[c, halves(par)], ss.at[4, c], rs.at[4, c], beside)

    def write(c):
        return pltpu.make_async_copy(fin.at[c], out_ref.at[rows(c)], os.at[c])

    def tiny(k, peer):
        return push(ta.at[k], tx.at[k], ts.at[k], tq.at[k], peer)

    def tiny_out(q):
        return push(ta.at[3], tz.at[mine], tzs.at[q], tzq.at[mine], device(q))

    def tiny_in(q):
        return push(ta.at[3], tz.at[q], tzs.at[q], tzq.at[q], device(q))

    peers = (sib, across, beside)
    ta[0] = t_ref[...]
    tiny(0, sib).start()

    @pl.loop(0, chunks + 6)
    def _(s):
        @pl.when(s < chunks)
        def _():
            for k in range(2):
                swap(s, k).start()
                load(s, k).start()

        for stage in (1, 2, 3):

            @pl.when(s == 2 * stage)
            def _():
                tiny(stage - 1, peers[stage - 1]).wait()
                ta[stage] = ta[stage - 1] + tx[stage - 1]
                if stage < 3:
                    tiny(stage, peers[stage]).start()
                else:

                    @pl.loop(1, m)
                    def _(j):
                        tiny_out(member(j)).start()

        c1 = s - 1

        @pl.when((c1 >= 0) & (c1 < chunks))
        def _():
            for k in (1, 0):
                load(c1, k).wait()
                swap(c1, k).wait_recv()
                pair[c1, k] = pair[c1, k] + loc[c1 % 2, k]
                if k == 1:
                    cross(c1).start()

        c2 = s - 2

        @pl.when((c2 >= 0) & (c2 < chunks))
        def _():
            cross(c2).wait_recv()
            pair[c2, 0] = pair[c2, 0] + xr[c2]
            side(c2).start()

        c3 = s - 3

        @pl.when((c3 >= 0) & (c3 < chunks))
        def _():
            side(c3).wait_recv()
            yr[c3] = yr[c3] + pair[c3, 0, halves(par)]

            @pl.loop(1, m)
            def _(j):
                spread(c3, member(j)).start()

        c4 = s - 4

        @pl.when((c4 >= 0) & (c4 < chunks))
        def _():
            fin[c4, place(mine)] = yr[c4, bit(mine)]

            @pl.loop(1, m)
            def _(j):
                spread_in(c4, member(j)).wait_recv()
                fin[c4, place(mine)] = fin[c4, place(mine)] + zr[c4, member(j)]

            @pl.loop(1, m)
            def _(j):
                share(c4, member(j)).start()

        c5 = s - 5

        @pl.when((c5 >= 0) & (c5 < chunks))
        def _():
            @pl.loop(1, m)
            def _(j):
                share_in(c5, member(j)).wait_recv()

            back(c5).start()

        c6 = s - 6

        @pl.when((c6 >= 0) & (c6 < chunks))
        def _():
            back(c6).wait_recv()
            write(c6).start()

    tz[mine] = ta[3]

    @pl.loop(1, m)
    def _(j):
        tiny_in(member(j)).wait_recv()

    tout_ref[...] = jnp.zeros_like(tout_ref)

    @pl.loop(0, m)
    def _(q):
        tout_ref[...] += tz[q]

    @pl.loop(1, m)
    def _(j):
        tiny_out(member(j)).wait_send()

    @pl.loop(0, chunks)
    def _(c):
        for k in range(2):
            swap(c, k).wait_send()
        cross(c).wait_send()
        side(c).wait_send()
        back(c).wait_send()
        write(c).wait()

        @pl.loop(1, m)
        def _(j):
            spread(c, member(j)).wait_send()
            share(c, member(j)).wait_send()


def reduce_all(grads, tiny, n, ident):
    chunks = grads.shape[1] // ROWS
    m = n // 2
    dma = pltpu.SemaphoreType.DMA
    tr = tiny.shape[0]
    return pl.pallas_call(
        functools.partial(reduce_kernel, n, chunks, tr),
        in_specs=[ANY, VM],
        out_specs=[ANY, VM],
        out_shape=[sds(grads.shape[1], 128), sds(tr, 128)],
        scratch_shapes=[
            pltpu.VMEM((2, 2, ROWS, 128), f32), pltpu.VMEM((chunks, 2, ROWS, 128), f32),
            pltpu.VMEM((chunks, ROWS, 128), f32), pltpu.VMEM((chunks, ROWS // 2, 128), f32),
            pltpu.VMEM((chunks, m, ROWS // 2 // m, 128), f32), pltpu.VMEM((chunks, ROWS, 128), f32),
            pltpu.VMEM((4, tr, 128), f32), pltpu.VMEM((3, tr, 128), f32), pltpu.VMEM((m, tr, 128), f32),
            dma((5, chunks)), dma((5, chunks)), dma((chunks, m)), dma((chunks, m)), dma((chunks, m)),
            dma((chunks, m)), dma((2, 2)), dma((chunks,)), dma((3,)), dma((3,)), dma((m,)), dma((m,)),
        ],
        compiler_params=pltpu.CompilerParams(
            collective_id=ident, has_side_effects=True, vmem_limit_bytes=60 << 20
        ),
        name="reduce",
    )(grads, tiny)


def column_pick():
    pick = np.zeros((19, WIN, WIN), np.float32)
    for a in range(WIN):
        for b in range(WIN):
            pick[a - b + WIN - 1, a, b] = 1.0
    return pick


def row_pick():
    pick = np.zeros((19, WIN, WIN, WIN, 2, 2, SUB), np.float32)
    for pr in range(WIN):
        for qr in range(WIN):
            for qc in range(WIN):
                pick[pr - qr + WIN - 1, qc, pr, 0, qr // 5, qc // 5, (qr % 5) * 5 + qc % 5] = 1.0
    return pick[:, :, :, 0].reshape(190, WIN * WT)


def bias_of(table):
    heads = table.shape[0]
    grid = table.reshape(heads, 19, 19)
    columns = jnp.einsum("hrd,dab->hary", grid, jnp.asarray(column_pick()).reshape(19, WIN, WIN).transpose(0, 1, 2), precision="highest") if False else jnp.einsum("hrd,dab->harb", grid, jnp.asarray(column_pick()), precision="highest")
    rows = jnp.dot(columns.reshape(heads * WIN, 190), jnp.asarray(row_pick()), precision="highest")
    rows = rows.reshape(heads, 2, 5, 2, 5, WT).transpose(0, 3, 1, 4, 2, 5)
    rows = rows.reshape(heads, 4, REAL, WT)
    return jnp.pad(rows, ((0, 0), (0, 0), (0, SUB - REAL), (0, 0))).reshape(heads, WT, WT)


def to_blocks(values):
    tail = values.shape[2:]
    return values.reshape((2, 2, NW, SUB) + tail) if False else values


def shift_along(x, axis, distance):
    count = lax.axis_size(axis)
    return lax.ppermute(x, axis, [((i - distance) % count, i) for i in range(count)])


def grid_of(tokens):
    return tokens.reshape(NW, 2, 2, SUB, -1).transpose(1, 0, 2, 3, 4).reshape(2, 6, SUB, -1)


def tokens_of(grid):
    return grid.reshape(2, NW, 2, SUB, -1).transpose(1, 0, 2, 3, 4).reshape(TOK, -1)


def shifted(tokens):
    grid = grid_of(tokens)
    right = shift_along(grid[:, :1], "tp", -1)
    grid = jnp.concatenate([grid[:, 1:], right], axis=1)
    below = shift_along(grid[:1], "sp", -1)
    return tokens_of(jnp.concatenate([grid[1:], below], axis=0))


def unshifted(tokens):
    grid = grid_of(tokens)
    above = shift_along(grid[1:], "sp", 1)
    grid = jnp.concatenate([above, grid[:1]], axis=0)
    left = shift_along(grid[:, 5:], "tp", 1)
    return tokens_of(jnp.concatenate([left, grid[:, :5]], axis=1))


def to_order(natural):
    values = natural.reshape(2, 5, NW, 2, 5, -1).transpose(2, 0, 3, 1, 4, 5).reshape(NW, 2, 2, REAL, -1)
    values = jnp.pad(values, ((0, 0), (0, 0), (0, 0), (0, SUB - REAL), (0, 0)))
    return values.reshape(TOK, -1)


def to_natural(tokens):
    values = tokens.reshape(NW, 2, 2, SUB, -1)[:, :, :, :REAL]
    values = values.reshape(NW, 2, 2, 5, 5, -1).transpose(1, 3, 0, 2, 4, 5)
    return values.reshape(10, 30, -1)


def shards(
    patches, merge_gain, merge_shift, merge_weight, first_gain, first_shift, input_weight,
    input_bias, position_table, output_weight, output_bias, second_gain, second_shift,
    expand_weight, expand_bias, shrink_weight, shrink_bias, page_map, valid_flags, cotangent,
):
    sp_count = lax.axis_size("sp")
    tp = lax.axis_index("tp")
    sp = lax.axis_index("sp")
    full_channels = 4.0 * C2

    small = jnp.concatenate(
        [input_bias.reshape(-1), expand_bias.reshape(-1), position_table.transpose(0, 2, 1).reshape(-1)]
    )
    small = jnp.pad(small, (0, 40 * 128 - small.shape[0])).reshape(40, 128)
    wqkv, wo, we, ws = [], [], [], []
    arrays = [small]
    for b in range(2):
        arrays += [input_weight[b].transpose(1, 0, 2), output_weight[b], expand_weight[b], shrink_weight[b]]
    full = gather_all(arrays, [None] + [1, 0, 0, 0] * 2, 1)
    small = full[0].reshape(4, 40 * 128)
    wqkv, wo, we, ws = full[1::4], full[2::4], full[3::4], full[4::4]
    bqkv, be, bias = [], [], []
    for b in range(2):
        ib = small[:, b * 256 : (b + 1) * 256].reshape(4, 2, 128)
        bqkv.append(jnp.concatenate([ib[:, :1], jnp.zeros((4, 1, 128), f32), ib[:, 1:]], axis=1).reshape(4, 1, 384))
        be.append(small[:, 512 + b * 512 : 1024 + b * 512].reshape(4, 1, 512))
    tables = small[:, 1536 : 1536 + 2888].reshape(4, 2, 4, 361).transpose(1, 0, 2, 3).reshape(2, 16, 361)
    bias, pull_bias = jax.vjp(lambda t: tuple(bias_of(t[b]) for b in range(2)), tables)

    valid = valid_flags.astype(f32)
    vgrid = valid.reshape(2, 5, 24, 5).transpose(0, 2, 1, 3).reshape(2, 24, REAL)
    vgrid = jnp.pad(vgrid, ((0, 0), (0, 0), (0, SUB - REAL)))
    below = shift_along(vgrid[:1], "sp", -1)
    vshift = jnp.roll(jnp.concatenate([vgrid[1:], below], axis=0), -1, axis=1)
    own = lambda grid: lax.dynamic_slice_in_dim(grid, 6 * tp, 6, 1)
    vtok = [tokens_of(own(vgrid)[..., None]), tokens_of(own(vshift)[..., None])]
    pages = jnp.concatenate([page_map, page_map[:1]], axis=0)
    pages = jnp.concatenate([pages, pages[:, :1]], axis=1)
    pages = lax.dynamic_slice(pages, (sp, 3 * tp), (2, 4))
    page = jnp.stack([pages[:, :3], pages[:, 1:]], axis=2).transpose(1, 0, 2)
    wrap_row = (jnp.arange(2) == 1) & (sp == sp_count - 1)
    wrap_col = (jnp.arange(2) == 1)[None, :] & (jnp.arange(NW) == NW - 1)[:, None] & (tp == 3)
    region = page * 4 + 2 * wrap_row[None, :, None].astype(jnp.int32) + wrap_col[:, None, :].astype(jnp.int32)
    region = jnp.broadcast_to(region[..., None], (NW, 2, 2, SUB)).reshape(TOK)
    regions = [jnp.zeros((TOK,), jnp.int32), region]
    mask_args = [
        (regions[b].reshape(TOK, 1), regions[b].reshape(NW, 1, WT), vtok[b].reshape(NW, 1, WT), vtok[b])
        for b in range(2)
    ]

    gain = merge_gain.reshape(2, 2, 64).transpose(1, 0, 2).reshape(256)
    offset = merge_shift.reshape(2, 2, 64).transpose(1, 0, 2).reshape(256)
    weight = merge_weight.reshape(2, 2, 64, C).transpose(1, 0, 2, 3).reshape(256, C)
    quads = patches.reshape(10, 2, 120, 128).transpose(0, 2, 1, 3).reshape(1200, 256)
    partial = jnp.dot(quads * gain, weight, precision="high").reshape(10, 4, 30, C).transpose(1, 0, 2, 3).reshape(4, 300, C)
    moment = lax.psum((jnp.sum(quads, axis=1), jnp.sum(quads * quads, axis=1)), "tp")
    vecs = lax.psum((jnp.dot(gain, weight, precision="highest"), jnp.dot(offset, weight, precision="highest")), "tp")
    mean = moment[0] / full_channels
    inverse = lax.rsqrt(moment[1] / full_channels - mean * mean + epsilon)
    total = lax.psum_scatter(partial, "tp", scatter_dimension=0, tiled=False)
    mine = lambda v: lax.dynamic_slice_in_dim(v.reshape(10, 4, 30), tp, 1, 1).reshape(300, 1)
    field_nat = mine(inverse) * (total - mine(mean) * vecs[0]) + vecs[1]
    field = to_order(field_nat)

    squares = []
    saved = []
    row = lambda x: x.reshape(1, C)
    for b in range(2):
        if b == 1:
            field = shifted(field)
        middle, qkv, p, att, sq = attn_fwd(
            field, row(first_gain[b]), row(first_shift[b]), wqkv[b], bqkv[b], wo[b], row(output_bias[b]),
            bias[b], mask_args[b],
        )
        out, hid, slope, sqb, sqo = mlp_fwd(
            middle, row(second_gain[b]), row(second_shift[b]), we[b], be[b], ws[b], row(shrink_bias[b]), vtok[b]
        )
        squares += [jnp.sum(sq), jnp.sum(sqb)]
        saved.append((field, qkv, p, att, middle, hid, slope))
        field = out
    squares.append(jnp.sum(sqo))
    out_nat = to_natural(unshifted(field))
    output = lax.all_to_all(out_nat.reshape(10, 30, 4, 128), "tp", 2, 1, tiled=True).reshape(10, 120, 128)

    cot = lax.all_to_all(cotangent.reshape(10, 120, 1, 128), "tp", 1, 2, tiled=True).reshape(10, 30, C)
    grad = shifted(to_order(cot))
    grads = [None, None]
    pack = None
    for b in (1, 0):
        field_in, qkv, p, att, middle, hid, slope = saved[b]
        gm, pack, dbe, small2 = mlp_bwd(
            grad, middle, row(second_gain[b]), row(second_shift[b]), we[b], ws[b], hid, slope, pack, 1 - b
        )
        grad, pack, dbqkv, dbias, small1 = attn_bwd(
            gm, field_in, row(first_gain[b]), row(first_shift[b]), wqkv[b], wo[b], qkv, p, att, pack, 5 - b
        )
        grads[b] = (dbqkv, dbe, dbias, small1, small2)
        if b == 1:
            grad = unshifted(grad)
    gf = to_natural(grad)
    m1 = jnp.sum(gf * vecs[0], axis=-1)
    m2 = jnp.sum(gf * (field_nat.reshape(10, 30, C) - vecs[1]), axis=-1)
    full = lax.all_gather(gf, "tp", axis=1, tiled=True).reshape(1200, C)
    m1 = lax.all_gather(m1, "tp", axis=1, tiled=True).reshape(1200, 1) / full_channels
    m2 = lax.all_gather(m2, "tp", axis=1, tiled=True).reshape(1200, 1) / full_channels
    xhat = (quads - mean[:, None]) * inverse[:, None]
    gmerged = lax.dot_general(full, weight, NT, precision="high")
    dmw = lax.dot_general(xhat * gain + offset, full, TN, precision="high")
    dmg = jnp.sum(gmerged * xhat, axis=0)
    dms = jnp.sum(gmerged, axis=0)
    gquads = inverse[:, None] * (gmerged * gain - m1 - xhat * m2)
    patches_grad = gquads.reshape(10, 120, 2, 128).transpose(0, 2, 1, 3).reshape(20, 240, 64)

    dtables = pull_bias((grads[0][2], grads[1][2]))[0]
    pieces = [
        jnp.stack([grads[b][0] for b in range(2)]), jnp.stack([grads[b][1] for b in range(2)]), dtables,
        jnp.stack([grads[b][3][:3] for b in range(2)]), jnp.stack([grads[b][4][:3] for b in range(2)]),
        jnp.stack(squares), jnp.sum(vtok[0]).reshape(1),
    ]
    line = jnp.concatenate([x.reshape(-1) for x in pieces])
    tiny = jnp.pad(line, (0, 200 * 128 - line.shape[0])).reshape(200, 128)
    packed, tiny = reduce_all(pack, tiny, sp_count, 2)
    line, parts, at = tiny.reshape(-1), [], 0
    for x in pieces:
        parts.append(line[at : at + x.size].reshape(x.shape))
        at += x.size
    dbqkv, dbe, dtab, small1, small2, sums, count = parts
    count = count[0]
    mlp = packed[:8192].reshape(2, 2, 4, 512, 128)[::-1]
    att = packed[8192:].reshape(2, 2048, 128)[::-1]
    g_qkv = att[:, :1536].reshape(2, 3, 512, 128).transpose(0, 2, 1, 3)
    g_wo = att[:, 1536:].reshape(2, 4, 128, 128).transpose(0, 2, 1, 3).reshape(2, 128, 512)
    g_we = mlp[:, 0].transpose(0, 2, 1, 3).reshape(2, 512, 512)
    g_ws = mlp[:, 1].transpose(0, 2, 1, 3).reshape(2, 512, 512)
    own4 = lambda x, axis: lax.dynamic_index_in_dim(x, tp, axis, keepdims=False)
    dbqkv = own4(dbqkv, 1).reshape(2, 3, 128)
    g_bias = jnp.stack([dbqkv[:, 0], dbqkv[:, 2]], axis=1)
    g_be = own4(dbe, 1).reshape(2, 512)
    g_tab = own4(dtab.reshape(2, 4, 4, 361), 1).transpose(0, 2, 1)
    dmw, dmg, dms = lax.psum((dmw, dmg, dms), "sp")
    back = lambda x: x.reshape((2, 2, 64) + x.shape[1:]).swapaxes(0, 1).reshape((4, 64) + x.shape[1:])
    rms = jnp.sqrt(sums / (count * C))
    return (
        output, patches_grad, back(dmg), back(dms), back(dmw), small1[:, 0], small1[:, 1], g_qkv, g_bias,
        g_tab, g_wo, small1[:, 2], small2[:, 0], small2[:, 1], g_we, g_be, g_ws, small2[:, 2], rms,
    )


def solution(mesh):
    placed = (
        P("sp", None, "tp"), P(None, "tp"), P(None, "tp"), P(None, "tp", None), P(), P(),
        P(None, None, None, "tp"), P(None, None, "tp"), P(None, None, "tp"), P(None, "tp", None),
        P(), P(), P(), P(None, None, "tp"), P(None, "tp"), P(None, "tp", None), P(), P(),
        P("sp", None), P("sp", None, "tp"),
    )
    results = (
        P("sp", None, "tp"), P("sp", None, "tp"), P(None, "tp"), P(None, "tp"), P(None, "tp", None),
        P(), P(), P(None, None, None, "tp"), P(None, None, "tp"), P(None, None, "tp"),
        P(None, "tp", None), P(), P(), P(), P(None, None, "tp"), P(None, "tp"), P(None, "tp", None),
        P(), P(),
    )
    return jax.shard_map(shards, mesh=mesh, in_specs=placed, out_specs=results, check_vma=False)
```

```python
import functools

import jax
import jax.numpy as jnp
import numpy as np
from jax import lax
from jax.experimental import pallas as pl
from jax.experimental.pallas import tpu as pltpu
from jax.sharding import PartitionSpec as P

C = 512
HD = 32
C2 = 256
WIN = 10
SHIFT = 5
SUB = 32
REAL = 25
WT = 128
TOK = 384
NW = 3
GROUP = 4

bf16 = jnp.bfloat16
f32 = jnp.float32
epsilon = 1e-05
masked = -1000000000.0

NN = (((1,), (0,)), ((), ()))
NT = (((1,), (1,)), ((), ()))
TN = (((0,), (0,)), ((), ()))


def split(x):
    high = x.astype(bf16)
    return high, (x - high.astype(f32)).astype(bf16)


def mm(a, b, dims):
    return lax.dot_general(a, b, dims, preferred_element_type=f32)


def mm3(a, b, dims):
    return mm(a[0], b[0], dims) + (mm(a[0], b[1], dims) + mm(a[1], b[0], dims))


def normalized(x):
    center = x - jnp.mean(x, axis=-1, keepdims=True)
    rho = lax.rsqrt(jnp.mean(center * center, axis=-1, keepdims=True) + epsilon)
    return center * rho, rho


def head_masks(dtype):
    lane = lax.broadcasted_iota(jnp.int32, (1, 128), 1) // HD
    return [(lane == h).astype(f32).astype(dtype) for h in range(GROUP)]


def stacked(pair, masks):
    return tuple(jnp.concatenate([part * m for m in masks], axis=0) for part in pair)


def side_by_side(pair):
    return tuple(
        jnp.concatenate([part[h * WT : (h + 1) * WT] for h in range(GROUP)], axis=1)
        for part in pair
    )


def colsum(x):
    return jnp.sum(x, axis=0, keepdims=True)


def attn_fwd_kernel(
    field_ref, gain_ref, shift_ref, wqkv_ref, bqkv_ref, wo_ref, bo_ref, bias_ref,
    regc_ref, regr_ref, valr_ref, valc_ref,
    middle_ref, qkv_ref, p_ref, att_ref, sq_ref,
    nh, nl, mixed,
):
    g = pl.program_id(0)

    @pl.when(g == 0)
    def _():
        xhat, _ = normalized(field_ref[...])
        nh[...], nl[...] = split(xhat * gain_ref[...] + shift_ref[...])
        mixed[...] = jnp.broadcast_to(bo_ref[...], mixed.shape)

    w = jnp.concatenate([wqkv_ref[0, j] for j in range(3)], axis=1)
    qkv = mm3((nh[...], nl[...]), split(w), NN) + bqkv_ref[0]
    lane = lax.broadcasted_iota(jnp.int32, (1, 3 * 128), 1)
    qkv = qkv * jnp.where(lane < 128, HD ** (-0.5), 1.0)
    qkv_ref[0] = qkv
    masks = head_masks(bf16)
    bias = bias_ref[...].reshape(GROUP * WT, WT)
    eye = lax.broadcasted_iota(jnp.int32, (WT, WT), 0) == lax.broadcasted_iota(jnp.int32, (WT, WT), 1)
    for i in range(NW):
        rows = pl.ds(i * WT, WT)
        here = qkv_ref[0, rows, :]
        q4 = stacked(split(here[:, :128]), masks)
        k = split(here[:, 128:256])
        v4 = stacked(split(here[:, 256:]), masks)
        allowed = (regc_ref[rows, :] == regr_ref[i]) & (valr_ref[i] > 0) | eye
        allowed = jnp.concatenate([allowed.astype(f32)] * GROUP, axis=0) > 0
        s = jnp.where(allowed, mm3(q4, k, NT) + bias, masked)
        e = jnp.exp(s - jnp.max(s, axis=-1, keepdims=True))
        p = e / jnp.sum(e, axis=-1, keepdims=True)
        p_ref[0, i] = p
        att_ref[0, rows, :] = mm3(side_by_side(split(p)), v4, NN)
    mixed[...] += mm3(split(att_ref[0]), split(wo_ref[0]), NN)

    @pl.when(g == GROUP - 1)
    def _():
        middle_ref[...] = field_ref[...] + mixed[...]
        sq_ref[...] = colsum(mixed[...] * mixed[...] * valc_ref[...])


def whole(shape):
    return pl.BlockSpec(shape, lambda g: (0,) * len(shape))


def part(shape):
    return pl.BlockSpec((1,) + shape, lambda g: (g,) + (0,) * len(shape))


def sds(*shape):
    return jax.ShapeDtypeStruct(shape, f32)


BIG = pltpu.CompilerParams(vmem_limit_bytes=56 << 20)


def attn_fwd(field, gain, shift, wqkv, bqkv, wo, bo, bias, masks):
    regc, regr, valr, valc = masks
    return pl.pallas_call(
        attn_fwd_kernel,
        grid=(4,),
        in_specs=[
            whole((TOK, C)), whole((1, C)), whole((1, C)), part((3, C, 128)), part((1, 384)),
            part((128, C)), whole((1, C)), pl.BlockSpec((GROUP, WT, WT), lambda g: (g, 0, 0)),
            whole((TOK, 1)), whole((NW, 1, WT)), whole((NW, 1, WT)), whole((TOK, 1)),
        ],
        out_specs=[
            whole((TOK, C)), part((TOK, 384)), part((NW, GROUP * WT, WT)), part((TOK, 128)),
            whole((1, C)),
        ],
        out_shape=[
            sds(TOK, C), sds(4, TOK, 384), sds(4, NW, GROUP * WT, WT), sds(4, TOK, 128), sds(1, C),
        ],
        scratch_shapes=[pltpu.VMEM((TOK, C), bf16), pltpu.VMEM((TOK, C), bf16), pltpu.VMEM((TOK, C), f32)],
        compiler_params=BIG,
        name="attn_fwd",
    )(field, gain, shift, wqkv, bqkv, wo, bo, bias, regc, regr, valr, valc)


def mlp_fwd_kernel(
    mid_ref, gain_ref, shift_ref, we_ref, be_ref, ws_ref, bs_ref, valc_ref,
    out_ref, hid_ref, slope_ref, sq_ref, sqo_ref,
    nh, nl, branch,
):
    g = pl.program_id(0)

    @pl.when(g == 0)
    def _():
        xhat, _ = normalized(mid_ref[...])
        nh[...], nl[...] = split(xhat * gain_ref[...] + shift_ref[...])
        branch[...] = jnp.broadcast_to(bs_ref[...], branch.shape)

    pre = mm3((nh[...], nl[...]), split(we_ref[0]), NN) + be_ref[0]
    phi = 0.5 * (1.0 + lax.erf(pre * (2 ** -0.5)))
    hidden = pre * phi
    hid_ref[0] = hidden
    slope_ref[0] = phi + pre * (jnp.exp(-0.5 * pre * pre) * ((2 * np.pi) ** -0.5))
    branch[...] += mm3(split(hidden), split(ws_ref[0]), NN)

    @pl.when(g == 3)
    def _():
        out = mid_ref[...] + branch[...]
        out_ref[...] = out
        sq_ref[...] = colsum(branch[...] * branch[...] * valc_ref[...])
        sqo_ref[...] = colsum(out * out * valc_ref[...])


def mlp_fwd(mid, gain, shift, we, be, ws, bs, valc):
    return pl.pallas_call(
        mlp_fwd_kernel,
        grid=(4,),
        in_specs=[
            whole((TOK, C)), whole((1, C)), whole((1, C)), part((C, 512)), part((1, 512)),
            part((512, C)), whole((1, C)), whole((TOK, 1)),
        ],
        out_specs=[whole((TOK, C)), part((TOK, 512)), part((TOK, 512)), whole((1, C)), whole((1, C))],
        out_shape=[sds(TOK, C), sds(4, TOK, 512), sds(4, TOK, 512), sds(1, C), sds(1, C)],
        scratch_shapes=[pltpu.VMEM((TOK, C), bf16), pltpu.VMEM((TOK, C), bf16), pltpu.VMEM((TOK, C), f32)],
        compiler_params=BIG,
        name="mlp_fwd",
    )(mid, gain, shift, we, be, ws, bs, valc)


def norm_back(x, gain, grad_y):
    xhat, rho = normalized(x)
    gh = grad_y * gain
    grad_x = rho * (
        gh - jnp.mean(gh, axis=-1, keepdims=True) - xhat * jnp.mean(gh * xhat, axis=-1, keepdims=True)
    )
    return grad_x, colsum(grad_y * xhat), colsum(grad_y)


MESH = pl.DeviceIdType.MESH
ANY = pl.BlockSpec(memory_space=pl.ANY)
VM = pl.BlockSpec(memory_space=pltpu.VMEM)


def here():
    sp, tp = lax.axis_index("sp"), lax.axis_index("tp")
    return sp, tp, (sp, tp ^ 1), (sp, tp ^ 2), (sp ^ 1, tp)


def meet(peers):
    barrier = pltpu.get_barrier_semaphore()
    for peer in peers:
        pl.semaphore_signal(barrier, inc=1, device_id=peer, device_id_type=MESH)
    pl.semaphore_wait(barrier, len(peers))


def push(src, dst, send, recv, peer):
    return pltpu.make_async_remote_copy(
        src_ref=src, dst_ref=dst, send_sem=send, recv_sem=recv, device_id=peer, device_id_type=MESH
    )


def gather_kernel(axes, count, *refs):
    ins, outs = refs[:count], refs[count : 2 * count]
    send, recv, local = refs[2 * count :]
    sp, tp, sib, across, beside = here()
    par = sp & 1
    meet((sib, across, beside))

    def cut(ref, axis, half):
        if axis is None:
            return ref
        size = ref.shape[axis] // 2
        index = [slice(None)] * len(ref.shape)
        index[axis] = pl.ds(pl.multiple_of(half * size, size), size)
        return ref.at[tuple(index)]

    def own(i):
        return pltpu.make_async_copy(ins[i], outs[i].at[tp], local.at[i])

    def to_sib(i):
        return push(ins[i], outs[i].at[tp], send.at[0, i], recv.at[0, i], sib)

    def to_across(i):
        return push(
            cut(ins[i], axes[i], par), cut(outs[i].at[tp], axes[i], par), send.at[1, i], recv.at[1, i], across
        )

    def far(i, half):
        return cut(outs[i].at[tp ^ 2], axes[i], half)

    def to_beside(i):
        return push(far(i, par), far(i, par), send.at[2, i], recv.at[2, i], beside)

    def on_first(i):
        return push(far(i, par), far(i, par), send.at[3, i], recv.at[3, i], sib)

    def on_second(i):
        return push(far(i, 1 - par), far(i, 1 - par), send.at[4, i], recv.at[4, i], sib)

    for i in range(count):
        to_across(i).start()
        to_sib(i).start()
        own(i).start()
    for i in range(count + 1):
        if i < count:
            to_across(i).wait_recv()
            on_first(i).start()
            if axes[i] is not None:
                to_beside(i).start()
        if i > 0 and axes[i - 1] is not None:
            to_beside(i - 1).wait_recv()
            on_second(i - 1).start()
    for i in range(count):
        own(i).wait()
        to_sib(i).wait()
        to_across(i).wait_send()
        on_first(i).wait()
        if axes[i] is not None:
            to_beside(i).wait_send()
            on_second(i).wait()


def gather_all(arrays, axes, ident):
    count = len(arrays)
    return pl.pallas_call(
        functools.partial(gather_kernel, axes, count),
        in_specs=[ANY] * count,
        out_specs=[ANY] * count,
        out_shape=[jax.ShapeDtypeStruct((4,) + a.shape, a.dtype) for a in arrays],
        scratch_shapes=[
            pltpu.SemaphoreType.DMA((5, count)), pltpu.SemaphoreType.DMA((5, count)),
            pltpu.SemaphoreType.DMA((count,)),
        ],
        compiler_params=pltpu.CompilerParams(collective_id=ident, has_side_effects=True),
        name="gather",
    )(*arrays)


ROWS = 512
HALF = ROWS // 2
MLP_ROWS, ATT_ROWS = 4096, 2560
MLP_CH, ATT_CH = MLP_ROWS // ROWS, ATT_ROWS // ROWS
FULL_CH = 2 * (MLP_CH + ATT_CH)
CHUNKS = FULL_CH + 2
BASE = (0, MLP_ROWS, MLP_ROWS + ATT_ROWS, 2 * MLP_ROWS + ATT_ROWS)
FIRST = 4
AG_STEP = 15
MERGE_STEP = 20
TINY_STEP = 25
STEPS = FIRST + CHUNKS + 6
TINY = 40
COLS = [(0, 0, 0, 1), (0, 1, 1, 0), (1, 0, 1, 1), (1, 1, 2, 0), (2, 0, 2, 1)]


def at(w, sr, sc):
    return pl.ds(w * WT + sr * 64 + sc * SUB, SUB)


def bwd_kernel(n, *refs):
    (
        cot_ref, mid_ref, field_ref, g1_ref, b1_ref, g2_ref, b2_ref, we_ref, ws_ref, wqkv_ref, wo_ref,
        hid_ref, slope_ref, qkv_ref, p_ref, att_ref, sq_ref, q_ref, mw_ref, vec_ref, mg_ref, stat_ref, f0_ref,
    ) = refs[:23]
    pack, gall, exall, out_ref, gq_ref, tout_ref = refs[23:29]
    (
        nth, ntl, gh, gl, acc, dqkv, gf, gbuf, moved, ext, extin, qbuf,
        loc, pair, yr, zr, fin, ta, tx, tz,
        gsem, mvs, mvr, ags, agr, agl, msem, ss, rs, zs, zq, fs, fq, ls, os, ts, tq, tzs, tzq,
    ) = refs[29:]
    step = pl.program_id(0)
    dmw, gqbuf = moved.at[pl.ds(0, 256)], dqkv.at[:, pl.ds(0, 256)]
    sp, tp, sib, across, beside = here()
    par, mine = sp & 1, sp // 2
    m = n // 2
    piece = HALF // m
    up, right = lax.rem(sp + 1, n), lax.rem(tp + 1, 4)
    down, left = lax.rem(sp + n - 1, n), lax.rem(tp + 3, 4)

    def member(j):
        return lax.rem(mine + j, m)

    def device(q):
        return (q * 2 + par, tp)

    @pl.when(step == 0)
    def _():
        barrier = pltpu.get_barrier_semaphore()
        near = [sib, across, beside, (up, tp), (down, tp), (sp, right), (sp, left), (up, right), (down, left)]
        for peer in near:
            pl.semaphore_signal(barrier, inc=1, device_id=peer, device_id_type=MESH)

        @pl.loop(1, m)
        def _(j):
            pl.semaphore_signal(barrier, inc=1, device_id=device(member(j)), device_id_type=MESH)

        pl.semaphore_wait(barrier, len(near) + m - 1)
        ta[...] = jnp.zeros_like(ta)
        ta[0, 28:36, :] = sq_ref[...]
        gf[...] = cot_ref[...]

    def packed(kind, t):
        size = MLP_ROWS if kind % 2 == 0 else ATT_ROWS
        slot = t % 2
        return pltpu.make_async_copy(
            gbuf.at[slot, pl.ds(0, size)], pack.at[t, pl.ds(BASE[kind], size)], gsem.at[slot]
        )

    def moves():
        todo = [
            (at(2, 0, 1), at(0, 1, 0), (sp, right)),
            (at(2, 1, 1), at(0, 0, 0), (up, right)),
        ]
        for w0, s0, w1, s1 in COLS:
            todo.append((at(w0, 1, s0), at(w1, 0, s1), (up, tp)))
        return [push(acc.at[src], moved.at[dst], mvs.at[i], mvr.at[i], peer) for i, (src, dst, peer) in enumerate(todo)]

    def kept():
        for w0, s0, w1, s1 in COLS:
            moved[at(w1, 1, s1), :] = acc[at(w0, 0, s0), :]

    for kind, b in ((0, 1), (2, 0)):
        lo = 4 * kind

        @pl.when((step >= lo) & (step < lo + 4))
        def _(kind=kind, b=b, lo=lo):
            t = step - lo

            @pl.when(step == lo)
            def _():
                if b == 0:
                    for copy in moves():
                        copy.wait()
                    gf[...] = moved[...]
                xhat, _ = normalized(mid_ref[0])
                nth[...], ntl[...] = split((xhat * g2_ref[b] + b2_ref[b]).T)
                gh[...], gl[...] = split(gf[...])
                acc[...] = jnp.zeros_like(acc)

            slot = t % 2
            grad = (gh[...], gl[...])
            dws = mm3(split(hid_ref[0].T), grad, NN)
            for j in range(4):
                gbuf[slot, 2048 + j * 512 : 2560 + j * 512, :] = dws[:, j * 128 : (j + 1) * 128]
            dpre = mm3(grad, split(ws_ref[0]), NT) * slope_ref[0]
            ta[0, pl.ds(12 + b * 4 + t, 1), :] = colsum(dpre)
            pair_ = split(dpre)
            dwe = mm3((nth[...], ntl[...]), pair_, NN)
            for j in range(4):
                gbuf[slot, j * 512 : (j + 1) * 512, :] = dwe[:, j * 128 : (j + 1) * 128]
            acc[...] += mm3(pair_, split(we_ref[0]), NT)

            @pl.when(t > 0)
            def _():
                packed(kind, t - 1).wait()

            packed(kind, t).start()

            @pl.when(t == 3)
            def _():
                grad_x, dgain, dshift = norm_back(mid_ref[0], g2_ref[b], acc[...])
                ta[0, 6 + 3 * b : 7 + 3 * b, :] = dgain
                ta[0, 7 + 3 * b : 8 + 3 * b, :] = dshift
                ta[0, 8 + 3 * b : 9 + 3 * b, :] = colsum(gf[...])
                gf[...] = gf[...] + grad_x
                packed(kind, 3).wait()

    for kind, b in ((1, 1), (3, 0)):
        lo = 4 * kind

        @pl.when((step >= lo) & (step < lo + 4))
        def _(kind=kind, b=b, lo=lo):
            t = step - lo

            @pl.when(step == lo)
            def _():
                xhat, _ = normalized(field_ref[0])
                nth[...], ntl[...] = split((xhat * g1_ref[b] + b1_ref[b]).T)
                gh[...], gl[...] = split(gf[...])
                acc[...] = jnp.zeros_like(acc)

            slot = t % 2
            grad = (gh[...], gl[...])
            dwo = mm3(split(att_ref[0].T), grad, NN)
            for j in range(4):
                gbuf[slot, 1536 + j * 128 : 1664 + j * 128, :] = dwo[:, j * 128 : (j + 1) * 128]
            dout = mm3(grad, split(wo_ref[0]), NT)
            masks = head_masks(bf16)
            dbias = jnp.zeros((GROUP * WT, WT), f32)
            for i in range(NW):
                rows = slice(i * WT, (i + 1) * WT)
                seen = qkv_ref[0, pl.ds(i * WT, WT), :]
                q4 = stacked(split(seen[:, :128]), masks)
                k4 = stacked(split(seen[:, 128:256]), masks)
                v = split(seen[:, 256:])
                p = p_ref[0, i]
                do4 = stacked(split(dout[rows]), masks)
                dp = mm3(do4, v, NT)
                ds = p * (dp - jnp.sum(p * dp, axis=-1, keepdims=True))
                dbias = dbias + ds
                dpair = split(ds)
                dqkv[pl.ds(i * WT, WT), 0:128] = mm3(side_by_side(dpair), k4, NN) * HD ** (-0.5)
                dqkv[pl.ds(i * WT, WT), 128:256] = mm3(dpair, q4, TN)
                dqkv[pl.ds(i * WT, WT), 256:384] = mm3(split(p), do4, TN)
            gbuf[slot, 2048:2560, :] = dbias
            grads = dqkv[...]
            ta[0, pl.ds(20 + b * 4 + t, 1), 0:384] = colsum(grads)
            pair_ = split(grads)
            dw = mm3((nth[...], ntl[...]), pair_, NN)
            for j in range(3):
                gbuf[slot, j * 512 : (j + 1) * 512, :] = dw[:, j * 128 : (j + 1) * 128]
            w = jnp.concatenate([wqkv_ref[0, j] for j in range(3)], axis=1)
            acc[...] += mm3(pair_, split(w), NT)

            @pl.when(t > 0)
            def _():
                packed(kind, t - 1).wait()

            packed(kind, t).start()

            @pl.when(t == 3)
            def _():
                grad_x, dgain, dshift = norm_back(field_ref[0], g1_ref[b], acc[...])
                ta[0, 3 * b : 1 + 3 * b, :] = dgain
                ta[0, 1 + 3 * b : 2 + 3 * b, :] = dshift
                ta[0, 2 + 3 * b : 3 + 3 * b, :] = colsum(gf[...])
                acc[...] = gf[...] + grad_x
                if b == 1:
                    for copy in moves():
                        copy.start()
                    kept()
                packed(kind, 3).wait()

    def ag(k, src, dst, peer, which):
        return push(src, dst, ags.at[which, k], agr.at[which, k], peer)

    def ag_copies(k):
        own = (acc, ext)
        whole_ = (gall, exall)
        return [
            ag(k, own[w], whole_[w].at[tp], (sib, across)[k], w) if k < 2
            else ag(k, whole_[w].at[tp ^ 2], whole_[w].at[tp ^ 2], sib, w)
            for w in range(2)
        ]

    @pl.when(step == AG_STEP)
    def _():
        m2 = jnp.sum(acc[...] * (f0_ref[...] - vec_ref[1:2, :]), axis=-1, keepdims=True)
        lane = lax.broadcasted_iota(jnp.int32, (TOK, 128), 1)
        tall = jnp.where(lane == 2, m2, stat_ref[...])
        ext[...] = tall.T[0:8, :]
        for k in range(2):
            for copy in ag_copies(k):
                copy.start()

    @pl.when(step == MERGE_STEP - 1)
    def _():
        for copy in ag_copies(1):
            copy.wait()
        for copy in ag_copies(2):
            copy.start()
        for copy in ag_copies(0):
            copy.wait()

    @pl.when((step >= MERGE_STEP) & (step < MERGE_STEP + 4))
    def _():
        i = step - MERGE_STEP
        t = tp ^ i

        @pl.when(i == 2)
        def _():
            for copy in ag_copies(2):
                copy.wait()

        fetch = [pltpu.make_async_copy(q_ref.at[t], qbuf, msem.at[0])]
        fetch[0].start()

        @pl.when(i == 0)
        def _():
            dmw[...] = jnp.zeros((256, C), f32)
            gf[...] = acc[...]
            extin[...] = ext[...]

        @pl.when(i > 0)
        def _():
            two = [
                pltpu.make_async_copy(gall.at[t], gf, msem.at[1]),
                pltpu.make_async_copy(exall.at[t], extin, msem.at[2]),
            ]
            for copy in two:
                copy.start()
            for copy in two:
                copy.wait()

        fetch[0].wait()
        wide = jnp.concatenate([extin[...], jnp.zeros((120, TOK), f32)], axis=0).T
        mean, inv, m2 = wide[:, 0:1], wide[:, 1:2], wide[:, 2:3]
        full = gf[...]
        m1 = jnp.sum(full * vec_ref[0:1, :], axis=-1, keepdims=True) / (4.0 * C2)
        m2 = m2 / (4.0 * C2)
        fpair = split(full)
        xhat = (qbuf[...] - mean) * inv
        gmerged = mm3(fpair, split(mw_ref[...]), NT)
        dmw[...] += mm3(split((xhat * mg_ref[0:1, :] + mg_ref[1:2, :]).T), fpair, NN)
        row = pl.ds(36 + tp, 1)
        ta[0, row, 0:256] += colsum(gmerged * xhat)
        ta[0, row, 256:512] += colsum(gmerged)

        @pl.when(i > 0)
        def _():
            pltpu.make_async_copy(gqbuf, gq_ref.at[t], msem.at[3]).wait()

        gqbuf[...] = inv * (gmerged * mg_ref[0:1, :] - m1 - xhat * m2)
        pltpu.make_async_copy(gqbuf, gq_ref.at[t], msem.at[3]).start()

        @pl.when(i == 3)
        def _():
            pltpu.make_async_copy(gqbuf, gq_ref.at[t], msem.at[3]).wait()
            for k in range(2):
                for j in range(2):
                    low = (2 * k + j) * 128
                    pair[FULL_CH + k, 0, j * 256 : (j + 1) * 256, :] = dmw[:, low : low + 128]

    def rows(c):
        return pl.ds(pl.multiple_of(c * ROWS, ROWS), ROWS)

    def load(c, k):
        return pltpu.make_async_copy(pack.at[tp ^ (2 * k), rows(c)], loc.at[c % 2, k], ls.at[c % 2, k])

    def swap(c, k):
        return push(pack.at[tp ^ 1 ^ (2 * k), rows(c)], pair.at[c, k], ss.at[k, c], rs.at[k, c], sib)

    def cross(c):
        return push(pair.at[c, 1], fin.at[c], ss.at[2, c], rs.at[2, c], across)

    def halves(h):
        return pl.ds(pl.multiple_of(h * HALF, HALF), HALF)

    def side(c):
        return push(pair.at[c, 0, halves(1 - par)], yr.at[c], ss.at[3, c], rs.at[3, c], beside)

    def bit(q):
        return pl.ds(pl.multiple_of(q * piece, piece), piece)

    def spread(c, q, slot):
        return push(yr.at[c, bit(q)], zr.at[c, slot], zs.at[c % 4, q], zq.at[c, slot], device(q))

    def place(q):
        return pl.ds(pl.multiple_of(par * HALF + q * piece, piece), piece)

    def share(c, q, slot):
        return push(fin.at[c, place(slot)], fin.at[c, place(slot)], fs.at[c % 4, q], fq.at[c, slot], device(q))

    def back(c):
        return push(fin.at[c, halves(par)], fin.at[c, halves(par)], ss.at[4, c], rs.at[4, c], beside)

    def write(c):
        return pltpu.make_async_copy(fin.at[c], out_ref.at[rows(c)], os.at[c])

    def tiny(k, peer):
        return push(ta.at[k], tx.at[k], ts.at[k], tq.at[k], peer)

    def tiny_z(q, slot):
        return push(ta.at[3], tz.at[slot], tzs.at[q], tzq.at[slot], device(q))

    def stage(lag, first, last):
        c = step - FIRST - lag
        return c, (c >= first) & (c < last)

    peers = (sib, across, beside)
    for k in range(4):

        @pl.when(step == TINY_STEP + 2 * k)
        def _(k=k):
            if k > 0:
                tiny(k - 1, peers[k - 1]).wait()
                ta[k] = ta[k - 1] + tx[k - 1]
            if k < 3:
                tiny(k, peers[k]).start()
            else:
                tz[mine] = ta[3]

                @pl.loop(1, m)
                def _(j):
                    tiny_z(member(j), mine).start()

    c0, on0 = stage(0, 0, FULL_CH)

    @pl.when(on0)
    def _():
        for k in (1, 0):
            swap(c0, k).start()
            load(c0, k).start()

    c1, on1 = stage(1, 0, FULL_CH)

    @pl.when(on1)
    def _():
        for k in (1, 0):
            load(c1, k).wait()
            swap(c1, k).wait_recv()
            pair[c1, k] = pair[c1, k] + loc[c1 % 2, k]
            if k == 1:
                cross(c1).start()

    c2, on2 = stage(2, 0, CHUNKS)

    @pl.when(on2)
    def _():
        @pl.when(c2 < FULL_CH)
        def _():
            cross(c2).wait_recv()
            pair[c2, 0] = pair[c2, 0] + fin[c2]

        side(c2).start()

    c3, on3 = stage(3, 0, CHUNKS)

    @pl.when(on3)
    def _():
        side(c3).wait_recv()
        yr[c3] = yr[c3] + pair[c3, 0, halves(par)]

        @pl.loop(1, m)
        def _(j):
            spread(c3, member(j), mine).start()

    c4, on4 = stage(4, 0, CHUNKS)

    @pl.when(on4)
    def _():
        fin[c4, place(mine)] = yr[c4, bit(mine)]

        @pl.loop(1, m)
        def _(j):
            spread(c4, member(j), member(j)).wait_recv()
            fin[c4, place(mine)] = fin[c4, place(mine)] + zr[c4, member(j)]

        @pl.loop(1, m)
        def _(j):
            share(c4, member(j), mine).start()

    c5, on5 = stage(5, 0, CHUNKS)

    @pl.when(on5)
    def _():
        @pl.loop(1, m)
        def _(j):
            share(c5, member(j), member(j)).wait_recv()
            spread(c5, member(j), mine).wait_send()

        back(c5).start()

    c6, on6 = stage(6, 0, CHUNKS)

    @pl.when(on6)
    def _():
        back(c6).wait_recv()
        write(c6).start()

        @pl.loop(1, m)
        def _(j):
            share(c6, member(j), mine).wait_send()

    @pl.when(step == STEPS - 1)
    def _():
        @pl.loop(1, m)
        def _(j):
            tiny_z(member(j), member(j)).wait_recv()
            tiny_z(member(j), mine).wait_send()

        total = tz[0]
        for q in range(1, m):
            total = total + tz[q]
        tout_ref[...] = total

        @pl.loop(0, CHUNKS)
        def _(c):
            @pl.when(c < FULL_CH)
            def _():
                for k in range(2):
                    swap(c, k).wait_send()
                cross(c).wait_send()

            side(c).wait_send()
            back(c).wait_send()
            write(c).wait()


def backward(n, args, ident):
    m = n // 2
    dma = pltpu.SemaphoreType.DMA

    def fixed(shape):
        return pl.BlockSpec(shape, lambda s: (0,) * len(shape), pipeline_mode=pl.Buffered(1))

    def mlp_at(s):
        return jnp.where(s < 4, 4 + s, jnp.where(s < 8, 0, jnp.where(s < 12, s - 8, 3)))

    def att_at(s):
        return jnp.where(s < 4, 4, jnp.where(s < 8, s, jnp.where(s < 12, 0, jnp.where(s < 16, s - 12, 3))))

    def by(index, shape, mode=None):
        zeros = (0,) * len(shape)
        return pl.BlockSpec((1,) + shape, lambda s: (index(s),) + zeros, pipeline_mode=mode)

    one = pl.Buffered(1)
    lanes = (CHUNKS, ROWS, 128)
    in_specs = [
        fixed((TOK, C)), by(lambda s: jnp.where(s < 4, 1, 0), (TOK, C), one),
        by(lambda s: jnp.where(s < 8, 1, 0), (TOK, C), one),
        fixed((2, 1, C)), fixed((2, 1, C)), fixed((2, 1, C)), fixed((2, 1, C)),
        by(mlp_at, (C, 512)), by(mlp_at, (512, C)), by(att_at, (3, C, 128)), by(att_at, (128, C)),
        by(mlp_at, (TOK, 512)), by(mlp_at, (TOK, 512)), by(att_at, (TOK, 384)),
        by(att_at, (NW, GROUP * WT, WT)), by(att_at, (TOK, 128)),
        fixed((8, C)), ANY, fixed((256, C)), fixed((8, C)), fixed((8, 256)), fixed((TOK, 128)), fixed((TOK, C)),
    ]
    return pl.pallas_call(
        functools.partial(bwd_kernel, n),
        grid=(STEPS,),
        in_specs=in_specs,
        out_specs=[ANY, ANY, ANY, ANY, ANY, fixed((TINY, C))],
        out_shape=[
            sds(4, FULL_CH * ROWS, 128), sds(4, TOK, C), sds(4, 8, TOK), sds(CHUNKS * ROWS, 128),
            sds(4, TOK, 256), sds(TINY, C),
        ],
        scratch_shapes=[
            pltpu.VMEM((C, TOK), bf16), pltpu.VMEM((C, TOK), bf16), pltpu.VMEM((TOK, C), bf16),
            pltpu.VMEM((TOK, C), bf16), pltpu.VMEM((TOK, C), f32), pltpu.VMEM((TOK, 384), f32),
            pltpu.VMEM((TOK, C), f32), pltpu.VMEM((2, MLP_ROWS, 128), f32), pltpu.VMEM((TOK, C), f32),
            pltpu.VMEM((8, TOK), f32), pltpu.VMEM((8, TOK), f32), pltpu.VMEM((TOK, 256), f32),
            pltpu.VMEM((2, 2, ROWS, 128), f32), pltpu.VMEM((CHUNKS, 2, ROWS, 128), f32),
            pltpu.VMEM((CHUNKS, HALF, 128), f32), pltpu.VMEM((CHUNKS, m, HALF // m, 128), f32),
            pltpu.VMEM(lanes, f32), pltpu.VMEM((4, TINY, C), f32), pltpu.VMEM((3, TINY, C), f32),
            pltpu.VMEM((m, TINY, C), f32),
            dma((2,)), dma((7,)), dma((7,)), dma((2, 3)), dma((2, 3)), dma((2,)), dma((4,)),
            dma((5, CHUNKS)), dma((5, CHUNKS)), dma((4, m)), dma((CHUNKS, m)), dma((4, m)),
            dma((CHUNKS, m)), dma((2, 2)), dma((CHUNKS,)), dma((3,)), dma((3,)), dma((m,)), dma((m,)),
        ],
        compiler_params=pltpu.CompilerParams(
            collective_id=ident, has_side_effects=True, vmem_limit_bytes=60 << 20,
            dimension_semantics=("arbitrary",),
        ),
        name="backward",
    )(*args)


def column_pick():
    pick = np.zeros((19, WIN, WIN), np.float32)
    for a in range(WIN):
        for b in range(WIN):
            pick[a - b + WIN - 1, a, b] = 1.0
    return pick


def row_pick():
    pick = np.zeros((19, WIN, WIN, WIN, 2, 2, SUB), np.float32)
    for pr in range(WIN):
        for qr in range(WIN):
            for qc in range(WIN):
                pick[pr - qr + WIN - 1, qc, pr, 0, qr // 5, qc // 5, (qr % 5) * 5 + qc % 5] = 1.0
    return pick[:, :, :, 0].reshape(190, WIN * WT)


def bias_of(table):
    heads = table.shape[0]
    grid = table.reshape(heads, 19, 19)
    columns = jnp.einsum("hrd,dab->harb", grid, jnp.asarray(column_pick()), precision="highest")
    rows = jnp.dot(columns.reshape(heads * WIN, 190), jnp.asarray(row_pick()), precision="highest")
    rows = rows.reshape(heads, 2, 5, 2, 5, WT).transpose(0, 3, 1, 4, 2, 5)
    rows = rows.reshape(heads, 4, REAL, WT)
    return jnp.pad(rows, ((0, 0), (0, 0), (0, SUB - REAL), (0, 0))).reshape(heads, WT, WT)


def table_of(dbias):
    heads = dbias.shape[0]
    rows = dbias.reshape(heads, 4, SUB, WT)[:, :, :REAL].reshape(heads, 2, 2, 5, 5, WT)
    rows = rows.transpose(0, 2, 4, 1, 3, 5).reshape(heads * WIN, WIN * WT)
    columns = lax.dot_general(rows, jnp.asarray(row_pick()), NT, precision="highest")
    columns = columns.reshape(heads, WIN, 19, WIN)
    return jnp.einsum("harb,dab->hrd", columns, jnp.asarray(column_pick()), precision="highest")


def shift_along(x, axis, distance):
    count = lax.axis_size(axis)
    return lax.ppermute(x, axis, [((i - distance) % count, i) for i in range(count)])


def grid_of(tokens):
    return tokens.reshape(NW, 2, 2, SUB, -1).transpose(1, 0, 2, 3, 4).reshape(2, 6, SUB, -1)


def tokens_of(grid):
    return grid.reshape(2, NW, 2, SUB, -1).transpose(1, 0, 2, 3, 4).reshape(TOK, -1)


def shifted(tokens):
    grid = grid_of(tokens)
    right = shift_along(grid[:, :1], "tp", -1)
    grid = jnp.concatenate([grid[:, 1:], right], axis=1)
    below = shift_along(grid[:1], "sp", -1)
    return tokens_of(jnp.concatenate([grid[1:], below], axis=0))


def unshifted(tokens):
    grid = grid_of(tokens)
    above = shift_along(grid[1:], "sp", 1)
    grid = jnp.concatenate([above, grid[:1]], axis=0)
    left = shift_along(grid[:, 5:], "tp", 1)
    return tokens_of(jnp.concatenate([left, grid[:, :5]], axis=1))


def to_order(natural):
    values = natural.reshape(2, 5, NW, 2, 5, -1).transpose(2, 0, 3, 1, 4, 5).reshape(NW, 2, 2, REAL, -1)
    values = jnp.pad(values, ((0, 0), (0, 0), (0, 0), (0, SUB - REAL), (0, 0)))
    return values.reshape(TOK, -1)


def to_natural(tokens):
    values = tokens.reshape(NW, 2, 2, SUB, -1)[:, :, :, :REAL]
    values = values.reshape(NW, 2, 2, 5, 5, -1).transpose(1, 3, 0, 2, 4, 5)
    return values.reshape(10, 30, -1)


def shards(
    patches, merge_gain, merge_shift, merge_weight, first_gain, first_shift, input_weight,
    input_bias, position_table, output_weight, output_bias, second_gain, second_shift,
    expand_weight, expand_bias, shrink_weight, shrink_bias, page_map, valid_flags, cotangent,
):
    sp_count = lax.axis_size("sp")
    tp = lax.axis_index("tp")
    sp = lax.axis_index("sp")
    full_channels = 4.0 * C2

    small = jnp.concatenate(
        [input_bias.reshape(-1), expand_bias.reshape(-1), position_table.transpose(0, 2, 1).reshape(-1)]
    )
    small = jnp.pad(small, (0, 40 * 128 - small.shape[0])).reshape(40, 128)
    wqkv, wo, we, ws = [], [], [], []
    arrays = [small]
    for b in range(2):
        arrays += [input_weight[b].transpose(1, 0, 2), output_weight[b], expand_weight[b], shrink_weight[b]]
    full = gather_all(arrays, [None] + [1, 0, 0, 0] * 2, 1)
    small = full[0].reshape(4, 40 * 128)
    wqkv, wo, we, ws = full[1::4], full[2::4], full[3::4], full[4::4]
    bqkv, be, bias = [], [], []
    for b in range(2):
        ib = small[:, b * 256 : (b + 1) * 256].reshape(4, 2, 128)
        bqkv.append(jnp.concatenate([ib[:, :1], jnp.zeros((4, 1, 128), f32), ib[:, 1:]], axis=1).reshape(4, 1, 384))
        be.append(small[:, 512 + b * 512 : 1024 + b * 512].reshape(4, 1, 512))
    tables = small[:, 1536 : 1536 + 2888].reshape(4, 2, 4, 361).transpose(1, 0, 2, 3).reshape(2, 16, 361)
    bias = [bias_of(tables[b]) for b in range(2)]

    valid = valid_flags.astype(f32)
    vgrid = valid.reshape(2, 5, 24, 5).transpose(0, 2, 1, 3).reshape(2, 24, REAL)
    vgrid = jnp.pad(vgrid, ((0, 0), (0, 0), (0, SUB - REAL)))
    below = shift_along(vgrid[:1], "sp", -1)
    vshift = jnp.roll(jnp.concatenate([vgrid[1:], below], axis=0), -1, axis=1)
    own = lambda grid: lax.dynamic_slice_in_dim(grid, 6 * tp, 6, 1)
    vtok = [tokens_of(own(vgrid)[..., None]), tokens_of(own(vshift)[..., None])]
    pages = jnp.concatenate([page_map, page_map[:1]], axis=0)
    pages = jnp.concatenate([pages, pages[:, :1]], axis=1)
    pages = lax.dynamic_slice(pages, (sp, 3 * tp), (2, 4))
    page = jnp.stack([pages[:, :3], pages[:, 1:]], axis=2).transpose(1, 0, 2)
    wrap_row = (jnp.arange(2) == 1) & (sp == sp_count - 1)
    wrap_col = (jnp.arange(2) == 1)[None, :] & (jnp.arange(NW) == NW - 1)[:, None] & (tp == 3)
    region = page * 4 + 2 * wrap_row[None, :, None].astype(jnp.int32) + wrap_col[:, None, :].astype(jnp.int32)
    region = jnp.broadcast_to(region[..., None], (NW, 2, 2, SUB)).reshape(TOK)
    regions = [jnp.zeros((TOK,), jnp.int32), region]
    mask_args = [
        (regions[b].reshape(TOK, 1), regions[b].reshape(NW, 1, WT), vtok[b].reshape(NW, 1, WT), vtok[b])
        for b in range(2)
    ]

    gain = merge_gain.reshape(2, 2, 64).transpose(1, 0, 2).reshape(256)
    offset = merge_shift.reshape(2, 2, 64).transpose(1, 0, 2).reshape(256)
    weight = merge_weight.reshape(2, 2, 64, C).transpose(1, 0, 2, 3).reshape(256, C)
    quads = patches.reshape(2, 5, 2, 4, NW, 2, 5, 128).transpose(3, 4, 0, 5, 1, 6, 2, 7).reshape(4, NW, 4, REAL, 256)
    quads = jnp.pad(quads, ((0, 0), (0, 0), (0, 0), (0, SUB - REAL), (0, 0))).reshape(4, TOK, 256)
    partial = jnp.einsum("tpk,kd->tpd", quads * gain, weight, precision="high")
    moment = lax.psum((jnp.sum(quads, axis=2), jnp.sum(quads * quads, axis=2)), "tp")
    vecs = lax.psum((jnp.dot(gain, weight, precision="highest"), jnp.dot(offset, weight, precision="highest")), "tp")
    mean = moment[0] / full_channels
    inverse = lax.rsqrt(moment[1] / full_channels - mean * mean + epsilon)
    total = lax.psum_scatter(partial, "tp", scatter_dimension=0, tiled=False)
    mean, inverse = mean[tp][:, None], inverse[tp][:, None]
    field = inverse * (total - mean * vecs[0]) + vecs[1]
    field0 = field
    stat = jnp.concatenate([mean, inverse, jnp.zeros((TOK, 126), f32)], axis=1)

    squares = []
    saved = []
    row = lambda x: x.reshape(1, C)
    for b in range(2):
        if b == 1:
            field = shifted(field)
        middle, qkv, p, att, sq = attn_fwd(
            field, row(first_gain[b]), row(first_shift[b]), wqkv[b], bqkv[b], wo[b], row(output_bias[b]),
            bias[b], mask_args[b],
        )
        out, hid, slope, sqb, sqo = mlp_fwd(
            middle, row(second_gain[b]), row(second_shift[b]), we[b], be[b], ws[b], row(shrink_bias[b]), vtok[b]
        )
        squares += [sq, sqb]
        saved.append((field, qkv, p, att, middle, hid, slope))
        field = out
    squares.append(sqo)
    out_nat = to_natural(unshifted(field))
    output = lax.all_to_all(out_nat.reshape(10, 30, 4, 128), "tp", 2, 1, tiled=True).reshape(10, 120, 128)

    cot = lax.all_to_all(cotangent.reshape(10, 120, 1, 128), "tp", 1, 2, tiled=True).reshape(10, 30, C)
    cot = shifted(to_order(cot))
    count = jnp.pad(jnp.sum(vtok[0]).reshape(1, 1), ((0, 0), (0, C - 1)))
    squares = jnp.concatenate(squares + [count, jnp.zeros((2, C), f32)], axis=0)
    both = lambda i: jnp.concatenate([saved[0][i], saved[1][i]], axis=0)
    pile = lambda i: jnp.stack([saved[0][i], saved[1][i]], axis=0)
    join = lambda xs: jnp.concatenate(xs, axis=0)
    three = lambda x: x.reshape(2, 1, C)
    zero = jnp.zeros((6, C), f32)
    _, _, _, packed, gquads, tiny = backward(
        sp_count,
        (
            cot, pile(4), pile(0), three(first_gain), three(first_shift), three(second_gain), three(second_shift),
            join(we), join(ws), join(wqkv), join(wo), both(5), both(6), both(1), both(2), both(3),
            squares, quads, weight, jnp.concatenate([vecs[0][None], vecs[1][None], zero], axis=0),
            jnp.concatenate([gain[None], offset[None], zero[:, :256]], axis=0), stat, field0,
        ),
        2,
    )
    gquads = gquads.reshape(4, NW, 4, SUB, 256)[:, :, :, :REAL].reshape(4, NW, 2, 2, 5, 5, 2, 128)
    patches_grad = gquads.transpose(2, 4, 6, 0, 1, 3, 5, 7).reshape(20, 240, 64)
    small1, small2 = tiny[0:6].reshape(2, 3, C), tiny[6:12].reshape(2, 3, C)
    dbe, dbqkv = tiny[12:20].reshape(2, 4, 512), tiny[20:28, :384].reshape(2, 4, 384)
    sums, count = jnp.sum(tiny[28:33], axis=1), tiny[33, 0]
    dmgs = lax.dynamic_index_in_dim(tiny[36:40], tp, 0, keepdims=False)
    dmg, dms = dmgs[:256], dmgs[256:]
    blocks = packed.reshape(CHUNKS, ROWS, 128)
    cut = lambda lo, hi: jnp.stack([blocks[13 + lo : 13 + hi], blocks[lo:hi]])
    lanes = lambda x: x.transpose(0, 2, 1, 3).reshape(2, x.shape[2], C)
    g_we, g_ws = lanes(cut(0, 4)), lanes(cut(4, 8))
    g_qkv = cut(8, 11).transpose(0, 2, 1, 3)
    g_wo = lanes(cut(11, 12).reshape(2, 4, 128, 128))
    dbias = cut(12, 13).reshape(8, WT, WT)
    g_tab = table_of(dbias).reshape(2, 4, 361).transpose(0, 2, 1)
    dmw = blocks[26:28].reshape(4, 256, 128).transpose(1, 0, 2).reshape(256, C)
    own4 = lambda x, axis: lax.dynamic_index_in_dim(x, tp, axis, keepdims=False)
    dbqkv = own4(dbqkv, 1).reshape(2, 3, 128)
    g_bias = jnp.stack([dbqkv[:, 0], dbqkv[:, 2]], axis=1)
    g_be = own4(dbe, 1).reshape(2, 512)
    back = lambda x: x.reshape((2, 2, 64) + x.shape[1:]).swapaxes(0, 1).reshape((4, 64) + x.shape[1:])
    rms = jnp.sqrt(sums / (count * C))
    return (
        output, patches_grad, back(dmg), back(dms), back(dmw), small1[:, 0], small1[:, 1], g_qkv, g_bias,
        g_tab, g_wo, small1[:, 2], small2[:, 0], small2[:, 1], g_we, g_be, g_ws, small2[:, 2], rms,
    )


def solution(mesh):
    placed = (
        P("sp", None, "tp"), P(None, "tp"), P(None, "tp"), P(None, "tp", None), P(), P(),
        P(None, None, None, "tp"), P(None, None, "tp"), P(None, None, "tp"), P(None, "tp", None),
        P(), P(), P(), P(None, None, "tp"), P(None, "tp"), P(None, "tp", None), P(), P(),
        P("sp", None), P("sp", None, "tp"),
    )
    results = (
        P("sp", None, "tp"), P("sp", None, "tp"), P(None, "tp"), P(None, "tp"), P(None, "tp", None),
        P(), P(), P(None, None, None, "tp"), P(None, None, "tp"), P(None, None, "tp"),
        P(None, "tp", None), P(), P(), P(), P(None, None, "tp"), P(None, "tp"), P(None, "tp", None),
        P(), P(),
    )
    return jax.shard_map(shards, mesh=mesh, in_specs=placed, out_specs=results, check_vma=False)
```

```python
import functools

import jax
import jax.numpy as jnp
import numpy as np
from jax import lax
from jax.experimental import pallas as pl
from jax.experimental.pallas import tpu as pltpu
from jax.sharding import PartitionSpec as P

C = 512
HD = 32
C2 = 256
WIN = 10
SHIFT = 5
SUB = 32
REAL = 25
WT = 128
TOK = 384
NW = 3
GROUP = 4

bf16 = jnp.bfloat16
f32 = jnp.float32
epsilon = 1e-05
masked = -1000000000.0

NN = (((1,), (0,)), ((), ()))
NT = (((1,), (1,)), ((), ()))
TN = (((0,), (0,)), ((), ()))


def split(x):
    high = x.astype(bf16)
    return high, (x - high.astype(f32)).astype(bf16)


def mm(a, b, dims):
    return lax.dot_general(a, b, dims, preferred_element_type=f32)


def mm3(a, b, dims):
    return mm(a[0], b[0], dims) + (mm(a[0], b[1], dims) + mm(a[1], b[0], dims))


def normalized(x):
    center = x - jnp.mean(x, axis=-1, keepdims=True)
    rho = lax.rsqrt(jnp.mean(center * center, axis=-1, keepdims=True) + epsilon)
    return center * rho, rho


def head_masks(dtype):
    lane = lax.broadcasted_iota(jnp.int32, (1, 128), 1) // HD
    return [(lane == h).astype(f32).astype(dtype) for h in range(GROUP)]


def stacked(pair, masks):
    return tuple(jnp.concatenate([part * m for m in masks], axis=0) for part in pair)


def side_by_side(pair):
    return tuple(
        jnp.concatenate([part[h * WT : (h + 1) * WT] for h in range(GROUP)], axis=1)
        for part in pair
    )


def colsum(x):
    return jnp.sum(x, axis=0, keepdims=True)


def sds(*shape):
    return jax.ShapeDtypeStruct(shape, f32)


def norm_back(x, gain, grad_y):
    xhat, rho = normalized(x)
    gh = grad_y * gain
    grad_x = rho * (
        gh - jnp.mean(gh, axis=-1, keepdims=True) - xhat * jnp.mean(gh * xhat, axis=-1, keepdims=True)
    )
    return grad_x, colsum(grad_y * xhat), colsum(grad_y)


MESH = pl.DeviceIdType.MESH
ANY = pl.BlockSpec(memory_space=pl.ANY)
VM = pl.BlockSpec(memory_space=pltpu.VMEM)


def here():
    sp, tp = lax.axis_index("sp"), lax.axis_index("tp")
    return sp, tp, (sp, tp ^ 1), (sp, tp ^ 2), (sp ^ 1, tp)


def meet(peers):
    barrier = pltpu.get_barrier_semaphore()
    for peer in peers:
        pl.semaphore_signal(barrier, inc=1, device_id=peer, device_id_type=MESH)
    pl.semaphore_wait(barrier, len(peers))


def push(src, dst, send, recv, peer):
    return pltpu.make_async_remote_copy(
        src_ref=src, dst_ref=dst, send_sem=send, recv_sem=recv, device_id=peer, device_id_type=MESH
    )


ROWS = 512
HALF = ROWS // 2
MLP_ROWS, ATT_ROWS = 4096, 2560
MLP_CH, ATT_CH = MLP_ROWS // ROWS, ATT_ROWS // ROWS
FULL_CH = 2 * (MLP_CH + ATT_CH)
CHUNKS = FULL_CH + 2
FIRST = 4
AG_STEP = 15
MERGE_STEP = 20
TINY_STEP = 25
STEPS = FIRST + CHUNKS + 6
TINY = 40
COLS = [(0, 0, 0, 1), (0, 1, 1, 0), (1, 0, 1, 1), (1, 1, 2, 0), (2, 0, 2, 1)]


def at(w, sr, sc):
    return pl.ds(w * WT + sr * 64 + sc * SUB, SUB)


NCH = 13
GCH = 2 * NCH
F_STEPS = 31


def fwd_order(s):
    att = jnp.where(s < 3, 0, jnp.where(s < 7, 1, jnp.where(s < 8, 2, jnp.where(s < 17, 3, jnp.where(
        s < 18, 4, jnp.where(s < 20, 5, jnp.where(s < 21, 6, 7)))))))
    mlp = jnp.where(s < 10, 0, jnp.where(s < 15, 1, jnp.where(s < 16, 2, jnp.where(s < 22, 3, jnp.where(
        s < 23, 4, jnp.where(s < 28, 5, jnp.where(s < 29, 6, 7)))))))
    return att, mlp


def among(step, steps):
    found = step == steps[0]
    for s in steps[1:]:
        found = found | (step == s)
    return found


def fwd_kernel(n, *refs):
    (
        q_ref, mw_ref, mg_ref, wi_ref, bi_ref, wo_ref, we_ref, ws_ref, sm_ref, g1_ref, b1_ref, bo_ref,
        g2_ref, b2_ref, bs_ref, regc_ref, regr_ref, v0_ref, v1_ref, vs_ref, cot_ref,
    ) = refs[:21]
    (
        nall, wall, cb, field_out, mid_out, qkv_ref, p_ref, att_ref, hid_ref, slope_ref, stat_ref, vec_ref,
        sq_ref, os_ref,
    ) = refs[21:35]
    (
        nb, wb, smb, pb, pr, px, stb, str_, stx, vp, vr, vc, field, nh, nl, mixed, moved,
        lsem, ss, sr, xs, xr, ys, yr, s2s, s2r, s3s, s3r, sms, smr, rss, rsr, vps, vpr, vvs, vvr,
        mvs, mvr, cbs, cbr, cbl, hn, hw,
    ) = refs[35:]
    step = pl.program_id(0)
    sp, tp, sib, across, beside = here()
    par = sp & 1
    up, down = lax.rem(sp + 1, n), lax.rem(sp + n - 1, n)
    left = lax.rem(tp + 3, 4)

    def own():
        todo = []
        for b in range(2):
            todo += [
                (wi_ref.at[b], nb.at[0, pl.ds(4 * b, 3)]), (bi_ref.at[b], nb.at[0, 4 * b + 3]),
                (we_ref.at[b], wb.at[0, pl.ds(9 * b, 4)]), (ws_ref.at[b], wb.at[0, pl.ds(9 * b + 4, 4)]),
                (wo_ref.at[b], wb.at[0, pl.ds(9 * b + 8, 1)]),
            ]
        todo.append((sm_ref, smb.at[0]))
        return [pltpu.make_async_copy(s, d, lsem.at[i]) for i, (s, d) in enumerate(todo)]

    def to_sib(b):
        parts = [(nb, pl.ds(4 * b, 4)), (wb, pl.ds(9 * b + 8, 1)), (wb, pl.ds(9 * b, 8))]
        return [
            push(buf.at[0, d], buf.at[1, d], ss.at[b, k], sr.at[b, k], sib) for k, (buf, d) in enumerate(parts)
        ]

    def narrow(c):
        b, r = c // NCH, c % NCH
        return r < 4, 4 * b + r, 9 * b + jnp.where(r == 4, 8, r - 5)

    def each(c, act):
        small, kn, kw = narrow(c)

        @pl.when(small)
        def _():
            act(nb, kn, 256)

        @pl.when(jnp.logical_not(small))
        def _():
            act(wb, kw, 64)

    def half(size, h):
        return pl.ds(pl.multiple_of(h * size, size), size)

    def x_copy(c, buf, k, size):
        return push(buf.at[0, k, half(size, par)], buf.at[2, k, half(size, par)], xs.at[c], xr.at[c], across)

    def y_copy(c, buf, k, size):
        return push(buf.at[2, k, half(size, par)], buf.at[2, k, half(size, par)], ys.at[c], yr.at[c], beside)

    def s2_copy(c, buf, k, size):
        return push(buf.at[2, k, half(size, par)], buf.at[3, k, half(size, par)], s2s.at[c], s2r.at[c], sib)

    def s3_copy(c, buf, k, size):
        return push(
            buf.at[2, k, half(size, 1 - par)], buf.at[3, k, half(size, 1 - par)], s3s.at[c], s3r.at[c], sib
        )

    def rs_copies(k):
        if k < 2:
            i = 1 + 2 * k
            return [
                push(pb.at[i], pr.at[k], rss.at[0, k], rsr.at[0, k], sib),
                push(stb.at[i], str_.at[k], rss.at[1, k], rsr.at[1, k], sib),
            ]
        return [
            push(pb.at[2], px, rss.at[0, 2], rsr.at[0, 2], across),
            push(stb.at[2], stx, rss.at[1, 2], rsr.at[1, 2], across),
        ]

    def vec_copies():
        return [push(vp.at[0], vp.at[i], vps.at[i - 1], vpr.at[i - 1], (sp, tp ^ i)) for i in (1, 2, 3)]

    def sm_copy(k):
        src, dst, peer = ((0, 1, sib), (0, 2, across), (2, 3, sib))[k]
        return push(smb.at[src], smb.at[dst], sms.at[k], smr.at[k], peer)

    def valid_copy():
        return push(vs_ref, vr, vvs.at[0], vvr.at[0], (down, tp))

    def moves():
        todo = [(at(0, 1, 0), at(2, 0, 1), (sp, left)), (at(0, 0, 0), at(2, 1, 1), (down, left))]
        for w0, s0, w1, s1 in COLS:
            todo.append((at(w1, 0, s1), at(w0, 1, s0), (down, tp)))
        return [push(field.at[s], moved.at[d], mvs.at[i], mvr.at[i], peer) for i, (s, d, peer) in enumerate(todo)]

    def cot_copy(k, i):
        t = tp ^ i
        src = cot_ref.at[1 - k, pl.ds(6 * t, 6)]
        return push(src, cb.at[tp, k], cbs.at[k, i], cbr.at[k, i], ((sp, t), (down, t))[k])

    def cot_in(k, i):
        src = cot_ref.at[1 - k, pl.ds(0, 6)]
        return push(src, cb.at[tp ^ i, k], cbs.at[k, i], cbr.at[k, i], (sp, tp ^ 1))

    def cot_own():
        return pltpu.make_async_copy(cot_ref.at[1, pl.ds(6 * tp, 6)], cb.at[tp, 0], cbl.at[0])

    @pl.when(step == 0)
    def _():
        for copy in own():
            copy.start()
        barrier = pltpu.get_barrier_semaphore()
        near = [beside] + [(sp, tp ^ i) for i in (1, 2, 3)]
        near += [(up, tp ^ i) for i in range(4)] + [(down, tp ^ i) for i in range(4)]
        for peer in near:
            pl.semaphore_signal(barrier, inc=1, device_id=peer, device_id_type=MESH)
        pl.semaphore_wait(barrier, len(near))
        gain, offset = mg_ref[0:1, :], mg_ref[1:2, :]
        wpair = split(mw_ref[...])
        rows8 = lax.broadcasted_iota(jnp.int32, (8, 256), 0)
        pick = jnp.where(rows8 == 0, gain, jnp.where(rows8 == 1, offset, 0.0))
        vp[0] = jnp.dot(pick, mw_ref[...], precision=lax.Precision.HIGHEST, preferred_element_type=f32)
        for copy in vec_copies():
            copy.start()
        valid_copy().start()
        lane = lax.broadcasted_iota(jnp.int32, (TOK, 128), 1)
        for i in (3, 1, 2, 0):
            quad = q_ref[tp ^ i]
            pb[i] = mm3(split(quad * gain), wpair, NN)
            s1 = jnp.sum(quad, axis=-1, keepdims=True)
            s2 = jnp.sum(quad * quad, axis=-1, keepdims=True)
            stb[i] = jnp.where(lane == 0, s1, jnp.where(lane == 1, s2, 0.0)).T[0:8, :]
            if i % 2 == 1:
                for copy in rs_copies((i - 1) // 2):
                    copy.start()
            if i == 1:
                for copy in own():
                    copy.wait()
                sm_copy(0).start()
                sm_copy(1).start()
                for c in (0, 1):
                    x_copy(c, nb, c, 256).start()
        for copy in rs_copies(1):
            copy.wait_recv()
        pb[2] = pb[2] + pr[1]
        stb[2] = stb[2] + str_[1]
        for copy in rs_copies(2):
            copy.start()
        for copy in to_sib(0):
            copy.start()
        for copy in rs_copies(0):
            copy.wait_recv()
        pb[0] = pb[0] + pr[0]
        stb[0] = stb[0] + str_[0]
        x_copy(2, nb, 2, 256).start()
        sq_ref[...] = jnp.zeros_like(sq_ref)
        os_ref[...] = jnp.zeros_like(os_ref)
        vec_ref[...] = jnp.zeros_like(vec_ref)

    @pl.when(step == 1)
    def _():
        sm_copy(1).wait_recv()
        sm_copy(2).start()
        for copy in vec_copies():
            copy.wait()
        vec_ref[...] = (vp[0] + vp[1]) + (vp[2] + vp[3])
        valid_copy().wait()
        for b in range(2):
            line = v0_ref[...] if b == 0 else v1_ref[...] + vr[...]
            tall = jnp.concatenate([line, jnp.zeros((120, 128), f32)], axis=0).T
            vc[b] = jnp.concatenate([tall[:, w : w + 1] for w in range(NW)], axis=0)
            if b == 1:
                vr[...] = line
        sq_ref[5:6, 0:128] = colsum(v0_ref[...])
        for k in range(2):
            for copy in rs_copies(k):
                copy.wait_send()
        for copy in rs_copies(2):
            copy.wait()
        sums = jnp.concatenate([stb[0] + stx[...], jnp.zeros((120, TOK), f32)], axis=0).T
        mean = sums[:, 0:1] / (4.0 * C2)
        inverse = lax.rsqrt(sums[:, 1:2] / (4.0 * C2) - mean * mean + epsilon)
        lane = lax.broadcasted_iota(jnp.int32, (TOK, 128), 1)
        stat_ref[...] = jnp.where(lane == 0, mean, jnp.where(lane == 1, inverse, 0.0))
        field[...] = inverse * (pb[0] + px[...] - mean * vec_ref[0:1, :]) + vec_ref[1:2, :]

    att, mlp = fwd_order(step)

    @pl.when(among(step, (2, 3, 7, 8, 17, 18, 20, 21)))
    def _():
        b, i = att // 4, att % 4

        @pl.when(i == 0)
        def _():
            @pl.when(b == 1)
            def _():
                for copy in moves():
                    copy.wait()
                field[...] = moved[...]

            field_out[0] = field[...]
            xhat, _ = normalized(field[...])
            nh[...], nl[...] = split(xhat * g1_ref[b] + b1_ref[b])
            mixed[...] = jnp.broadcast_to(bo_ref[b], mixed.shape)

        for k in range(2):

            @pl.when((i == 1) & (b == k))
            def _(k=k):
                for copy in to_sib(k)[:2]:
                    copy.wait_recv()
                if k == 0:
                    sm_copy(0).wait()
                    sm_copy(1).wait_send()
                    sm_copy(2).wait()

        @pl.when(i == 3)
        def _():
            for r in range(5):
                c = b * NCH + r
                buf, k, size = (nb, 4 * b + r, 256) if r < 4 else (wb, 9 * b + 8, 64)
                s2_copy(c, buf, k, size).wait_recv()
                s3_copy(c, buf, k, size).wait_recv()

        pltpu.make_async_copy(nb.at[i, pl.ds(4 * b, 4)], nall.at[i, b], hn.at[b, i]).start()
        w = jnp.concatenate([nb[i, 4 * b + j] for j in range(3)], axis=1)
        lane = lax.broadcasted_iota(jnp.int32, (1, 384), 1)
        qkv = mm3((nh[...], nl[...]), split(w), NN) + smb[i, pl.ds(2 + b, 1), 0:384]
        qkv_ref[0] = qkv * jnp.where(lane < 128, HD ** (-0.5), 1.0)
        masks = head_masks(bf16)
        bias = nb[i, 4 * b + 3]
        eye = lax.broadcasted_iota(jnp.int32, (WT, WT), 0) == lax.broadcasted_iota(jnp.int32, (WT, WT), 1)
        for j in range(NW):
            rows = pl.ds(j * WT, WT)
            seen = qkv_ref[0, rows, :]
            q4 = stacked(split(seen[:, :128]), masks)
            k = split(seen[:, 128:256])
            v4 = stacked(split(seen[:, 256:]), masks)
            flags = jnp.where(b == 0, v0_ref[j : j + 1, :], vr[j : j + 1, :])
            allowed = (regc_ref[b, rows, :] == regr_ref[b, j : j + 1, :]) & (flags > 0) | eye
            allowed = jnp.concatenate([allowed.astype(f32)] * GROUP, axis=0) > 0
            s = jnp.where(allowed, mm3(q4, k, NT) + bias, masked)
            e = jnp.exp(s - jnp.max(s, axis=-1, keepdims=True))
            p = e / jnp.sum(e, axis=-1, keepdims=True)
            p_ref[0, j] = p
            att_ref[0, rows, :] = mm3(side_by_side(split(p)), v4, NN)
        mixed[...] += mm3(split(att_ref[0]), split(wb[i, 9 * b + 8]), NN)

        @pl.when(i == 3)
        def _():
            middle = field[...] + mixed[...]
            mid_out[0] = middle
            sq_ref[pl.ds(2 * b, 1), :] = colsum(mixed[...] * mixed[...] * vc[b])

    @pl.when(among(step, (9, 10, 15, 16, 22, 23, 28, 29)))
    def _():
        b, i = mlp // 4, mlp % 4

        @pl.when(i == 0)
        def _():
            xhat, _ = normalized(mid_out[0])
            nh[...], nl[...] = split(xhat * g2_ref[b] + b2_ref[b])
            mixed[...] = jnp.broadcast_to(bs_ref[b], mixed.shape)

            @pl.when(b == 0)
            def _():
                for copy in to_sib(1):
                    copy.start()

        for k in range(2):

            @pl.when((i == 1) & (b == k))
            def _(k=k):
                to_sib(k)[2].wait_recv()

        @pl.when(i == 3)
        def _():
            for r in range(8):
                c = b * NCH + 5 + r
                s2_copy(c, wb, 9 * b + r, 64).wait_recv()
                s3_copy(c, wb, 9 * b + r, 64).wait_recv()

        pltpu.make_async_copy(wb.at[i, pl.ds(9 * b, 9)], wall.at[i, b], hw.at[b, i]).start()
        we = wb[i, pl.ds(9 * b, 4)].reshape(512, 512)
        ws = wb[i, pl.ds(9 * b + 4, 4)].reshape(512, 512)
        pre = mm3((nh[...], nl[...]), split(we), NN) + smb[i, pl.ds(b, 1), :]
        phi = 0.5 * (1.0 + lax.erf(pre * (2 ** -0.5)))
        hidden = pre * phi
        hid_ref[0] = hidden
        slope_ref[0] = phi + pre * (jnp.exp(-0.5 * pre * pre) * ((2 * np.pi) ** -0.5))
        mixed[...] += mm3(split(hidden), split(ws), NN)

        @pl.when(i == 3)
        def _():
            out = mid_out[0] + mixed[...]
            field[...] = out
            sq_ref[pl.ds(2 * b + 1, 1), :] = colsum(mixed[...] * mixed[...] * vc[b])

            @pl.when(b == 0)
            def _():
                for copy in moves():
                    copy.start()
                for w0, s0, w1, s1 in COLS:
                    moved[at(w0, 0, s0), :] = field[at(w1, 1, s1), :]

            @pl.when(b == 1)
            def _():
                sq_ref[4:5, :] = colsum(out * out * vc[1])
                for t in range(4):
                    for w in range(NW):
                        for r in range(2):
                            os_ref[t, r, w * 64 : w * 64 + 64, :] = out[
                                w * WT + r * 64 : w * WT + r * 64 + 64, t * 128 : (t + 1) * 128
                            ]

    p = step - 1

    @pl.when((p >= 1) & (p + 2 < GCH))
    def _():
        each(p + 2, lambda buf, k, size: x_copy(p + 2, buf, k, size).start())

    @pl.when(step == GCH - 1)
    def _():
        cot_own().start()
        for k in range(2):
            for i in range(4):
                if k + i > 0:
                    cot_copy(k, i).start()

    @pl.when((p >= 0) & (p < GCH))
    def _():
        def act(buf, k, size):
            x_copy(p, buf, k, size).wait_recv()
            y_copy(p, buf, k, size).start()
            s2_copy(p, buf, k, size).start()

        each(p, act)

    @pl.when((p >= 1) & (p <= GCH))
    def _():
        def act(buf, k, size):
            y_copy(p - 1, buf, k, size).wait_recv()
            s3_copy(p - 1, buf, k, size).start()

        each(p - 1, act)

    @pl.when(step == F_STEPS - 1)
    def _():
        cot_own().wait()
        for k in range(2):
            for i in range(4):
                if k + i > 0:
                    cot_copy(k, i).wait_send()
                    cot_in(k, i).wait_recv()
        for b in range(2):
            for copy in to_sib(b):
                copy.wait_send()
            for i in range(4):
                pltpu.make_async_copy(nb.at[i, pl.ds(4 * b, 4)], nall.at[i, b], hn.at[b, i]).wait()
                pltpu.make_async_copy(wb.at[i, pl.ds(9 * b, 9)], wall.at[i, b], hw.at[b, i]).wait()

        @pl.loop(0, GCH)
        def _(c):
            def act(buf, k, size):
                x_copy(c, buf, k, size).wait_send()
                y_copy(c, buf, k, size).wait_send()
                s2_copy(c, buf, k, size).wait_send()
                s3_copy(c, buf, k, size).wait_send()

            each(c, act)


def forward(n, args, ident):
    dma = pltpu.SemaphoreType.DMA

    def fixed(shape):
        return pl.BlockSpec(shape, lambda s: (0,) * len(shape), pipeline_mode=pl.Buffered(1))

    def by(index, shape):
        zeros = (0,) * len(shape)
        return pl.BlockSpec((1,) + shape, lambda s: (index(s),) + zeros)

    att_at = lambda s: fwd_order(s)[0]
    mlp_at = lambda s: fwd_order(s)[1]
    second = lambda s: jnp.where(s < 17, 0, 1)
    vm = lambda *shape: pltpu.VMEM(shape, f32)
    two = fixed((2, 1, C))
    return pl.pallas_call(
        functools.partial(fwd_kernel, n),
        grid=(F_STEPS,),
        in_specs=[
            fixed((4, TOK, 256)), fixed((256, C)), fixed((8, 256)), ANY, ANY, ANY, ANY, ANY, ANY,
            two, two, two, two, two, two, fixed((2, TOK, 1)), fixed((2, 8, 128)), fixed((8, 128)),
            fixed((8, 128)), fixed((8, 128)), ANY,
        ],
        out_specs=[
            ANY, ANY, ANY, by(second, (TOK, C)), by(second, (TOK, C)), by(att_at, (TOK, 384)),
            by(att_at, (NW, GROUP * WT, WT)), by(att_at, (TOK, 128)), by(mlp_at, (TOK, 512)),
            by(mlp_at, (TOK, 512)), fixed((TOK, 128)), fixed((8, C)), fixed((8, C)), fixed((4, 2, 192, 128)),
        ],
        out_shape=[
            sds(4, 2, 4, 512, 128), sds(4, 2, 9, 128, 512), sds(4, 2, 6, SUB, 128), sds(2, TOK, C), sds(2, TOK, C),
            sds(8, TOK, 384), sds(8, NW, GROUP * WT, WT), sds(8, TOK, 128), sds(8, TOK, 512), sds(8, TOK, 512),
            sds(TOK, 128), sds(8, C), sds(8, C), sds(4, 2, 192, 128),
        ],
        scratch_shapes=[
            vm(4, 8, 512, 128), vm(4, 18, 128, 512), vm(4, 8, C), vm(4, TOK, C), vm(2, TOK, C), vm(TOK, C),
            vm(4, 8, TOK), vm(2, 8, TOK), vm(8, TOK), vm(4, 8, C), vm(8, 128), vm(2, TOK, 1), vm(TOK, C),
            pltpu.VMEM((TOK, C), bf16), pltpu.VMEM((TOK, C), bf16), vm(TOK, C), vm(TOK, C),
            dma((11,)), dma((2, 3)), dma((2, 3)), dma((GCH,)), dma((GCH,)), dma((GCH,)), dma((GCH,)),
            dma((GCH,)), dma((GCH,)), dma((GCH,)), dma((GCH,)), dma((3,)), dma((3,)), dma((2, 3)), dma((2, 3)),
            dma((3,)), dma((3,)), dma((1,)), dma((1,)), dma((7,)), dma((7,)), dma((2, 4)), dma((2, 4)),
            dma((1,)), dma((2, 4)), dma((2, 4)),
        ],
        compiler_params=pltpu.CompilerParams(
            collective_id=ident, has_side_effects=True, vmem_limit_bytes=60 << 20,
            dimension_semantics=("arbitrary",),
        ),
        name="forward",
    )(*args)


def bwd_kernel(n, *refs):
    (
        cot_ref, mid_ref, field_ref, g1_ref, b1_ref, g2_ref, b2_ref, we_ref, ws_ref, wqkv_ref, wo_ref,
        hid_ref, slope_ref, qkv_ref, p_ref, att_ref, sq_ref, q_ref, mw_ref, vec_ref, mg_ref, stat_ref, os_ref,
    ) = refs[:23]
    pack, gall, exall, ob, out_ref, gq_ref, tout_ref = refs[23:30]
    (
        nth, ntl, gh, gl, acc, dqkv, gf, gbuf, moved, ext, extin, qbuf,
        loc, pair, yr, zr, fin, ta, tx, tz,
        gsem, mvs, mvr, ags, agr, agl, msem, ss, rs, zs, zq, fs, fq, ls, os, ts, tq, tzs, tzq, obs, obr, obl,
    ) = refs[30:]
    step = pl.program_id(0)
    dmw, gqbuf = moved.at[pl.ds(0, 256)], dqkv.at[:, pl.ds(0, 256)]
    sp, tp, sib, across, beside = here()
    par, mine = sp & 1, sp // 2
    m = n // 2
    piece = HALF // m
    up, down, right = lax.rem(sp + 1, n), lax.rem(sp + n - 1, n), lax.rem(tp + 1, 4)

    def member(j):
        return lax.rem(mine + j, m)

    def device(q):
        return (q * 2 + par, tp)

    def out_copy(k, i):
        t = tp ^ i
        return push(
            os_ref.at[t, k], ob.at[1 - k, pl.ds(6 * tp, 6)], obs.at[k, i], obr.at[k, i], ((sp, t), (up, t))[k]
        )

    def out_in(k, i):
        return push(
            os_ref.at[0, k], ob.at[1 - k, pl.ds(6 * (tp ^ i), 6)], obs.at[k, i], obr.at[k, i], (sp, tp ^ 1)
        )

    def out_own():
        return pltpu.make_async_copy(os_ref.at[tp, 0], ob.at[1, pl.ds(6 * tp, 6)], obl.at[0])

    @pl.when(step == 0)
    def _():
        barrier = pltpu.get_barrier_semaphore()
        near = [beside] + [(sp, tp ^ i) for i in (1, 2, 3)]
        near += [(up, tp ^ i) for i in range(4)] + [(down, tp ^ i) for i in range(4)]
        for peer in near:
            pl.semaphore_signal(barrier, inc=1, device_id=peer, device_id_type=MESH)

        @pl.loop(1, m)
        def _(j):
            pl.semaphore_signal(barrier, inc=1, device_id=device(member(j)), device_id_type=MESH)

        ta[...] = jnp.zeros_like(ta)
        ta[0, 28:36, :] = sq_ref[...]
        for t in range(4):
            for w in range(NW):
                for r in range(2):
                    gf[w * WT + r * 64 : w * WT + r * 64 + 64, t * 128 : (t + 1) * 128] = cot_ref[
                        t, r, w * 64 : w * 64 + 64, :
                    ]
        pl.semaphore_wait(barrier, len(near) + m - 1)
        out_own().start()
        for k in range(2):
            for i in range(4):
                if k + i > 0:
                    out_copy(k, i).start()

    def packed(b, i, late):
        size = ATT_ROWS if late else MLP_ROWS
        base = pl.multiple_of((1 - b) * (MLP_ROWS + ATT_ROWS) + (MLP_ROWS if late else 0), ROWS)
        slot = i % 2
        return pltpu.make_async_copy(
            gbuf.at[slot, pl.ds(0, size)], pack.at[tp ^ i, pl.ds(base, size)], gsem.at[slot]
        )

    def moves():
        todo = [
            (at(2, 0, 1), at(0, 1, 0), (sp, right)),
            (at(2, 1, 1), at(0, 0, 0), (up, right)),
        ]
        for w0, s0, w1, s1 in COLS:
            todo.append((at(w0, 1, s0), at(w1, 0, s1), (up, tp)))
        return [push(acc.at[src], moved.at[dst], mvs.at[i], mvr.at[i], peer) for i, (src, dst, peer) in enumerate(todo)]

    def kept():
        for w0, s0, w1, s1 in COLS:
            moved[at(w1, 1, s1), :] = acc[at(w0, 0, s0), :]

    phase = step // 4

    @pl.when((phase == 0) | (phase == 2))
    def _():
        b = 1 - phase // 2
        i = step % 4

        @pl.when(i == 0)
        def _():
            @pl.when(b == 0)
            def _():
                for copy in moves():
                    copy.wait()
                gf[...] = moved[...]

            xhat, _ = normalized(mid_ref[0])
            nth[...], ntl[...] = split((xhat * g2_ref[b] + b2_ref[b]).T)
            gh[...], gl[...] = split(gf[...])
            acc[...] = jnp.zeros_like(acc)

        slot = i % 2
        grad = (gh[...], gl[...])
        dws = mm3(split(hid_ref[0].T), grad, NN)
        for j in range(4):
            gbuf[slot, 2048 + j * 512 : 2560 + j * 512, :] = dws[:, j * 128 : (j + 1) * 128]
        dpre = mm3(grad, split(ws_ref[0, 0].reshape(512, C)), NT) * slope_ref[0]
        ta[0, pl.ds(12 + b * 4 + (tp ^ i), 1), :] = colsum(dpre)
        pair_ = split(dpre)
        dwe = mm3((nth[...], ntl[...]), pair_, NN)
        for j in range(4):
            gbuf[slot, j * 512 : (j + 1) * 512, :] = dwe[:, j * 128 : (j + 1) * 128]
        acc[...] += mm3(pair_, split(we_ref[0, 0].reshape(C, 512)), NT)

        @pl.when(i > 0)
        def _():
            packed(b, i - 1, False).wait()

        packed(b, i, False).start()

        @pl.when(i == 3)
        def _():
            grad_x, dgain, dshift = norm_back(mid_ref[0], g2_ref[b], acc[...])
            ta[0, pl.ds(6 + 3 * b, 1), :] = dgain
            ta[0, pl.ds(7 + 3 * b, 1), :] = dshift
            ta[0, pl.ds(8 + 3 * b, 1), :] = colsum(gf[...])
            gf[...] = gf[...] + grad_x
            packed(b, 3, False).wait()

    @pl.when((phase == 1) | (phase == 3))
    def _():
        b = 1 - phase // 2
        i = step % 4

        @pl.when(i == 0)
        def _():
            xhat, _ = normalized(field_ref[0])
            nth[...], ntl[...] = split((xhat * g1_ref[b] + b1_ref[b]).T)
            gh[...], gl[...] = split(gf[...])
            acc[...] = jnp.zeros_like(acc)

        slot = i % 2
        grad = (gh[...], gl[...])
        dwo = mm3(split(att_ref[0].T), grad, NN)
        for j in range(4):
            gbuf[slot, 1536 + j * 128 : 1664 + j * 128, :] = dwo[:, j * 128 : (j + 1) * 128]
        dout = mm3(grad, split(wo_ref[0, 0, 0]), NT)
        masks = head_masks(bf16)
        dbias = jnp.zeros((GROUP * WT, WT), f32)
        for w in range(NW):
            rows = slice(w * WT, (w + 1) * WT)
            seen = qkv_ref[0, pl.ds(w * WT, WT), :]
            q4 = stacked(split(seen[:, :128]), masks)
            k4 = stacked(split(seen[:, 128:256]), masks)
            v = split(seen[:, 256:])
            p = p_ref[0, w]
            do4 = stacked(split(dout[rows]), masks)
            dp = mm3(do4, v, NT)
            ds = p * (dp - jnp.sum(p * dp, axis=-1, keepdims=True))
            dbias = dbias + ds
            dpair = split(ds)
            dqkv[pl.ds(w * WT, WT), 0:128] = mm3(side_by_side(dpair), k4, NN) * HD ** (-0.5)
            dqkv[pl.ds(w * WT, WT), 128:256] = mm3(dpair, q4, TN)
            dqkv[pl.ds(w * WT, WT), 256:384] = mm3(split(p), do4, TN)
        gbuf[slot, 2048:2560, :] = dbias
        grads = dqkv[...]
        ta[0, pl.ds(20 + b * 4 + (tp ^ i), 1), 0:384] = colsum(grads)
        pair_ = split(grads)
        dw = mm3((nth[...], ntl[...]), pair_, NN)
        for j in range(3):
            gbuf[slot, j * 512 : (j + 1) * 512, :] = dw[:, j * 128 : (j + 1) * 128]
        w = jnp.concatenate([wqkv_ref[0, 0, j] for j in range(3)], axis=1)
        acc[...] += mm3(pair_, split(w), NT)

        @pl.when(i > 0)
        def _():
            packed(b, i - 1, True).wait()

        packed(b, i, True).start()

        @pl.when(i == 3)
        def _():
            grad_x, dgain, dshift = norm_back(field_ref[0], g1_ref[b], acc[...])
            ta[0, pl.ds(3 * b, 1), :] = dgain
            ta[0, pl.ds(1 + 3 * b, 1), :] = dshift
            ta[0, pl.ds(2 + 3 * b, 1), :] = colsum(gf[...])
            acc[...] = gf[...] + grad_x

            @pl.when(b == 1)
            def _():
                for copy in moves():
                    copy.start()
                kept()

            packed(b, 3, True).wait()

    def ag(k, src, dst, peer, which):
        return push(src, dst, ags.at[which, k], agr.at[which, k], peer)

    def ag_copies(k):
        own = (acc, ext)
        whole_ = (gall, exall)
        return [
            ag(k, own[w], whole_[w].at[tp], (sib, across)[k], w) if k < 2
            else ag(k, whole_[w].at[tp ^ 2], whole_[w].at[tp ^ 2], sib, w)
            for w in range(2)
        ]

    @pl.when(step == AG_STEP)
    def _():
        m2 = jnp.sum(acc[...] * (field_ref[0] - vec_ref[1:2, :]), axis=-1, keepdims=True)
        lane = lax.broadcasted_iota(jnp.int32, (TOK, 128), 1)
        tall = jnp.where(lane == 2, m2, stat_ref[...])
        ext[...] = tall.T[0:8, :]
        for k in range(2):
            for copy in ag_copies(k):
                copy.start()

    @pl.when(step == MERGE_STEP - 1)
    def _():
        for copy in ag_copies(1):
            copy.wait()
        for copy in ag_copies(2):
            copy.start()
        for copy in ag_copies(0):
            copy.wait()

    @pl.when((step >= MERGE_STEP) & (step < MERGE_STEP + 4))
    def _():
        i = step - MERGE_STEP
        t = tp ^ i

        @pl.when(i == 2)
        def _():
            for copy in ag_copies(2):
                copy.wait()

        fetch = [pltpu.make_async_copy(q_ref.at[t], qbuf, msem.at[0])]
        fetch[0].start()

        @pl.when(i == 0)
        def _():
            dmw[...] = jnp.zeros((256, C), f32)
            gf[...] = acc[...]
            extin[...] = ext[...]

        @pl.when(i > 0)
        def _():
            two = [
                pltpu.make_async_copy(gall.at[t], gf, msem.at[1]),
                pltpu.make_async_copy(exall.at[t], extin, msem.at[2]),
            ]
            for copy in two:
                copy.start()
            for copy in two:
                copy.wait()

        fetch[0].wait()
        wide = jnp.concatenate([extin[...], jnp.zeros((120, TOK), f32)], axis=0).T
        mean, inv, m2 = wide[:, 0:1], wide[:, 1:2], wide[:, 2:3]
        full = gf[...]
        m1 = jnp.sum(full * vec_ref[0:1, :], axis=-1, keepdims=True) / (4.0 * C2)
        m2 = m2 / (4.0 * C2)
        fpair = split(full)
        xhat = (qbuf[...] - mean) * inv
        gmerged = mm3(fpair, split(mw_ref[...]), NT)
        dmw[...] += mm3(split((xhat * mg_ref[0:1, :] + mg_ref[1:2, :]).T), fpair, NN)
        row = pl.ds(36 + tp, 1)
        ta[0, row, 0:256] += colsum(gmerged * xhat)
        ta[0, row, 256:512] += colsum(gmerged)

        @pl.when(i > 0)
        def _():
            pltpu.make_async_copy(gqbuf, gq_ref.at[t], msem.at[3]).wait()

        gqbuf[...] = inv * (gmerged * mg_ref[0:1, :] - m1 - xhat * m2)
        pltpu.make_async_copy(gqbuf, gq_ref.at[t], msem.at[3]).start()

        @pl.when(i == 3)
        def _():
            pltpu.make_async_copy(gqbuf, gq_ref.at[t], msem.at[3]).wait()
            for k in range(2):
                for j in range(2):
                    low = (2 * k + j) * 128
                    pair[FULL_CH + k, 0, j * 256 : (j + 1) * 256, :] = dmw[:, low : low + 128]

    def rows(c):
        return pl.ds(pl.multiple_of(c * ROWS, ROWS), ROWS)

    def load(c, k):
        return pltpu.make_async_copy(pack.at[tp ^ (2 * k), rows(c)], loc.at[c % 2, k], ls.at[c % 2, k])

    def swap(c, k):
        return push(pack.at[tp ^ 1 ^ (2 * k), rows(c)], pair.at[c, k], ss.at[k, c], rs.at[k, c], sib)

    def cross(c):
        return push(pair.at[c, 1], fin.at[c], ss.at[2, c], rs.at[2, c], across)

    def halves(h):
        return pl.ds(pl.multiple_of(h * HALF, HALF), HALF)

    def side(c):
        return push(pair.at[c, 0, halves(1 - par)], yr.at[c], ss.at[3, c], rs.at[3, c], beside)

    def bit(q):
        return pl.ds(pl.multiple_of(q * piece, piece), piece)

    def spread(c, q, slot):
        return push(yr.at[c, bit(q)], zr.at[c, slot], zs.at[c % 4, q], zq.at[c, slot], device(q))

    def place(q):
        return pl.ds(pl.multiple_of(par * HALF + q * piece, piece), piece)

    def share(c, q, slot):
        return push(fin.at[c, place(slot)], fin.at[c, place(slot)], fs.at[c % 4, q], fq.at[c, slot], device(q))

    def back(c):
        return push(fin.at[c, halves(par)], fin.at[c, halves(par)], ss.at[4, c], rs.at[4, c], beside)

    def write(c):
        return pltpu.make_async_copy(fin.at[c], out_ref.at[rows(c)], os.at[c])

    def tiny(k, peer):
        return push(ta.at[k], tx.at[k], ts.at[k], tq.at[k], peer)

    def tiny_z(q, slot):
        return push(ta.at[3], tz.at[slot], tzs.at[q], tzq.at[slot], device(q))

    def stage(lag, first, last):
        c = step - FIRST - lag
        return c, (c >= first) & (c < last)

    peers = (sib, across, beside)
    for k in range(4):

        @pl.when(step == TINY_STEP + 2 * k)
        def _(k=k):
            if k > 0:
                tiny(k - 1, peers[k - 1]).wait()
                ta[k] = ta[k - 1] + tx[k - 1]
            if k < 3:
                tiny(k, peers[k]).start()
            else:
                tz[mine] = ta[3]

                @pl.loop(1, m)
                def _(j):
                    tiny_z(member(j), mine).start()

    c0, on0 = stage(0, 0, FULL_CH)

    @pl.when(on0)
    def _():
        for k in (1, 0):
            swap(c0, k).start()
            load(c0, k).start()

    c1, on1 = stage(1, 0, FULL_CH)

    @pl.when(on1)
    def _():
        for k in (1, 0):
            load(c1, k).wait()
            swap(c1, k).wait_recv()
            pair[c1, k] = pair[c1, k] + loc[c1 % 2, k]
            if k == 1:
                cross(c1).start()

    c2, on2 = stage(2, 0, CHUNKS)

    @pl.when(on2)
    def _():
        @pl.when(c2 < FULL_CH)
        def _():
            cross(c2).wait_recv()
            pair[c2, 0] = pair[c2, 0] + fin[c2]

        side(c2).start()

    c3, on3 = stage(3, 0, CHUNKS)

    @pl.when(on3)
    def _():
        side(c3).wait_recv()
        yr[c3] = yr[c3] + pair[c3, 0, halves(par)]

        @pl.loop(1, m)
        def _(j):
            spread(c3, member(j), mine).start()

    c4, on4 = stage(4, 0, CHUNKS)

    @pl.when(on4)
    def _():
        fin[c4, place(mine)] = yr[c4, bit(mine)]

        @pl.loop(1, m)
        def _(j):
            spread(c4, member(j), member(j)).wait_recv()
            fin[c4, place(mine)] = fin[c4, place(mine)] + zr[c4, member(j)]

        @pl.loop(1, m)
        def _(j):
            share(c4, member(j), mine).start()

    c5, on5 = stage(5, 0, CHUNKS)

    @pl.when(on5)
    def _():
        @pl.loop(1, m)
        def _(j):
            share(c5, member(j), member(j)).wait_recv()
            spread(c5, member(j), mine).wait_send()

        back(c5).start()

    c6, on6 = stage(6, 0, CHUNKS)

    @pl.when(on6)
    def _():
        back(c6).wait_recv()
        write(c6).start()

        @pl.loop(1, m)
        def _(j):
            share(c6, member(j), mine).wait_send()

    @pl.when(step == STEPS - 1)
    def _():
        @pl.loop(1, m)
        def _(j):
            tiny_z(member(j), member(j)).wait_recv()
            tiny_z(member(j), mine).wait_send()

        out_own().wait()
        for k in range(2):
            for i in range(4):
                if k + i > 0:
                    out_copy(k, i).wait_send()
                    out_in(k, i).wait_recv()
        total = tz[0]
        for q in range(1, m):
            total = total + tz[q]
        tout_ref[...] = total

        @pl.loop(0, CHUNKS)
        def _(c):
            @pl.when(c < FULL_CH)
            def _():
                for k in range(2):
                    swap(c, k).wait_send()
                cross(c).wait_send()

            side(c).wait_send()
            back(c).wait_send()
            write(c).wait()


def backward(n, args, ident):
    m = n // 2
    dma = pltpu.SemaphoreType.DMA

    def fixed(shape):
        return pl.BlockSpec(shape, lambda s: (0,) * len(shape), pipeline_mode=pl.Buffered(1))

    def mlp_at(s):
        return jnp.where(s < 4, 4 + s, jnp.where(s < 8, 0, jnp.where(s < 12, s - 8, 3)))

    def att_at(s):
        return jnp.where(s < 4, 4, jnp.where(s < 8, s, jnp.where(s < 12, 0, jnp.where(s < 16, s - 12, 3))))

    def by(index, shape, mode=None):
        zeros = (0,) * len(shape)
        return pl.BlockSpec((1,) + shape, lambda s: (index(s),) + zeros, pipeline_mode=mode)

    def spot(index, shape, k):
        return pl.BlockSpec((1, 1) + shape, lambda s: (index(s) % 4, index(s) // 4, k, 0, 0))

    one = pl.Buffered(1)
    lanes = (CHUNKS, ROWS, 128)
    in_specs = [
        fixed((4, 2, 192, 128)), by(lambda s: jnp.where(s < 4, 1, 0), (TOK, C), one),
        by(lambda s: jnp.where(s < 8, 1, 0), (TOK, C), one),
        fixed((2, 1, C)), fixed((2, 1, C)), fixed((2, 1, C)), fixed((2, 1, C)),
        spot(mlp_at, (4, 128, 512), 0), spot(mlp_at, (4, 128, 512), 1), spot(att_at, (3, C, 128), 0),
        spot(att_at, (1, 128, C), 8),
        by(mlp_at, (TOK, 512)), by(mlp_at, (TOK, 512)), by(att_at, (TOK, 384)),
        by(att_at, (NW, GROUP * WT, WT)), by(att_at, (TOK, 128)),
        fixed((8, C)), ANY, fixed((256, C)), fixed((8, C)), fixed((8, 256)), fixed((TOK, 128)), ANY,
    ]
    return pl.pallas_call(
        functools.partial(bwd_kernel, n),
        grid=(STEPS,),
        in_specs=in_specs,
        out_specs=[ANY, ANY, ANY, ANY, ANY, ANY, fixed((TINY, C))],
        out_shape=[
            sds(4, FULL_CH * ROWS, 128), sds(4, TOK, C), sds(4, 8, TOK), sds(2, 24, SUB, 128), sds(CHUNKS * ROWS, 128),
            sds(4, TOK, 256), sds(TINY, C),
        ],
        scratch_shapes=[
            pltpu.VMEM((C, TOK), bf16), pltpu.VMEM((C, TOK), bf16), pltpu.VMEM((TOK, C), bf16),
            pltpu.VMEM((TOK, C), bf16), pltpu.VMEM((TOK, C), f32), pltpu.VMEM((TOK, 384), f32),
            pltpu.VMEM((TOK, C), f32), pltpu.VMEM((2, MLP_ROWS, 128), f32), pltpu.VMEM((TOK, C), f32),
            pltpu.VMEM((8, TOK), f32), pltpu.VMEM((8, TOK), f32), pltpu.VMEM((TOK, 256), f32),
            pltpu.VMEM((2, 2, ROWS, 128), f32), pltpu.VMEM((CHUNKS, 2, ROWS, 128), f32),
            pltpu.VMEM((CHUNKS, HALF, 128), f32), pltpu.VMEM((CHUNKS, m, HALF // m, 128), f32),
            pltpu.VMEM(lanes, f32), pltpu.VMEM((4, TINY, C), f32), pltpu.VMEM((3, TINY, C), f32),
            pltpu.VMEM((m, TINY, C), f32),
            dma((2,)), dma((7,)), dma((7,)), dma((2, 3)), dma((2, 3)), dma((2,)), dma((4,)),
            dma((5, CHUNKS)), dma((5, CHUNKS)), dma((4, m)), dma((CHUNKS, m)), dma((4, m)),
            dma((CHUNKS, m)), dma((2, 2)), dma((CHUNKS,)), dma((3,)), dma((3,)), dma((m,)), dma((m,)),
            dma((2, 4)), dma((2, 4)), dma((1,)),
        ],
        compiler_params=pltpu.CompilerParams(
            collective_id=ident, has_side_effects=True, vmem_limit_bytes=60 << 20,
            dimension_semantics=("arbitrary",),
        ),
        name="backward",
    )(*args)


def column_pick():
    pick = np.zeros((19, WIN, WIN), np.float32)
    for a in range(WIN):
        for b in range(WIN):
            pick[a - b + WIN - 1, a, b] = 1.0
    return pick


def row_pick():
    pick = np.zeros((19, WIN, WIN, WIN, 2, 2, SUB), np.float32)
    for pr in range(WIN):
        for qr in range(WIN):
            for qc in range(WIN):
                pick[pr - qr + WIN - 1, qc, pr, 0, qr // 5, qc // 5, (qr % 5) * 5 + qc % 5] = 1.0
    return pick[:, :, :, 0].reshape(190, WIN * WT)


def bias_of(table):
    heads = table.shape[0]
    grid = table.reshape(heads, 19, 19)
    columns = jnp.einsum("hrd,dab->harb", grid, jnp.asarray(column_pick()), precision="highest")
    rows = jnp.dot(columns.reshape(heads * WIN, 190), jnp.asarray(row_pick()), precision="highest")
    rows = rows.reshape(heads, 2, 5, 2, 5, WT).transpose(0, 3, 1, 4, 2, 5)
    rows = rows.reshape(heads, 4, REAL, WT)
    return jnp.pad(rows, ((0, 0), (0, 0), (0, SUB - REAL), (0, 0))).reshape(heads, WT, WT)


def table_of(dbias):
    heads = dbias.shape[0]
    rows = dbias.reshape(heads, 4, SUB, WT)[:, :, :REAL].reshape(heads, 2, 2, 5, 5, WT)
    rows = rows.transpose(0, 2, 4, 1, 3, 5).reshape(heads * WIN, WIN * WT)
    columns = lax.dot_general(rows, jnp.asarray(row_pick()), NT, precision="highest")
    columns = columns.reshape(heads, WIN, 19, WIN)
    return jnp.einsum("harb,dab->hrd", columns, jnp.asarray(column_pick()), precision="highest")


def shards(
    patches, merge_gain, merge_shift, merge_weight, first_gain, first_shift, input_weight,
    input_bias, position_table, output_weight, output_bias, second_gain, second_shift,
    expand_weight, expand_bias, shrink_weight, shrink_bias, page_map, valid_flags, cotangent,
):
    sp_count = lax.axis_size("sp")
    tp = lax.axis_index("tp")
    sp = lax.axis_index("sp")

    tables = position_table.transpose(0, 2, 1).reshape(8, 361)
    bias = bias_of(tables).reshape(2, 512, 128)
    pairs = jnp.concatenate([input_bias, jnp.zeros_like(input_bias)], axis=2).reshape(2, 512)
    small = jnp.concatenate([expand_bias, pairs, jnp.zeros((4, 512), f32)], axis=0)
    three = lambda x: x.reshape(2, 1, C)

    valid = valid_flags.astype(f32).reshape(2, 5, 24, 5).transpose(0, 2, 1, 3).reshape(2, 24, REAL)
    valid = jnp.pad(valid, ((0, 0), (0, 0), (0, SUB - REAL)))
    own = lambda grid: lax.dynamic_slice_in_dim(grid, 6 * tp, 6, 1).reshape(2, NW, 2 * SUB)
    here_ = own(valid)
    next_ = own(jnp.roll(valid, -1, axis=1))
    blank = jnp.zeros((NW, 2 * SUB), f32)
    line = lambda a, c: jnp.pad(jnp.concatenate([a, c], axis=1), ((0, 5), (0, 0)))
    valid0, valid1, valids = line(here_[0], here_[1]), line(next_[1], blank), line(blank, next_[0])
    pages = jnp.concatenate([page_map, page_map[:1]], axis=0)
    pages = jnp.concatenate([pages, pages[:, :1]], axis=1)
    pages = lax.dynamic_slice(pages, (sp, 3 * tp), (2, 4))
    page = jnp.stack([pages[:, :3], pages[:, 1:]], axis=2).transpose(1, 0, 2)
    wrap_row = (jnp.arange(2) == 1) & (sp == sp_count - 1)
    wrap_col = (jnp.arange(2) == 1)[None, :] & (jnp.arange(NW) == NW - 1)[:, None] & (tp == 3)
    region = page * 4 + 2 * wrap_row[None, :, None].astype(jnp.int32) + wrap_col[:, None, :].astype(jnp.int32)
    region = jnp.broadcast_to(region[..., None], (NW, 2, 2, SUB)).reshape(NW, WT)
    region = jnp.stack([jnp.zeros_like(region), region])
    regc, regr = region.reshape(2, TOK, 1), jnp.pad(region, ((0, 0), (0, 5), (0, 0)))

    gain = merge_gain.reshape(2, 2, 64).transpose(1, 0, 2).reshape(1, 256)
    offset = merge_shift.reshape(2, 2, 64).transpose(1, 0, 2).reshape(1, 256)
    mgain = jnp.concatenate([gain, offset, jnp.zeros((6, 256), f32)], axis=0)
    weight = merge_weight.reshape(2, 2, 64, C).transpose(1, 0, 2, 3).reshape(256, C)
    quads = patches.reshape(2, 5, 2, 4, NW, 2, 5, 128).transpose(3, 4, 0, 5, 1, 6, 2, 7).reshape(4, NW, 4, REAL, 256)
    quads = jnp.pad(quads, ((0, 0), (0, 0), (0, 0), (0, SUB - REAL), (0, 0))).reshape(4, TOK, 256)
    cot = jnp.roll(cotangent.reshape(2, 5, 24, 5, 128), -1, axis=2).transpose(0, 2, 1, 3, 4).reshape(2, 24, REAL, 128)
    cot = jnp.pad(cot, ((0, 0), (0, 0), (0, SUB - REAL), (0, 0)))

    nall, wall, cot, fields, middles, qkv, p, att, hid, slope, stat, vecs, squares, out = forward(
        sp_count,
        (
            quads, weight, mgain, input_weight.transpose(0, 2, 1, 3), bias, output_weight.reshape(2, 1, 128, C),
            expand_weight.reshape(2, 4, 128, 512), shrink_weight.reshape(2, 4, 128, C), small,
            three(first_gain), three(first_shift), three(output_bias), three(second_gain), three(second_shift),
            three(shrink_bias), regc, regr, valid0, valid1, valids, cot,
        ),
        1,
    )
    _, _, _, output, packed, gquads, tiny = backward(
        sp_count,
        (
            cot.reshape(4, 2, 192, 128), middles, fields, three(first_gain), three(first_shift),
            three(second_gain), three(second_shift), wall, wall, nall, wall, hid, slope, qkv, p, att,
            squares, quads, weight, vecs, mgain, stat, out.reshape(4, 2, 6, SUB, 128),
        ),
        2,
    )
    output = jnp.roll(output[:, :, :REAL], 1, axis=1).reshape(2, 24, 5, 5, 128)
    output = output.transpose(0, 2, 1, 3, 4).reshape(10, 120, 128)
    gquads = gquads.reshape(4, NW, 4, SUB, 256)[:, :, :, :REAL].reshape(4, NW, 2, 2, 5, 5, 2, 128)
    patches_grad = gquads.transpose(2, 4, 6, 0, 1, 3, 5, 7).reshape(20, 240, 64)
    small1, small2 = tiny[0:6].reshape(2, 3, C), tiny[6:12].reshape(2, 3, C)
    dbe, dbqkv = tiny[12:20].reshape(2, 4, 512), tiny[20:28, :384].reshape(2, 4, 384)
    sums = jnp.sum(tiny[28:34], axis=1)
    sums, count = sums[:5], sums[5]
    dmgs = lax.dynamic_index_in_dim(tiny[36:40], tp, 0, keepdims=False)
    dmg, dms = dmgs[:256], dmgs[256:]
    blocks = packed.reshape(CHUNKS, ROWS, 128)
    cut = lambda lo, hi: jnp.stack([blocks[13 + lo : 13 + hi], blocks[lo:hi]])
    lanes = lambda x: x.transpose(0, 2, 1, 3).reshape(2, x.shape[2], C)
    g_we, g_ws = lanes(cut(0, 4)), lanes(cut(4, 8))
    g_qkv = cut(8, 11).transpose(0, 2, 1, 3)
    g_wo = lanes(cut(11, 12).reshape(2, 4, 128, 128))
    dbias = cut(12, 13).reshape(8, WT, WT)
    g_tab = table_of(dbias).reshape(2, 4, 361).transpose(0, 2, 1)
    dmw = blocks[26:28].reshape(4, 256, 128).transpose(1, 0, 2).reshape(256, C)
    own4 = lambda x, axis: lax.dynamic_index_in_dim(x, tp, axis, keepdims=False)
    dbqkv = own4(dbqkv, 1).reshape(2, 3, 128)
    g_bias = jnp.stack([dbqkv[:, 0], dbqkv[:, 2]], axis=1)
    g_be = own4(dbe, 1).reshape(2, 512)
    back = lambda x: x.reshape((2, 2, 64) + x.shape[1:]).swapaxes(0, 1).reshape((4, 64) + x.shape[1:])
    rms = jnp.sqrt(sums / (count * C))
    return (
        output, patches_grad, back(dmg), back(dms), back(dmw), small1[:, 0], small1[:, 1], g_qkv, g_bias,
        g_tab, g_wo, small1[:, 2], small2[:, 0], small2[:, 1], g_we, g_be, g_ws, small2[:, 2], rms,
    )


def solution(mesh):
    placed = (
        P("sp", None, "tp"), P(None, "tp"), P(None, "tp"), P(None, "tp", None), P(), P(),
        P(None, None, None, "tp"), P(None, None, "tp"), P(None, None, "tp"), P(None, "tp", None),
        P(), P(), P(), P(None, None, "tp"), P(None, "tp"), P(None, "tp", None), P(), P(),
        P("sp", None), P("sp", None, "tp"),
    )
    results = (
        P("sp", None, "tp"), P("sp", None, "tp"), P(None, "tp"), P(None, "tp"), P(None, "tp", None),
        P(), P(), P(None, None, None, "tp"), P(None, None, "tp"), P(None, None, "tp"),
        P(None, "tp", None), P(), P(), P(), P(None, None, "tp"), P(None, "tp"), P(None, "tp", None),
        P(), P(),
    )
    return jax.shard_map(shards, mesh=mesh, in_specs=placed, out_specs=results, check_vma=False)
```

```python
import functools

import jax
import jax.numpy as jnp
import numpy as np
from jax import lax
from jax.experimental import pallas as pl
from jax.experimental.pallas import tpu as pltpu
from jax.sharding import PartitionSpec as P

C = 512
HD = 32
C2 = 256
WIN = 10
SHIFT = 5
SUB = 32
REAL = 25
WT = 128
TOK = 384
NW = 3
GROUP = 4

bf16 = jnp.bfloat16
f32 = jnp.float32
epsilon = 1e-05
masked = -1000000000.0

NN = (((1,), (0,)), ((), ()))
NT = (((1,), (1,)), ((), ()))
TN = (((0,), (0,)), ((), ()))


def split(x):
    high = x.astype(bf16)
    return high, (x - high.astype(f32)).astype(bf16)


def mm(a, b, dims):
    return lax.dot_general(a, b, dims, preferred_element_type=f32)


def mm3(a, b, dims):
    return mm(a[0], b[0], dims) + (mm(a[0], b[1], dims) + mm(a[1], b[0], dims))


def normalized(x):
    center = x - jnp.mean(x, axis=-1, keepdims=True)
    rho = lax.rsqrt(jnp.mean(center * center, axis=-1, keepdims=True) + epsilon)
    return center * rho, rho


def head_masks(dtype):
    lane = lax.broadcasted_iota(jnp.int32, (1, 128), 1) // HD
    return [(lane == h).astype(f32).astype(dtype) for h in range(GROUP)]


def stacked(pair, masks):
    return tuple(jnp.concatenate([part * m for m in masks], axis=0) for part in pair)


def side_by_side(pair):
    return tuple(
        jnp.concatenate([part[h * WT : (h + 1) * WT] for h in range(GROUP)], axis=1)
        for part in pair
    )


def colsum(x):
    return jnp.sum(x, axis=0, keepdims=True)


def sds(*shape):
    return jax.ShapeDtypeStruct(shape, f32)


def norm_back(x, gain, grad_y):
    xhat, rho = normalized(x)
    gh = grad_y * gain
    grad_x = rho * (
        gh - jnp.mean(gh, axis=-1, keepdims=True) - xhat * jnp.mean(gh * xhat, axis=-1, keepdims=True)
    )
    return grad_x, colsum(grad_y * xhat), colsum(grad_y)


MESH = pl.DeviceIdType.MESH
ANY = pl.BlockSpec(memory_space=pl.ANY)
VM = pl.BlockSpec(memory_space=pltpu.VMEM)


def here():
    sp, tp = lax.axis_index("sp"), lax.axis_index("tp")
    return sp, tp, (sp, tp ^ 1), (sp, tp ^ 2), (sp ^ 1, tp)


def meet(peers):
    barrier = pltpu.get_barrier_semaphore()
    for peer in peers:
        pl.semaphore_signal(barrier, inc=1, device_id=peer, device_id_type=MESH)
    pl.semaphore_wait(barrier, len(peers))


def push(src, dst, send, recv, peer):
    return pltpu.make_async_remote_copy(
        src_ref=src, dst_ref=dst, send_sem=send, recv_sem=recv, device_id=peer, device_id_type=MESH
    )


MLP_ROWS, ATT_ROWS = 4096, 2048
BLOCK_ROWS = MLP_ROWS + ATT_ROWS
FIRST = 2
AG_STEP = 15
STEPS = 17


def chunk_plan(n):
    rows = 256 if n <= 16 else 512
    every = 2 * BLOCK_ROWS // rows
    return rows, every, every + 1024 // rows, 3 if rows == 256 else 1


TINY = 40
COLS = [(0, 0, 0, 1), (0, 1, 1, 0), (1, 0, 1, 1), (1, 1, 2, 0), (2, 0, 2, 1)]


def at(w, sr, sc):
    return pl.ds(w * WT + sr * 64 + sc * SUB, SUB)


NCH = 13
GCH = 2 * NCH
F_STEPS = 19


GATHERED = (0, 0, 0, 3, 9, 10, 11, 13, 17, 18, 19, 20, 22, 24, 26, 28, 30, 30, 30, 30)
AHEAD = 6


def fwd_order(s):
    att = jnp.where(s < 2, 0, jnp.where(s < 6, s - 2, jnp.where(s < 10, 3, jnp.where(s < 14, s - 6, 7))))
    mlp = jnp.where(s < 6, 0, jnp.where(s < 10, s - 6, jnp.where(s < 14, 3, jnp.where(s < 18, s - 10, 7))))
    return att, mlp


def gathered(s):
    found = jnp.int32(GATHERED[0])
    for k in range(1, len(GATHERED)):
        if GATHERED[k] != GATHERED[k - 1]:
            found = jnp.where(s >= k, GATHERED[k], found)
    return found


def fwd_kernel(n, *refs):
    (
        q_ref, mw_ref, mg_ref, wi_ref, bi_ref, wo_ref, we_ref, ws_ref, sm_ref, g1_ref, b1_ref, bo_ref,
        g2_ref, b2_ref, bs_ref, regc_ref, regr_ref, v0_ref, v1_ref, vs_ref, cot_ref,
    ) = refs[:21]
    (
        nall, wall, cb, field_out, mid_out, qkv_ref, p_ref, att_ref, hid_ref, slope_ref, stat_ref, vec_ref,
        sq_ref, os_ref,
    ) = refs[21:35]
    (
        nb, wb, smb, pb, pr, px, stb, str_, stx, vp, vr, vc, field, nh, nl, mixed, moved,
        lsem, ss, sr, xs, xr, ys, yr, zs, zr, s2s, s2r, sms, smr, rss, rsr, vps, vpr, vvs, vvr,
        mvs, mvr, cbs, cbr, cbl, hn, hw,
    ) = refs[35:]
    step = pl.program_id(0)
    sp, tp, sib, across, beside = here()
    par = sp & 1
    up, down = lax.rem(sp + 1, n), lax.rem(sp + n - 1, n)
    left = lax.rem(tp + 3, 4)

    def own():
        todo = []
        for b in range(2):
            todo += [
                (wi_ref.at[b], nb.at[0, pl.ds(4 * b, 3)]), (bi_ref.at[b], nb.at[0, 4 * b + 3]),
                (we_ref.at[b], wb.at[0, pl.ds(9 * b, 4)]), (ws_ref.at[b], wb.at[0, pl.ds(9 * b + 4, 4)]),
                (wo_ref.at[b], wb.at[0, pl.ds(9 * b + 8, 1)]),
            ]
        todo.append((sm_ref, smb.at[0]))
        return [pltpu.make_async_copy(s, d, lsem.at[i]) for i, (s, d) in enumerate(todo)]

    def to_sib(b):
        parts = [(nb, pl.ds(4 * b, 4)), (wb, pl.ds(9 * b + 8, 1)), (wb, pl.ds(9 * b, 8))]
        return [
            push(buf.at[0, d], buf.at[1, d], ss.at[b, k], sr.at[b, k], sib) for k, (buf, d) in enumerate(parts)
        ]

    def narrow(c):
        b, r = c // NCH, c % NCH
        return r < 4, 4 * b + r, 9 * b + jnp.where(r == 4, 8, r - 5)

    def each(c, act):
        small, kn, kw = narrow(c)

        @pl.when(small)
        def _():
            act(nb, kn, 512)

        @pl.when(jnp.logical_not(small))
        def _():
            act(wb, kw, 128)

    zpar = lax.rem(sp // 2, 2)
    far = (sp ^ 2, tp)

    def deep(c):
        return c % 3 != 0

    def cut(size, k):
        return pl.ds(pl.multiple_of(k * size, size), size)

    def x_copy(c, buf, k, size, low):
        d = cut(size // 4, 2 * zpar + par) if low else cut(size // 2, par)
        return push(buf.at[0, k, d], buf.at[2, k, d], xs.at[c], xr.at[c], across)

    def y_copy(c, buf, k, size, low):
        d = cut(size // 4, 2 * zpar + par) if low else cut(size // 2, par)
        return push(buf.at[2, k, d], buf.at[2, k, d], ys.at[c], yr.at[c], beside)

    def z_copy(c, buf, k, size):
        d = cut(size // 2, zpar)
        return push(buf.at[2, k, d], buf.at[2, k, d], zs.at[c], zr.at[c], far)

    def s_copy(which, c, buf, k, size):
        d = cut(size // 2, which)
        send, recv = (s2s, s2r)
        return push(buf.at[2, k, d], buf.at[3, k, d], send.at[which, c], recv.at[which, c], sib)

    def x_start(c):
        def act(buf, k, size):
            for low in (False, True):

                @pl.when(deep(c) == low)
                def _(low=low):
                    x_copy(c, buf, k, size, low).start()

        each(c, act)

    def s_in(c, buf, k, size):
        for h in range(2):
            s_copy(h, c, buf, k, size).wait_recv()

    def rs_copies(k):
        if k < 2:
            i = 1 + 2 * k
            return [
                push(pb.at[i], pr.at[k], rss.at[0, k], rsr.at[0, k], sib),
                push(stb.at[i], str_.at[k], rss.at[1, k], rsr.at[1, k], sib),
            ]
        return [
            push(pb.at[2], px, rss.at[0, 2], rsr.at[0, 2], across),
            push(stb.at[2], stx, rss.at[1, 2], rsr.at[1, 2], across),
        ]

    def vec_copies():
        return [push(vp.at[0], vp.at[i], vps.at[i - 1], vpr.at[i - 1], (sp, tp ^ i)) for i in (1, 2, 3)]

    def sm_copy(k):
        src, dst, peer = ((0, 1, sib), (0, 2, across), (2, 3, sib))[k]
        return push(smb.at[src], smb.at[dst], sms.at[k], smr.at[k], peer)

    def valid_copy():
        return push(vs_ref, vr, vvs.at[0], vvr.at[0], (down, tp))

    def moves():
        todo = [(at(0, 1, 0), at(2, 0, 1), (sp, left)), (at(0, 0, 0), at(2, 1, 1), (down, left))]
        for w0, s0, w1, s1 in COLS:
            todo.append((at(w1, 0, s1), at(w0, 1, s0), (down, tp)))
        return [push(field.at[s], moved.at[d], mvs.at[i], mvr.at[i], peer) for i, (s, d, peer) in enumerate(todo)]

    def cot_copy(k, i):
        t = tp ^ i
        src = cot_ref.at[1 - k, pl.ds(6 * t, 6)]
        return push(src, cb.at[tp, k], cbs.at[k, i], cbr.at[k, i], ((sp, t), (down, t))[k])

    def cot_in(k, i):
        src = cot_ref.at[1 - k, pl.ds(0, 6)]
        return push(src, cb.at[tp ^ i, k], cbs.at[k, i], cbr.at[k, i], (sp, tp ^ 1))

    def cot_own():
        return pltpu.make_async_copy(cot_ref.at[1, pl.ds(6 * tp, 6)], cb.at[tp, 0], cbl.at[0])

    @pl.when(step == 0)
    def _():
        for copy in own():
            copy.start()
        barrier = pltpu.get_barrier_semaphore()
        near = [beside, far] + [(sp, tp ^ i) for i in (1, 2, 3)]
        near += [(up, tp ^ i) for i in range(4)] + [(down, tp ^ i) for i in range(4)]
        for peer in near:
            pl.semaphore_signal(barrier, inc=1, device_id=peer, device_id_type=MESH)
        pl.semaphore_wait(barrier, len(near))
        gain, offset = mg_ref[0:1, :], mg_ref[1:2, :]
        wpair = split(mw_ref[...])
        rows8 = lax.broadcasted_iota(jnp.int32, (8, 256), 0)
        pick = jnp.where(rows8 == 0, gain, jnp.where(rows8 == 1, offset, 0.0))
        vp[0] = jnp.dot(pick, mw_ref[...], precision=lax.Precision.HIGHEST, preferred_element_type=f32)
        for copy in vec_copies():
            copy.start()
        valid_copy().start()
        lane = lax.broadcasted_iota(jnp.int32, (TOK, 128), 1)
        for i in (3, 1, 2, 0):
            quad = q_ref[tp ^ i]
            pb[i] = mm3(split(quad * gain), wpair, NN)
            s1 = jnp.sum(quad, axis=-1, keepdims=True)
            s2 = jnp.sum(quad * quad, axis=-1, keepdims=True)
            stb[i] = jnp.where(lane == 0, s1, jnp.where(lane == 1, s2, 0.0)).T[0:8, :]
            if i % 2 == 1:
                for copy in rs_copies((i - 1) // 2):
                    copy.start()
            if i == 1:
                for copy in own():
                    copy.wait()
                sm_copy(0).start()
                sm_copy(1).start()
                for c in (0, 1):
                    x_copy(c, nb, c, 512, c % 3 != 0).start()
        for copy in rs_copies(1):
            copy.wait_recv()
        pb[2] = pb[2] + pr[1]
        stb[2] = stb[2] + str_[1]
        for copy in rs_copies(2):
            copy.start()
        for copy in to_sib(0):
            copy.start()
        for copy in rs_copies(0):
            copy.wait_recv()
        pb[0] = pb[0] + pr[0]
        stb[0] = stb[0] + str_[0]
        for c in range(2, AHEAD):
            x_copy(c, nb if c < 4 else wb, c if c < 4 else (8 if c == 4 else c - 5), 512 if c < 4 else 128, c % 3 != 0).start()
        sq_ref[...] = jnp.zeros_like(sq_ref)
        os_ref[...] = jnp.zeros_like(os_ref)
        vec_ref[...] = jnp.zeros_like(vec_ref)

    @pl.when(step == 1)
    def _():
        sm_copy(1).wait_recv()
        sm_copy(2).start()
        for copy in vec_copies():
            copy.wait()
        vec_ref[...] = (vp[0] + vp[1]) + (vp[2] + vp[3])
        valid_copy().wait()
        for b in range(2):
            line = v0_ref[...] if b == 0 else v1_ref[...] + vr[...]
            tall = jnp.concatenate([line, jnp.zeros((120, 128), f32)], axis=0).T
            vc[b] = jnp.concatenate([tall[:, w : w + 1] for w in range(NW)], axis=0)
            if b == 1:
                vr[...] = line
        sq_ref[5:6, 0:128] = colsum(v0_ref[...])
        for k in range(2):
            for copy in rs_copies(k):
                copy.wait_send()
        for copy in rs_copies(2):
            copy.wait()
        sums = jnp.concatenate([stb[0] + stx[...], jnp.zeros((120, TOK), f32)], axis=0).T
        mean = sums[:, 0:1] / (4.0 * C2)
        inverse = lax.rsqrt(sums[:, 1:2] / (4.0 * C2) - mean * mean + epsilon)
        lane = lax.broadcasted_iota(jnp.int32, (TOK, 128), 1)
        stat_ref[...] = jnp.where(lane == 0, mean, jnp.where(lane == 1, inverse, 0.0))
        field[...] = inverse * (pb[0] + px[...] - mean * vec_ref[0:1, :]) + vec_ref[1:2, :]

    att, mlp = fwd_order(step)

    @pl.when(((step >= 2) & (step < 6)) | ((step >= 10) & (step < 14)))
    def _():
        b, i = att // 4, att % 4

        @pl.when(i == 0)
        def _():
            @pl.when(b == 1)
            def _():
                for copy in moves():
                    copy.wait()
                field[...] = moved[...]

            field_out[0] = field[...]
            xhat, _ = normalized(field[...])
            nh[...], nl[...] = split(xhat * g1_ref[b] + b1_ref[b])
            mixed[...] = jnp.broadcast_to(bo_ref[b], mixed.shape)

        for k in range(2):

            @pl.when((i == 1) & (b == k))
            def _(k=k):
                for copy in to_sib(k)[:2]:
                    copy.wait_recv()
                if k == 0:
                    sm_copy(0).wait()
                    sm_copy(1).wait_send()
                    sm_copy(2).wait()

        @pl.when(i == 3)
        def _():
            for r in range(5):
                c = b * NCH + r
                buf, k, size = (nb, 4 * b + r, 512) if r < 4 else (wb, 9 * b + 8, 128)
                s_in(c, buf, k, size)

        pltpu.make_async_copy(nb.at[i, pl.ds(4 * b, 4)], nall.at[i, b], hn.at[b, i]).start()
        w = jnp.concatenate([nb[i, 4 * b + j] for j in range(3)], axis=1)
        lane = lax.broadcasted_iota(jnp.int32, (1, 384), 1)
        qkv = mm3((nh[...], nl[...]), split(w), NN) + smb[i, pl.ds(2 + b, 1), 0:384]
        qkv_ref[0] = qkv * jnp.where(lane < 128, HD ** (-0.5), 1.0)
        masks = head_masks(bf16)
        bias = nb[i, 4 * b + 3]
        eye = lax.broadcasted_iota(jnp.int32, (WT, WT), 0) == lax.broadcasted_iota(jnp.int32, (WT, WT), 1)
        for j in range(NW):
            rows = pl.ds(j * WT, WT)
            seen = qkv_ref[0, rows, :]
            q4 = stacked(split(seen[:, :128]), masks)
            k = split(seen[:, 128:256])
            v4 = stacked(split(seen[:, 256:]), masks)
            flags = jnp.where(b == 0, v0_ref[j : j + 1, :], vr[j : j + 1, :])
            allowed = (regc_ref[b, rows, :] == regr_ref[b, j : j + 1, :]) & (flags > 0) | eye
            allowed = jnp.concatenate([allowed.astype(f32)] * GROUP, axis=0) > 0
            s = jnp.where(allowed, mm3(q4, k, NT) + bias, masked)
            e = jnp.exp(s - jnp.max(s, axis=-1, keepdims=True))
            p = e / jnp.sum(e, axis=-1, keepdims=True)
            p_ref[0, j] = p
            att_ref[0, rows, :] = mm3(side_by_side(split(p)), v4, NN)
        mixed[...] += mm3(split(att_ref[0]), split(wb[i, 9 * b + 8]), NN)

        @pl.when(i == 3)
        def _():
            middle = field[...] + mixed[...]
            mid_out[0] = middle
            sq_ref[pl.ds(2 * b, 1), :] = colsum(mixed[...] * mixed[...] * vc[b])

    @pl.when(((step >= 6) & (step < 10)) | ((step >= 14) & (step < 18)))
    def _():
        b, i = mlp // 4, mlp % 4

        @pl.when(i == 0)
        def _():
            xhat, _ = normalized(mid_out[0])
            nh[...], nl[...] = split(xhat * g2_ref[b] + b2_ref[b])
            mixed[...] = jnp.broadcast_to(bs_ref[b], mixed.shape)

            @pl.when(b == 0)
            def _():
                for copy in to_sib(1):
                    copy.start()

        for k in range(2):

            @pl.when((i == 1) & (b == k))
            def _(k=k):
                to_sib(k)[2].wait_recv()

        @pl.when(i == 3)
        def _():
            for r in range(8):
                c = b * NCH + 5 + r
                s_in(c, wb, 9 * b + r, 128)

        pltpu.make_async_copy(wb.at[i, pl.ds(9 * b, 9)], wall.at[i, b], hw.at[b, i]).start()
        we = wb[i, pl.ds(9 * b, 4)].reshape(512, 512)
        ws = wb[i, pl.ds(9 * b + 4, 4)].reshape(512, 512)
        pre = mm3((nh[...], nl[...]), split(we), NN) + smb[i, pl.ds(b, 1), :]
        phi = 0.5 * (1.0 + lax.erf(pre * (2 ** -0.5)))
        hidden = pre * phi
        hid_ref[0] = hidden
        slope_ref[0] = phi + pre * (jnp.exp(-0.5 * pre * pre) * ((2 * np.pi) ** -0.5))
        mixed[...] += mm3(split(hidden), split(ws), NN)

        @pl.when(i == 3)
        def _():
            out = mid_out[0] + mixed[...]
            field[...] = out
            sq_ref[pl.ds(2 * b + 1, 1), :] = colsum(mixed[...] * mixed[...] * vc[b])

            @pl.when(b == 0)
            def _():
                for copy in moves():
                    copy.start()
                for w0, s0, w1, s1 in COLS:
                    moved[at(w0, 0, s0), :] = field[at(w1, 1, s1), :]

            @pl.when(b == 1)
            def _():
                sq_ref[4:5, :] = colsum(out * out * vc[1])
                for t in range(4):
                    for w in range(NW):
                        for r in range(2):
                            os_ref[t, r, w * 64 : w * 64 + 64, :] = out[
                                w * WT + r * 64 : w * WT + r * 64 + 64, t * 128 : (t + 1) * 128
                            ]

    @pl.when(step == 15)
    def _():
        cot_own().start()
        for k in range(2):
            for i in range(4):
                if k + i > 0:
                    cot_copy(k, i).start()

    def both(c, act):
        def run(buf, k, size):
            for low in (False, True):

                @pl.when(deep(c) == low)
                def _(low=low):
                    act(buf, k, size, low)

        each(c, run)

    @pl.loop(gathered(step), gathered(step + 1))
    def _(p):
        @pl.when(p + AHEAD < GCH)
        def _():
            x_start(p + AHEAD)

        @pl.when(p < GCH)
        def _():
            def act(buf, k, size, low):
                x_copy(p, buf, k, size, low).wait_recv()
                y_copy(p, buf, k, size, low).start()
                if not low:
                    for h in range(2):

                        @pl.when(par == h)
                        def _(h=h):
                            s_copy(h, p, buf, k, size).start()

            both(p, act)

        @pl.when((p >= 2) & (p - 2 < GCH))
        def _():
            def act(buf, k, size, low):
                y_copy(p - 2, buf, k, size, low).wait_recv()
                half_here = zpar if low else 1 - par
                if low:
                    z_copy(p - 2, buf, k, size).start()
                for h in range(2):

                    @pl.when(half_here == h)
                    def _(h=h):
                        s_copy(h, p - 2, buf, k, size).start()

            both(p - 2, act)

        @pl.when((p >= 4) & (p - 4 < GCH))
        def _():
            def act(buf, k, size, low):
                if low:
                    z_copy(p - 4, buf, k, size).wait_recv()
                    for h in range(2):

                        @pl.when(1 - zpar == h)
                        def _(h=h):
                            s_copy(h, p - 4, buf, k, size).start()

            both(p - 4, act)

    @pl.when(step == F_STEPS - 1)
    def _():
        cot_own().wait()
        for k in range(2):
            for i in range(4):
                if k + i > 0:
                    cot_copy(k, i).wait_send()
                    cot_in(k, i).wait_recv()
        for b in range(2):
            for copy in to_sib(b):
                copy.wait_send()
            for i in range(4):
                pltpu.make_async_copy(nb.at[i, pl.ds(4 * b, 4)], nall.at[i, b], hn.at[b, i]).wait()
                pltpu.make_async_copy(wb.at[i, pl.ds(9 * b, 9)], wall.at[i, b], hw.at[b, i]).wait()

        @pl.loop(0, GCH)
        def _(c):
            def act(buf, k, size, low):
                x_copy(c, buf, k, size, low).wait_send()
                y_copy(c, buf, k, size, low).wait_send()
                if low:
                    z_copy(c, buf, k, size).wait_send()
                for h in range(2):
                    s_copy(h, c, buf, k, size).wait_send()

            both(c, act)


def forward(n, args, ident):
    dma = pltpu.SemaphoreType.DMA

    def fixed(shape):
        return pl.BlockSpec(shape, lambda s: (0,) * len(shape), pipeline_mode=pl.Buffered(1))

    def by(index, shape):
        zeros = (0,) * len(shape)
        return pl.BlockSpec((1,) + shape, lambda s: (index(s),) + zeros)

    att_at = lambda s: fwd_order(s)[0]
    mlp_at = lambda s: fwd_order(s)[1]
    second = lambda s: jnp.where(s < 10, 0, 1)
    vm = lambda *shape: pltpu.VMEM(shape, f32)
    two = fixed((2, 1, C))
    return pl.pallas_call(
        functools.partial(fwd_kernel, n),
        grid=(F_STEPS,),
        in_specs=[
            fixed((4, TOK, 256)), fixed((256, C)), fixed((8, 256)), ANY, ANY, ANY, ANY, ANY, ANY,
            two, two, two, two, two, two, fixed((2, TOK, 1)), fixed((2, 8, 128)), fixed((8, 128)),
            fixed((8, 128)), fixed((8, 128)), ANY,
        ],
        out_specs=[
            ANY, ANY, ANY, by(second, (TOK, C)), by(second, (TOK, C)), by(att_at, (TOK, 384)),
            by(att_at, (NW, GROUP * WT, WT)), by(att_at, (TOK, 128)), by(mlp_at, (TOK, 512)),
            by(mlp_at, (TOK, 512)), fixed((TOK, 128)), fixed((8, C)), fixed((8, C)), fixed((4, 2, 192, 128)),
        ],
        out_shape=[
            sds(4, 2, 4, 512, 128), sds(4, 2, 9, 128, 512), sds(4, 2, 6, SUB, 128), sds(2, TOK, C), sds(2, TOK, C),
            sds(8, TOK, 384), sds(8, NW, GROUP * WT, WT), sds(8, TOK, 128), sds(8, TOK, 512), sds(8, TOK, 512),
            sds(TOK, 128), sds(8, C), sds(8, C), sds(4, 2, 192, 128),
        ],
        scratch_shapes=[
            vm(4, 8, 512, 128), vm(4, 18, 128, 512), vm(4, 8, C), vm(4, TOK, C), vm(2, TOK, C), vm(TOK, C),
            vm(4, 8, TOK), vm(2, 8, TOK), vm(8, TOK), vm(4, 8, C), vm(8, 128), vm(2, TOK, 1), vm(TOK, C),
            pltpu.VMEM((TOK, C), bf16), pltpu.VMEM((TOK, C), bf16), vm(TOK, C), vm(TOK, C),
            dma((11,)), dma((2, 3)), dma((2, 3)), dma((GCH,)), dma((GCH,)), dma((GCH,)), dma((GCH,)),
            dma((GCH,)), dma((GCH,)), dma((2, GCH)), dma((2, GCH)), dma((3,)), dma((3,)), dma((2, 3)), dma((2, 3)),
            dma((3,)), dma((3,)), dma((1,)), dma((1,)), dma((7,)), dma((7,)), dma((2, 4)), dma((2, 4)),
            dma((1,)), dma((2, 4)), dma((2, 4)),
        ],
        compiler_params=pltpu.CompilerParams(
            collective_id=ident, has_side_effects=True, vmem_limit_bytes=60 << 20,
            dimension_semantics=("arbitrary",),
        ),
        name="forward",
    )(*args)


def table_line(dbias, pick, pile):
    high, low = split(dbias)
    spread = mm(high, pick, NN) + mm(low, pick, NN)
    spread = jnp.concatenate([spread[h * WT : (h + 1) * WT] for h in range(GROUP)], axis=1)
    high, low = split(spread)
    piled = mm(pile, high, NN) + mm(pile, low, NN)
    total = piled[0:16]
    for pc in range(1, WIN):
        total = total + pltpu.roll(piled[pc * 16 : pc * 16 + 16], pc, 1)
    row = lax.broadcasted_iota(jnp.int32, total.shape, 0)
    line = jnp.where(row == 0, total, 0.0)
    for pr in range(1, WIN):
        line = line + jnp.where(row == pr, pltpu.roll(total, 19 * pr, 1), 0.0)
    return colsum(line)


def table_picks():
    pick = np.zeros((WT, 384), np.float32)
    pile = np.zeros((WIN, 16, WT), np.float32)
    for r in range(WIN):
        for c in range(WIN):
            place = (r // 5) * 64 + (c // 5) * SUB + (r % 5) * 5 + c % 5
            pick[place, (9 - r) * 19 + 9 - c] = 1.0
            pile[c, r, place] = 1.0
    return jnp.asarray(pick, bf16), jnp.asarray(pile.reshape(160, WT), bf16)


def bwd_kernel(n, *refs):
    (
        cot_ref, mid_ref, field_ref, g1_ref, b1_ref, g2_ref, b2_ref, we_ref, ws_ref, wqkv_ref, wo_ref,
        hid_ref, slope_ref, qkv_ref, p_ref, att_ref, sq_ref, q_ref, mw_ref, vec_ref, mg_ref, stat_ref, os_ref,
        pick_ref, pile_ref,
    ) = refs[:25]
    pack, gall, exall, ob, out_ref, gq_ref, tout_ref = refs[25:32]
    (
        nth, ntl, gh, gl, acc, dqkv, gf, gbuf, moved, ext, extin, qbuf,
        loc, pair, yr, zr, fin, ta, tx, tz, tsh, tr,
        gsem, mvs, mvr, ags, agr, agl, msem, ss, rs, zs, zq, fs, fq, ls, os, tzs, tzq, obs, obr, obl, tss, tsq,
    ) = refs[32:]
    step = pl.program_id(0)
    dmw, gqbuf = moved.at[pl.ds(0, 256)], dqkv.at[:, pl.ds(0, 256)]
    sp, tp, sib, across, beside = here()
    par, mine = sp & 1, sp // 2
    m = n // 2
    ROWS, FULL_CH, CHUNKS, RATE = chunk_plan(n)
    HALF = ROWS // 2
    piece = HALF // m
    up, down, right = lax.rem(sp + 1, n), lax.rem(sp + n - 1, n), lax.rem(tp + 1, 4)

    def member(j):
        return lax.rem(mine + j, m)

    def device(q):
        return (q * 2 + par, tp)

    def out_copy(k, i):
        t = tp ^ i
        return push(
            os_ref.at[t, k], ob.at[1 - k, pl.ds(6 * tp, 6)], obs.at[k, i], obr.at[k, i], ((sp, t), (up, t))[k]
        )

    def out_in(k, i):
        return push(
            os_ref.at[0, k], ob.at[1 - k, pl.ds(6 * (tp ^ i), 6)], obs.at[k, i], obr.at[k, i], (sp, tp ^ 1)
        )

    def out_own():
        return pltpu.make_async_copy(os_ref.at[tp, 0], ob.at[1, pl.ds(6 * tp, 6)], obl.at[0])

    @pl.when(step == 0)
    def _():
        barrier = pltpu.get_barrier_semaphore()
        near = [beside] + [(sp, tp ^ i) for i in (1, 2, 3)]
        near += [(up, tp ^ i) for i in range(4)] + [(down, tp ^ i) for i in range(4)]
        for peer in near:
            pl.semaphore_signal(barrier, inc=1, device_id=peer, device_id_type=MESH)

        @pl.loop(1, m)
        def _(j):
            pl.semaphore_signal(barrier, inc=1, device_id=device(member(j)), device_id_type=MESH)

        ta[...] = jnp.zeros_like(ta)
        tsh[...] = jnp.zeros_like(tsh)
        ta[0, 28:36, :] = sq_ref[...]
        for t in range(4):
            for w in range(NW):
                for r in range(2):
                    gf[w * WT + r * 64 : w * WT + r * 64 + 64, t * 128 : (t + 1) * 128] = cot_ref[
                        t, r, w * 64 : w * 64 + 64, :
                    ]
        pl.semaphore_wait(barrier, len(near) + m - 1)
        out_own().start()
        for k in range(2):
            for i in range(4):
                if k + i > 0:
                    out_copy(k, i).start()

    def packed(b, j, late):
        size = ATT_ROWS if late else MLP_ROWS
        base = pl.multiple_of((1 - b) * BLOCK_ROWS + (MLP_ROWS if late else 0), 512)
        slot = j % 2
        return pltpu.make_async_copy(
            gbuf.at[slot, pl.ds(0, size)], pack.at[tp ^ j ^ 2, pl.ds(base, size)], gsem.at[slot]
        )

    def moves():
        todo = [
            (at(2, 0, 1), at(0, 1, 0), (sp, right)),
            (at(2, 1, 1), at(0, 0, 0), (up, right)),
        ]
        for w0, s0, w1, s1 in COLS:
            todo.append((at(w0, 1, s0), at(w1, 0, s1), (up, tp)))
        return [push(acc.at[src], moved.at[dst], mvs.at[i], mvr.at[i], peer) for i, (src, dst, peer) in enumerate(todo)]

    def kept():
        for w0, s0, w1, s1 in COLS:
            moved[at(w1, 1, s1), :] = acc[at(w0, 0, s0), :]

    phase = step // 4

    @pl.when((phase == 0) | (phase == 2))
    def _():
        b = 1 - phase // 2
        j = step % 4
        i = j ^ 2

        @pl.when(j == 0)
        def _():
            @pl.when(b == 0)
            def _():
                for copy in moves():
                    copy.wait()
                gf[...] = moved[...]

            xhat, _ = normalized(mid_ref[0])
            nth[...], ntl[...] = split((xhat * g2_ref[b] + b2_ref[b]).T)
            gh[...], gl[...] = split(gf[...])
            acc[...] = jnp.zeros_like(acc)

        slot = j % 2
        grad = (gh[...], gl[...])
        dws = mm3(split(hid_ref[0].T), grad, NN)
        for q in range(4):
            gbuf[slot, 2048 + q * 512 : 2560 + q * 512, :] = dws[:, q * 128 : (q + 1) * 128]
        dpre = mm3(grad, split(ws_ref[0, 0].reshape(512, C)), NT) * slope_ref[0]
        tsh[i, pl.ds(b, 1), :] = colsum(dpre)
        pair_ = split(dpre)
        dwe = mm3((nth[...], ntl[...]), pair_, NN)
        for q in range(4):
            gbuf[slot, q * 512 : (q + 1) * 512, :] = dwe[:, q * 128 : (q + 1) * 128]
        acc[...] += mm3(pair_, split(we_ref[0, 0].reshape(C, 512)), NT)

        @pl.when(j > 0)
        def _():
            packed(b, j - 1, False).wait()

        packed(b, j, False).start()

        @pl.when(j == 3)
        def _():
            grad_x, dgain, dshift = norm_back(mid_ref[0], g2_ref[b], acc[...])
            ta[0, pl.ds(22 + 3 * b, 1), :] = dgain
            ta[0, pl.ds(23 + 3 * b, 1), :] = dshift
            ta[0, pl.ds(24 + 3 * b, 1), :] = colsum(gf[...])
            gf[...] = gf[...] + grad_x
            packed(b, 3, False).wait()

    @pl.when((phase == 1) | (phase == 3))
    def _():
        b = 1 - phase // 2
        j = step % 4
        i = j ^ 2

        @pl.when(j == 0)
        def _():
            xhat, _ = normalized(field_ref[0])
            nth[...], ntl[...] = split((xhat * g1_ref[b] + b1_ref[b]).T)
            gh[...], gl[...] = split(gf[...])
            acc[...] = jnp.zeros_like(acc)

        slot = j % 2
        grad = (gh[...], gl[...])
        dwo = mm3(split(att_ref[0].T), grad, NN)
        for q in range(4):
            gbuf[slot, 1536 + q * 128 : 1664 + q * 128, :] = dwo[:, q * 128 : (q + 1) * 128]
        dout = mm3(grad, split(wo_ref[0, 0, 0]), NT)
        masks = head_masks(bf16)
        dbias = jnp.zeros((GROUP * WT, WT), f32)
        for w in range(NW):
            rows = slice(w * WT, (w + 1) * WT)
            seen = qkv_ref[0, pl.ds(w * WT, WT), :]
            q4 = stacked(split(seen[:, :128]), masks)
            k4 = stacked(split(seen[:, 128:256]), masks)
            v = split(seen[:, 256:])
            p = p_ref[0, w]
            do4 = stacked(split(dout[rows]), masks)
            dp = mm3(do4, v, NT)
            ds = p * (dp - jnp.sum(p * dp, axis=-1, keepdims=True))
            dbias = dbias + ds
            dpair = split(ds)
            dqkv[pl.ds(w * WT, WT), 0:128] = mm3(side_by_side(dpair), k4, NN) * HD ** (-0.5)
            dqkv[pl.ds(w * WT, WT), 128:256] = mm3(dpair, q4, TN)
            dqkv[pl.ds(w * WT, WT), 256:384] = mm3(split(p), do4, TN)
        line = table_line(dbias, pick_ref[...], pile_ref[...])
        for q in range(3):
            tsh[i, pl.ds(4 + 3 * b + q, 1), :] = line[:, q * 512 : (q + 1) * 512]
        grads = dqkv[...]
        tsh[i, pl.ds(2 + b, 1), 0:384] = colsum(grads)
        pair_ = split(grads)
        dw = mm3((nth[...], ntl[...]), pair_, NN)
        for q in range(3):
            gbuf[slot, q * 512 : (q + 1) * 512, :] = dw[:, q * 128 : (q + 1) * 128]
        w = jnp.concatenate([wqkv_ref[0, 0, q] for q in range(3)], axis=1)
        acc[...] += mm3(pair_, split(w), NT)

        @pl.when(j > 0)
        def _():
            packed(b, j - 1, True).wait()

        packed(b, j, True).start()

        @pl.when(j == 3)
        def _():
            grad_x, dgain, dshift = norm_back(field_ref[0], g1_ref[b], acc[...])
            ta[0, pl.ds(16 + 3 * b, 1), :] = dgain
            ta[0, pl.ds(17 + 3 * b, 1), :] = dshift
            ta[0, pl.ds(18 + 3 * b, 1), :] = colsum(gf[...])
            acc[...] = gf[...] + grad_x

            @pl.when(b == 1)
            def _():
                for copy in moves():
                    copy.start()
                kept()

            packed(b, 3, True).wait()

    def ag(k, src, dst, peer, which):
        return push(src, dst, ags.at[which, k], agr.at[which, k], peer)

    def ag_copies(k):
        own = (acc, ext)
        whole_ = (gall, exall)
        return [
            ag(k, own[w], whole_[w].at[tp], (sib, across)[k], w) if k < 2
            else ag(k, whole_[w].at[tp ^ 2], whole_[w].at[tp ^ 2], sib, w)
            for w in range(2)
        ]

    @pl.when(step == AG_STEP)
    def _():
        m2 = jnp.sum(acc[...] * (field_ref[0] - vec_ref[1:2, :]), axis=-1, keepdims=True)
        lane = lax.broadcasted_iota(jnp.int32, (TOK, 128), 1)
        tall = jnp.where(lane == 2, m2, stat_ref[...])
        ext[...] = tall.T[0:8, :]
        for k in range(2):
            for copy in ag_copies(k):
                copy.start()

    def ag_pass():
        for copy in ag_copies(1):
            copy.wait()
        for copy in ag_copies(2):
            copy.start()

    def merge(i):
        t = tp ^ i

        for k in (0, 2):

            @pl.when(i == (1 if k == 0 else 2))
            def _(k=k):
                for copy in ag_copies(k):
                    copy.wait()

        fetch = [pltpu.make_async_copy(q_ref.at[t], qbuf, msem.at[0])]
        fetch[0].start()

        @pl.when(i == 0)
        def _():
            dmw[...] = jnp.zeros((256, C), f32)
            gf[...] = acc[...]
            extin[...] = ext[...]

        @pl.when(i > 0)
        def _():
            two = [
                pltpu.make_async_copy(gall.at[t], gf, msem.at[1]),
                pltpu.make_async_copy(exall.at[t], extin, msem.at[2]),
            ]
            for copy in two:
                copy.start()
            for copy in two:
                copy.wait()

        fetch[0].wait()
        wide = jnp.concatenate([extin[...], jnp.zeros((120, TOK), f32)], axis=0).T
        mean, inv, m2 = wide[:, 0:1], wide[:, 1:2], wide[:, 2:3]
        full = gf[...]
        m1 = jnp.sum(full * vec_ref[0:1, :], axis=-1, keepdims=True) / (4.0 * C2)
        m2 = m2 / (4.0 * C2)
        fpair = split(full)
        xhat = (qbuf[...] - mean) * inv
        gmerged = mm3(fpair, split(mw_ref[...]), NT)
        dmw[...] += mm3(split((xhat * mg_ref[0:1, :] + mg_ref[1:2, :]).T), fpair, NN)
        tsh[0, 10:11, 0:256] += colsum(gmerged * xhat)
        tsh[0, 10:11, 256:512] += colsum(gmerged)

        @pl.when(i > 0)
        def _():
            pltpu.make_async_copy(gqbuf, gq_ref.at[t], msem.at[3]).wait()

        gqbuf[...] = inv * (gmerged * mg_ref[0:1, :] - m1 - xhat * m2)
        pltpu.make_async_copy(gqbuf, gq_ref.at[t], msem.at[3]).start()

        @pl.when(i == 3)
        def _():
            pltpu.make_async_copy(gqbuf, gq_ref.at[t], msem.at[3]).wait()
            for k in range(4):
                row = k * 256
                pair[FULL_CH + row // ROWS, 0, row % ROWS : row % ROWS + 256, :] = dmw[:, k * 128 : (k + 1) * 128]

    def rows(c):
        return pl.ds(pl.multiple_of(c * ROWS, ROWS), ROWS)

    def load(c, k):
        return pltpu.make_async_copy(pack.at[tp ^ (2 * k), rows(c)], loc.at[c % 4, k], ls.at[c % 4, k])

    def swap(c, k):
        return push(pack.at[tp ^ 1 ^ (2 * k), rows(c)], pair.at[c, k], ss.at[k, c], rs.at[k, c], sib)

    def cross(c):
        return push(pair.at[c, 1], fin.at[c], ss.at[2, c], rs.at[2, c], across)

    def halves(h):
        return pl.ds(pl.multiple_of(h * HALF, HALF), HALF)

    def side(c):
        return push(pair.at[c, 0, halves(1 - par)], yr.at[c], ss.at[3, c], rs.at[3, c], beside)

    def bit(q):
        return pl.ds(pl.multiple_of(q * piece, piece), piece)

    def spread(c, q, slot):
        return push(yr.at[c, bit(q)], zr.at[c, slot], zs.at[c % 4, q], zq.at[c, slot], device(q))

    def place(q):
        return pl.ds(pl.multiple_of(par * HALF + q * piece, piece), piece)

    def share(c, q, slot):
        return push(fin.at[c, place(slot)], fin.at[c, place(slot)], fs.at[c % 4, q], fq.at[c, slot], device(q))

    def back(c):
        return push(fin.at[c, halves(par)], fin.at[c, halves(par)], ss.at[4, c], rs.at[4, c], beside)

    def write(c):
        return pltpu.make_async_copy(fin.at[c], out_ref.at[rows(c)], os.at[c])

    low, high = pl.ds(0, 16), pl.ds(16, 24)

    def tiny(k):
        if k == 0:
            todo = [(tsh.at[1], tr.at[0]), (tsh.at[3], tr.at[1]), (ta.at[0, high], tx.at[0, high])]
        elif k == 1:
            todo = [(tsh.at[2], tx.at[1, low]), (ta.at[1, high], tx.at[1, high])]
        else:
            todo = [(ta.at[2], tx.at[2])]
        peer = (sib, across, beside)[k]
        return [push(a, b, tss.at[k, i], tsq.at[k, i], peer) for i, (a, b) in enumerate(todo)]

    def tiny_sum(k):
        if k == 0:
            ta[1, low] = tsh[0] + tr[0]
            ta[1, high] = ta[0, high] + tx[0, high]
            tsh[2] = tsh[2] + tr[1]
        else:
            ta[k + 1] = ta[k] + tx[k]

    def tiny_z(q, slot):
        return push(ta.at[3], tz.at[slot], tzs.at[q], tzq.at[slot], device(q))

    late = RATE * (16 - FIRST)
    tiny_turn = late + 10

    def begun(s):
        return jnp.where(s < FIRST, 0, jnp.where(s < STEPS, RATE * (s - FIRST), CHUNKS + 18))

    def turn(p):
        @pl.when(p == late + 5)
        def _():
            ag_pass()

        due = p - late

        @pl.when((due >= 0) & (due < 12) & (due % 3 == 0))
        def _():
            merge(due // 3)

        def stage(lag, end):
            c = p - lag
            return c, (c >= 0) & (c < end)

        for k in range(4):

            @pl.when(p == tiny_turn + 4 * k)
            def _(k=k):
                if k > 0:
                    for copy in tiny(k - 1):
                        copy.wait()
                    tiny_sum(k - 1)
                if k < 3:
                    for copy in tiny(k):
                        copy.start()
                else:
                    tz[mine] = ta[3]

                    @pl.loop(1, m)
                    def _(j):
                        tiny_z(member(j), mine).start()

        c0, on0 = stage(0, FULL_CH)

        @pl.when(on0)
        def _():
            swap(c0, 1).start()
            load(c0, 1).start()

        c1, on1 = stage(2, FULL_CH)

        @pl.when(on1)
        def _():
            load(c1, 1).wait()
            swap(c1, 1).wait_recv()
            pair[c1, 1] = pair[c1, 1] + loc[c1 % 4, 1]
            cross(c1).start()

        c2, on2 = stage(3, FULL_CH)

        @pl.when(on2)
        def _():
            swap(c2, 0).start()
            load(c2, 0).start()

        c3, on3 = stage(6, CHUNKS)

        @pl.when(on3)
        def _():
            @pl.when(c3 < FULL_CH)
            def _():
                load(c3, 0).wait()
                swap(c3, 0).wait_recv()
                cross(c3).wait_recv()
                pair[c3, 0] = (pair[c3, 0] + loc[c3 % 4, 0]) + fin[c3]

            side(c3).start()

        c4, on4 = stage(9, CHUNKS)

        @pl.when(on4)
        def _():
            side(c4).wait_recv()
            yr[c4] = yr[c4] + pair[c4, 0, halves(par)]

            @pl.loop(1, m)
            def _(j):
                spread(c4, member(j), mine).start()

        c5, on5 = stage(12, CHUNKS)

        @pl.when(on5)
        def _():
            fin[c5, place(mine)] = yr[c5, bit(mine)]

            @pl.loop(1, m)
            def _(j):
                spread(c5, member(j), member(j)).wait_recv()
                fin[c5, place(mine)] = fin[c5, place(mine)] + zr[c5, member(j)]

            @pl.loop(1, m)
            def _(j):
                share(c5, member(j), mine).start()
                spread(c5, member(j), mine).wait_send()

        c6, on6 = stage(15, CHUNKS)

        @pl.when(on6)
        def _():
            @pl.loop(1, m)
            def _(j):
                share(c6, member(j), member(j)).wait_recv()
                share(c6, member(j), mine).wait_send()

            back(c6).start()

        c7, on7 = stage(18, CHUNKS)

        @pl.when(on7)
        def _():
            back(c7).wait_recv()
            write(c7).start()

    @pl.loop(begun(step), begun(step + 1))
    def _(p):
        turn(p)

    @pl.when(step == STEPS - 1)
    def _():
        @pl.loop(1, m)
        def _(j):
            tiny_z(member(j), member(j)).wait_recv()
            tiny_z(member(j), mine).wait_send()

        out_own().wait()
        for k in range(2):
            for i in range(4):
                if k + i > 0:
                    out_copy(k, i).wait_send()
                    out_in(k, i).wait_recv()
        total = tz[0]
        for q in range(1, m):
            total = total + tz[q]
        tout_ref[...] = total

        @pl.loop(0, CHUNKS)
        def _(c):
            @pl.when(c < FULL_CH)
            def _():
                for k in range(2):
                    swap(c, k).wait_send()
                cross(c).wait_send()

            side(c).wait_send()
            back(c).wait_send()
            write(c).wait()


def backward(n, args, ident):
    m = n // 2
    ROWS, FULL_CH, CHUNKS, _ = chunk_plan(n)
    HALF = ROWS // 2
    dma = pltpu.SemaphoreType.DMA

    def fixed(shape):
        return pl.BlockSpec(shape, lambda s: (0,) * len(shape), pipeline_mode=pl.Buffered(1))

    def mlp_at(s):
        return jnp.where(s < 4, 4 + (s ^ 2), jnp.where(s < 8, 2, jnp.where(s < 12, (s - 8) ^ 2, 1)))

    def att_at(s):
        return jnp.where(s < 4, 6, jnp.where(s < 8, 4 + ((s - 4) ^ 2), jnp.where(
            s < 12, 2, jnp.where(s < 16, (s - 12) ^ 2, 1))))

    def by(index, shape, mode=None):
        zeros = (0,) * len(shape)
        return pl.BlockSpec((1,) + shape, lambda s: (index(s),) + zeros, pipeline_mode=mode)

    def spot(index, shape, k):
        return pl.BlockSpec((1, 1) + shape, lambda s: (index(s) % 4, index(s) // 4, k, 0, 0))

    one = pl.Buffered(1)
    lanes = (CHUNKS, ROWS, 128)
    in_specs = [
        fixed((4, 2, 192, 128)), by(lambda s: jnp.where(s < 4, 1, 0), (TOK, C), one),
        by(lambda s: jnp.where(s < 8, 1, 0), (TOK, C), one),
        fixed((2, 1, C)), fixed((2, 1, C)), fixed((2, 1, C)), fixed((2, 1, C)),
        spot(mlp_at, (4, 128, 512), 0), spot(mlp_at, (4, 128, 512), 1), spot(att_at, (3, C, 128), 0),
        spot(att_at, (1, 128, C), 8),
        by(mlp_at, (TOK, 512)), by(mlp_at, (TOK, 512)), by(att_at, (TOK, 384)),
        by(att_at, (NW, GROUP * WT, WT)), by(att_at, (TOK, 128)),
        fixed((8, C)), ANY, fixed((256, C)), fixed((8, C)), fixed((8, 256)), fixed((TOK, 128)), ANY,
        fixed((WT, 384)), fixed((160, WT)),
    ]
    return pl.pallas_call(
        functools.partial(bwd_kernel, n),
        grid=(STEPS,),
        in_specs=in_specs,
        out_specs=[ANY, ANY, ANY, ANY, ANY, ANY, fixed((TINY, C))],
        out_shape=[
            sds(4, FULL_CH * ROWS, 128), sds(4, TOK, C), sds(4, 8, TOK), sds(2, 24, SUB, 128), sds(CHUNKS * ROWS, 128),
            sds(4, TOK, 256), sds(TINY, C),
        ],
        scratch_shapes=[
            pltpu.VMEM((C, TOK), bf16), pltpu.VMEM((C, TOK), bf16), pltpu.VMEM((TOK, C), bf16),
            pltpu.VMEM((TOK, C), bf16), pltpu.VMEM((TOK, C), f32), pltpu.VMEM((TOK, 384), f32),
            pltpu.VMEM((TOK, C), f32), pltpu.VMEM((2, MLP_ROWS, 128), f32), pltpu.VMEM((TOK, C), f32),
            pltpu.VMEM((8, TOK), f32), pltpu.VMEM((8, TOK), f32), pltpu.VMEM((TOK, 256), f32),
            pltpu.VMEM((4, 2, ROWS, 128), f32), pltpu.VMEM((CHUNKS, 2, ROWS, 128), f32),
            pltpu.VMEM((CHUNKS, HALF, 128), f32), pltpu.VMEM((CHUNKS, m, HALF // m, 128), f32),
            pltpu.VMEM(lanes, f32), pltpu.VMEM((4, TINY, C), f32), pltpu.VMEM((3, TINY, C), f32),
            pltpu.VMEM((m, TINY, C), f32), pltpu.VMEM((4, 16, C), f32), pltpu.VMEM((2, 16, C), f32),
            dma((2,)), dma((7,)), dma((7,)), dma((2, 3)), dma((2, 3)), dma((2,)), dma((4,)),
            dma((5, CHUNKS)), dma((5, CHUNKS)), dma((4, m)), dma((CHUNKS, m)), dma((4, m)),
            dma((CHUNKS, m)), dma((4, 2)), dma((CHUNKS,)), dma((m,)), dma((m,)),
            dma((2, 4)), dma((2, 4)), dma((1,)), dma((3, 3)), dma((3, 3)),
        ],
        compiler_params=pltpu.CompilerParams(
            collective_id=ident, has_side_effects=True, vmem_limit_bytes=60 << 20,
            dimension_semantics=("arbitrary",),
        ),
        name="backward",
    )(*args)


def column_pick():
    pick = np.zeros((19, WIN, WIN), np.float32)
    for a in range(WIN):
        for b in range(WIN):
            pick[a - b + WIN - 1, a, b] = 1.0
    return pick


def row_pick():
    pick = np.zeros((19, WIN, WIN, WIN, 2, 2, SUB), np.float32)
    for pr in range(WIN):
        for qr in range(WIN):
            for qc in range(WIN):
                pick[pr - qr + WIN - 1, qc, pr, 0, qr // 5, qc // 5, (qr % 5) * 5 + qc % 5] = 1.0
    return pick[:, :, :, 0].reshape(190, WIN * WT)


def bias_of(table):
    heads = table.shape[0]
    grid = table.reshape(heads, 19, 19)
    columns = jnp.einsum("hrd,dab->harb", grid, jnp.asarray(column_pick()), precision="highest")
    rows = jnp.dot(columns.reshape(heads * WIN, 190), jnp.asarray(row_pick()), precision="highest")
    rows = rows.reshape(heads, 2, 5, 2, 5, WT).transpose(0, 3, 1, 4, 2, 5)
    rows = rows.reshape(heads, 4, REAL, WT)
    return jnp.pad(rows, ((0, 0), (0, 0), (0, SUB - REAL), (0, 0))).reshape(heads, WT, WT)


def shards(
    patches, merge_gain, merge_shift, merge_weight, first_gain, first_shift, input_weight,
    input_bias, position_table, output_weight, output_bias, second_gain, second_shift,
    expand_weight, expand_bias, shrink_weight, shrink_bias, page_map, valid_flags, cotangent,
):
    sp_count = lax.axis_size("sp")
    tp = lax.axis_index("tp")
    sp = lax.axis_index("sp")

    tables = position_table.transpose(0, 2, 1).reshape(8, 361)
    bias = bias_of(tables).reshape(2, 512, 128)
    pairs = jnp.concatenate([input_bias, jnp.zeros_like(input_bias)], axis=2).reshape(2, 512)
    small = jnp.concatenate([expand_bias, pairs, jnp.zeros((4, 512), f32)], axis=0)
    three = lambda x: x.reshape(2, 1, C)

    valid = valid_flags.astype(f32).reshape(2, 5, 24, 5).transpose(0, 2, 1, 3).reshape(2, 24, REAL)
    valid = jnp.pad(valid, ((0, 0), (0, 0), (0, SUB - REAL)))
    own = lambda grid: lax.dynamic_slice_in_dim(grid, 6 * tp, 6, 1).reshape(2, NW, 2 * SUB)
    here_ = own(valid)
    next_ = own(jnp.roll(valid, -1, axis=1))
    blank = jnp.zeros((NW, 2 * SUB), f32)
    line = lambda a, c: jnp.pad(jnp.concatenate([a, c], axis=1), ((0, 5), (0, 0)))
    valid0, valid1, valids = line(here_[0], here_[1]), line(next_[1], blank), line(blank, next_[0])
    pages = jnp.concatenate([page_map, page_map[:1]], axis=0)
    pages = jnp.concatenate([pages, pages[:, :1]], axis=1)
    pages = lax.dynamic_slice(pages, (sp, 3 * tp), (2, 4))
    page = jnp.stack([pages[:, :3], pages[:, 1:]], axis=2).transpose(1, 0, 2)
    wrap_row = (jnp.arange(2) == 1) & (sp == sp_count - 1)
    wrap_col = (jnp.arange(2) == 1)[None, :] & (jnp.arange(NW) == NW - 1)[:, None] & (tp == 3)
    region = page * 4 + 2 * wrap_row[None, :, None].astype(jnp.int32) + wrap_col[:, None, :].astype(jnp.int32)
    region = jnp.broadcast_to(region[..., None], (NW, 2, 2, SUB)).reshape(NW, WT)
    region = jnp.stack([jnp.zeros_like(region), region])
    regc, regr = region.reshape(2, TOK, 1), jnp.pad(region, ((0, 0), (0, 5), (0, 0)))

    gain = merge_gain.reshape(2, 2, 64).transpose(1, 0, 2).reshape(1, 256)
    offset = merge_shift.reshape(2, 2, 64).transpose(1, 0, 2).reshape(1, 256)
    mgain = jnp.concatenate([gain, offset, jnp.zeros((6, 256), f32)], axis=0)
    weight = merge_weight.reshape(2, 2, 64, C).transpose(1, 0, 2, 3).reshape(256, C)
    quads = patches.reshape(2, 5, 2, 4, NW, 2, 5, 128).transpose(3, 4, 0, 5, 1, 6, 2, 7).reshape(4, NW, 4, REAL, 256)
    quads = jnp.pad(quads, ((0, 0), (0, 0), (0, 0), (0, SUB - REAL), (0, 0))).reshape(4, TOK, 256)
    cot = jnp.roll(cotangent.reshape(2, 5, 24, 5, 128), -1, axis=2).transpose(0, 2, 1, 3, 4).reshape(2, 24, REAL, 128)
    cot = jnp.pad(cot, ((0, 0), (0, 0), (0, SUB - REAL), (0, 0)))

    nall, wall, cot, fields, middles, qkv, p, att, hid, slope, stat, vecs, squares, out = forward(
        sp_count,
        (
            quads, weight, mgain, input_weight.transpose(0, 2, 1, 3), bias, output_weight.reshape(2, 1, 128, C),
            expand_weight.reshape(2, 4, 128, 512), shrink_weight.reshape(2, 4, 128, C), small,
            three(first_gain), three(first_shift), three(output_bias), three(second_gain), three(second_shift),
            three(shrink_bias), regc, regr, valid0, valid1, valids, cot,
        ),
        1,
    )
    _, _, _, output, packed, gquads, tiny = backward(
        sp_count,
        (
            cot.reshape(4, 2, 192, 128), middles, fields, three(first_gain), three(first_shift),
            three(second_gain), three(second_shift), wall, wall, nall, wall, hid, slope, qkv, p, att,
            squares, quads, weight, vecs, mgain, stat, out.reshape(4, 2, 6, SUB, 128),
            *table_picks(),
        ),
        2,
    )
    output = jnp.roll(output[:, :, :REAL], 1, axis=1).reshape(2, 24, 5, 5, 128)
    output = output.transpose(0, 2, 1, 3, 4).reshape(10, 120, 128)
    gquads = gquads.reshape(4, NW, 4, SUB, 256)[:, :, :, :REAL].reshape(4, NW, 2, 2, 5, 5, 2, 128)
    patches_grad = gquads.transpose(2, 4, 6, 0, 1, 3, 5, 7).reshape(20, 240, 64)
    small1, small2 = tiny[16:22].reshape(2, 3, C), tiny[22:28].reshape(2, 3, C)
    sums = jnp.sum(tiny[28:34], axis=1)
    sums, count = sums[:5], sums[5]
    g_be, dbqkv, dmg, dms = tiny[0:2], tiny[2:4, :384].reshape(2, 3, 128), tiny[10, :256], tiny[10, 256:]
    g_bias = jnp.stack([dbqkv[:, 0], dbqkv[:, 2]], axis=1)
    g_tab = tiny[4:10].reshape(2, 4, 384)[:, :, :361].transpose(0, 2, 1)
    blocks = packed.reshape(26, 512, 128)
    cut = lambda lo, hi: jnp.stack([blocks[12 + lo : 12 + hi], blocks[lo:hi]])
    lanes = lambda x: x.transpose(0, 2, 1, 3).reshape(2, x.shape[2], C)
    g_we, g_ws = lanes(cut(0, 4)), lanes(cut(4, 8))
    g_qkv = cut(8, 11).transpose(0, 2, 1, 3)
    g_wo = lanes(cut(11, 12).reshape(2, 4, 128, 128))
    dmw = blocks[24:26].reshape(4, 256, 128).transpose(1, 0, 2).reshape(256, C)
    back = lambda x: x.reshape((2, 2, 64) + x.shape[1:]).swapaxes(0, 1).reshape((4, 64) + x.shape[1:])
    rms = jnp.sqrt(sums / (count * C))
    return (
        output, patches_grad, back(dmg), back(dms), back(dmw), small1[:, 0], small1[:, 1], g_qkv, g_bias,
        g_tab, g_wo, small1[:, 2], small2[:, 0], small2[:, 1], g_we, g_be, g_ws, small2[:, 2], rms,
    )


def solution(mesh):
    placed = (
        P("sp", None, "tp"), P(None, "tp"), P(None, "tp"), P(None, "tp", None), P(), P(),
        P(None, None, None, "tp"), P(None, None, "tp"), P(None, None, "tp"), P(None, "tp", None),
        P(), P(), P(), P(None, None, "tp"), P(None, "tp"), P(None, "tp", None), P(), P(),
        P("sp", None), P("sp", None, "tp"),
    )
    results = (
        P("sp", None, "tp"), P("sp", None, "tp"), P(None, "tp"), P(None, "tp"), P(None, "tp", None),
        P(), P(), P(None, None, None, "tp"), P(None, None, "tp"), P(None, None, "tp"),
        P(None, "tp", None), P(), P(), P(), P(None, None, "tp"), P(None, "tp"), P(None, "tp", None),
        P(), P(),
    )
    return jax.shard_map(shards, mesh=mesh, in_specs=placed, out_specs=results, check_vma=False)
```

```python
import functools

import jax
import jax.numpy as jnp
import numpy as np
from jax import lax
from jax.experimental import pallas as pl
from jax.experimental.pallas import tpu as pltpu
from jax.sharding import PartitionSpec as P

C = 512
HD = 32
C2 = 256
WIN = 10
SHIFT = 5
SUB = 32
REAL = 25
WT = 128
TOK = 384
NW = 3
GROUP = 4

bf16 = jnp.bfloat16
f32 = jnp.float32
epsilon = 1e-05
masked = -1000000000.0

NN = (((1,), (0,)), ((), ()))
NT = (((1,), (1,)), ((), ()))
TN = (((0,), (0,)), ((), ()))


def split(x):
    high = x.astype(bf16)
    return high, (x - high.astype(f32)).astype(bf16)


def mm(a, b, dims):
    return lax.dot_general(a, b, dims, preferred_element_type=f32)


def mm3(a, b, dims):
    return mm(a[0], b[0], dims) + (mm(a[0], b[1], dims) + mm(a[1], b[0], dims))


def normalized(x):
    center = x - jnp.mean(x, axis=-1, keepdims=True)
    rho = lax.rsqrt(jnp.mean(center * center, axis=-1, keepdims=True) + epsilon)
    return center * rho, rho


def head_masks(dtype):
    lane = lax.broadcasted_iota(jnp.int32, (1, 128), 1) // HD
    return [(lane == h).astype(f32).astype(dtype) for h in range(GROUP)]


def stacked(pair, masks):
    return tuple(jnp.concatenate([part * m for m in masks], axis=0) for part in pair)


def side_by_side(pair):
    return tuple(
        jnp.concatenate([part[h * WT : (h + 1) * WT] for h in range(GROUP)], axis=1)
        for part in pair
    )


def colsum(x):
    return jnp.sum(x, axis=0, keepdims=True)


def sds(*shape):
    return jax.ShapeDtypeStruct(shape, f32)


def norm_back(x, gain, grad_y):
    xhat, rho = normalized(x)
    gh = grad_y * gain
    grad_x = rho * (
        gh - jnp.mean(gh, axis=-1, keepdims=True) - xhat * jnp.mean(gh * xhat, axis=-1, keepdims=True)
    )
    return grad_x, colsum(grad_y * xhat), colsum(grad_y)


MESH = pl.DeviceIdType.MESH
ANY = pl.BlockSpec(memory_space=pl.ANY)
VM = pl.BlockSpec(memory_space=pltpu.VMEM)


def here():
    sp, tp = lax.axis_index("sp"), lax.axis_index("tp")
    return sp, tp, (sp, tp ^ 1), (sp, tp ^ 2), (sp ^ 1, tp)


def meet(peers):
    barrier = pltpu.get_barrier_semaphore()
    for peer in peers:
        pl.semaphore_signal(barrier, inc=1, device_id=peer, device_id_type=MESH)
    pl.semaphore_wait(barrier, len(peers))


def push(src, dst, send, recv, peer):
    return pltpu.make_async_remote_copy(
        src_ref=src, dst_ref=dst, send_sem=send, recv_sem=recv, device_id=peer, device_id_type=MESH
    )


MLP_ROWS, ATT_ROWS = 4096, 2048
BLOCK_ROWS = MLP_ROWS + ATT_ROWS
FIRST = 2
AG_STEP = 15
STEPS = 17


def chunk_plan(n):
    rows = 256 if n <= 16 else 512
    every = 2 * BLOCK_ROWS // rows
    return rows, every, every + 1024 // rows, 3 if rows == 256 else 1


TINY = 40
COLS = [(0, 0, 0, 1), (0, 1, 1, 0), (1, 0, 1, 1), (1, 1, 2, 0), (2, 0, 2, 1)]


def at(w, sr, sc):
    return pl.ds(w * WT + sr * 64 + sc * SUB, SUB)


NCH = 13
GCH = 2 * NCH
F_STEPS = 19


TURNS = (0, 0, 0, 5, 11, 13, 15, 18, 21, 23, 25, 27, 28, 29, 30, 30, 30, 30, 30, 30)
LAG = 2
AHEAD = 6


def fwd_order(s):
    att = jnp.where(s < 2, 0, jnp.where(s < 6, s - 2, jnp.where(s < 10, 3, jnp.where(s < 14, s - 6, 7))))
    mlp = jnp.where(s < 6, 0, jnp.where(s < 10, s - 6, jnp.where(s < 14, 3, jnp.where(s < 18, s - 10, 7))))
    return att, mlp


def so_far(table, s):
    found = jnp.int32(table[0])
    for k in range(1, len(table)):
        if table[k] != table[k - 1]:
            found = jnp.where(s >= k, table[k], found)
    return found


def fwd_kernel(n, *refs):
    (
        q_ref, mw_ref, mg_ref, wi_ref, bi_ref, wo_ref, we_ref, ws_ref, sm_ref, g1_ref, b1_ref, bo_ref,
        g2_ref, b2_ref, bs_ref, page_ref, grid_ref, cot_ref,
    ) = refs[:18]
    (
        nall, wall, cb, field_out, mid_out, qkv_ref, p_ref, att_ref, hid_ref, slope_ref, stat_ref, vec_ref,
        sq_ref, os_ref,
    ) = refs[18:32]
    (
        nb, wb, smb, pb, pr, px, stb, str_, stx, vp, v0_ref, v1_ref, vs_ref, vr, vc, regr_ref, regc_ref, field, nh, nl, mixed, moved,
        lsem, ss, sr, xs, xr, ys, yr, zs, zr, s2s, s2r, sms, smr, rss, rsr, vps, vpr, vvs, vvr,
        mvs, mvr, cbs, cbr, cbl, hn, hw,
    ) = refs[32:]
    step = pl.program_id(0)
    sp, tp, sib, across, beside = here()
    par = sp & 1
    up, down = lax.rem(sp + 1, n), lax.rem(sp + n - 1, n)
    left = lax.rem(tp + 3, 4)

    def own():
        todo = []
        for b in range(2):
            todo += [
                (wi_ref.at[b], nb.at[0, pl.ds(4 * b, 3)]), (bi_ref.at[b], nb.at[0, 4 * b + 3]),
                (we_ref.at[b], wb.at[0, pl.ds(9 * b, 4)]), (ws_ref.at[b], wb.at[0, pl.ds(9 * b + 4, 4)]),
                (wo_ref.at[b], wb.at[0, pl.ds(9 * b + 8, 1)]),
            ]
        todo.append((sm_ref, smb.at[0]))
        return [pltpu.make_async_copy(s, d, lsem.at[i]) for i, (s, d) in enumerate(todo)]

    def to_sib(b):
        parts = [(nb, pl.ds(4 * b, 4)), (wb, pl.ds(9 * b + 8, 1)), (wb, pl.ds(9 * b, 8))]
        return [
            push(buf.at[0, d], buf.at[1, d], ss.at[b, k], sr.at[b, k], sib) for k, (buf, d) in enumerate(parts)
        ]

    def narrow(c):
        b, r = c // NCH, c % NCH
        return r < 4, 4 * b + r, 9 * b + jnp.where(r == 4, 8, r - 5)

    def each(c, act):
        small, kn, kw = narrow(c)

        @pl.when(small)
        def _():
            act(nb, kn, 512)

        @pl.when(jnp.logical_not(small))
        def _():
            act(wb, kw, 128)

    zpar = lax.rem(sp // 2, 2)
    far = (sp ^ 2, tp)

    def deep(c):
        return c % 3 != 0

    def cut(size, k):
        return pl.ds(pl.multiple_of(k * size, size), size)

    def x_copy(c, buf, k, size, low):
        d = cut(size // 4, 2 * zpar + par) if low else cut(size // 2, par)
        return push(buf.at[0, k, d], buf.at[2, k, d], xs.at[c], xr.at[c], across)

    def y_copy(c, buf, k, size, low):
        d = cut(size // 4, 2 * zpar + par) if low else cut(size // 2, par)
        return push(buf.at[2, k, d], buf.at[2, k, d], ys.at[c], yr.at[c], beside)

    def z_copy(c, buf, k, size):
        d = cut(size // 2, zpar)
        return push(buf.at[2, k, d], buf.at[2, k, d], zs.at[c], zr.at[c], far)

    def s_copy(which, c, buf, k, size):
        d = cut(size // 2, which)
        send, recv = (s2s, s2r)
        return push(buf.at[2, k, d], buf.at[3, k, d], send.at[which, c], recv.at[which, c], sib)

    def x_start(c):
        def act(buf, k, size):
            for low in (False, True):

                @pl.when(deep(c) == low)
                def _(low=low):
                    x_copy(c, buf, k, size, low).start()

        each(c, act)

    def s_in(c, buf, k, size):
        for h in range(2):
            s_copy(h, c, buf, k, size).wait_recv()

    def rs_copies(k):
        if k < 2:
            i = 1 + 2 * k
            return [
                push(pb.at[i], pr.at[k], rss.at[0, k], rsr.at[0, k], sib),
                push(stb.at[i], str_.at[k], rss.at[1, k], rsr.at[1, k], sib),
            ]
        return [
            push(pb.at[2], px, rss.at[0, 2], rsr.at[0, 2], across),
            push(stb.at[2], stx, rss.at[1, 2], rsr.at[1, 2], across),
        ]

    def vec_copies():
        return [push(vp.at[0], vp.at[i], vps.at[i - 1], vpr.at[i - 1], (sp, tp ^ i)) for i in (1, 2, 3)]

    def sm_copy(k):
        src, dst, peer = ((0, 1, sib), (0, 2, across), (2, 3, sib))[k]
        return push(smb.at[src], smb.at[dst], sms.at[k], smr.at[k], peer)

    def valid_copy():
        return push(vs_ref, vr, vvs.at[0], vvr.at[0], (down, tp))

    def moves():
        todo = [(at(0, 1, 0), at(2, 0, 1), (sp, left)), (at(0, 0, 0), at(2, 1, 1), (down, left))]
        for w0, s0, w1, s1 in COLS:
            todo.append((at(w1, 0, s1), at(w0, 1, s0), (down, tp)))
        return [push(field.at[s], moved.at[d], mvs.at[i], mvr.at[i], peer) for i, (s, d, peer) in enumerate(todo)]

    def cot_copy(k, i):
        t = tp ^ i
        src = cot_ref.at[1 - k, pl.ds(6 * t, 6)]
        return push(src, cb.at[tp, k], cbs.at[k, i], cbr.at[k, i], ((sp, t), (down, t))[k])

    def cot_in(k, i):
        src = cot_ref.at[1 - k, pl.ds(0, 6)]
        return push(src, cb.at[tp ^ i, k], cbs.at[k, i], cbr.at[k, i], (sp, tp ^ 1))

    def cot_own():
        return pltpu.make_async_copy(cot_ref.at[1, pl.ds(6 * tp, 6)], cb.at[tp, 0], cbl.at[0])

    @pl.when(step == 0)
    def _():
        for copy in own():
            copy.start()
        barrier = pltpu.get_barrier_semaphore()
        near = [beside, far] + [(sp, tp ^ i) for i in (1, 2, 3)]
        near += [(up, tp ^ i) for i in range(4)] + [(down, tp ^ i) for i in range(4)]
        for peer in near:
            pl.semaphore_signal(barrier, inc=1, device_id=peer, device_id_type=MESH)
        pl.semaphore_wait(barrier, len(near))
        gain, offset = mg_ref[0:1, :], mg_ref[1:2, :]
        wpair = split(mw_ref[...])
        rows8 = lax.broadcasted_iota(jnp.int32, (8, 256), 0)
        pick = jnp.where(rows8 == 0, gain, jnp.where(rows8 == 1, offset, 0.0))
        vp[0] = jnp.dot(pick, mw_ref[...], precision=lax.Precision.HIGHEST, preferred_element_type=f32)
        for copy in vec_copies():
            copy.start()
        lane1 = lax.broadcasted_iota(jnp.int32, (1, 128), 1) // SUB
        for buf in (v0_ref, v1_ref, vs_ref, regr_ref):
            buf[...] = jnp.zeros_like(buf)
        for w in range(NW):
            here_, next_, sent, region = [jnp.zeros((1, 128), f32) for _ in range(4)]
            for k in range(4):
                sr, sc = k // 2, k % 2
                column = 6 * tp + 2 * w + sc
                after = lax.rem(column + 1, 24)
                bring = lambda r, c: pltpu.roll(grid_ref[r, pl.ds(c, 1), :], SUB * k, 1)
                here_ = here_ + bring(sr, column)
                if sr == 0:
                    next_ = next_ + bring(1, after)
                else:
                    sent = sent + bring(0, after)
                page = page_ref[lax.rem(sp + sr, n), lax.rem(3 * tp + w + sc, 12)] * 4
                if sr == 1:
                    page = page + 2 * (sp == n - 1).astype(jnp.int32)
                if sc == 1 and w == NW - 1:
                    page = page + (tp == 3).astype(jnp.int32)
                region = region + jnp.where(lane1 == k, page, 0).astype(f32)
            v0_ref[w : w + 1, :] = here_
            v1_ref[w : w + 1, :] = next_
            vs_ref[w : w + 1, :] = sent
            regr_ref[1, w : w + 1, :] = region
        valid_copy().start()
        lane = lax.broadcasted_iota(jnp.int32, (TOK, 128), 1)

        def project(i):
            quad = q_ref[tp ^ i]
            pb[i] = mm3(split(quad * gain), wpair, NN)
            s1 = jnp.sum(quad, axis=-1, keepdims=True)
            s2 = jnp.sum(quad * quad, axis=-1, keepdims=True)
            stb[i] = jnp.where(lane == 0, s1, jnp.where(lane == 1, s2, 0.0)).T[0:8, :]

        project(3)
        for copy in rs_copies(1):
            copy.start()
        project(1)
        for copy in rs_copies(0):
            copy.start()
        for copy in own():
            copy.wait()
        sm_copy(0).start()
        sm_copy(1).start()
        for c in range(2):
            x_copy(c, nb, c, 512, c % 3 != 0).start()
        project(2)
        project(0)
        for copy in rs_copies(1):
            copy.wait_recv()
        pb[2] = pb[2] + pr[1]
        stb[2] = stb[2] + str_[1]
        for copy in rs_copies(2):
            copy.start()
        for copy in to_sib(0):
            copy.start()
        for c in range(2, AHEAD):
            buf, k, size = (nb, c, 512) if c < 4 else (wb, 8 if c == 4 else c - 5, 128)
            x_copy(c, buf, k, size, c % 3 != 0).start()
        sq_ref[...] = jnp.zeros_like(sq_ref)
        os_ref[...] = jnp.zeros_like(os_ref)
        vec_ref[...] = jnp.zeros_like(vec_ref)

    @pl.when(step == 1)
    def _():
        sm_copy(1).wait_recv()
        sm_copy(2).start()
        for copy in vec_copies():
            copy.wait()
        vec_ref[...] = (vp[0] + vp[1]) + (vp[2] + vp[3])
        valid_copy().wait()
        for b in range(2):
            line = v0_ref[...] if b == 0 else v1_ref[...] + vr[...]
            tall = jnp.concatenate([line, jnp.zeros((120, 128), f32)], axis=0).T
            vc[b] = jnp.concatenate([tall[:, w : w + 1] for w in range(NW)], axis=0)
            if b == 1:
                vr[...] = line
            tall = jnp.concatenate([regr_ref[b], jnp.zeros((120, 128), f32)], axis=0).T
            regc_ref[b] = jnp.concatenate([tall[:, w : w + 1] for w in range(NW)], axis=0)
        sq_ref[5:6, 0:128] = colsum(v0_ref[...])
        for copy in rs_copies(0):
            copy.wait_recv()
        pb[0] = pb[0] + pr[0]
        stb[0] = stb[0] + str_[0]
        for k in range(2):
            for copy in rs_copies(k):
                copy.wait_send()
        for copy in rs_copies(2):
            copy.wait()
        sums = jnp.concatenate([stb[0] + stx[...], jnp.zeros((120, TOK), f32)], axis=0).T
        mean = sums[:, 0:1] / (4.0 * C2)
        inverse = lax.rsqrt(sums[:, 1:2] / (4.0 * C2) - mean * mean + epsilon)
        lane = lax.broadcasted_iota(jnp.int32, (TOK, 128), 1)
        stat_ref[...] = jnp.where(lane == 0, mean, jnp.where(lane == 1, inverse, 0.0))
        field[...] = inverse * (pb[0] + px[...] - mean * vec_ref[0:1, :]) + vec_ref[1:2, :]

    att, mlp = fwd_order(step)

    @pl.when(((step >= 2) & (step < 6)) | ((step >= 10) & (step < 14)))
    def _():
        b, i = att // 4, att % 4

        @pl.when(i == 0)
        def _():
            @pl.when(b == 1)
            def _():
                for copy in moves():
                    copy.wait()
                field[...] = moved[...]

            field_out[0] = field[...]
            xhat, _ = normalized(field[...])
            nh[...], nl[...] = split(xhat * g1_ref[pl.ds(b, 1), :] + b1_ref[pl.ds(b, 1), :])
            mixed[...] = jnp.broadcast_to(bo_ref[pl.ds(b, 1), :], mixed.shape)

        for k in range(2):

            @pl.when((i == 1) & (b == k))
            def _(k=k):
                for copy in to_sib(k)[:2]:
                    copy.wait_recv()
                if k == 0:
                    sm_copy(0).wait()
                    sm_copy(1).wait_send()
                    sm_copy(2).wait()

        @pl.when(i == 3)
        def _():
            for r in range(5):
                c = b * NCH + r
                buf, k, size = (nb, 4 * b + r, 512) if r < 4 else (wb, 9 * b + 8, 128)
                s_in(c, buf, k, size)

        pltpu.make_async_copy(nb.at[i, pl.ds(4 * b, 4)], nall.at[i, b], hn.at[b, i]).start()
        w = jnp.concatenate([nb[i, 4 * b + j] for j in range(3)], axis=1)
        lane = lax.broadcasted_iota(jnp.int32, (1, 384), 1)
        qkv = mm3((nh[...], nl[...]), split(w), NN) + smb[i, pl.ds(2 + b, 1), 0:384]
        qkv_ref[0] = qkv * jnp.where(lane < 128, HD ** (-0.5), 1.0)
        masks = head_masks(bf16)
        bias = nb[i, 4 * b + 3]
        eye = lax.broadcasted_iota(jnp.int32, (WT, WT), 0) == lax.broadcasted_iota(jnp.int32, (WT, WT), 1)
        for j in range(NW):
            rows = pl.ds(j * WT, WT)
            seen = qkv_ref[0, rows, :]
            q4 = stacked(split(seen[:, :128]), masks)
            k = split(seen[:, 128:256])
            v4 = stacked(split(seen[:, 256:]), masks)
            flags = jnp.where(b == 0, v0_ref[j : j + 1, :], vr[j : j + 1, :])
            allowed = (regc_ref[b, rows, :] == regr_ref[b, j : j + 1, :]) & (flags > 0) | eye
            allowed = jnp.concatenate([allowed.astype(f32)] * GROUP, axis=0) > 0
            s = jnp.where(allowed, mm3(q4, k, NT) + bias, masked)
            e = jnp.exp(s - jnp.max(s, axis=-1, keepdims=True))
            p = e / jnp.sum(e, axis=-1, keepdims=True)
            p_ref[0, j] = p
            att_ref[0, rows, :] = mm3(side_by_side(split(p)), v4, NN)
        mixed[...] += mm3(split(att_ref[0]), split(wb[i, 9 * b + 8]), NN)

        @pl.when(i == 3)
        def _():
            middle = field[...] + mixed[...]
            mid_out[0] = middle
            sq_ref[pl.ds(2 * b, 1), :] = colsum(mixed[...] * mixed[...] * vc[b])

    @pl.when(((step >= 6) & (step < 10)) | ((step >= 14) & (step < 18)))
    def _():
        b, i = mlp // 4, mlp % 4

        @pl.when(i == 0)
        def _():
            xhat, _ = normalized(mid_out[0])
            nh[...], nl[...] = split(xhat * g2_ref[pl.ds(b, 1), :] + b2_ref[pl.ds(b, 1), :])
            mixed[...] = jnp.broadcast_to(bs_ref[pl.ds(b, 1), :], mixed.shape)

            @pl.when(b == 0)
            def _():
                for copy in to_sib(1):
                    copy.start()

        for k in range(2):

            @pl.when((i == 1) & (b == k))
            def _(k=k):
                to_sib(k)[2].wait_recv()

        @pl.when(i == 3)
        def _():
            for r in range(8):
                c = b * NCH + 5 + r
                s_in(c, wb, 9 * b + r, 128)

        pltpu.make_async_copy(wb.at[i, pl.ds(9 * b, 9)], wall.at[i, b], hw.at[b, i]).start()
        we = wb[i, pl.ds(9 * b, 4)].reshape(512, 512)
        ws = wb[i, pl.ds(9 * b + 4, 4)].reshape(512, 512)
        pre = mm3((nh[...], nl[...]), split(we), NN) + smb[i, pl.ds(b, 1), :]
        phi = 0.5 * (1.0 + lax.erf(pre * (2 ** -0.5)))
        hidden = pre * phi
        hid_ref[0] = hidden
        slope_ref[0] = phi + pre * (jnp.exp(-0.5 * pre * pre) * ((2 * np.pi) ** -0.5))
        mixed[...] += mm3(split(hidden), split(ws), NN)

        @pl.when(i == 3)
        def _():
            out = mid_out[0] + mixed[...]
            field[...] = out
            sq_ref[pl.ds(2 * b + 1, 1), :] = colsum(mixed[...] * mixed[...] * vc[b])

            @pl.when(b == 0)
            def _():
                for copy in moves():
                    copy.start()
                for w0, s0, w1, s1 in COLS:
                    moved[at(w0, 0, s0), :] = field[at(w1, 1, s1), :]

            @pl.when(b == 1)
            def _():
                sq_ref[4:5, :] = colsum(out * out * vc[1])
                for t in range(4):
                    for w in range(NW):
                        for r in range(2):
                            os_ref[t, r, w * 64 : w * 64 + 64, :] = out[
                                w * WT + r * 64 : w * WT + r * 64 + 64, t * 128 : (t + 1) * 128
                            ]

    @pl.when(step == 15)
    def _():
        cot_own().start()
        for k in range(2):
            for i in range(4):
                if k + i > 0:
                    cot_copy(k, i).start()

    def both(c, act):
        def run(buf, k, size):
            for low in (False, True):

                @pl.when(deep(c) == low)
                def _(low=low):
                    act(buf, k, size, low)

        each(c, run)

    @pl.loop(so_far(TURNS, step), so_far(TURNS, step + 1))
    def _(p):
        @pl.when(p + AHEAD < GCH)
        def _():
            x_start(p + AHEAD)

        @pl.when(p < GCH)
        def _():
            def act(buf, k, size, low):
                x_copy(p, buf, k, size, low).wait_recv()
                y_copy(p, buf, k, size, low).start()
                if not low:
                    for h in range(2):

                        @pl.when(par == h)
                        def _(h=h):
                            s_copy(h, p, buf, k, size).start()

            both(p, act)

        y = p - LAG

        @pl.when((y >= 0) & (y < GCH))
        def _():
            def act(buf, k, size, low):
                y_copy(y, buf, k, size, low).wait_recv()
                x_copy(y, buf, k, size, low).wait_send()
                half_here = zpar if low else 1 - par
                if low:
                    z_copy(y, buf, k, size).start()
                for h in range(2):

                    @pl.when(half_here == h)
                    def _(h=h):
                        s_copy(h, y, buf, k, size).start()

            both(y, act)

        z = p - 2 * LAG

        @pl.when((z >= 0) & (z < GCH))
        def _():
            def act(buf, k, size, low):
                y_copy(z, buf, k, size, low).wait_send()
                if low:
                    z_copy(z, buf, k, size).wait_recv()
                    for h in range(2):

                        @pl.when(1 - zpar == h)
                        def _(h=h):
                            s_copy(h, z, buf, k, size).start()

            both(z, act)

    @pl.when(step == F_STEPS - 1)
    def _():
        cot_own().wait()
        for k in range(2):
            for i in range(4):
                if k + i > 0:
                    cot_copy(k, i).wait_send()
                    cot_in(k, i).wait_recv()
        for b in range(2):
            for copy in to_sib(b):
                copy.wait_send()
            for i in range(4):
                pltpu.make_async_copy(nb.at[i, pl.ds(4 * b, 4)], nall.at[i, b], hn.at[b, i]).wait()
                pltpu.make_async_copy(wb.at[i, pl.ds(9 * b, 9)], wall.at[i, b], hw.at[b, i]).wait()

        @pl.loop(0, GCH)
        def _(c):
            def act(buf, k, size, low):
                if low:
                    z_copy(c, buf, k, size).wait_send()
                for h in range(2):
                    s_copy(h, c, buf, k, size).wait_send()

            both(c, act)


def forward(n, args, ident):
    dma = pltpu.SemaphoreType.DMA

    def fixed(shape):
        return pl.BlockSpec(shape, lambda s: (0,) * len(shape), pipeline_mode=pl.Buffered(1))

    def by(index, shape):
        zeros = (0,) * len(shape)
        return pl.BlockSpec((1,) + shape, lambda s: (index(s),) + zeros)

    att_at = lambda s: fwd_order(s)[0]
    mlp_at = lambda s: fwd_order(s)[1]
    second = lambda s: jnp.where(s < 10, 0, 1)
    vm = lambda *shape: pltpu.VMEM(shape, f32)
    two = fixed((2, C))
    return pl.pallas_call(
        functools.partial(fwd_kernel, n),
        grid=(F_STEPS,),
        in_specs=[
            fixed((4, TOK, 256)), fixed((256, C)), fixed((8, 256)), ANY, ANY, ANY, ANY, ANY, ANY,
            two, two, two, two, two, two, pl.BlockSpec(memory_space=pltpu.SMEM), fixed((2, 24, 128)), ANY,
        ],
        out_specs=[
            ANY, ANY, ANY, by(second, (TOK, C)), by(second, (TOK, C)), by(att_at, (TOK, 384)),
            by(att_at, (NW, GROUP * WT, WT)), by(att_at, (TOK, 128)), by(mlp_at, (TOK, 512)),
            by(mlp_at, (TOK, 512)), fixed((TOK, 128)), fixed((8, C)), fixed((8, C)), fixed((4, 2, 192, 128)),
        ],
        out_shape=[
            sds(4, 2, 4, 512, 128), sds(4, 2, 9, 128, 512), sds(4, 2, 6, SUB, 128), sds(2, TOK, C), sds(2, TOK, C),
            sds(8, TOK, 384), sds(8, NW, GROUP * WT, WT), sds(8, TOK, 128), sds(8, TOK, 512), sds(8, TOK, 512),
            sds(TOK, 128), sds(8, C), sds(8, C), sds(4, 2, 192, 128),
        ],
        scratch_shapes=[
            vm(4, 8, 512, 128), vm(4, 18, 128, 512), vm(4, 8, C), vm(4, TOK, C), vm(2, TOK, C), vm(TOK, C),
            vm(4, 8, TOK), vm(2, 8, TOK), vm(8, TOK), vm(4, 8, C), vm(8, 128), vm(8, 128), vm(8, 128), vm(8, 128), vm(2, TOK, 1), vm(2, 8, 128), vm(2, TOK, 1),
            vm(TOK, C),
            pltpu.VMEM((TOK, C), bf16), pltpu.VMEM((TOK, C), bf16), vm(TOK, C), vm(TOK, C),
            dma((11,)), dma((2, 3)), dma((2, 3)), dma((GCH,)), dma((GCH,)), dma((GCH,)), dma((GCH,)),
            dma((GCH,)), dma((GCH,)), dma((2, GCH)), dma((2, GCH)), dma((3,)), dma((3,)), dma((2, 3)), dma((2, 3)),
            dma((3,)), dma((3,)), dma((1,)), dma((1,)), dma((7,)), dma((7,)), dma((2, 4)), dma((2, 4)),
            dma((1,)), dma((2, 4)), dma((2, 4)),
        ],
        compiler_params=pltpu.CompilerParams(
            collective_id=ident, has_side_effects=True, vmem_limit_bytes=60 << 20,
            dimension_semantics=("arbitrary",),
        ),
        name="forward",
    )(*args)


def table_line(dbias, pick, pile):
    high, low = split(dbias)
    spread = mm(high, pick, NN) + mm(low, pick, NN)
    spread = jnp.concatenate([spread[h * WT : (h + 1) * WT] for h in range(GROUP)], axis=1)
    high, low = split(spread)
    piled = mm(pile, high, NN) + mm(pile, low, NN)
    total = piled[0:16]
    for pc in range(1, WIN):
        total = total + pltpu.roll(piled[pc * 16 : pc * 16 + 16], pc, 1)
    row = lax.broadcasted_iota(jnp.int32, total.shape, 0)
    line = jnp.where(row == 0, total, 0.0)
    for pr in range(1, WIN):
        line = line + jnp.where(row == pr, pltpu.roll(total, 19 * pr, 1), 0.0)
    return colsum(line)


def table_picks():
    pick = np.zeros((WT, 384), np.float32)
    pile = np.zeros((WIN, 16, WT), np.float32)
    for r in range(WIN):
        for c in range(WIN):
            place = (r // 5) * 64 + (c // 5) * SUB + (r % 5) * 5 + c % 5
            pick[place, (9 - r) * 19 + 9 - c] = 1.0
            pile[c, r, place] = 1.0
    return jnp.asarray(pick, bf16), jnp.asarray(pile.reshape(160, WT), bf16)


def bwd_kernel(n, *refs):
    (
        cot_ref, mid_ref, field_ref, g1_ref, b1_ref, g2_ref, b2_ref, we_ref, ws_ref, wqkv_ref, wo_ref,
        hid_ref, slope_ref, qkv_ref, p_ref, att_ref, sq_ref, q_ref, mw_ref, vec_ref, mg_ref, stat_ref, os_ref,
        pick_ref, pile_ref,
    ) = refs[:25]
    pack, gall, exall, ob, out_ref, gq_ref, tout_ref = refs[25:32]
    (
        nth, ntl, gh, gl, acc, dqkv, gf, gbuf, moved, ext, extin, qbuf,
        loc, pair, yr, zr, fin, ta, tx, tz, tsh, tr,
        gsem, mvs, mvr, ags, agr, agl, msem, ss, rs, zs, zq, fs, fq, ls, os, tzs, tzq, obs, obr, obl, tss, tsq,
    ) = refs[32:]
    step = pl.program_id(0)
    dmw, gqbuf = moved.at[pl.ds(0, 256)], dqkv.at[:, pl.ds(0, 256)]
    sp, tp, sib, across, beside = here()
    par, mine = sp & 1, sp // 2
    m = n // 2
    ROWS, FULL_CH, CHUNKS, RATE = chunk_plan(n)
    HALF = ROWS // 2
    piece = HALF // m
    up, down, right = lax.rem(sp + 1, n), lax.rem(sp + n - 1, n), lax.rem(tp + 1, 4)

    def member(j):
        return lax.rem(mine + j, m)

    def device(q):
        return (q * 2 + par, tp)

    def out_copy(k, i):
        t = tp ^ i
        return push(
            os_ref.at[t, k], ob.at[1 - k, pl.ds(6 * tp, 6)], obs.at[k, i], obr.at[k, i], ((sp, t), (up, t))[k]
        )

    def out_in(k, i):
        return push(
            os_ref.at[0, k], ob.at[1 - k, pl.ds(6 * (tp ^ i), 6)], obs.at[k, i], obr.at[k, i], (sp, tp ^ 1)
        )

    def out_own():
        return pltpu.make_async_copy(os_ref.at[tp, 0], ob.at[1, pl.ds(6 * tp, 6)], obl.at[0])

    @pl.when(step == 0)
    def _():
        barrier = pltpu.get_barrier_semaphore()
        near = [beside] + [(sp, tp ^ i) for i in (1, 2, 3)]
        near += [(up, tp ^ i) for i in range(4)] + [(down, tp ^ i) for i in range(4)]
        for peer in near:
            pl.semaphore_signal(barrier, inc=1, device_id=peer, device_id_type=MESH)

        @pl.loop(1, m)
        def _(j):
            pl.semaphore_signal(barrier, inc=1, device_id=device(member(j)), device_id_type=MESH)

        ta[...] = jnp.zeros_like(ta)
        tsh[...] = jnp.zeros_like(tsh)
        ta[0, 28:36, :] = sq_ref[...]
        for t in range(4):
            for w in range(NW):
                for r in range(2):
                    gf[w * WT + r * 64 : w * WT + r * 64 + 64, t * 128 : (t + 1) * 128] = cot_ref[
                        t, r, w * 64 : w * 64 + 64, :
                    ]
        pl.semaphore_wait(barrier, len(near) + m - 1)
        out_own().start()
        for k in range(2):
            for i in range(4):
                if k + i > 0:
                    out_copy(k, i).start()

    def packed(b, j, late):
        size = ATT_ROWS if late else MLP_ROWS
        base = pl.multiple_of((1 - b) * BLOCK_ROWS + (MLP_ROWS if late else 0), 512)
        slot = j % 2
        return pltpu.make_async_copy(
            gbuf.at[slot, pl.ds(0, size)], pack.at[tp ^ j ^ 2, pl.ds(base, size)], gsem.at[slot]
        )

    def moves():
        todo = [
            (at(2, 0, 1), at(0, 1, 0), (sp, right)),
            (at(2, 1, 1), at(0, 0, 0), (up, right)),
        ]
        for w0, s0, w1, s1 in COLS:
            todo.append((at(w0, 1, s0), at(w1, 0, s1), (up, tp)))
        return [push(acc.at[src], moved.at[dst], mvs.at[i], mvr.at[i], peer) for i, (src, dst, peer) in enumerate(todo)]

    def kept():
        for w0, s0, w1, s1 in COLS:
            moved[at(w1, 1, s1), :] = acc[at(w0, 0, s0), :]

    phase = step // 4

    @pl.when((phase == 0) | (phase == 2))
    def _():
        b = 1 - phase // 2
        j = step % 4
        i = j ^ 2

        @pl.when(j == 0)
        def _():
            @pl.when(b == 0)
            def _():
                for copy in moves():
                    copy.wait()
                gf[...] = moved[...]

            xhat, _ = normalized(mid_ref[0])
            nth[...], ntl[...] = split((xhat * g2_ref[pl.ds(b, 1), :] + b2_ref[pl.ds(b, 1), :]).T)
            gh[...], gl[...] = split(gf[...])
            acc[...] = jnp.zeros_like(acc)

        slot = j % 2
        grad = (gh[...], gl[...])
        dws = mm3(split(hid_ref[0].T), grad, NN)
        for q in range(4):
            gbuf[slot, 2048 + q * 512 : 2560 + q * 512, :] = dws[:, q * 128 : (q + 1) * 128]
        dpre = mm3(grad, split(ws_ref[0, 0].reshape(512, C)), NT) * slope_ref[0]
        tsh[i, pl.ds(b, 1), :] = colsum(dpre)
        pair_ = split(dpre)
        dwe = mm3((nth[...], ntl[...]), pair_, NN)
        for q in range(4):
            gbuf[slot, q * 512 : (q + 1) * 512, :] = dwe[:, q * 128 : (q + 1) * 128]
        acc[...] += mm3(pair_, split(we_ref[0, 0].reshape(C, 512)), NT)

        @pl.when(j > 0)
        def _():
            packed(b, j - 1, False).wait()

        packed(b, j, False).start()

        @pl.when(j == 3)
        def _():
            grad_x, dgain, dshift = norm_back(mid_ref[0], g2_ref[pl.ds(b, 1), :], acc[...])
            ta[0, pl.ds(22 + 3 * b, 1), :] = dgain
            ta[0, pl.ds(23 + 3 * b, 1), :] = dshift
            ta[0, pl.ds(24 + 3 * b, 1), :] = colsum(gf[...])
            gf[...] = gf[...] + grad_x
            packed(b, 3, False).wait()

    @pl.when((phase == 1) | (phase == 3))
    def _():
        b = 1 - phase // 2
        j = step % 4
        i = j ^ 2

        @pl.when(j == 0)
        def _():
            xhat, _ = normalized(field_ref[0])
            nth[...], ntl[...] = split((xhat * g1_ref[pl.ds(b, 1), :] + b1_ref[pl.ds(b, 1), :]).T)
            gh[...], gl[...] = split(gf[...])
            acc[...] = jnp.zeros_like(acc)

        slot = j % 2
        grad = (gh[...], gl[...])
        dwo = mm3(split(att_ref[0].T), grad, NN)
        for q in range(4):
            gbuf[slot, 1536 + q * 128 : 1664 + q * 128, :] = dwo[:, q * 128 : (q + 1) * 128]
        dout = mm3(grad, split(wo_ref[0, 0, 0]), NT)
        masks = head_masks(bf16)
        dbias = jnp.zeros((GROUP * WT, WT), f32)
        for w in range(NW):
            rows = slice(w * WT, (w + 1) * WT)
            seen = qkv_ref[0, pl.ds(w * WT, WT), :]
            q4 = stacked(split(seen[:, :128]), masks)
            k4 = stacked(split(seen[:, 128:256]), masks)
            v = split(seen[:, 256:])
            p = p_ref[0, w]
            do4 = stacked(split(dout[rows]), masks)
            dp = mm3(do4, v, NT)
            ds = p * (dp - jnp.sum(p * dp, axis=-1, keepdims=True))
            dbias = dbias + ds
            dpair = split(ds)
            dqkv[pl.ds(w * WT, WT), 0:128] = mm3(side_by_side(dpair), k4, NN) * HD ** (-0.5)
            dqkv[pl.ds(w * WT, WT), 128:256] = mm3(dpair, q4, TN)
            dqkv[pl.ds(w * WT, WT), 256:384] = mm3(split(p), do4, TN)
        line = table_line(dbias, pick_ref[...], pile_ref[...])
        for q in range(3):
            tsh[i, pl.ds(4 + 3 * b + q, 1), :] = line[:, q * 512 : (q + 1) * 512]
        grads = dqkv[...]
        tsh[i, pl.ds(2 + b, 1), 0:384] = colsum(grads)
        pair_ = split(grads)
        dw = mm3((nth[...], ntl[...]), pair_, NN)
        for q in range(3):
            gbuf[slot, q * 512 : (q + 1) * 512, :] = dw[:, q * 128 : (q + 1) * 128]
        w = jnp.concatenate([wqkv_ref[0, 0, q] for q in range(3)], axis=1)
        acc[...] += mm3(pair_, split(w), NT)

        @pl.when(j > 0)
        def _():
            packed(b, j - 1, True).wait()

        packed(b, j, True).start()

        @pl.when(j == 3)
        def _():
            grad_x, dgain, dshift = norm_back(field_ref[0], g1_ref[pl.ds(b, 1), :], acc[...])
            ta[0, pl.ds(16 + 3 * b, 1), :] = dgain
            ta[0, pl.ds(17 + 3 * b, 1), :] = dshift
            ta[0, pl.ds(18 + 3 * b, 1), :] = colsum(gf[...])
            acc[...] = gf[...] + grad_x

            @pl.when(b == 1)
            def _():
                for copy in moves():
                    copy.start()
                kept()

            packed(b, 3, True).wait()

    def ag(k, src, dst, peer, which):
        return push(src, dst, ags.at[which, k], agr.at[which, k], peer)

    def ag_copies(k):
        own = (acc, ext)
        whole_ = (gall, exall)
        return [
            ag(k, own[w], whole_[w].at[tp], (sib, across)[k], w) if k < 2
            else ag(k, whole_[w].at[tp ^ 2], whole_[w].at[tp ^ 2], sib, w)
            for w in range(2)
        ]

    @pl.when(step == AG_STEP)
    def _():
        m2 = jnp.sum(acc[...] * (field_ref[0] - vec_ref[1:2, :]), axis=-1, keepdims=True)
        lane = lax.broadcasted_iota(jnp.int32, (TOK, 128), 1)
        tall = jnp.where(lane == 2, m2, stat_ref[...])
        ext[...] = tall.T[0:8, :]
        for k in range(2):
            for copy in ag_copies(k):
                copy.start()

    def ag_pass():
        for copy in ag_copies(1):
            copy.wait()
        for copy in ag_copies(2):
            copy.start()

    def merge(i):
        t = tp ^ i

        for k in (0, 2):

            @pl.when(i == (1 if k == 0 else 2))
            def _(k=k):
                for copy in ag_copies(k):
                    copy.wait()

        fetch = [pltpu.make_async_copy(q_ref.at[t], qbuf, msem.at[0])]
        fetch[0].start()

        @pl.when(i == 0)
        def _():
            dmw[...] = jnp.zeros((256, C), f32)
            gf[...] = acc[...]
            extin[...] = ext[...]

        @pl.when(i > 0)
        def _():
            two = [
                pltpu.make_async_copy(gall.at[t], gf, msem.at[1]),
                pltpu.make_async_copy(exall.at[t], extin, msem.at[2]),
            ]
            for copy in two:
                copy.start()
            for copy in two:
                copy.wait()

        fetch[0].wait()
        wide = jnp.concatenate([extin[...], jnp.zeros((120, TOK), f32)], axis=0).T
        mean, inv, m2 = wide[:, 0:1], wide[:, 1:2], wide[:, 2:3]
        full = gf[...]
        m1 = jnp.sum(full * vec_ref[0:1, :], axis=-1, keepdims=True) / (4.0 * C2)
        m2 = m2 / (4.0 * C2)
        fpair = split(full)
        xhat = (qbuf[...] - mean) * inv
        gmerged = mm3(fpair, split(mw_ref[...]), NT)
        dmw[...] += mm3(split((xhat * mg_ref[0:1, :] + mg_ref[1:2, :]).T), fpair, NN)
        tsh[0, 10:11, 0:256] += colsum(gmerged * xhat)
        tsh[0, 10:11, 256:512] += colsum(gmerged)

        @pl.when(i > 0)
        def _():
            pltpu.make_async_copy(gqbuf, gq_ref.at[t], msem.at[3]).wait()

        gqbuf[...] = inv * (gmerged * mg_ref[0:1, :] - m1 - xhat * m2)
        pltpu.make_async_copy(gqbuf, gq_ref.at[t], msem.at[3]).start()

        @pl.when(i == 3)
        def _():
            pltpu.make_async_copy(gqbuf, gq_ref.at[t], msem.at[3]).wait()
            for k in range(4):
                row = k * 256
                pair[FULL_CH + row // ROWS, 0, row % ROWS : row % ROWS + 256, :] = dmw[:, k * 128 : (k + 1) * 128]

    def rows(c):
        return pl.ds(pl.multiple_of(c * ROWS, ROWS), ROWS)

    def load(c, k):
        return pltpu.make_async_copy(pack.at[tp ^ (2 * k), rows(c)], loc.at[c % 4, k], ls.at[c % 4, k])

    def swap(c, k):
        return push(pack.at[tp ^ 1 ^ (2 * k), rows(c)], pair.at[c, k], ss.at[k, c], rs.at[k, c], sib)

    def cross(c):
        return push(pair.at[c, 1], fin.at[c], ss.at[2, c], rs.at[2, c], across)

    def halves(h):
        return pl.ds(pl.multiple_of(h * HALF, HALF), HALF)

    def side(c):
        return push(pair.at[c, 0, halves(1 - par)], yr.at[c], ss.at[3, c], rs.at[3, c], beside)

    def bit(q):
        return pl.ds(pl.multiple_of(q * piece, piece), piece)

    def spread(c, q, slot):
        return push(yr.at[c, bit(q)], zr.at[c, slot], zs.at[c % 4, q], zq.at[c, slot], device(q))

    def place(q):
        return pl.ds(pl.multiple_of(par * HALF + q * piece, piece), piece)

    def share(c, q, slot):
        return push(fin.at[c, place(slot)], fin.at[c, place(slot)], fs.at[c % 4, q], fq.at[c, slot], device(q))

    def back(c):
        return push(fin.at[c, halves(par)], fin.at[c, halves(par)], ss.at[4, c], rs.at[4, c], beside)

    def write(c):
        return pltpu.make_async_copy(fin.at[c], out_ref.at[rows(c)], os.at[c])

    low, high = pl.ds(0, 16), pl.ds(16, 24)

    def tiny(k):
        if k == 0:
            todo = [(tsh.at[1], tr.at[0]), (tsh.at[3], tr.at[1]), (ta.at[0, high], tx.at[0, high])]
        elif k == 1:
            todo = [(tsh.at[2], tx.at[1, low]), (ta.at[1, high], tx.at[1, high])]
        else:
            todo = [(ta.at[2], tx.at[2])]
        peer = (sib, across, beside)[k]
        return [push(a, b, tss.at[k, i], tsq.at[k, i], peer) for i, (a, b) in enumerate(todo)]

    def tiny_sum(k):
        if k == 0:
            ta[1, low] = tsh[0] + tr[0]
            ta[1, high] = ta[0, high] + tx[0, high]
            tsh[2] = tsh[2] + tr[1]
        else:
            ta[k + 1] = ta[k] + tx[k]

    def tiny_z(q, slot):
        return push(ta.at[3], tz.at[slot], tzs.at[q], tzq.at[slot], device(q))

    late = RATE * (16 - FIRST)
    tiny_turn = late + 10

    def begun(s):
        return jnp.where(s < FIRST, 0, jnp.where(s < STEPS, RATE * (s - FIRST), CHUNKS + 21))

    def turn(p):
        @pl.when(p == late + 5)
        def _():
            ag_pass()

        due = p - late

        @pl.when((due >= 0) & (due < 12) & (due % 3 == 0))
        def _():
            merge(due // 3)

        def stage(lag, end):
            c = p - lag
            return c, (c >= 0) & (c < end)

        for k in range(4):

            @pl.when(p == tiny_turn + 4 * k)
            def _(k=k):
                if k > 0:
                    for copy in tiny(k - 1):
                        copy.wait()
                    tiny_sum(k - 1)
                if k < 3:
                    for copy in tiny(k):
                        copy.start()
                else:
                    tz[mine] = ta[3]

                    @pl.loop(1, m)
                    def _(j):
                        tiny_z(member(j), mine).start()

        c0, on0 = stage(0, FULL_CH)

        @pl.when(on0)
        def _():
            swap(c0, 1).start()
            load(c0, 1).start()

        c1, on1 = stage(2, FULL_CH)

        @pl.when(on1)
        def _():
            load(c1, 1).wait()
            swap(c1, 1).wait_recv()
            pair[c1, 1] = pair[c1, 1] + loc[c1 % 4, 1]
            cross(c1).start()

        c2, on2 = stage(3, FULL_CH)

        @pl.when(on2)
        def _():
            swap(c2, 0).start()
            load(c2, 0).start()

        c3, on3 = stage(6, CHUNKS)

        @pl.when(on3)
        def _():
            @pl.when(c3 < FULL_CH)
            def _():
                load(c3, 0).wait()
                swap(c3, 0).wait_recv()
                cross(c3).wait_recv()
                pair[c3, 0] = (pair[c3, 0] + loc[c3 % 4, 0]) + fin[c3]
                swap(c3, 1).wait_send()

            side(c3).start()

        c4, on4 = stage(9, CHUNKS)

        @pl.when(on4)
        def _():
            @pl.when(c4 < FULL_CH)
            def _():
                swap(c4, 0).wait_send()
                cross(c4).wait_send()

            side(c4).wait_recv()
            yr[c4] = yr[c4] + pair[c4, 0, halves(par)]

            @pl.loop(1, m)
            def _(j):
                spread(c4, member(j), mine).start()

        c5, on5 = stage(12, CHUNKS)

        @pl.when(on5)
        def _():
            side(c5).wait_send()
            fin[c5, place(mine)] = yr[c5, bit(mine)]

            @pl.loop(1, m)
            def _(j):
                spread(c5, member(j), member(j)).wait_recv()
                fin[c5, place(mine)] = fin[c5, place(mine)] + zr[c5, member(j)]

            @pl.loop(1, m)
            def _(j):
                share(c5, member(j), mine).start()
                spread(c5, member(j), mine).wait_send()

        c6, on6 = stage(15, CHUNKS)

        @pl.when(on6)
        def _():
            @pl.loop(1, m)
            def _(j):
                share(c6, member(j), member(j)).wait_recv()
                share(c6, member(j), mine).wait_send()

            back(c6).start()

        c7, on7 = stage(18, CHUNKS)

        @pl.when(on7)
        def _():
            back(c7).wait()
            write(c7).start()

        c8, on8 = stage(21, CHUNKS)

        @pl.when(on8)
        def _():
            write(c8).wait()

    @pl.loop(begun(step), begun(step + 1))
    def _(p):
        turn(p)

    @pl.when(step == STEPS - 1)
    def _():
        @pl.loop(1, m)
        def _(j):
            tiny_z(member(j), member(j)).wait_recv()
            tiny_z(member(j), mine).wait_send()

        out_own().wait()
        for k in range(2):
            for i in range(4):
                if k + i > 0:
                    out_copy(k, i).wait_send()
                    out_in(k, i).wait_recv()
        total = tz[0]
        for q in range(1, m):
            total = total + tz[q]
        tout_ref[...] = total


def backward(n, args, ident):
    m = n // 2
    ROWS, FULL_CH, CHUNKS, _ = chunk_plan(n)
    HALF = ROWS // 2
    dma = pltpu.SemaphoreType.DMA

    def fixed(shape):
        return pl.BlockSpec(shape, lambda s: (0,) * len(shape), pipeline_mode=pl.Buffered(1))

    def mlp_at(s):
        return jnp.where(s < 4, 4 + (s ^ 2), jnp.where(s < 8, 2, jnp.where(s < 12, (s - 8) ^ 2, 1)))

    def att_at(s):
        return jnp.where(s < 4, 6, jnp.where(s < 8, 4 + ((s - 4) ^ 2), jnp.where(
            s < 12, 2, jnp.where(s < 16, (s - 12) ^ 2, 1))))

    def by(index, shape, mode=None):
        zeros = (0,) * len(shape)
        return pl.BlockSpec((1,) + shape, lambda s: (index(s),) + zeros, pipeline_mode=mode)

    def spot(index, shape, k):
        return pl.BlockSpec((1, 1) + shape, lambda s: (index(s) % 4, index(s) // 4, k, 0, 0))

    one = pl.Buffered(1)
    lanes = (CHUNKS, ROWS, 128)
    in_specs = [
        fixed((4, 2, 192, 128)), by(lambda s: jnp.where(s < 4, 1, 0), (TOK, C), one),
        by(lambda s: jnp.where(s < 8, 1, 0), (TOK, C), one),
        fixed((2, C)), fixed((2, C)), fixed((2, C)), fixed((2, C)),
        spot(mlp_at, (4, 128, 512), 0), spot(mlp_at, (4, 128, 512), 1), spot(att_at, (3, C, 128), 0),
        spot(att_at, (1, 128, C), 8),
        by(mlp_at, (TOK, 512)), by(mlp_at, (TOK, 512)), by(att_at, (TOK, 384)),
        by(att_at, (NW, GROUP * WT, WT)), by(att_at, (TOK, 128)),
        fixed((8, C)), ANY, fixed((256, C)), fixed((8, C)), fixed((8, 256)), fixed((TOK, 128)), ANY,
        fixed((WT, 384)), fixed((160, WT)),
    ]
    return pl.pallas_call(
        functools.partial(bwd_kernel, n),
        grid=(STEPS,),
        in_specs=in_specs,
        out_specs=[ANY, ANY, ANY, ANY, ANY, ANY, fixed((TINY, C))],
        out_shape=[
            sds(4, FULL_CH * ROWS, 128), sds(4, TOK, C), sds(4, 8, TOK), sds(2, 24, SUB, 128), sds(CHUNKS * ROWS, 128),
            sds(4, TOK, 256), sds(TINY, C),
        ],
        scratch_shapes=[
            pltpu.VMEM((C, TOK), bf16), pltpu.VMEM((C, TOK), bf16), pltpu.VMEM((TOK, C), bf16),
            pltpu.VMEM((TOK, C), bf16), pltpu.VMEM((TOK, C), f32), pltpu.VMEM((TOK, 384), f32),
            pltpu.VMEM((TOK, C), f32), pltpu.VMEM((2, MLP_ROWS, 128), f32), pltpu.VMEM((TOK, C), f32),
            pltpu.VMEM((8, TOK), f32), pltpu.VMEM((8, TOK), f32), pltpu.VMEM((TOK, 256), f32),
            pltpu.VMEM((4, 2, ROWS, 128), f32), pltpu.VMEM((CHUNKS, 2, ROWS, 128), f32),
            pltpu.VMEM((CHUNKS, HALF, 128), f32), pltpu.VMEM((CHUNKS, m, HALF // m, 128), f32),
            pltpu.VMEM(lanes, f32), pltpu.VMEM((4, TINY, C), f32), pltpu.VMEM((3, TINY, C), f32),
            pltpu.VMEM((m, TINY, C), f32), pltpu.VMEM((4, 16, C), f32), pltpu.VMEM((2, 16, C), f32),
            dma((2,)), dma((7,)), dma((7,)), dma((2, 3)), dma((2, 3)), dma((2,)), dma((4,)),
            dma((5, CHUNKS)), dma((5, CHUNKS)), dma((4, m)), dma((CHUNKS, m)), dma((4, m)),
            dma((CHUNKS, m)), dma((4, 2)), dma((CHUNKS,)), dma((m,)), dma((m,)),
            dma((2, 4)), dma((2, 4)), dma((1,)), dma((3, 3)), dma((3, 3)),
        ],
        compiler_params=pltpu.CompilerParams(
            collective_id=ident, has_side_effects=True, vmem_limit_bytes=60 << 20,
            dimension_semantics=("arbitrary",),
        ),
        name="backward",
    )(*args)


def unpack_kernel(
    pack_ref, merge_ref, tiny_ref,
    we_ref, ws_ref, qkv_ref, wo_ref, mw_ref, mg_ref, ms_ref, g1_ref, b1_ref, bias_ref, tab_ref, bo_ref, g2_ref,
    b2_ref, be_ref, bs_ref, rms_ref,
):
    for q in range(4):
        lanes = slice(q * 128, (q + 1) * 128)
        we_ref[0, :, lanes] = pack_ref[q]
        ws_ref[0, :, lanes] = pack_ref[4 + q]
        wo_ref[0, :, lanes] = pack_ref[11, q * 128 : (q + 1) * 128, :]
    for j in range(3):
        qkv_ref[0, j] = pack_ref[8 + j]

    @pl.when(pl.program_id(0) == 0)
    def _():
        for i in range(2):
            for j in range(2):
                k, low = 2 * j + i, (2 * i + j) * 64
                for q in range(4):
                    mw_ref[k, :, q * 128 : (q + 1) * 128] = merge_ref[q, low : low + 64, :]
                mg_ref[k : k + 1, :] = tiny_ref[10:11, low : low + 64]
                ms_ref[k : k + 1, :] = tiny_ref[10:11, 256 + low : 320 + low]
        be_ref[...] = tiny_ref[0:2, :]
        for b in range(2):
            bias_ref[b, 0:1, :] = tiny_ref[2 + b : 3 + b, 0:128]
            bias_ref[b, 1:2, :] = tiny_ref[2 + b : 3 + b, 256:384]
            line = jnp.concatenate([tiny_ref[4 + 3 * b + q : 5 + 3 * b + q, :] for q in range(3)], axis=1)
            for h in range(4):
                tab_ref[b, h : h + 1, :] = line[:, h * 384 : h * 384 + 361]
            for k, ref in enumerate((g1_ref, b1_ref, bo_ref)):
                ref[b : b + 1, :] = tiny_ref[16 + 3 * b + k : 17 + 3 * b + k, :]
            for k, ref in enumerate((g2_ref, b2_ref, bs_ref)):
                ref[b : b + 1, :] = tiny_ref[22 + 3 * b + k : 23 + 3 * b + k, :]
        sums = jnp.sum(tiny_ref[28:36, :], axis=1, keepdims=True)
        rms_ref[...] = jnp.broadcast_to(jnp.sqrt(sums / (sums[5:6] * C)), (8, 128))


def unpack(packed, tiny):
    blocks = packed.reshape(-1, 512, 128)
    merged = packed.reshape(-1, 256, 128)
    whole = lambda *shape: pl.BlockSpec(shape, lambda b: (0,) * len(shape))
    layer = lambda *shape: pl.BlockSpec((1,) + shape, lambda b: (b,) + (0,) * len(shape))
    row = (2, C)
    return pl.pallas_call(
        unpack_kernel,
        grid=(2,),
        in_specs=[
            pl.BlockSpec((12, 512, 128), lambda b: (1 - b, 0, 0)),
            pl.BlockSpec((4, 256, 128), lambda b: (12, 0, 0)),
            whole(TINY, C),
        ],
        out_specs=[
            layer(512, 512), layer(512, 512), layer(3, 512, 128), layer(128, 512), whole(4, 64, C), whole(4, 64),
            whole(4, 64), whole(*row), whole(*row), whole(2, 2, 128), whole(2, 4, 361), whole(*row), whole(*row),
            whole(*row), whole(*row), whole(*row), whole(8, 128),
        ],
        out_shape=[
            sds(2, 512, 512), sds(2, 512, 512), sds(2, 3, 512, 128), sds(2, 128, 512), sds(4, 64, C), sds(4, 64),
            sds(4, 64), sds(*row), sds(*row), sds(2, 2, 128), sds(2, 4, 361), sds(*row), sds(*row), sds(*row),
            sds(*row), sds(*row), sds(8, 128),
        ],
        compiler_params=pltpu.CompilerParams(vmem_limit_bytes=48 << 20),
        name="unpack",
    )(blocks, merged, tiny)


def column_pick():
    pick = np.zeros((19, WIN, WIN), np.float32)
    for a in range(WIN):
        for b in range(WIN):
            pick[a - b + WIN - 1, a, b] = 1.0
    return pick


def row_pick():
    pick = np.zeros((19, WIN, WIN, WIN, 2, 2, SUB), np.float32)
    for pr in range(WIN):
        for qr in range(WIN):
            for qc in range(WIN):
                pick[pr - qr + WIN - 1, qc, pr, 0, qr // 5, qc // 5, (qr % 5) * 5 + qc % 5] = 1.0
    return pick[:, :, :, 0].reshape(190, WIN * WT)


def bias_of(table):
    heads = table.shape[0]
    grid = table.reshape(heads, 19, 19)
    columns = jnp.einsum("hrd,dab->harb", grid, jnp.asarray(column_pick()), precision="highest")
    rows = jnp.dot(columns.reshape(heads * WIN, 190), jnp.asarray(row_pick()), precision="highest")
    rows = rows.reshape(heads, 2, 5, 2, 5, WT).transpose(0, 3, 1, 4, 2, 5)
    rows = rows.reshape(heads, 4, REAL, WT)
    return jnp.pad(rows, ((0, 0), (0, 0), (0, SUB - REAL), (0, 0))).reshape(heads, WT, WT)


def shards(
    patches, merge_gain, merge_shift, merge_weight, first_gain, first_shift, input_weight,
    input_bias, position_table, output_weight, output_bias, second_gain, second_shift,
    expand_weight, expand_bias, shrink_weight, shrink_bias, page_map, valid_flags, cotangent,
):
    sp_count = lax.axis_size("sp")
    tp = lax.axis_index("tp")

    tables = position_table.transpose(0, 2, 1).reshape(8, 361)
    bias = bias_of(tables).reshape(2, 512, 128)
    pairs = jnp.concatenate([input_bias, jnp.zeros_like(input_bias)], axis=2).reshape(2, 512)
    small = jnp.concatenate([expand_bias, pairs, jnp.zeros((4, 512), f32)], axis=0)

    valid = valid_flags.astype(f32).reshape(2, 5, 24, 5).transpose(0, 2, 1, 3).reshape(2, 24, REAL)
    valid = jnp.pad(valid, ((0, 0), (0, 0), (0, 128 - REAL)))

    gain = merge_gain.reshape(2, 2, 64).transpose(1, 0, 2).reshape(1, 256)
    offset = merge_shift.reshape(2, 2, 64).transpose(1, 0, 2).reshape(1, 256)
    mgain = jnp.concatenate([gain, offset, jnp.zeros((6, 256), f32)], axis=0)
    weight = merge_weight.reshape(2, 2, 64, C).transpose(1, 0, 2, 3).reshape(256, C)
    quads = patches.reshape(2, 5, 2, 4, NW, 2, 5, 128).transpose(3, 4, 0, 5, 1, 6, 2, 7).reshape(4, NW, 4, REAL, 256)
    quads = jnp.pad(quads, ((0, 0), (0, 0), (0, 0), (0, SUB - REAL), (0, 0))).reshape(4, TOK, 256)
    cot = jnp.roll(cotangent.reshape(2, 5, 24, 5, 128), -1, axis=2).transpose(0, 2, 1, 3, 4).reshape(2, 24, REAL, 128)
    cot = jnp.pad(cot, ((0, 0), (0, 0), (0, SUB - REAL), (0, 0)))

    nall, wall, cot, fields, middles, qkv, p, att, hid, slope, stat, vecs, squares, out = forward(
        sp_count,
        (
            quads, weight, mgain, input_weight.transpose(0, 2, 1, 3), bias, output_weight.reshape(2, 1, 128, C),
            expand_weight.reshape(2, 4, 128, 512), shrink_weight.reshape(2, 4, 128, C), small,
            first_gain, first_shift, output_bias, second_gain, second_shift,
            shrink_bias, page_map, valid, cot,
        ),
        1,
    )
    _, _, _, output, packed, gquads, tiny = backward(
        sp_count,
        (
            cot.reshape(4, 2, 192, 128), middles, fields, first_gain, first_shift,
            second_gain, second_shift, wall, wall, nall, wall, hid, slope, qkv, p, att,
            squares, quads, weight, vecs, mgain, stat, out.reshape(4, 2, 6, SUB, 128),
            *table_picks(),
        ),
        2,
    )
    output = jnp.roll(output[:, :, :REAL], 1, axis=1).reshape(2, 24, 5, 5, 128)
    output = output.transpose(0, 2, 1, 3, 4).reshape(10, 120, 128)
    gquads = gquads.reshape(4, NW, 4, SUB, 256)[:, :, :, :REAL].reshape(4, NW, 2, 2, 5, 5, 2, 128)
    patches_grad = gquads.transpose(2, 4, 6, 0, 1, 3, 5, 7).reshape(20, 240, 64)
    we, ws, qkv, wo, dmw, dmg, dms, dg1, db1, dbias, table, dbo, dg2, db2, dbe, dbs, rms = unpack(packed, tiny)
    return (
        output, patches_grad, dmg, dms, dmw, dg1, db1, qkv.transpose(0, 2, 1, 3), dbias, table.transpose(0, 2, 1),
        wo, dbo, dg2, db2, we, dbe, ws, dbs, rms[:5, 0],
    )


def solution(mesh):
    placed = (
        P("sp", None, "tp"), P(None, "tp"), P(None, "tp"), P(None, "tp", None), P(), P(),
        P(None, None, None, "tp"), P(None, None, "tp"), P(None, None, "tp"), P(None, "tp", None),
        P(), P(), P(), P(None, None, "tp"), P(None, "tp"), P(None, "tp", None), P(), P(),
        P("sp", None), P("sp", None, "tp"),
    )
    results = (
        P("sp", None, "tp"), P("sp", None, "tp"), P(None, "tp"), P(None, "tp"), P(None, "tp", None),
        P(), P(), P(None, None, None, "tp"), P(None, None, "tp"), P(None, None, "tp"),
        P(None, "tp", None), P(), P(), P(), P(None, None, "tp"), P(None, "tp"), P(None, "tp", None),
        P(), P(),
    )
    return jax.shard_map(shards, mesh=mesh, in_specs=placed, out_specs=results, check_vma=False)
```

```python
import functools

import jax
import jax.numpy as jnp
import numpy as np
from jax import lax
from jax.experimental import pallas as pl
from jax.experimental.pallas import tpu as pltpu
from jax.sharding import PartitionSpec as P

C = 512
HD = 32
C2 = 256
WIN = 10
SHIFT = 5
SUB = 32
REAL = 25
WT = 128
TOK = 384
NW = 3
DENSE = 304
GROUP = 4

bf16 = jnp.bfloat16
f32 = jnp.float32
epsilon = 1e-05
masked = -1000000000.0

NN = (((1,), (0,)), ((), ()))
NT = (((1,), (1,)), ((), ()))
TN = (((0,), (0,)), ((), ()))


def split(x):
    high = x.astype(bf16)
    return high, (x - high.astype(f32)).astype(bf16)


def mm(a, b, dims):
    return lax.dot_general(a, b, dims, preferred_element_type=f32)


def mm3(a, b, dims):
    return mm(a[0], b[0], dims) + (mm(a[0], b[1], dims) + mm(a[1], b[0], dims))


def normalized(x):
    center = x - jnp.mean(x, axis=-1, keepdims=True)
    rho = lax.rsqrt(jnp.mean(center * center, axis=-1, keepdims=True) + epsilon)
    return center * rho, rho


def placing():
    token = lax.broadcasted_iota(jnp.int32, (TOK, DENSE), 0)
    column = lax.broadcasted_iota(jnp.int32, (TOK, DENSE), 1)
    inner = token % SUB
    return ((inner < REAL) & (column == (token // SUB) * REAL + inner)).astype(f32).astype(bf16)


def selected(pick, x, dims):
    high, rest = x.astype(bf16), x - x.astype(bf16).astype(f32)
    mid, low = split(rest)
    return mm(pick, high, dims) + (mm(pick, mid, dims) + mm(pick, low, dims))


def upright(columns):
    return jnp.concatenate([columns, jnp.zeros((TOK - DENSE, 128), f32)], axis=0).T[0:8, :]


def head_masks(dtype):
    lane = lax.broadcasted_iota(jnp.int32, (1, 128), 1) // HD
    return [(lane == h).astype(f32).astype(dtype) for h in range(GROUP)]


def stacked(pair, masks):
    return tuple(jnp.concatenate([part * m for m in masks], axis=0) for part in pair)


def side_by_side(pair):
    return tuple(
        jnp.concatenate([part[h * WT : (h + 1) * WT] for h in range(GROUP)], axis=1)
        for part in pair
    )


def colsum(x):
    return jnp.sum(x, axis=0, keepdims=True)


def sds(*shape):
    return jax.ShapeDtypeStruct(shape, f32)


def norm_back(x, gain, grad_y):
    xhat, rho = normalized(x)
    gh = grad_y * gain
    grad_x = rho * (
        gh - jnp.mean(gh, axis=-1, keepdims=True) - xhat * jnp.mean(gh * xhat, axis=-1, keepdims=True)
    )
    return grad_x, colsum(grad_y * xhat), colsum(grad_y)


MESH = pl.DeviceIdType.MESH
ANY = pl.BlockSpec(memory_space=pl.ANY)
VM = pl.BlockSpec(memory_space=pltpu.VMEM)


def here():
    sp, tp = lax.axis_index("sp"), lax.axis_index("tp")
    return sp, tp, (sp, tp ^ 1), (sp, tp ^ 2), (sp ^ 1, tp)


def meet(peers):
    barrier = pltpu.get_barrier_semaphore()
    for peer in peers:
        pl.semaphore_signal(barrier, inc=1, device_id=peer, device_id_type=MESH)
    pl.semaphore_wait(barrier, len(peers))


def push(src, dst, send, recv, peer):
    return pltpu.make_async_remote_copy(
        src_ref=src, dst_ref=dst, send_sem=send, recv_sem=recv, device_id=peer, device_id_type=MESH
    )


MLP_ROWS, ATT_ROWS = 4096, 2048
BLOCK_ROWS = MLP_ROWS + ATT_ROWS
FIRST = 2
AG_STEP = 15
STEPS = 17


def chunk_plan(n):
    rows = 256 if n <= 16 else 512
    every = 2 * BLOCK_ROWS // rows
    return rows, every, every + 1024 // rows, 3 if rows == 256 else 1


TINY = 40
COLS = [(0, 0, 0, 1), (0, 1, 1, 0), (1, 0, 1, 1), (1, 1, 2, 0), (2, 0, 2, 1)]


def at(w, sr, sc):
    return pl.ds(w * WT + sr * 64 + sc * SUB, SUB)


NCH = 13
GCH = 2 * NCH
F_STEPS = 19


TURNS = (0, 0, 0, 2, 9, 11, 13, 15, 17, 19, 21, 23, 25, 27, 29, 30, 30, 30, 30, 30)
LAG = 2
AHEAD = 6


def fwd_order(s):
    att = jnp.where(s < 2, 0, jnp.where(s < 6, s - 2, jnp.where(s < 10, 3, jnp.where(s < 14, s - 6, 7))))
    mlp = jnp.where(s < 6, 0, jnp.where(s < 10, s - 6, jnp.where(s < 14, 3, jnp.where(s < 18, s - 10, 7))))
    return att, mlp


def so_far(table, s):
    found = jnp.int32(table[0])
    for k in range(1, len(table)):
        if table[k] != table[k - 1]:
            found = jnp.where(s >= k, table[k], found)
    return found


def fwd_kernel(n, *refs):
    (
        q_ref, mw_ref, mg_ref, wi_ref, bi_ref, wo_ref, we_ref, ws_ref, sm_ref, g1_ref, b1_ref, bo_ref,
        g2_ref, b2_ref, bs_ref, page_ref, grid_ref, cot_ref,
    ) = refs[:18]
    (
        nall, wall, cb, field_out, mid_out, qkv_ref, p_ref, att_ref, hid_ref, slope_ref, stat_ref, vec_ref,
        sq_ref, os_ref,
    ) = refs[18:32]
    (
        nb, wb, smb, pb, pr, px, stb, str_, stx, vp, v0_ref, v1_ref, vs_ref, vr, vc, regr_ref, regc_ref, field, nh, nl, mixed, moved,
        lsem, ss, sr, xs, xr, ys, yr, zs, zr, s2s, s2r, sms, smr, rss, rsr, vps, vpr, vvs, vvr,
        mvs, mvr, cbs, cbr, cbl, hn, hw,
    ) = refs[32:]
    step = pl.program_id(0)
    sp, tp, sib, across, beside = here()
    par = sp & 1
    up, down = lax.rem(sp + 1, n), lax.rem(sp + n - 1, n)
    left = lax.rem(tp + 3, 4)

    def own():
        todo = []
        for b in range(2):
            todo += [
                (wi_ref.at[b], nb.at[0, pl.ds(4 * b, 3)]), (bi_ref.at[b], nb.at[0, 4 * b + 3]),
                (we_ref.at[b], wb.at[0, pl.ds(9 * b, 4)]), (ws_ref.at[b], wb.at[0, pl.ds(9 * b + 4, 4)]),
                (wo_ref.at[b], wb.at[0, pl.ds(9 * b + 8, 1)]),
            ]
        todo.append((sm_ref, smb.at[0]))
        return [pltpu.make_async_copy(s, d, lsem.at[i]) for i, (s, d) in enumerate(todo)]

    def to_sib(b):
        parts = [(nb, pl.ds(4 * b, 4)), (wb, pl.ds(9 * b + 8, 1)), (wb, pl.ds(9 * b, 8))]
        return [
            push(buf.at[0, d], buf.at[1, d], ss.at[b, k], sr.at[b, k], sib) for k, (buf, d) in enumerate(parts)
        ]

    def narrow(c):
        b, r = c // NCH, c % NCH
        return r < 4, 4 * b + r, 9 * b + jnp.where(r == 4, 8, r - 5)

    def each(c, act):
        small, kn, kw = narrow(c)

        @pl.when(small)
        def _():
            act(nb, kn, 512)

        @pl.when(jnp.logical_not(small))
        def _():
            act(wb, kw, 128)

    zpar = lax.rem(sp // 2, 2)
    far = (sp ^ 2, tp)

    def deep(c):
        return c % 3 != 0

    def cut(size, k):
        return pl.ds(pl.multiple_of(k * size, size), size)

    def x_copy(c, buf, k, size, low):
        d = cut(size // 4, 2 * zpar + par) if low else cut(size // 2, par)
        return push(buf.at[0, k, d], buf.at[2, k, d], xs.at[c], xr.at[c], across)

    def y_copy(c, buf, k, size, low):
        d = cut(size // 4, 2 * zpar + par) if low else cut(size // 2, par)
        return push(buf.at[2, k, d], buf.at[2, k, d], ys.at[c], yr.at[c], beside)

    def z_copy(c, buf, k, size):
        d = cut(size // 2, zpar)
        return push(buf.at[2, k, d], buf.at[2, k, d], zs.at[c], zr.at[c], far)

    def s_copy(which, c, buf, k, size):
        d = cut(size // 2, which)
        send, recv = (s2s, s2r)
        return push(buf.at[2, k, d], buf.at[3, k, d], send.at[which, c], recv.at[which, c], sib)

    def x_start(c):
        def act(buf, k, size):
            for low in (False, True):

                @pl.when(deep(c) == low)
                def _(low=low):
                    x_copy(c, buf, k, size, low).start()

        each(c, act)

    def s_in(c, buf, k, size):
        for h in range(2):
            s_copy(h, c, buf, k, size).wait_recv()

    def rs_copies(k):
        if k < 2:
            i = 1 + 2 * k
            return [
                push(pb.at[i], pr.at[k], rss.at[0, k], rsr.at[0, k], sib),
                push(stb.at[i], str_.at[k], rss.at[1, k], rsr.at[1, k], sib),
            ]
        return [
            push(pb.at[2], px, rss.at[0, 2], rsr.at[0, 2], across),
            push(stb.at[2], stx, rss.at[1, 2], rsr.at[1, 2], across),
        ]

    def vec_copies():
        return [push(vp.at[0], vp.at[i], vps.at[i - 1], vpr.at[i - 1], (sp, tp ^ i)) for i in (1, 2, 3)]

    def sm_copy(k):
        src, dst, peer = ((0, 1, sib), (0, 2, across), (2, 3, sib))[k]
        return push(smb.at[src], smb.at[dst], sms.at[k], smr.at[k], peer)

    def valid_copy():
        return push(vs_ref, vr, vvs.at[0], vvr.at[0], (down, tp))

    def moves():
        todo = [(at(0, 1, 0), at(2, 0, 1), (sp, left)), (at(0, 0, 0), at(2, 1, 1), (down, left))]
        for w0, s0, w1, s1 in COLS:
            todo.append((at(w1, 0, s1), at(w0, 1, s0), (down, tp)))
        return [push(field.at[s], moved.at[d], mvs.at[i], mvr.at[i], peer) for i, (s, d, peer) in enumerate(todo)]

    def cot_copy(k, i):
        t = tp ^ i
        src = cot_ref.at[1 - k, pl.ds(6 * t, 6)]
        return push(src, cb.at[tp, k], cbs.at[k, i], cbr.at[k, i], ((sp, t), (down, t))[k])

    def cot_in(k, i):
        src = cot_ref.at[1 - k, pl.ds(0, 6)]
        return push(src, cb.at[tp ^ i, k], cbs.at[k, i], cbr.at[k, i], (sp, tp ^ 1))

    def cot_own():
        return pltpu.make_async_copy(cot_ref.at[1, pl.ds(6 * tp, 6)], cb.at[tp, 0], cbl.at[0])

    @pl.when(step == 0)
    def _():
        for copy in own():
            copy.start()
        barrier = pltpu.get_barrier_semaphore()
        near = [beside, far] + [(sp, tp ^ i) for i in (1, 2, 3)]
        near += [(up, tp ^ i) for i in range(4)] + [(down, tp ^ i) for i in range(4)]
        for peer in near:
            pl.semaphore_signal(barrier, inc=1, device_id=peer, device_id_type=MESH)
        pl.semaphore_wait(barrier, len(near))
        gain, offset = mg_ref[0:1, :], mg_ref[1:2, :]
        wpair = split(mw_ref[...])
        rows8 = lax.broadcasted_iota(jnp.int32, (8, 256), 0)
        pick = jnp.where(rows8 == 0, gain, jnp.where(rows8 == 1, offset, 0.0))
        vp[0] = jnp.dot(pick, mw_ref[...], precision=lax.Precision.HIGHEST, preferred_element_type=f32)
        for copy in vec_copies():
            copy.start()
        lane1 = lax.broadcasted_iota(jnp.int32, (1, 128), 1) // SUB
        for buf in (v0_ref, v1_ref, vs_ref, regr_ref):
            buf[...] = jnp.zeros_like(buf)
        for w in range(NW):
            here_, next_, sent, region = [jnp.zeros((1, 128), f32) for _ in range(4)]
            for k in range(4):
                sr, sc = k // 2, k % 2
                column = 6 * tp + 2 * w + sc
                after = lax.rem(column + 1, 24)
                bring = lambda r, c: pltpu.roll(grid_ref[r, pl.ds(c, 1), :], SUB * k, 1)
                here_ = here_ + bring(sr, column)
                if sr == 0:
                    next_ = next_ + bring(1, after)
                else:
                    sent = sent + bring(0, after)
                page = page_ref[lax.rem(sp + sr, n), lax.rem(3 * tp + w + sc, 12)] * 4
                if sr == 1:
                    page = page + 2 * (sp == n - 1).astype(jnp.int32)
                if sc == 1 and w == NW - 1:
                    page = page + (tp == 3).astype(jnp.int32)
                region = region + jnp.where(lane1 == k, page, 0).astype(f32)
            v0_ref[w : w + 1, :] = here_
            v1_ref[w : w + 1, :] = next_
            vs_ref[w : w + 1, :] = sent
            regr_ref[1, w : w + 1, :] = region
        valid_copy().start()
        lane = lax.broadcasted_iota(jnp.int32, (DENSE, 128), 1)

        def project(i):
            quad = q_ref[tp ^ i]
            pb[i] = mm3(split(quad * gain), wpair, NN)
            s1 = jnp.sum(quad, axis=-1, keepdims=True)
            s2 = jnp.sum(quad * quad, axis=-1, keepdims=True)
            stb[i] = upright(jnp.where(lane == 0, s1, jnp.where(lane == 1, s2, 0.0)))

        project(3)
        for copy in rs_copies(1):
            copy.start()
        project(1)
        for copy in rs_copies(0):
            copy.start()
        for copy in own():
            copy.wait()
        sm_copy(0).start()
        sm_copy(1).start()
        for c in range(2):
            x_copy(c, nb, c, 512, c % 3 != 0).start()
        project(2)
        project(0)
        for copy in rs_copies(1):
            copy.wait_recv()
        pb[2] = pb[2] + pr[1]
        stb[2] = stb[2] + str_[1]
        for copy in rs_copies(2):
            copy.start()
        for copy in to_sib(0):
            copy.start()
        for c in range(2, AHEAD):
            buf, k, size = (nb, c, 512) if c < 4 else (wb, 8 if c == 4 else c - 5, 128)
            x_copy(c, buf, k, size, c % 3 != 0).start()
        sq_ref[...] = jnp.zeros_like(sq_ref)
        os_ref[...] = jnp.zeros_like(os_ref)
        vec_ref[...] = jnp.zeros_like(vec_ref)

    @pl.when(step == 1)
    def _():
        sm_copy(1).wait_recv()
        sm_copy(2).start()
        for copy in vec_copies():
            copy.wait()
        vec_ref[...] = (vp[0] + vp[1]) + (vp[2] + vp[3])
        valid_copy().wait()
        for b in range(2):
            line = v0_ref[...] if b == 0 else v1_ref[...] + vr[...]
            tall = jnp.concatenate([line, jnp.zeros((120, 128), f32)], axis=0).T
            vc[b] = jnp.concatenate([tall[:, w : w + 1] for w in range(NW)], axis=0)
            if b == 1:
                vr[...] = line
            tall = jnp.concatenate([regr_ref[b], jnp.zeros((120, 128), f32)], axis=0).T
            regc_ref[b] = jnp.concatenate([tall[:, w : w + 1] for w in range(NW)], axis=0)
        sq_ref[5:6, 0:128] = colsum(v0_ref[...])
        for copy in rs_copies(0):
            copy.wait_recv()
        pb[0] = pb[0] + pr[0]
        stb[0] = stb[0] + str_[0]
        for k in range(2):
            for copy in rs_copies(k):
                copy.wait_send()
        for copy in rs_copies(2):
            copy.wait()
        sums = jnp.concatenate([stb[0] + stx[...], jnp.zeros((120, TOK), f32)], axis=0).T[0:DENSE, :]
        mean = sums[:, 0:1] / (4.0 * C2)
        inverse = lax.rsqrt(sums[:, 1:2] / (4.0 * C2) - mean * mean + epsilon)
        lane = lax.broadcasted_iota(jnp.int32, (DENSE, 128), 1)
        stat_ref[...] = jnp.where(lane == 0, mean, jnp.where(lane == 1, inverse, 0.0))
        dense = inverse * (pb[0] + px[...] - mean * vec_ref[0:1, :]) + vec_ref[1:2, :]
        field[...] = selected(placing(), dense, NN)

    def both(c, act):
        def run(buf, k, size):
            for low in (False, True):

                @pl.when(deep(c) == low)
                def _(low=low):
                    act(buf, k, size, low)

        each(c, run)

    def gather_turn(p):
        @pl.when(p + AHEAD < GCH)
        def _():
            x_start(p + AHEAD)

        @pl.when(p < GCH)
        def _():
            def act(buf, k, size, low):
                x_copy(p, buf, k, size, low).wait_recv()
                y_copy(p, buf, k, size, low).start()
                if not low:
                    for h in range(2):

                        @pl.when(par == h)
                        def _(h=h):
                            s_copy(h, p, buf, k, size).start()

            both(p, act)

        y = p - LAG

        @pl.when((y >= 0) & (y < GCH))
        def _():
            def act(buf, k, size, low):
                y_copy(y, buf, k, size, low).wait_recv()
                x_copy(y, buf, k, size, low).wait_send()
                half_here = zpar if low else 1 - par
                if low:
                    z_copy(y, buf, k, size).start()
                for h in range(2):

                    @pl.when(half_here == h)
                    def _(h=h):
                        s_copy(h, y, buf, k, size).start()

            both(y, act)

        z = p - 2 * LAG

        @pl.when((z >= 0) & (z < GCH))
        def _():
            def act(buf, k, size, low):
                y_copy(z, buf, k, size, low).wait_send()
                if low:
                    z_copy(z, buf, k, size).wait_recv()
                    for h in range(2):

                        @pl.when(1 - zpar == h)
                        def _(h=h):
                            s_copy(h, z, buf, k, size).start()

            both(z, act)

    def midway():
        first = so_far(TURNS, step)

        @pl.when(first < so_far(TURNS, step + 1))
        def _():
            gather_turn(first)

    att, mlp = fwd_order(step)

    @pl.when(((step >= 2) & (step < 6)) | ((step >= 10) & (step < 14)))
    def _():
        b, i = att // 4, att % 4

        @pl.when(i == 0)
        def _():
            @pl.when(b == 1)
            def _():
                for copy in moves():
                    copy.wait()
                field[...] = moved[...]

            field_out[0] = field[...]
            xhat, _ = normalized(field[...])
            nh[...], nl[...] = split(xhat * g1_ref[pl.ds(b, 1), :] + b1_ref[pl.ds(b, 1), :])
            mixed[...] = jnp.broadcast_to(bo_ref[pl.ds(b, 1), :], mixed.shape)

        for k in range(2):

            @pl.when((i == 1) & (b == k))
            def _(k=k):
                for copy in to_sib(k)[:2]:
                    copy.wait_recv()
                if k == 0:
                    sm_copy(0).wait()
                    sm_copy(1).wait_send()
                    sm_copy(2).wait()

        @pl.when(i == 3)
        def _():
            for r in range(5):
                c = b * NCH + r
                buf, k, size = (nb, 4 * b + r, 512) if r < 4 else (wb, 9 * b + 8, 128)
                s_in(c, buf, k, size)

        pltpu.make_async_copy(nb.at[i, pl.ds(4 * b, 4)], nall.at[i, b], hn.at[b, i]).start()
        w = jnp.concatenate([nb[i, 4 * b + j] for j in range(3)], axis=1)
        lane = lax.broadcasted_iota(jnp.int32, (1, 384), 1)
        qkv = mm3((nh[...], nl[...]), split(w), NN) + smb[i, pl.ds(2 + b, 1), 0:384]
        qkv_ref[0] = qkv * jnp.where(lane < 128, HD ** (-0.5), 1.0)
        masks = head_masks(bf16)
        bias = nb[i, 4 * b + 3]
        eye = lax.broadcasted_iota(jnp.int32, (WT, WT), 0) == lax.broadcasted_iota(jnp.int32, (WT, WT), 1)
        for j in range(NW):
            rows = pl.ds(j * WT, WT)
            seen = qkv_ref[0, rows, :]
            q4 = stacked(split(seen[:, :128]), masks)
            k = split(seen[:, 128:256])
            v4 = stacked(split(seen[:, 256:]), masks)
            flags = jnp.where(b == 0, v0_ref[j : j + 1, :], vr[j : j + 1, :])
            allowed = (regc_ref[b, rows, :] == regr_ref[b, j : j + 1, :]) & (flags > 0) | eye
            allowed = jnp.concatenate([allowed.astype(f32)] * GROUP, axis=0) > 0
            s = jnp.where(allowed, mm3(q4, k, NT) + bias, masked)
            e = jnp.exp(s - jnp.max(s, axis=-1, keepdims=True))
            p = e / jnp.sum(e, axis=-1, keepdims=True)
            p_ref[0, j] = p
            att_ref[0, rows, :] = mm3(side_by_side(split(p)), v4, NN)
            if j == 1:
                midway()
        mixed[...] += mm3(split(att_ref[0]), split(wb[i, 9 * b + 8]), NN)

        @pl.when(i == 3)
        def _():
            middle = field[...] + mixed[...]
            mid_out[0] = middle
            sq_ref[pl.ds(2 * b, 1), :] = colsum(mixed[...] * mixed[...] * vc[b])

    @pl.when(((step >= 6) & (step < 10)) | ((step >= 14) & (step < 18)))
    def _():
        b, i = mlp // 4, mlp % 4

        @pl.when(i == 0)
        def _():
            xhat, _ = normalized(mid_out[0])
            nh[...], nl[...] = split(xhat * g2_ref[pl.ds(b, 1), :] + b2_ref[pl.ds(b, 1), :])
            mixed[...] = jnp.broadcast_to(bs_ref[pl.ds(b, 1), :], mixed.shape)

            @pl.when(b == 0)
            def _():
                for copy in to_sib(1):
                    copy.start()

        for k in range(2):

            @pl.when((i == 1) & (b == k))
            def _(k=k):
                to_sib(k)[2].wait_recv()

        @pl.when(i == 3)
        def _():
            for r in range(8):
                c = b * NCH + 5 + r
                s_in(c, wb, 9 * b + r, 128)

        pltpu.make_async_copy(wb.at[i, pl.ds(9 * b, 9)], wall.at[i, b], hw.at[b, i]).start()
        we = wb[i, pl.ds(9 * b, 4)].reshape(512, 512)
        ws = wb[i, pl.ds(9 * b + 4, 4)].reshape(512, 512)
        pre = mm3((nh[...], nl[...]), split(we), NN) + smb[i, pl.ds(b, 1), :]
        phi = 0.5 * (1.0 + lax.erf(pre * (2 ** -0.5)))
        hidden = pre * phi
        hid_ref[0] = hidden
        slope_ref[0] = phi + pre * (jnp.exp(-0.5 * pre * pre) * ((2 * np.pi) ** -0.5))
        midway()
        mixed[...] += mm3(split(hidden), split(ws), NN)

        @pl.when(i == 3)
        def _():
            out = mid_out[0] + mixed[...]
            field[...] = out
            sq_ref[pl.ds(2 * b + 1, 1), :] = colsum(mixed[...] * mixed[...] * vc[b])

            @pl.when(b == 0)
            def _():
                for copy in moves():
                    copy.start()
                for w0, s0, w1, s1 in COLS:
                    moved[at(w0, 0, s0), :] = field[at(w1, 1, s1), :]

            @pl.when(b == 1)
            def _():
                sq_ref[4:5, :] = colsum(out * out * vc[1])
                for t in range(4):
                    for w in range(NW):
                        for r in range(2):
                            os_ref[t, r, w * 64 : w * 64 + 64, :] = out[
                                w * WT + r * 64 : w * WT + r * 64 + 64, t * 128 : (t + 1) * 128
                            ]

    @pl.when(step == 15)
    def _():
        cot_own().start()
        for k in range(2):
            for i in range(4):
                if k + i > 0:
                    cot_copy(k, i).start()

    @pl.loop(so_far(TURNS, step) + 1, so_far(TURNS, step + 1))
    def _(p):
        gather_turn(p)

    @pl.when(step == F_STEPS - 1)
    def _():
        cot_own().wait()
        for k in range(2):
            for i in range(4):
                if k + i > 0:
                    cot_copy(k, i).wait_send()
                    cot_in(k, i).wait_recv()
        for b in range(2):
            for copy in to_sib(b):
                copy.wait_send()
            for i in range(4):
                pltpu.make_async_copy(nb.at[i, pl.ds(4 * b, 4)], nall.at[i, b], hn.at[b, i]).wait()
                pltpu.make_async_copy(wb.at[i, pl.ds(9 * b, 9)], wall.at[i, b], hw.at[b, i]).wait()

        @pl.loop(0, GCH)
        def _(c):
            def act(buf, k, size, low):
                if low:
                    z_copy(c, buf, k, size).wait_send()
                for h in range(2):
                    s_copy(h, c, buf, k, size).wait_send()

            both(c, act)


def forward(n, args, ident):
    dma = pltpu.SemaphoreType.DMA

    def fixed(shape):
        return pl.BlockSpec(shape, lambda s: (0,) * len(shape), pipeline_mode=pl.Buffered(1))

    def by(index, shape):
        zeros = (0,) * len(shape)
        return pl.BlockSpec((1,) + shape, lambda s: (index(s),) + zeros)

    att_at = lambda s: fwd_order(s)[0]
    mlp_at = lambda s: fwd_order(s)[1]
    second = lambda s: jnp.where(s < 10, 0, 1)
    vm = lambda *shape: pltpu.VMEM(shape, f32)
    two = fixed((2, C))
    return pl.pallas_call(
        functools.partial(fwd_kernel, n),
        grid=(F_STEPS,),
        in_specs=[
            fixed((4, DENSE, 256)), fixed((256, C)), fixed((8, 256)), ANY, ANY, ANY, ANY, ANY, ANY,
            two, two, two, two, two, two, pl.BlockSpec(memory_space=pltpu.SMEM), fixed((2, 24, 128)), ANY,
        ],
        out_specs=[
            ANY, ANY, ANY, by(second, (TOK, C)), by(second, (TOK, C)), by(att_at, (TOK, 384)),
            by(att_at, (NW, GROUP * WT, WT)), by(att_at, (TOK, 128)), by(mlp_at, (TOK, 512)),
            by(mlp_at, (TOK, 512)), fixed((DENSE, 128)), fixed((8, C)), fixed((8, C)), fixed((4, 2, 192, 128)),
        ],
        out_shape=[
            sds(4, 2, 4, 512, 128), sds(4, 2, 9, 128, 512), sds(4, 2, 6, SUB, 128), sds(2, TOK, C), sds(2, TOK, C),
            sds(8, TOK, 384), sds(8, NW, GROUP * WT, WT), sds(8, TOK, 128), sds(8, TOK, 512), sds(8, TOK, 512),
            sds(DENSE, 128), sds(8, C), sds(8, C), sds(4, 2, 192, 128),
        ],
        scratch_shapes=[
            vm(4, 8, 512, 128), vm(4, 18, 128, 512), vm(4, 8, C), vm(4, DENSE, C), vm(2, DENSE, C), vm(DENSE, C),
            vm(4, 8, TOK), vm(2, 8, TOK), vm(8, TOK), vm(4, 8, C), vm(8, 128), vm(8, 128), vm(8, 128), vm(8, 128), vm(2, TOK, 1), vm(2, 8, 128), vm(2, TOK, 1),
            vm(TOK, C),
            pltpu.VMEM((TOK, C), bf16), pltpu.VMEM((TOK, C), bf16), vm(TOK, C), vm(TOK, C),
            dma((11,)), dma((2, 3)), dma((2, 3)), dma((GCH,)), dma((GCH,)), dma((GCH,)), dma((GCH,)),
            dma((GCH,)), dma((GCH,)), dma((2, GCH)), dma((2, GCH)), dma((3,)), dma((3,)), dma((2, 3)), dma((2, 3)),
            dma((3,)), dma((3,)), dma((1,)), dma((1,)), dma((7,)), dma((7,)), dma((2, 4)), dma((2, 4)),
            dma((1,)), dma((2, 4)), dma((2, 4)),
        ],
        compiler_params=pltpu.CompilerParams(
            collective_id=ident, has_side_effects=True, vmem_limit_bytes=60 << 20,
            dimension_semantics=("arbitrary",),
        ),
        name="forward",
    )(*args)


def table_line(dbias, pick, pile):
    high, low = split(dbias)
    spread = mm(high, pick, NN) + mm(low, pick, NN)
    spread = jnp.concatenate([spread[h * WT : (h + 1) * WT] for h in range(GROUP)], axis=1)
    high, low = split(spread)
    piled = mm(pile, high, NN) + mm(pile, low, NN)
    total = piled[0:16]
    for pc in range(1, WIN):
        total = total + pltpu.roll(piled[pc * 16 : pc * 16 + 16], pc, 1)
    row = lax.broadcasted_iota(jnp.int32, total.shape, 0)
    line = jnp.where(row == 0, total, 0.0)
    for pr in range(1, WIN):
        line = line + jnp.where(row == pr, pltpu.roll(total, 19 * pr, 1), 0.0)
    return colsum(line)


def table_picks():
    pick = np.zeros((WT, 384), np.float32)
    pile = np.zeros((WIN, 16, WT), np.float32)
    for r in range(WIN):
        for c in range(WIN):
            place = (r // 5) * 64 + (c // 5) * SUB + (r % 5) * 5 + c % 5
            pick[place, (9 - r) * 19 + 9 - c] = 1.0
            pile[c, r, place] = 1.0
    return jnp.asarray(pick, bf16), jnp.asarray(pile.reshape(160, WT), bf16)


def bwd_kernel(n, *refs):
    (
        cot_ref, mid_ref, field_ref, g1_ref, b1_ref, g2_ref, b2_ref, we_ref, ws_ref, wqkv_ref, wo_ref,
        hid_ref, slope_ref, qkv_ref, p_ref, att_ref, sq_ref, q_ref, mw_ref, vec_ref, mg_ref, stat_ref, os_ref,
        pick_ref, pile_ref,
    ) = refs[:25]
    pack, gall, exall, ob, out_ref, gq_ref, tout_ref = refs[25:32]
    (
        nth, ntl, gh, gl, acc, dqkv, gf, gbuf, moved, ext, extin, qbuf, gdense,
        loc, pair, yr, zr, fin, ta, tx, tz, tsh, tr,
        gsem, mvs, mvr, ags, agr, agl, msem, ss, rs, zs, zq, fs, fq, ls, os, tzs, tzq, obs, obr, obl, tss, tsq,
    ) = refs[32:]
    step = pl.program_id(0)
    dmw, gqbuf = moved.at[pl.ds(0, 256)], dqkv.at[pl.ds(0, DENSE), pl.ds(0, 256)]
    sp, tp, sib, across, beside = here()
    par, mine = sp & 1, sp // 2
    m = n // 2
    ROWS, FULL_CH, CHUNKS, RATE = chunk_plan(n)
    HALF = ROWS // 2
    piece = HALF // m
    up, down, right = lax.rem(sp + 1, n), lax.rem(sp + n - 1, n), lax.rem(tp + 1, 4)

    def member(j):
        return lax.rem(mine + j, m)

    def device(q):
        return (q * 2 + par, tp)

    def out_copy(k, i):
        t = tp ^ i
        return push(
            os_ref.at[t, k], ob.at[1 - k, pl.ds(6 * tp, 6)], obs.at[k, i], obr.at[k, i], ((sp, t), (up, t))[k]
        )

    def out_in(k, i):
        return push(
            os_ref.at[0, k], ob.at[1 - k, pl.ds(6 * (tp ^ i), 6)], obs.at[k, i], obr.at[k, i], (sp, tp ^ 1)
        )

    def out_own():
        return pltpu.make_async_copy(os_ref.at[tp, 0], ob.at[1, pl.ds(6 * tp, 6)], obl.at[0])

    @pl.when(step == 0)
    def _():
        barrier = pltpu.get_barrier_semaphore()
        near = [beside] + [(sp, tp ^ i) for i in (1, 2, 3)]
        near += [(up, tp ^ i) for i in range(4)] + [(down, tp ^ i) for i in range(4)]
        for peer in near:
            pl.semaphore_signal(barrier, inc=1, device_id=peer, device_id_type=MESH)

        @pl.loop(1, m)
        def _(j):
            pl.semaphore_signal(barrier, inc=1, device_id=device(member(j)), device_id_type=MESH)

        ta[...] = jnp.zeros_like(ta)
        tsh[...] = jnp.zeros_like(tsh)
        ta[0, 28:36, :] = sq_ref[...]
        for t in range(4):
            for w in range(NW):
                for r in range(2):
                    gf[w * WT + r * 64 : w * WT + r * 64 + 64, t * 128 : (t + 1) * 128] = cot_ref[
                        t, r, w * 64 : w * 64 + 64, :
                    ]
        pl.semaphore_wait(barrier, len(near) + m - 1)
        out_own().start()
        for k in range(2):
            for i in range(4):
                if k + i > 0:
                    out_copy(k, i).start()

    def packed(b, j, late):
        size = ATT_ROWS if late else MLP_ROWS
        base = pl.multiple_of((1 - b) * BLOCK_ROWS + (MLP_ROWS if late else 0), 512)
        slot = j % 2
        return pltpu.make_async_copy(
            gbuf.at[slot, pl.ds(0, size)], pack.at[tp ^ j ^ 2, pl.ds(base, size)], gsem.at[slot]
        )

    def moves():
        todo = [
            (at(2, 0, 1), at(0, 1, 0), (sp, right)),
            (at(2, 1, 1), at(0, 0, 0), (up, right)),
        ]
        for w0, s0, w1, s1 in COLS:
            todo.append((at(w0, 1, s0), at(w1, 0, s1), (up, tp)))
        return [push(acc.at[src], moved.at[dst], mvs.at[i], mvr.at[i], peer) for i, (src, dst, peer) in enumerate(todo)]

    def kept():
        for w0, s0, w1, s1 in COLS:
            moved[at(w1, 1, s1), :] = acc[at(w0, 0, s0), :]

    phase = step // 4

    @pl.when((phase == 0) | (phase == 2))
    def _():
        b = 1 - phase // 2
        j = step % 4
        i = j ^ 2

        @pl.when(j == 0)
        def _():
            @pl.when(b == 0)
            def _():
                for copy in moves():
                    copy.wait()
                gf[...] = moved[...]

            xhat, _ = normalized(mid_ref[0])
            nth[...], ntl[...] = split((xhat * g2_ref[pl.ds(b, 1), :] + b2_ref[pl.ds(b, 1), :]).T)
            gh[...], gl[...] = split(gf[...])
            acc[...] = jnp.zeros_like(acc)

        slot = j % 2
        grad = (gh[...], gl[...])
        dws = mm3(split(hid_ref[0].T), grad, NN)
        for q in range(4):
            gbuf[slot, 2048 + q * 512 : 2560 + q * 512, :] = dws[:, q * 128 : (q + 1) * 128]
        dpre = mm3(grad, split(ws_ref[0, 0].reshape(512, C)), NT) * slope_ref[0]
        tsh[i, pl.ds(b, 1), :] = colsum(dpre)
        pair_ = split(dpre)
        dwe = mm3((nth[...], ntl[...]), pair_, NN)
        for q in range(4):
            gbuf[slot, q * 512 : (q + 1) * 512, :] = dwe[:, q * 128 : (q + 1) * 128]
        acc[...] += mm3(pair_, split(we_ref[0, 0].reshape(C, 512)), NT)

        @pl.when(j > 0)
        def _():
            packed(b, j - 1, False).wait()

        packed(b, j, False).start()

        @pl.when(j == 3)
        def _():
            grad_x, dgain, dshift = norm_back(mid_ref[0], g2_ref[pl.ds(b, 1), :], acc[...])
            ta[0, pl.ds(22 + 3 * b, 1), :] = dgain
            ta[0, pl.ds(23 + 3 * b, 1), :] = dshift
            ta[0, pl.ds(24 + 3 * b, 1), :] = colsum(gf[...])
            gf[...] = gf[...] + grad_x
            packed(b, 3, False).wait()

    @pl.when((phase == 1) | (phase == 3))
    def _():
        b = 1 - phase // 2
        j = step % 4
        i = j ^ 2

        @pl.when(j == 0)
        def _():
            xhat, _ = normalized(field_ref[0])
            nth[...], ntl[...] = split((xhat * g1_ref[pl.ds(b, 1), :] + b1_ref[pl.ds(b, 1), :]).T)
            gh[...], gl[...] = split(gf[...])
            acc[...] = jnp.zeros_like(acc)

        slot = j % 2
        grad = (gh[...], gl[...])
        dwo = mm3(split(att_ref[0].T), grad, NN)
        for q in range(4):
            gbuf[slot, 1536 + q * 128 : 1664 + q * 128, :] = dwo[:, q * 128 : (q + 1) * 128]
        dout = mm3(grad, split(wo_ref[0, 0, 0]), NT)
        masks = head_masks(bf16)
        dbias = jnp.zeros((GROUP * WT, WT), f32)
        for w in range(NW):
            rows = slice(w * WT, (w + 1) * WT)
            seen = qkv_ref[0, pl.ds(w * WT, WT), :]
            q4 = stacked(split(seen[:, :128]), masks)
            k4 = stacked(split(seen[:, 128:256]), masks)
            v = split(seen[:, 256:])
            p = p_ref[0, w]
            do4 = stacked(split(dout[rows]), masks)
            dp = mm3(do4, v, NT)
            ds = p * (dp - jnp.sum(p * dp, axis=-1, keepdims=True))
            dbias = dbias + ds
            dpair = split(ds)
            dqkv[pl.ds(w * WT, WT), 0:128] = mm3(side_by_side(dpair), k4, NN) * HD ** (-0.5)
            dqkv[pl.ds(w * WT, WT), 128:256] = mm3(dpair, q4, TN)
            dqkv[pl.ds(w * WT, WT), 256:384] = mm3(split(p), do4, TN)
        line = table_line(dbias, pick_ref[...], pile_ref[...])
        for q in range(3):
            tsh[i, pl.ds(4 + 3 * b + q, 1), :] = line[:, q * 512 : (q + 1) * 512]
        grads = dqkv[...]
        tsh[i, pl.ds(2 + b, 1), 0:384] = colsum(grads)
        pair_ = split(grads)
        dw = mm3((nth[...], ntl[...]), pair_, NN)
        for q in range(3):
            gbuf[slot, q * 512 : (q + 1) * 512, :] = dw[:, q * 128 : (q + 1) * 128]
        w = jnp.concatenate([wqkv_ref[0, 0, q] for q in range(3)], axis=1)
        acc[...] += mm3(pair_, split(w), NT)

        @pl.when(j > 0)
        def _():
            packed(b, j - 1, True).wait()

        packed(b, j, True).start()

        @pl.when(j == 3)
        def _():
            grad_x, dgain, dshift = norm_back(field_ref[0], g1_ref[pl.ds(b, 1), :], acc[...])
            ta[0, pl.ds(16 + 3 * b, 1), :] = dgain
            ta[0, pl.ds(17 + 3 * b, 1), :] = dshift
            ta[0, pl.ds(18 + 3 * b, 1), :] = colsum(gf[...])
            acc[...] = gf[...] + grad_x

            @pl.when(b == 1)
            def _():
                for copy in moves():
                    copy.start()
                kept()

            packed(b, 3, True).wait()

    def ag(k, src, dst, peer, which):
        return push(src, dst, ags.at[which, k], agr.at[which, k], peer)

    def ag_copies(k):
        own = (gdense, ext)
        whole_ = (gall, exall)
        return [
            ag(k, own[w], whole_[w].at[tp], (sib, across)[k], w) if k < 2
            else ag(k, whole_[w].at[tp ^ 2], whole_[w].at[tp ^ 2], sib, w)
            for w in range(2)
        ]

    @pl.when(step == AG_STEP)
    def _():
        m2 = jnp.sum(acc[...] * (field_ref[0] - vec_ref[1:2, :]), axis=-1, keepdims=True)
        pick = placing()
        gdense[...] = selected(pick, acc[...], TN)
        lane = lax.broadcasted_iota(jnp.int32, (DENSE, 128), 1)
        tall = selected(pick, jnp.broadcast_to(m2, (TOK, 128)), TN)
        ext[...] = upright(jnp.where(lane == 2, tall, stat_ref[...]))
        for k in range(2):
            for copy in ag_copies(k):
                copy.start()

    def ag_pass():
        for copy in ag_copies(1):
            copy.wait()
        for copy in ag_copies(2):
            copy.start()

    def merge(i):
        t = tp ^ i

        for k in (0, 2):

            @pl.when(i == (1 if k == 0 else 2))
            def _(k=k):
                for copy in ag_copies(k):
                    copy.wait()

        fetch = [pltpu.make_async_copy(q_ref.at[t], qbuf, msem.at[0])]
        fetch[0].start()

        @pl.when(i == 0)
        def _():
            dmw[...] = jnp.zeros((256, C), f32)
            gf[0:DENSE, :] = gdense[...]
            extin[...] = ext[...]

        @pl.when(i > 0)
        def _():
            two = [
                pltpu.make_async_copy(gall.at[t], gf.at[pl.ds(0, DENSE)], msem.at[1]),
                pltpu.make_async_copy(exall.at[t], extin, msem.at[2]),
            ]
            for copy in two:
                copy.start()
            for copy in two:
                copy.wait()

        fetch[0].wait()
        wide = jnp.concatenate([extin[...], jnp.zeros((120, TOK), f32)], axis=0).T[0:DENSE, :]
        mean, inv, m2 = wide[:, 0:1], wide[:, 1:2], wide[:, 2:3]
        full = gf[0:DENSE, :]
        m1 = jnp.sum(full * vec_ref[0:1, :], axis=-1, keepdims=True) / (4.0 * C2)
        m2 = m2 / (4.0 * C2)
        fpair = split(full)
        xhat = (qbuf[...] - mean) * inv
        gmerged = mm3(fpair, split(mw_ref[...]), NT)
        dmw[...] += mm3(split(xhat * mg_ref[0:1, :] + mg_ref[1:2, :]), fpair, TN)
        tsh[0, 10:11, 0:256] += colsum(gmerged * xhat)
        tsh[0, 10:11, 256:512] += colsum(gmerged)

        @pl.when(i > 0)
        def _():
            pltpu.make_async_copy(gqbuf, gq_ref.at[t], msem.at[3]).wait()

        gqbuf[...] = inv * (gmerged * mg_ref[0:1, :] - m1 - xhat * m2)
        pltpu.make_async_copy(gqbuf, gq_ref.at[t], msem.at[3]).start()

        @pl.when(i == 3)
        def _():
            pltpu.make_async_copy(gqbuf, gq_ref.at[t], msem.at[3]).wait()
            for k in range(4):
                row = k * 256
                pair[FULL_CH + row // ROWS, 0, row % ROWS : row % ROWS + 256, :] = dmw[:, k * 128 : (k + 1) * 128]

    def rows(c):
        return pl.ds(pl.multiple_of(c * ROWS, ROWS), ROWS)

    def load(c, k):
        return pltpu.make_async_copy(pack.at[tp ^ (2 * k), rows(c)], loc.at[c % 4, k], ls.at[c % 4, k])

    def swap(c, k):
        return push(pack.at[tp ^ 1 ^ (2 * k), rows(c)], pair.at[c, k], ss.at[k, c], rs.at[k, c], sib)

    def cross(c):
        return push(pair.at[c, 1], fin.at[c], ss.at[2, c], rs.at[2, c], across)

    def halves(h):
        return pl.ds(pl.multiple_of(h * HALF, HALF), HALF)

    def side(c):
        return push(pair.at[c, 0, halves(1 - par)], yr.at[c], ss.at[3, c], rs.at[3, c], beside)

    def bit(q):
        return pl.ds(pl.multiple_of(q * piece, piece), piece)

    def spread(c, q, slot):
        return push(yr.at[c, bit(q)], zr.at[c, slot], zs.at[c % 4, q], zq.at[c, slot], device(q))

    def place(q):
        return pl.ds(pl.multiple_of(par * HALF + q * piece, piece), piece)

    def share(c, q, slot):
        return push(fin.at[c, place(slot)], fin.at[c, place(slot)], fs.at[c % 4, q], fq.at[c, slot], device(q))

    def back(c):
        return push(fin.at[c, halves(par)], fin.at[c, halves(par)], ss.at[4, c], rs.at[4, c], beside)

    def write(c):
        return pltpu.make_async_copy(fin.at[c], out_ref.at[rows(c)], os.at[c])

    low, high = pl.ds(0, 16), pl.ds(16, 24)

    def tiny(k):
        if k == 0:
            todo = [(tsh.at[1], tr.at[0]), (tsh.at[3], tr.at[1]), (ta.at[0, high], tx.at[0, high])]
        elif k == 1:
            todo = [(tsh.at[2], tx.at[1, low]), (ta.at[1, high], tx.at[1, high])]
        else:
            todo = [(ta.at[2], tx.at[2])]
        peer = (sib, across, beside)[k]
        return [push(a, b, tss.at[k, i], tsq.at[k, i], peer) for i, (a, b) in enumerate(todo)]

    def tiny_sum(k):
        if k == 0:
            ta[1, low] = tsh[0] + tr[0]
            ta[1, high] = ta[0, high] + tx[0, high]
            tsh[2] = tsh[2] + tr[1]
        else:
            ta[k + 1] = ta[k] + tx[k]

    def tiny_z(q, slot):
        return push(ta.at[3], tz.at[slot], tzs.at[q], tzq.at[slot], device(q))

    late = RATE * (16 - FIRST)
    tiny_turn = late + 10

    def begun(s):
        return jnp.where(s < FIRST, 0, jnp.where(s < STEPS, RATE * (s - FIRST), CHUNKS + 21))

    def turn(p):
        @pl.when(p == late + 5)
        def _():
            ag_pass()

        due = p - late

        @pl.when((due >= 0) & (due < 12) & (due % 3 == 0))
        def _():
            merge(due // 3)

        def stage(lag, end):
            c = p - lag
            return c, (c >= 0) & (c < end)

        for k in range(4):

            @pl.when(p == tiny_turn + 4 * k)
            def _(k=k):
                if k > 0:
                    for copy in tiny(k - 1):
                        copy.wait()
                    tiny_sum(k - 1)
                if k < 3:
                    for copy in tiny(k):
                        copy.start()
                else:
                    tz[mine] = ta[3]

                    @pl.loop(1, m)
                    def _(j):
                        tiny_z(member(j), mine).start()

        c0, on0 = stage(0, FULL_CH)

        @pl.when(on0)
        def _():
            swap(c0, 1).start()
            load(c0, 1).start()

        c1, on1 = stage(2, FULL_CH)

        @pl.when(on1)
        def _():
            load(c1, 1).wait()
            swap(c1, 1).wait_recv()
            pair[c1, 1] = pair[c1, 1] + loc[c1 % 4, 1]
            cross(c1).start()

        c2, on2 = stage(3, FULL_CH)

        @pl.when(on2)
        def _():
            swap(c2, 0).start()
            load(c2, 0).start()

        c3, on3 = stage(6, CHUNKS)

        @pl.when(on3)
        def _():
            @pl.when(c3 < FULL_CH)
            def _():
                load(c3, 0).wait()
                swap(c3, 0).wait_recv()
                cross(c3).wait_recv()
                pair[c3, 0] = (pair[c3, 0] + loc[c3 % 4, 0]) + fin[c3]
                swap(c3, 1).wait_send()

            side(c3).start()

        c4, on4 = stage(9, CHUNKS)

        @pl.when(on4)
        def _():
            @pl.when(c4 < FULL_CH)
            def _():
                swap(c4, 0).wait_send()
                cross(c4).wait_send()

            side(c4).wait_recv()
            yr[c4] = yr[c4] + pair[c4, 0, halves(par)]

            @pl.loop(1, m)
            def _(j):
                spread(c4, member(j), mine).start()

        c5, on5 = stage(12, CHUNKS)

        @pl.when(on5)
        def _():
            side(c5).wait_send()
            fin[c5, place(mine)] = yr[c5, bit(mine)]

            @pl.loop(1, m)
            def _(j):
                spread(c5, member(j), member(j)).wait_recv()
                fin[c5, place(mine)] = fin[c5, place(mine)] + zr[c5, member(j)]

            @pl.loop(1, m)
            def _(j):
                share(c5, member(j), mine).start()
                spread(c5, member(j), mine).wait_send()

        c6, on6 = stage(15, CHUNKS)

        @pl.when(on6)
        def _():
            @pl.loop(1, m)
            def _(j):
                share(c6, member(j), member(j)).wait_recv()
                share(c6, member(j), mine).wait_send()

            back(c6).start()

        c7, on7 = stage(18, CHUNKS)

        @pl.when(on7)
        def _():
            back(c7).wait()
            write(c7).start()

        c8, on8 = stage(21, CHUNKS)

        @pl.when(on8)
        def _():
            write(c8).wait()

    @pl.loop(begun(step), begun(step + 1))
    def _(p):
        turn(p)

    @pl.when(step == STEPS - 1)
    def _():
        @pl.loop(1, m)
        def _(j):
            tiny_z(member(j), member(j)).wait_recv()
            tiny_z(member(j), mine).wait_send()

        out_own().wait()
        for k in range(2):
            for i in range(4):
                if k + i > 0:
                    out_copy(k, i).wait_send()
                    out_in(k, i).wait_recv()
        total = tz[0]
        for q in range(1, m):
            total = total + tz[q]
        tout_ref[...] = total


def backward(n, args, ident):
    m = n // 2
    ROWS, FULL_CH, CHUNKS, _ = chunk_plan(n)
    HALF = ROWS // 2
    dma = pltpu.SemaphoreType.DMA

    def fixed(shape):
        return pl.BlockSpec(shape, lambda s: (0,) * len(shape), pipeline_mode=pl.Buffered(1))

    def mlp_at(s):
        return jnp.where(s < 4, 4 + (s ^ 2), jnp.where(s < 8, 2, jnp.where(s < 12, (s - 8) ^ 2, 1)))

    def att_at(s):
        return jnp.where(s < 4, 6, jnp.where(s < 8, 4 + ((s - 4) ^ 2), jnp.where(
            s < 12, 2, jnp.where(s < 16, (s - 12) ^ 2, 1))))

    def by(index, shape, mode=None):
        zeros = (0,) * len(shape)
        return pl.BlockSpec((1,) + shape, lambda s: (index(s),) + zeros, pipeline_mode=mode)

    def spot(index, shape, k):
        return pl.BlockSpec((1, 1) + shape, lambda s: (index(s) % 4, index(s) // 4, k, 0, 0))

    one = pl.Buffered(1)
    lanes = (CHUNKS, ROWS, 128)
    in_specs = [
        fixed((4, 2, 192, 128)), by(lambda s: jnp.where(s < 4, 1, 0), (TOK, C), one),
        by(lambda s: jnp.where(s < 8, 1, 0), (TOK, C), one),
        fixed((2, C)), fixed((2, C)), fixed((2, C)), fixed((2, C)),
        spot(mlp_at, (4, 128, 512), 0), spot(mlp_at, (4, 128, 512), 1), spot(att_at, (3, C, 128), 0),
        spot(att_at, (1, 128, C), 8),
        by(mlp_at, (TOK, 512)), by(mlp_at, (TOK, 512)), by(att_at, (TOK, 384)),
        by(att_at, (NW, GROUP * WT, WT)), by(att_at, (TOK, 128)),
        fixed((8, C)), ANY, fixed((256, C)), fixed((8, C)), fixed((8, 256)), fixed((DENSE, 128)), ANY,
        fixed((WT, 384)), fixed((160, WT)),
    ]
    return pl.pallas_call(
        functools.partial(bwd_kernel, n),
        grid=(STEPS,),
        in_specs=in_specs,
        out_specs=[ANY, ANY, ANY, ANY, ANY, ANY, fixed((TINY, C))],
        out_shape=[
            sds(4, FULL_CH * ROWS, 128), sds(4, DENSE, C), sds(4, 8, TOK), sds(2, 24, SUB, 128), sds(CHUNKS * ROWS, 128),
            sds(4, DENSE, 256), sds(TINY, C),
        ],
        scratch_shapes=[
            pltpu.VMEM((C, TOK), bf16), pltpu.VMEM((C, TOK), bf16), pltpu.VMEM((TOK, C), bf16),
            pltpu.VMEM((TOK, C), bf16), pltpu.VMEM((TOK, C), f32), pltpu.VMEM((TOK, 384), f32),
            pltpu.VMEM((TOK, C), f32), pltpu.VMEM((2, MLP_ROWS, 128), f32), pltpu.VMEM((TOK, C), f32),
            pltpu.VMEM((8, TOK), f32), pltpu.VMEM((8, TOK), f32), pltpu.VMEM((DENSE, 256), f32),
            pltpu.VMEM((DENSE, C), f32),
            pltpu.VMEM((4, 2, ROWS, 128), f32), pltpu.VMEM((CHUNKS, 2, ROWS, 128), f32),
            pltpu.VMEM((CHUNKS, HALF, 128), f32), pltpu.VMEM((CHUNKS, m, HALF // m, 128), f32),
            pltpu.VMEM(lanes, f32), pltpu.VMEM((4, TINY, C), f32), pltpu.VMEM((3, TINY, C), f32),
            pltpu.VMEM((m, TINY, C), f32), pltpu.VMEM((4, 16, C), f32), pltpu.VMEM((2, 16, C), f32),
            dma((2,)), dma((7,)), dma((7,)), dma((2, 3)), dma((2, 3)), dma((2,)), dma((4,)),
            dma((5, CHUNKS)), dma((5, CHUNKS)), dma((4, m)), dma((CHUNKS, m)), dma((4, m)),
            dma((CHUNKS, m)), dma((4, 2)), dma((CHUNKS,)), dma((m,)), dma((m,)),
            dma((2, 4)), dma((2, 4)), dma((1,)), dma((3, 3)), dma((3, 3)),
        ],
        compiler_params=pltpu.CompilerParams(
            collective_id=ident, has_side_effects=True, vmem_limit_bytes=60 << 20,
            dimension_semantics=("arbitrary",),
        ),
        name="backward",
    )(*args)


def unpack_kernel(
    pack_ref, merge_ref, tiny_ref,
    we_ref, ws_ref, qkv_ref, wo_ref, mw_ref, mg_ref, ms_ref, g1_ref, b1_ref, bias_ref, tab_ref, bo_ref, g2_ref,
    b2_ref, be_ref, bs_ref, rms_ref,
):
    for q in range(4):
        lanes = slice(q * 128, (q + 1) * 128)
        we_ref[0, :, lanes] = pack_ref[q]
        ws_ref[0, :, lanes] = pack_ref[4 + q]
        wo_ref[0, :, lanes] = pack_ref[11, q * 128 : (q + 1) * 128, :]
    for j in range(3):
        qkv_ref[0, j] = pack_ref[8 + j]

    @pl.when(pl.program_id(0) == 0)
    def _():
        for i in range(2):
            for j in range(2):
                k, low = 2 * j + i, (2 * i + j) * 64
                for q in range(4):
                    mw_ref[k, :, q * 128 : (q + 1) * 128] = merge_ref[q, low : low + 64, :]
                mg_ref[k : k + 1, :] = tiny_ref[10:11, low : low + 64]
                ms_ref[k : k + 1, :] = tiny_ref[10:11, 256 + low : 320 + low]
        be_ref[...] = tiny_ref[0:2, :]
        for b in range(2):
            bias_ref[b, 0:1, :] = tiny_ref[2 + b : 3 + b, 0:128]
            bias_ref[b, 1:2, :] = tiny_ref[2 + b : 3 + b, 256:384]
            line = jnp.concatenate([tiny_ref[4 + 3 * b + q : 5 + 3 * b + q, :] for q in range(3)], axis=1)
            for h in range(4):
                tab_ref[b, h : h + 1, :] = line[:, h * 384 : h * 384 + 361]
            for k, ref in enumerate((g1_ref, b1_ref, bo_ref)):
                ref[b : b + 1, :] = tiny_ref[16 + 3 * b + k : 17 + 3 * b + k, :]
            for k, ref in enumerate((g2_ref, b2_ref, bs_ref)):
                ref[b : b + 1, :] = tiny_ref[22 + 3 * b + k : 23 + 3 * b + k, :]
        sums = jnp.sum(tiny_ref[28:36, :], axis=1, keepdims=True)
        rms_ref[...] = jnp.broadcast_to(jnp.sqrt(sums / (sums[5:6] * C)), (8, 128))


def unpack(packed, tiny):
    blocks = packed.reshape(-1, 512, 128)
    merged = packed.reshape(-1, 256, 128)
    whole = lambda *shape: pl.BlockSpec(shape, lambda b: (0,) * len(shape))
    layer = lambda *shape: pl.BlockSpec((1,) + shape, lambda b: (b,) + (0,) * len(shape))
    row = (2, C)
    return pl.pallas_call(
        unpack_kernel,
        grid=(2,),
        in_specs=[
            pl.BlockSpec((12, 512, 128), lambda b: (1 - b, 0, 0)),
            pl.BlockSpec((4, 256, 128), lambda b: (12, 0, 0)),
            whole(TINY, C),
        ],
        out_specs=[
            layer(512, 512), layer(512, 512), layer(3, 512, 128), layer(128, 512), whole(4, 64, C), whole(4, 64),
            whole(4, 64), whole(*row), whole(*row), whole(2, 2, 128), whole(2, 4, 361), whole(*row), whole(*row),
            whole(*row), whole(*row), whole(*row), whole(8, 128),
        ],
        out_shape=[
            sds(2, 512, 512), sds(2, 512, 512), sds(2, 3, 512, 128), sds(2, 128, 512), sds(4, 64, C), sds(4, 64),
            sds(4, 64), sds(*row), sds(*row), sds(2, 2, 128), sds(2, 4, 361), sds(*row), sds(*row), sds(*row),
            sds(*row), sds(*row), sds(8, 128),
        ],
        compiler_params=pltpu.CompilerParams(vmem_limit_bytes=48 << 20),
        name="unpack",
    )(blocks, merged, tiny)


def column_pick():
    pick = np.zeros((19, WIN, WIN), np.float32)
    for a in range(WIN):
        for b in range(WIN):
            pick[a - b + WIN - 1, a, b] = 1.0
    return pick


def row_pick():
    pick = np.zeros((19, WIN, WIN, WIN, 2, 2, SUB), np.float32)
    for pr in range(WIN):
        for qr in range(WIN):
            for qc in range(WIN):
                pick[pr - qr + WIN - 1, qc, pr, 0, qr // 5, qc // 5, (qr % 5) * 5 + qc % 5] = 1.0
    return pick[:, :, :, 0].reshape(190, WIN * WT)


def bias_of(table):
    heads = table.shape[0]
    grid = table.reshape(heads, 19, 19)
    columns = jnp.einsum("hrd,dab->harb", grid, jnp.asarray(column_pick()), precision="highest")
    rows = jnp.dot(columns.reshape(heads * WIN, 190), jnp.asarray(row_pick()), precision="highest")
    rows = rows.reshape(heads, 2, 5, 2, 5, WT).transpose(0, 3, 1, 4, 2, 5)
    rows = rows.reshape(heads, 4, REAL, WT)
    return jnp.pad(rows, ((0, 0), (0, 0), (0, SUB - REAL), (0, 0))).reshape(heads, WT, WT)


def shards(
    patches, merge_gain, merge_shift, merge_weight, first_gain, first_shift, input_weight,
    input_bias, position_table, output_weight, output_bias, second_gain, second_shift,
    expand_weight, expand_bias, shrink_weight, shrink_bias, page_map, valid_flags, cotangent,
):
    sp_count = lax.axis_size("sp")
    tp = lax.axis_index("tp")

    tables = position_table.transpose(0, 2, 1).reshape(8, 361)
    bias = bias_of(tables).reshape(2, 512, 128)
    pairs = jnp.concatenate([input_bias, jnp.zeros_like(input_bias)], axis=2).reshape(2, 512)
    small = jnp.concatenate([expand_bias, pairs, jnp.zeros((4, 512), f32)], axis=0)

    valid = valid_flags.astype(f32).reshape(2, 5, 24, 5).transpose(0, 2, 1, 3).reshape(2, 24, REAL)
    valid = jnp.pad(valid, ((0, 0), (0, 0), (0, 128 - REAL)))

    gain = merge_gain.reshape(2, 2, 64).transpose(1, 0, 2).reshape(1, 256)
    offset = merge_shift.reshape(2, 2, 64).transpose(1, 0, 2).reshape(1, 256)
    mgain = jnp.concatenate([gain, offset, jnp.zeros((6, 256), f32)], axis=0)
    weight = merge_weight.reshape(2, 2, 64, C).transpose(1, 0, 2, 3).reshape(256, C)
    quads = patches.reshape(2, 5, 2, 4, NW, 2, 5, 128).transpose(3, 4, 0, 5, 1, 6, 2, 7).reshape(4, 300, 256)
    quads = jnp.pad(quads, ((0, 0), (0, DENSE - 300), (0, 0)))
    cot = jnp.roll(cotangent.reshape(2, 5, 24, 5, 128), -1, axis=2).transpose(0, 2, 1, 3, 4).reshape(2, 24, REAL, 128)
    cot = jnp.pad(cot, ((0, 0), (0, 0), (0, SUB - REAL), (0, 0)))

    nall, wall, cot, fields, middles, qkv, p, att, hid, slope, stat, vecs, squares, out = forward(
        sp_count,
        (
            quads, weight, mgain, input_weight.transpose(0, 2, 1, 3), bias, output_weight.reshape(2, 1, 128, C),
            expand_weight.reshape(2, 4, 128, 512), shrink_weight.reshape(2, 4, 128, C), small,
            first_gain, first_shift, output_bias, second_gain, second_shift,
            shrink_bias, page_map, valid, cot,
        ),
        1,
    )
    _, _, _, output, packed, gquads, tiny = backward(
        sp_count,
        (
            cot.reshape(4, 2, 192, 128), middles, fields, first_gain, first_shift,
            second_gain, second_shift, wall, wall, nall, wall, hid, slope, qkv, p, att,
            squares, quads, weight, vecs, mgain, stat, out.reshape(4, 2, 6, SUB, 128),
            *table_picks(),
        ),
        2,
    )
    output = jnp.roll(output[:, :, :REAL], 1, axis=1).reshape(2, 24, 5, 5, 128)
    output = output.transpose(0, 2, 1, 3, 4).reshape(10, 120, 128)
    gquads = gquads[:, :300].reshape(4, NW, 2, 2, 5, 5, 2, 128)
    patches_grad = gquads.transpose(2, 4, 6, 0, 1, 3, 5, 7).reshape(20, 240, 64)
    we, ws, qkv, wo, dmw, dmg, dms, dg1, db1, dbias, table, dbo, dg2, db2, dbe, dbs, rms = unpack(packed, tiny)
    return (
        output, patches_grad, dmg, dms, dmw, dg1, db1, qkv.transpose(0, 2, 1, 3), dbias, table.transpose(0, 2, 1),
        wo, dbo, dg2, db2, we, dbe, ws, dbs, rms[:5, 0],
    )


def solution(mesh):
    placed = (
        P("sp", None, "tp"), P(None, "tp"), P(None, "tp"), P(None, "tp", None), P(), P(),
        P(None, None, None, "tp"), P(None, None, "tp"), P(None, None, "tp"), P(None, "tp", None),
        P(), P(), P(), P(None, None, "tp"), P(None, "tp"), P(None, "tp", None), P(), P(),
        P("sp", None), P("sp", None, "tp"),
    )
    results = (
        P("sp", None, "tp"), P("sp", None, "tp"), P(None, "tp"), P(None, "tp"), P(None, "tp", None),
        P(), P(), P(None, None, None, "tp"), P(None, None, "tp"), P(None, None, "tp"),
        P(None, "tp", None), P(), P(), P(), P(None, None, "tp"), P(None, "tp"), P(None, "tp", None),
        P(), P(),
    )
    return jax.shard_map(shards, mesh=mesh, in_specs=placed, out_specs=results, check_vma=False)
```

```python
import functools

import jax
import jax.numpy as jnp
import numpy as np
from jax import lax
from jax.experimental import pallas as pl
from jax.experimental.pallas import tpu as pltpu
from jax.sharding import PartitionSpec as P

C = 512
HD = 32
C2 = 256
WIN = 10
SHIFT = 5
SUB = 32
REAL = 25
WT = 128
TOK = 384
NW = 3
DENSE = 304
GROUP = 4

bf16 = jnp.bfloat16
f32 = jnp.float32
epsilon = 1e-05
masked = -1000000000.0

NN = (((1,), (0,)), ((), ()))
NT = (((1,), (1,)), ((), ()))
TN = (((0,), (0,)), ((), ()))


def split(x):
    high = x.astype(bf16)
    return high, (x - high.astype(f32)).astype(bf16)


def mm(a, b, dims):
    return lax.dot_general(a, b, dims, preferred_element_type=f32)


def mm3(a, b, dims):
    return mm(a[0], b[0], dims) + (mm(a[0], b[1], dims) + mm(a[1], b[0], dims))


def normalized(x):
    center = x - jnp.mean(x, axis=-1, keepdims=True)
    rho = lax.rsqrt(jnp.mean(center * center, axis=-1, keepdims=True) + epsilon)
    return center * rho, rho


def placing():
    token = lax.broadcasted_iota(jnp.int32, (TOK, DENSE), 0)
    column = lax.broadcasted_iota(jnp.int32, (TOK, DENSE), 1)
    inner = token % SUB
    return ((inner < REAL) & (column == (token // SUB) * REAL + inner)).astype(f32).astype(bf16)


def selected(pick, x, dims):
    high, rest = x.astype(bf16), x - x.astype(bf16).astype(f32)
    mid, low = split(rest)
    return mm(pick, high, dims) + (mm(pick, mid, dims) + mm(pick, low, dims))


def upright(columns):
    return jnp.concatenate([columns, jnp.zeros((TOK - DENSE, 128), f32)], axis=0).T[0:8, :]


def head_masks(dtype):
    lane = lax.broadcasted_iota(jnp.int32, (1, 128), 1) // HD
    return [(lane == h).astype(f32).astype(dtype) for h in range(GROUP)]


def stacked(pair, masks):
    return tuple(jnp.concatenate([part * m for m in masks], axis=0) for part in pair)


def side_by_side(pair):
    return tuple(
        jnp.concatenate([part[h * WT : (h + 1) * WT] for h in range(GROUP)], axis=1)
        for part in pair
    )


def colsum(x):
    return jnp.sum(x, axis=0, keepdims=True)


def sds(*shape):
    return jax.ShapeDtypeStruct(shape, f32)


def norm_back(x, gain, grad_y):
    xhat, rho = normalized(x)
    gh = grad_y * gain
    grad_x = rho * (
        gh - jnp.mean(gh, axis=-1, keepdims=True) - xhat * jnp.mean(gh * xhat, axis=-1, keepdims=True)
    )
    return grad_x, colsum(grad_y * xhat), colsum(grad_y)


MESH = pl.DeviceIdType.MESH
ANY = pl.BlockSpec(memory_space=pl.ANY)
VM = pl.BlockSpec(memory_space=pltpu.VMEM)


def here():
    sp, tp = lax.axis_index("sp"), lax.axis_index("tp")
    return sp, tp, (sp, tp ^ 1), (sp, tp ^ 2), (sp ^ 1, tp)


def meet(peers):
    barrier = pltpu.get_barrier_semaphore()
    for peer in peers:
        pl.semaphore_signal(barrier, inc=1, device_id=peer, device_id_type=MESH)
    pl.semaphore_wait(barrier, len(peers))


def push(src, dst, send, recv, peer):
    return pltpu.make_async_remote_copy(
        src_ref=src, dst_ref=dst, send_sem=send, recv_sem=recv, device_id=peer, device_id_type=MESH
    )


MLP_ROWS, ATT_ROWS = 4096, 2048
BLOCK_ROWS = MLP_ROWS + ATT_ROWS
FIRST = 2
AG_STEP = 15
STEPS = 17


def chunk_plan(n):
    rows = 256 if n <= 16 else 512
    every = 2 * BLOCK_ROWS // rows
    return rows, every, every + 1024 // rows, 3 if rows == 256 else 1


TINY = 40
COLS = [(0, 0, 0, 1), (0, 1, 1, 0), (1, 0, 1, 1), (1, 1, 2, 0), (2, 0, 2, 1)]


def at(w, sr, sc):
    return pl.ds(w * WT + sr * 64 + sc * SUB, SUB)


NCH = 13
GCH = 2 * NCH
F_STEPS = 19


TURNS = (0, 0, 0, 2, 9, 11, 13, 15, 17, 19, 21, 23, 25, 27, 29, 30, 30, 30, 30, 30)
LAG = 2
AHEAD = 6


def fwd_order(s):
    att = jnp.where(s < 2, 0, jnp.where(s < 6, s - 2, jnp.where(s < 10, 3, jnp.where(s < 14, s - 6, 7))))
    mlp = jnp.where(s < 6, 0, jnp.where(s < 10, s - 6, jnp.where(s < 14, 3, jnp.where(s < 18, s - 10, 7))))
    return att, mlp


def so_far(table, s):
    found = jnp.int32(table[0])
    for k in range(1, len(table)):
        if table[k] != table[k - 1]:
            found = jnp.where(s >= k, table[k], found)
    return found


def fwd_kernel(n, *refs):
    (
        q_ref, mw_ref, mg_ref, wi_ref, bi_ref, wo_ref, we_ref, ws_ref, sm_ref, g1_ref, b1_ref, bo_ref,
        g2_ref, b2_ref, bs_ref, page_ref, grid_ref, cot_ref,
    ) = refs[:18]
    (
        nall, wall, cb, field_out, mid_out, qkv_ref, p_ref, att_ref, hid_ref, slope_ref, stat_ref, vec_ref,
        sq_ref, os_ref,
    ) = refs[18:32]
    (
        nb, wb, smb, pb, pr, px, stb, str_, stx, vp, v0_ref, v1_ref, vs_ref, vr, vc, regr_ref, regc_ref, field, nh, nl, mixed, moved,
        lsem, ss, sr, xs, xr, ys, yr, zs, zr, s2s, s2r, sms, smr, rss, rsr, vps, vpr, vvs, vvr,
        mvs, mvr, cbs, cbr, cbl, hn, hw,
    ) = refs[32:]
    step = pl.program_id(0)
    sp, tp, sib, across, beside = here()
    par = sp & 1
    up, down = lax.rem(sp + 1, n), lax.rem(sp + n - 1, n)
    left = lax.rem(tp + 3, 4)

    def own():
        todo = []
        for b in range(2):
            todo += [
                (wi_ref.at[b], nb.at[0, pl.ds(4 * b, 3)]), (bi_ref.at[b], nb.at[0, 4 * b + 3]),
                (we_ref.at[b], wb.at[0, pl.ds(9 * b, 4)]), (ws_ref.at[b], wb.at[0, pl.ds(9 * b + 4, 4)]),
                (wo_ref.at[b], wb.at[0, pl.ds(9 * b + 8, 1)]),
            ]
        todo.append((sm_ref, smb.at[0]))
        return [pltpu.make_async_copy(s, d, lsem.at[i]) for i, (s, d) in enumerate(todo)]

    def to_sib(b):
        parts = [(nb, pl.ds(4 * b, 4)), (wb, pl.ds(9 * b + 8, 1)), (wb, pl.ds(9 * b, 8))]
        return [
            push(buf.at[0, d], buf.at[1, d], ss.at[b, k], sr.at[b, k], sib) for k, (buf, d) in enumerate(parts)
        ]

    def narrow(c):
        b, r = c // NCH, c % NCH
        return r < 4, 4 * b + r, 9 * b + jnp.where(r == 4, 8, r - 5)

    def each(c, act):
        small, kn, kw = narrow(c)

        @pl.when(small)
        def _():
            act(nb, kn, 512)

        @pl.when(jnp.logical_not(small))
        def _():
            act(wb, kw, 128)

    zpar = lax.rem(sp // 2, 2)
    far = (sp ^ 2, tp)

    def deep(c):
        return c % 3 != 0

    def cut(size, k):
        return pl.ds(pl.multiple_of(k * size, size), size)

    def x_copy(c, buf, k, size, low):
        d = cut(size // 4, 2 * zpar + par) if low else cut(size // 2, par)
        return push(buf.at[0, k, d], buf.at[2, k, d], xs.at[c], xr.at[c], across)

    def y_copy(c, buf, k, size, low):
        d = cut(size // 4, 2 * zpar + par) if low else cut(size // 2, par)
        return push(buf.at[2, k, d], buf.at[2, k, d], ys.at[c], yr.at[c], beside)

    def z_copy(c, buf, k, size):
        d = cut(size // 2, zpar)
        return push(buf.at[2, k, d], buf.at[2, k, d], zs.at[c], zr.at[c], far)

    def s_copy(which, c, buf, k, size):
        d = cut(size // 2, which)
        send, recv = (s2s, s2r)
        return push(buf.at[2, k, d], buf.at[3, k, d], send.at[which, c], recv.at[which, c], sib)

    def x_start(c):
        def act(buf, k, size):
            for low in (False, True):

                @pl.when(deep(c) == low)
                def _(low=low):
                    x_copy(c, buf, k, size, low).start()

        each(c, act)

    def s_in(c, buf, k, size):
        for h in range(2):
            s_copy(h, c, buf, k, size).wait_recv()

    def rs_copies(k):
        if k < 2:
            i = 1 + 2 * k
            return [
                push(pb.at[i], pr.at[k], rss.at[0, k], rsr.at[0, k], sib),
                push(stb.at[i], str_.at[k], rss.at[1, k], rsr.at[1, k], sib),
            ]
        return [
            push(pb.at[2], px, rss.at[0, 2], rsr.at[0, 2], across),
            push(stb.at[2], stx, rss.at[1, 2], rsr.at[1, 2], across),
        ]

    def vec_copies():
        return [push(vp.at[0], vp.at[i], vps.at[i - 1], vpr.at[i - 1], (sp, tp ^ i)) for i in (1, 2, 3)]

    def sm_copy(k):
        src, dst, peer = ((0, 1, sib), (0, 2, across), (2, 3, sib))[k]
        return push(smb.at[src], smb.at[dst], sms.at[k], smr.at[k], peer)

    def valid_copy():
        return push(vs_ref, vr, vvs.at[0], vvr.at[0], (down, tp))

    def moves():
        todo = [(at(0, 1, 0), at(2, 0, 1), (sp, left)), (at(0, 0, 0), at(2, 1, 1), (down, left))]
        for w0, s0, w1, s1 in COLS:
            todo.append((at(w1, 0, s1), at(w0, 1, s0), (down, tp)))
        return [push(field.at[s], moved.at[d], mvs.at[i], mvr.at[i], peer) for i, (s, d, peer) in enumerate(todo)]

    def cot_copy(k, i):
        t = tp ^ i
        src = cot_ref.at[1 - k, pl.ds(6 * t, 6)]
        return push(src, cb.at[tp, k], cbs.at[k, i], cbr.at[k, i], ((sp, t), (down, t))[k])

    def cot_in(k, i):
        src = cot_ref.at[1 - k, pl.ds(0, 6)]
        return push(src, cb.at[tp ^ i, k], cbs.at[k, i], cbr.at[k, i], (sp, tp ^ 1))

    def cot_own():
        return pltpu.make_async_copy(cot_ref.at[1, pl.ds(6 * tp, 6)], cb.at[tp, 0], cbl.at[0])

    @pl.when(step == 0)
    def _():
        for copy in own():
            copy.start()
        barrier = pltpu.get_barrier_semaphore()
        near = [beside, far] + [(sp, tp ^ i) for i in (1, 2, 3)]
        near += [(up, tp ^ i) for i in range(4)] + [(down, tp ^ i) for i in range(4)]
        for peer in near:
            pl.semaphore_signal(barrier, inc=1, device_id=peer, device_id_type=MESH)
        pl.semaphore_wait(barrier, len(near))
        gain, offset = mg_ref[0:1, :], mg_ref[1:2, :]
        wpair = split(mw_ref[...])
        rows8 = lax.broadcasted_iota(jnp.int32, (8, 256), 0)
        pick = jnp.where(rows8 == 0, gain, jnp.where(rows8 == 1, offset, 0.0))
        vp[0] = jnp.dot(pick, mw_ref[...], precision=lax.Precision.HIGHEST, preferred_element_type=f32)
        for copy in vec_copies():
            copy.start()
        lane1 = lax.broadcasted_iota(jnp.int32, (1, 128), 1) // SUB
        for buf in (v0_ref, v1_ref, vs_ref, regr_ref):
            buf[...] = jnp.zeros_like(buf)
        for w in range(NW):
            here_, next_, sent, region = [jnp.zeros((1, 128), f32) for _ in range(4)]
            for k in range(4):
                sr, sc = k // 2, k % 2
                column = 6 * tp + 2 * w + sc
                after = lax.rem(column + 1, 24)
                bring = lambda r, c: pltpu.roll(grid_ref[r, pl.ds(c, 1), :], SUB * k, 1)
                here_ = here_ + bring(sr, column)
                if sr == 0:
                    next_ = next_ + bring(1, after)
                else:
                    sent = sent + bring(0, after)
                page = page_ref[lax.rem(sp + sr, n), lax.rem(3 * tp + w + sc, 12)] * 4
                if sr == 1:
                    page = page + 2 * (sp == n - 1).astype(jnp.int32)
                if sc == 1 and w == NW - 1:
                    page = page + (tp == 3).astype(jnp.int32)
                region = region + jnp.where(lane1 == k, page, 0).astype(f32)
            v0_ref[w : w + 1, :] = here_
            v1_ref[w : w + 1, :] = next_
            vs_ref[w : w + 1, :] = sent
            regr_ref[1, w : w + 1, :] = region
        valid_copy().start()
        lane = lax.broadcasted_iota(jnp.int32, (DENSE, 128), 1)

        def project(i):
            quad = q_ref[tp ^ i]
            pb[i] = mm3(split(quad * gain), wpair, NN)
            s1 = jnp.sum(quad, axis=-1, keepdims=True)
            s2 = jnp.sum(quad * quad, axis=-1, keepdims=True)
            stb[i] = upright(jnp.where(lane == 0, s1, jnp.where(lane == 1, s2, 0.0)))

        project(3)
        for copy in rs_copies(1):
            copy.start()
        project(1)
        for copy in rs_copies(0):
            copy.start()
        for copy in own():
            copy.wait()
        sm_copy(0).start()
        sm_copy(1).start()
        for c in range(2):
            x_copy(c, nb, c, 512, c % 3 != 0).start()
        project(2)
        project(0)
        for copy in rs_copies(1):
            copy.wait_recv()
        pb[2] = pb[2] + pr[1]
        stb[2] = stb[2] + str_[1]
        for copy in rs_copies(2):
            copy.start()
        for copy in to_sib(0):
            copy.start()
        for c in range(2, AHEAD):
            buf, k, size = (nb, c, 512) if c < 4 else (wb, 8 if c == 4 else c - 5, 128)
            x_copy(c, buf, k, size, c % 3 != 0).start()
        sq_ref[...] = jnp.zeros_like(sq_ref)
        os_ref[...] = jnp.zeros_like(os_ref)
        vec_ref[...] = jnp.zeros_like(vec_ref)

    @pl.when(step == 1)
    def _():
        sm_copy(1).wait_recv()
        sm_copy(2).start()
        for copy in vec_copies():
            copy.wait()
        vec_ref[...] = (vp[0] + vp[1]) + (vp[2] + vp[3])
        valid_copy().wait()
        for b in range(2):
            line = v0_ref[...] if b == 0 else v1_ref[...] + vr[...]
            tall = jnp.concatenate([line, jnp.zeros((120, 128), f32)], axis=0).T
            vc[b] = jnp.concatenate([tall[:, w : w + 1] for w in range(NW)], axis=0)
            if b == 1:
                vr[...] = line
            tall = jnp.concatenate([regr_ref[b], jnp.zeros((120, 128), f32)], axis=0).T
            regc_ref[b] = jnp.concatenate([tall[:, w : w + 1] for w in range(NW)], axis=0)
        sq_ref[5:6, 0:128] = colsum(v0_ref[...])
        for copy in rs_copies(0):
            copy.wait_recv()
        pb[0] = pb[0] + pr[0]
        stb[0] = stb[0] + str_[0]
        for k in range(2):
            for copy in rs_copies(k):
                copy.wait_send()
        for copy in rs_copies(2):
            copy.wait()
        sums = jnp.concatenate([stb[0] + stx[...], jnp.zeros((120, TOK), f32)], axis=0).T[0:DENSE, :]
        mean = sums[:, 0:1] / (4.0 * C2)
        inverse = lax.rsqrt(sums[:, 1:2] / (4.0 * C2) - mean * mean + epsilon)
        lane = lax.broadcasted_iota(jnp.int32, (DENSE, 128), 1)
        stat_ref[...] = jnp.where(lane == 0, mean, jnp.where(lane == 1, inverse, 0.0))
        dense = inverse * (pb[0] + px[...] - mean * vec_ref[0:1, :]) + vec_ref[1:2, :]
        field[...] = selected(placing(), dense, NN)

    def both(c, act):
        def run(buf, k, size):
            for low in (False, True):

                @pl.when(deep(c) == low)
                def _(low=low):
                    act(buf, k, size, low)

        each(c, run)

    def gather_turn(p):
        @pl.when(p + AHEAD < GCH)
        def _():
            x_start(p + AHEAD)

        @pl.when(p < GCH)
        def _():
            def act(buf, k, size, low):
                x_copy(p, buf, k, size, low).wait_recv()
                y_copy(p, buf, k, size, low).start()
                if not low:
                    for h in range(2):

                        @pl.when(par == h)
                        def _(h=h):
                            s_copy(h, p, buf, k, size).start()

            both(p, act)

        y = p - LAG

        @pl.when((y >= 0) & (y < GCH))
        def _():
            def act(buf, k, size, low):
                y_copy(y, buf, k, size, low).wait_recv()
                x_copy(y, buf, k, size, low).wait_send()
                half_here = zpar if low else 1 - par
                if low:
                    z_copy(y, buf, k, size).start()
                for h in range(2):

                    @pl.when(half_here == h)
                    def _(h=h):
                        s_copy(h, y, buf, k, size).start()

            both(y, act)

        z = p - 2 * LAG

        @pl.when((z >= 0) & (z < GCH))
        def _():
            def act(buf, k, size, low):
                y_copy(z, buf, k, size, low).wait_send()
                if low:
                    z_copy(z, buf, k, size).wait_recv()
                    for h in range(2):

                        @pl.when(1 - zpar == h)
                        def _(h=h):
                            s_copy(h, z, buf, k, size).start()

            both(z, act)

    def midway():
        first = so_far(TURNS, step)

        @pl.when(first < so_far(TURNS, step + 1))
        def _():
            gather_turn(first)

    att, mlp = fwd_order(step)

    @pl.when(((step >= 2) & (step < 6)) | ((step >= 10) & (step < 14)))
    def _():
        b, i = att // 4, att % 4

        @pl.when(i == 0)
        def _():
            @pl.when(b == 1)
            def _():
                for copy in moves():
                    copy.wait()
                field[...] = moved[...]

            field_out[0] = field[...]
            xhat, _ = normalized(field[...])
            nh[...], nl[...] = split(xhat * g1_ref[pl.ds(b, 1), :] + b1_ref[pl.ds(b, 1), :])
            mixed[...] = jnp.broadcast_to(bo_ref[pl.ds(b, 1), :], mixed.shape)

        for k in range(2):

            @pl.when((i == 1) & (b == k))
            def _(k=k):
                for copy in to_sib(k)[:2]:
                    copy.wait_recv()
                if k == 0:
                    sm_copy(0).wait()
                    sm_copy(1).wait_send()
                    sm_copy(2).wait()

        @pl.when(i == 3)
        def _():
            for r in range(5):
                c = b * NCH + r
                buf, k, size = (nb, 4 * b + r, 512) if r < 4 else (wb, 9 * b + 8, 128)
                s_in(c, buf, k, size)

        pltpu.make_async_copy(nb.at[i, pl.ds(4 * b, 4)], nall.at[i, b], hn.at[b, i]).start()
        w = jnp.concatenate([nb[i, 4 * b + j] for j in range(3)], axis=1)
        lane = lax.broadcasted_iota(jnp.int32, (1, 384), 1)
        qkv = mm3((nh[...], nl[...]), split(w), NN) + smb[i, pl.ds(2 + b, 1), 0:384]
        qkv_ref[0] = qkv * jnp.where(lane < 128, HD ** (-0.5), 1.0)
        masks = head_masks(bf16)
        bias = nb[i, 4 * b + 3]
        eye = lax.broadcasted_iota(jnp.int32, (WT, WT), 0) == lax.broadcasted_iota(jnp.int32, (WT, WT), 1)
        for j in range(NW):
            rows = pl.ds(j * WT, WT)
            seen = qkv_ref[0, rows, :]
            q4 = stacked(split(seen[:, :128]), masks)
            k = split(seen[:, 128:256])
            v4 = stacked(split(seen[:, 256:]), masks)
            flags = jnp.where(b == 0, v0_ref[j : j + 1, :], vr[j : j + 1, :])
            allowed = (regc_ref[b, rows, :] == regr_ref[b, j : j + 1, :]) & (flags > 0) | eye
            allowed = jnp.concatenate([allowed.astype(f32)] * GROUP, axis=0) > 0
            s = jnp.where(allowed, mm3(q4, k, NT) + bias, masked)
            e = jnp.exp(s - jnp.max(s, axis=-1, keepdims=True))
            p = e / jnp.sum(e, axis=-1, keepdims=True)
            p_ref[0, j] = p
            att_ref[0, rows, :] = mm3(side_by_side(split(p)), v4, NN)
            if j == 1:
                midway()
        mixed[...] += mm3(split(att_ref[0]), split(wb[i, 9 * b + 8]), NN)

        @pl.when(i == 3)
        def _():
            middle = field[...] + mixed[...]
            mid_out[0] = middle
            sq_ref[pl.ds(2 * b, 1), :] = colsum(mixed[...] * mixed[...] * vc[b])

    @pl.when(((step >= 6) & (step < 10)) | ((step >= 14) & (step < 18)))
    def _():
        b, i = mlp // 4, mlp % 4

        @pl.when(i == 0)
        def _():
            xhat, _ = normalized(mid_out[0])
            nh[...], nl[...] = split(xhat * g2_ref[pl.ds(b, 1), :] + b2_ref[pl.ds(b, 1), :])
            mixed[...] = jnp.broadcast_to(bs_ref[pl.ds(b, 1), :], mixed.shape)

            @pl.when(b == 0)
            def _():
                for copy in to_sib(1):
                    copy.start()

        for k in range(2):

            @pl.when((i == 1) & (b == k))
            def _(k=k):
                to_sib(k)[2].wait_recv()

        @pl.when(i == 3)
        def _():
            for r in range(8):
                c = b * NCH + 5 + r
                s_in(c, wb, 9 * b + r, 128)

        pltpu.make_async_copy(wb.at[i, pl.ds(9 * b, 9)], wall.at[i, b], hw.at[b, i]).start()
        we = wb[i, pl.ds(9 * b, 4)].reshape(512, 512)
        ws = wb[i, pl.ds(9 * b + 4, 4)].reshape(512, 512)
        pre = mm3((nh[...], nl[...]), split(we), NN) + smb[i, pl.ds(b, 1), :]
        phi = 0.5 * (1.0 + lax.erf(pre * (2 ** -0.5)))
        hidden = pre * phi
        hid_ref[0] = hidden
        slope_ref[0] = phi + pre * (jnp.exp(-0.5 * pre * pre) * ((2 * np.pi) ** -0.5))
        midway()
        mixed[...] += mm3(split(hidden), split(ws), NN)

        @pl.when(i == 3)
        def _():
            out = mid_out[0] + mixed[...]
            field[...] = out
            sq_ref[pl.ds(2 * b + 1, 1), :] = colsum(mixed[...] * mixed[...] * vc[b])

            @pl.when(b == 0)
            def _():
                for copy in moves():
                    copy.start()
                for w0, s0, w1, s1 in COLS:
                    moved[at(w0, 0, s0), :] = field[at(w1, 1, s1), :]

            @pl.when(b == 1)
            def _():
                sq_ref[4:5, :] = colsum(out * out * vc[1])
                for t in range(4):
                    for w in range(NW):
                        for r in range(2):
                            os_ref[t, r, w * 64 : w * 64 + 64, :] = out[
                                w * WT + r * 64 : w * WT + r * 64 + 64, t * 128 : (t + 1) * 128
                            ]

    @pl.when(step == 15)
    def _():
        cot_own().start()
        for k in range(2):
            for i in range(4):
                if k + i > 0:
                    cot_copy(k, i).start()

    @pl.loop(so_far(TURNS, step) + 1, so_far(TURNS, step + 1))
    def _(p):
        gather_turn(p)

    @pl.when(step == F_STEPS - 1)
    def _():
        cot_own().wait()
        for k in range(2):
            for i in range(4):
                if k + i > 0:
                    cot_copy(k, i).wait_send()
                    cot_in(k, i).wait_recv()
        for b in range(2):
            for copy in to_sib(b):
                copy.wait_send()
            for i in range(4):
                pltpu.make_async_copy(nb.at[i, pl.ds(4 * b, 4)], nall.at[i, b], hn.at[b, i]).wait()
                pltpu.make_async_copy(wb.at[i, pl.ds(9 * b, 9)], wall.at[i, b], hw.at[b, i]).wait()

        @pl.loop(0, GCH)
        def _(c):
            def act(buf, k, size, low):
                if low:
                    z_copy(c, buf, k, size).wait_send()
                for h in range(2):
                    s_copy(h, c, buf, k, size).wait_send()

            both(c, act)


def forward(n, args, ident):
    dma = pltpu.SemaphoreType.DMA

    def fixed(shape):
        return pl.BlockSpec(shape, lambda s: (0,) * len(shape), pipeline_mode=pl.Buffered(1))

    def by(index, shape):
        zeros = (0,) * len(shape)
        return pl.BlockSpec((1,) + shape, lambda s: (index(s),) + zeros)

    att_at = lambda s: fwd_order(s)[0]
    mlp_at = lambda s: fwd_order(s)[1]
    second = lambda s: jnp.where(s < 10, 0, 1)
    vm = lambda *shape: pltpu.VMEM(shape, f32)
    two = fixed((2, C))
    return pl.pallas_call(
        functools.partial(fwd_kernel, n),
        grid=(F_STEPS,),
        in_specs=[
            fixed((4, DENSE, 256)), fixed((256, C)), fixed((8, 256)), ANY, ANY, ANY, ANY, ANY, ANY,
            two, two, two, two, two, two, pl.BlockSpec(memory_space=pltpu.SMEM), fixed((2, 24, 128)), ANY,
        ],
        out_specs=[
            ANY, ANY, ANY, by(second, (TOK, C)), by(second, (TOK, C)), by(att_at, (TOK, 384)),
            by(att_at, (NW, GROUP * WT, WT)), by(att_at, (TOK, 128)), by(mlp_at, (TOK, 512)),
            by(mlp_at, (TOK, 512)), fixed((DENSE, 128)), fixed((8, C)), fixed((8, C)), fixed((4, 2, 192, 128)),
        ],
        out_shape=[
            sds(4, 2, 4, 512, 128), sds(4, 2, 9, 128, 512), sds(4, 2, 6, SUB, 128), sds(2, TOK, C), sds(2, TOK, C),
            sds(8, TOK, 384), sds(8, NW, GROUP * WT, WT), sds(8, TOK, 128), sds(8, TOK, 512), sds(8, TOK, 512),
            sds(DENSE, 128), sds(8, C), sds(8, C), sds(4, 2, 192, 128),
        ],
        scratch_shapes=[
            vm(4, 8, 512, 128), vm(4, 18, 128, 512), vm(4, 8, C), vm(4, DENSE, C), vm(2, DENSE, C), vm(DENSE, C),
            vm(4, 8, TOK), vm(2, 8, TOK), vm(8, TOK), vm(4, 8, C), vm(8, 128), vm(8, 128), vm(8, 128), vm(8, 128), vm(2, TOK, 1), vm(2, 8, 128), vm(2, TOK, 1),
            vm(TOK, C),
            pltpu.VMEM((TOK, C), bf16), pltpu.VMEM((TOK, C), bf16), vm(TOK, C), vm(TOK, C),
            dma((11,)), dma((2, 3)), dma((2, 3)), dma((GCH,)), dma((GCH,)), dma((GCH,)), dma((GCH,)),
            dma((GCH,)), dma((GCH,)), dma((2, GCH)), dma((2, GCH)), dma((3,)), dma((3,)), dma((2, 3)), dma((2, 3)),
            dma((3,)), dma((3,)), dma((1,)), dma((1,)), dma((7,)), dma((7,)), dma((2, 4)), dma((2, 4)),
            dma((1,)), dma((2, 4)), dma((2, 4)),
        ],
        compiler_params=pltpu.CompilerParams(
            collective_id=ident, has_side_effects=True, vmem_limit_bytes=60 << 20,
            dimension_semantics=("arbitrary",),
        ),
        name="forward",
    )(*args)


def table_line(dbias, pick, pile):
    high, low = split(dbias)
    spread = mm(high, pick, NN) + mm(low, pick, NN)
    spread = jnp.concatenate([spread[h * WT : (h + 1) * WT] for h in range(GROUP)], axis=1)
    high, low = split(spread)
    piled = mm(pile, high, NN) + mm(pile, low, NN)
    total = piled[0:16]
    for pc in range(1, WIN):
        total = total + pltpu.roll(piled[pc * 16 : pc * 16 + 16], pc, 1)
    row = lax.broadcasted_iota(jnp.int32, total.shape, 0)
    line = jnp.where(row == 0, total, 0.0)
    for pr in range(1, WIN):
        line = line + jnp.where(row == pr, pltpu.roll(total, 19 * pr, 1), 0.0)
    return colsum(line)


def table_picks():
    pick = np.zeros((WT, 384), np.float32)
    pile = np.zeros((WIN, 16, WT), np.float32)
    for r in range(WIN):
        for c in range(WIN):
            place = (r // 5) * 64 + (c // 5) * SUB + (r % 5) * 5 + c % 5
            pick[place, (9 - r) * 19 + 9 - c] = 1.0
            pile[c, r, place] = 1.0
    return jnp.asarray(pick, bf16), jnp.asarray(pile.reshape(160, WT), bf16)


def bwd_kernel(n, *refs):
    (
        cot_ref, mid_ref, field_ref, g1_ref, b1_ref, g2_ref, b2_ref, we_ref, ws_ref, wqkv_ref, wo_ref,
        hid_ref, slope_ref, qkv_ref, p_ref, att_ref, sq_ref, q_ref, mw_ref, vec_ref, mg_ref, stat_ref, os_ref,
        pick_ref, pile_ref,
    ) = refs[:25]
    pack, gall, exall, ob, out_ref, gq_ref, tout_ref = refs[25:32]
    (
        nth, ntl, gh, gl, acc, dqkv, gf, gbuf, moved, ext, extin, qbuf, gdense,
        loc, pair, yr, zr, fin, ta, tx, tsh, tr,
        gsem, mvs, mvr, ags, agr, agl, msem, ss, rs, zs, zq, fs, fq, ls, os, obs, obr, obl, tss, tsq,
    ) = refs[32:]
    step = pl.program_id(0)
    dmw, gqbuf = moved.at[pl.ds(0, 256)], dqkv.at[pl.ds(0, DENSE), pl.ds(0, 256)]
    sp, tp, sib, across, beside = here()
    par, mine = sp & 1, sp // 2
    m = n // 2
    ROWS, FULL_CH, CHUNKS, RATE = chunk_plan(n)
    HALF = ROWS // 2
    piece = HALF // m
    up, down, right = lax.rem(sp + 1, n), lax.rem(sp + n - 1, n), lax.rem(tp + 1, 4)

    def member(j):
        return lax.rem(mine + j, m)

    def device(q):
        return (q * 2 + par, tp)

    def out_copy(k, i):
        t = tp ^ i
        return push(
            os_ref.at[t, k], ob.at[1 - k, pl.ds(6 * tp, 6)], obs.at[k, i], obr.at[k, i], ((sp, t), (up, t))[k]
        )

    def out_in(k, i):
        return push(
            os_ref.at[0, k], ob.at[1 - k, pl.ds(6 * (tp ^ i), 6)], obs.at[k, i], obr.at[k, i], (sp, tp ^ 1)
        )

    def out_own():
        return pltpu.make_async_copy(os_ref.at[tp, 0], ob.at[1, pl.ds(6 * tp, 6)], obl.at[0])

    @pl.when(step == 0)
    def _():
        barrier = pltpu.get_barrier_semaphore()
        near = [beside] + [(sp, tp ^ i) for i in (1, 2, 3)]
        near += [(up, tp ^ i) for i in range(4)] + [(down, tp ^ i) for i in range(4)]
        for peer in near:
            pl.semaphore_signal(barrier, inc=1, device_id=peer, device_id_type=MESH)

        @pl.loop(1, m)
        def _(j):
            pl.semaphore_signal(barrier, inc=1, device_id=device(member(j)), device_id_type=MESH)

        ta[...] = jnp.zeros_like(ta)
        tsh[...] = jnp.zeros_like(tsh)
        ta[0, 28:36, :] = sq_ref[...]
        for t in range(4):
            for w in range(NW):
                for r in range(2):
                    gf[w * WT + r * 64 : w * WT + r * 64 + 64, t * 128 : (t + 1) * 128] = cot_ref[
                        t, r, w * 64 : w * 64 + 64, :
                    ]
        pl.semaphore_wait(barrier, len(near) + m - 1)
        out_own().start()
        for k in range(2):
            for i in range(4):
                if k + i > 0:
                    out_copy(k, i).start()

    def packed(b, j, late):
        size = ATT_ROWS if late else MLP_ROWS
        base = pl.multiple_of((1 - b) * BLOCK_ROWS + (MLP_ROWS if late else 0), 512)
        slot = j % 2
        return pltpu.make_async_copy(
            gbuf.at[slot, pl.ds(0, size)], pack.at[tp ^ j ^ 2, pl.ds(base, size)], gsem.at[slot]
        )

    def moves():
        todo = [
            (at(2, 0, 1), at(0, 1, 0), (sp, right)),
            (at(2, 1, 1), at(0, 0, 0), (up, right)),
        ]
        for w0, s0, w1, s1 in COLS:
            todo.append((at(w0, 1, s0), at(w1, 0, s1), (up, tp)))
        return [push(acc.at[src], moved.at[dst], mvs.at[i], mvr.at[i], peer) for i, (src, dst, peer) in enumerate(todo)]

    def kept():
        for w0, s0, w1, s1 in COLS:
            moved[at(w1, 1, s1), :] = acc[at(w0, 0, s0), :]

    def ag(k, src, dst, peer, which):
        return push(src, dst, ags.at[which, k], agr.at[which, k], peer)

    def ag_copies(k):
        own = (gdense, ext)
        whole_ = (gall, exall)
        return [
            ag(k, own[w], whole_[w].at[tp], (sib, across)[k], w) if k < 2
            else ag(k, whole_[w].at[tp ^ 2], whole_[w].at[tp ^ 2], sib, w)
            for w in range(2)
        ]

    def ag_pass():
        for copy in ag_copies(1):
            copy.wait()
        for copy in ag_copies(2):
            copy.start()

    def merge(i):
        t = tp ^ i

        for k in (0, 2):

            @pl.when(i == (1 if k == 0 else 2))
            def _(k=k):
                for copy in ag_copies(k):
                    copy.wait()

        fetch = [pltpu.make_async_copy(q_ref.at[t], qbuf, msem.at[0])]
        fetch[0].start()

        @pl.when(i == 0)
        def _():
            dmw[...] = jnp.zeros((256, C), f32)
            gf[0:DENSE, :] = gdense[...]
            extin[...] = ext[...]

        @pl.when(i > 0)
        def _():
            two = [
                pltpu.make_async_copy(gall.at[t], gf.at[pl.ds(0, DENSE)], msem.at[1]),
                pltpu.make_async_copy(exall.at[t], extin, msem.at[2]),
            ]
            for copy in two:
                copy.start()
            for copy in two:
                copy.wait()

        fetch[0].wait()
        wide = jnp.concatenate([extin[...], jnp.zeros((120, TOK), f32)], axis=0).T[0:DENSE, :]
        mean, inv, m2 = wide[:, 0:1], wide[:, 1:2], wide[:, 2:3]
        full = gf[0:DENSE, :]
        m1 = jnp.sum(full * vec_ref[0:1, :], axis=-1, keepdims=True) / (4.0 * C2)
        m2 = m2 / (4.0 * C2)
        fpair = split(full)
        xhat = (qbuf[...] - mean) * inv
        gmerged = mm3(fpair, split(mw_ref[...]), NT)
        dmw[...] += mm3(split(xhat * mg_ref[0:1, :] + mg_ref[1:2, :]), fpair, TN)
        tsh[0, 10:11, 0:256] += colsum(gmerged * xhat)
        tsh[0, 10:11, 256:512] += colsum(gmerged)

        @pl.when(i > 0)
        def _():
            pltpu.make_async_copy(gqbuf, gq_ref.at[t], msem.at[3]).wait()

        gqbuf[...] = inv * (gmerged * mg_ref[0:1, :] - m1 - xhat * m2)
        pltpu.make_async_copy(gqbuf, gq_ref.at[t], msem.at[3]).start()

        @pl.when(i == 3)
        def _():
            pltpu.make_async_copy(gqbuf, gq_ref.at[t], msem.at[3]).wait()
            for k in range(4):
                row = k * 256
                pair[FULL_CH + row // ROWS, 0, row % ROWS : row % ROWS + 256, :] = dmw[:, k * 128 : (k + 1) * 128]

    def rows(c):
        return pl.ds(pl.multiple_of(c * ROWS, ROWS), ROWS)

    def load(c, k):
        return pltpu.make_async_copy(pack.at[tp ^ (2 * k), rows(c)], loc.at[c % 4, k], ls.at[c % 4, k])

    def swap(c, k):
        return push(pack.at[tp ^ 1 ^ (2 * k), rows(c)], pair.at[c, k], ss.at[k, c], rs.at[k, c], sib)

    def cross(c):
        return push(pair.at[c, 1], fin.at[c], ss.at[2, c], rs.at[2, c], across)

    def halves(h):
        return pl.ds(pl.multiple_of(h * HALF, HALF), HALF)

    def side(c):
        return push(pair.at[c, 0, halves(1 - par)], yr.at[c], ss.at[3, c], rs.at[3, c], beside)

    def bit(q):
        return pl.ds(pl.multiple_of(q * piece, piece), piece)

    def spread(c, q, slot):
        return push(yr.at[c, bit(q)], zr.at[c, slot], zs.at[c % 4, q], zq.at[c, slot], device(q))

    def place(q):
        return pl.ds(pl.multiple_of(par * HALF + q * piece, piece), piece)

    def share(c, q, slot):
        return push(fin.at[c, place(slot)], fin.at[c, place(slot)], fs.at[c % 4, q], fq.at[c, slot], device(q))

    def back(c):
        return push(fin.at[c, halves(par)], fin.at[c, halves(par)], ss.at[4, c], rs.at[4, c], beside)

    def write(c):
        return pltpu.make_async_copy(fin.at[c], out_ref.at[rows(c)], os.at[c])

    low, high = pl.ds(0, 16), pl.ds(16, 24)

    bits = m.bit_length() - 1

    def tiny(k):
        if k == 0:
            todo = [(tsh.at[1], tr.at[0]), (tsh.at[3], tr.at[1]), (ta.at[0, high], tx.at[0, high])]
        elif k == 1:
            todo = [(tsh.at[2], tx.at[1, low]), (ta.at[1, high], tx.at[1, high])]
        else:
            todo = [(ta.at[k], tx.at[k])]
        peer = (sib, across, beside)[k] if k < 3 else device(mine ^ (1 << (k - 3)))
        return [push(a, b, tss.at[k, i], tsq.at[k, i], peer) for i, (a, b) in enumerate(todo)]

    def tiny_sum(k):
        if k == 0:
            ta[1, low] = tsh[0] + tr[0]
            ta[1, high] = ta[0, high] + tx[0, high]
            tsh[2] = tsh[2] + tr[1]
        else:
            ta[k + 1] = ta[k] + tx[k]

    late = RATE * (16 - FIRST)
    tiny_turn = late + 10

    def begun(s):
        return jnp.where(s < FIRST, 0, jnp.where(s < STEPS, RATE * (s - FIRST), CHUNKS + 21))

    def turn(p, last=False):
        if last:
            extra(p)
        stages(p)

    def extra(p):
        @pl.when(p == late + 5)
        def _():
            ag_pass()

        due = p - late

        @pl.when((due >= 0) & (due < 12) & (due % 3 == 0))
        def _():
            merge(due // 3)

        for k in range(4 + bits):

            @pl.when(p == tiny_turn + 2 * k)
            def _(k=k):
                if k > 0:
                    for copy in tiny(k - 1):
                        copy.wait()
                    tiny_sum(k - 1)
                if k < 3 + bits:
                    for copy in tiny(k):
                        copy.start()

    def stages(p):
        def stage(lag, end):
            c = p - lag
            return c, (c >= 0) & (c < end)

        c0, on0 = stage(0, FULL_CH)

        @pl.when(on0)
        def _():
            swap(c0, 1).start()
            load(c0, 1).start()

        c1, on1 = stage(2, FULL_CH)

        @pl.when(on1)
        def _():
            load(c1, 1).wait()
            swap(c1, 1).wait_recv()
            pair[c1, 1] = pair[c1, 1] + loc[c1 % 4, 1]
            cross(c1).start()

        c2, on2 = stage(4, FULL_CH)

        @pl.when(on2)
        def _():
            swap(c2, 0).start()
            load(c2, 0).start()

        c3, on3 = stage(6, CHUNKS)

        @pl.when(on3)
        def _():
            @pl.when(c3 < FULL_CH)
            def _():
                load(c3, 0).wait()
                swap(c3, 0).wait_recv()
                cross(c3).wait_recv()
                pair[c3, 0] = (pair[c3, 0] + loc[c3 % 4, 0]) + fin[c3]
                swap(c3, 1).wait_send()

            side(c3).start()

        c4, on4 = stage(9, CHUNKS)

        @pl.when(on4)
        def _():
            @pl.when(c4 < FULL_CH)
            def _():
                swap(c4, 0).wait_send()
                cross(c4).wait_send()

            side(c4).wait_recv()
            yr[c4] = yr[c4] + pair[c4, 0, halves(par)]

            @pl.loop(1, m)
            def _(j):
                spread(c4, member(j), mine).start()

        c5, on5 = stage(12, CHUNKS)

        @pl.when(on5)
        def _():
            side(c5).wait_send()
            fin[c5, place(mine)] = yr[c5, bit(mine)]

            @pl.loop(1, m)
            def _(j):
                spread(c5, member(j), member(j)).wait_recv()
                fin[c5, place(mine)] = fin[c5, place(mine)] + zr[c5, member(j)]

            @pl.loop(1, m)
            def _(j):
                share(c5, member(j), mine).start()
                spread(c5, member(j), mine).wait_send()

        c6, on6 = stage(15, CHUNKS)

        @pl.when(on6)
        def _():
            @pl.loop(1, m)
            def _(j):
                share(c6, member(j), member(j)).wait_recv()
                share(c6, member(j), mine).wait_send()

            back(c6).start()

        c7, on7 = stage(18, CHUNKS)

        @pl.when(on7)
        def _():
            back(c7).wait()
            write(c7).start()

        c8, on8 = stage(21, CHUNKS)

        @pl.when(on8)
        def _():
            write(c8).wait()

    def midway():
        first = begun(step)

        @pl.when(first < begun(step + 1))
        def _():
            turn(first)

    phase = step // 4

    @pl.when((phase == 0) | (phase == 2))
    def _():
        b = 1 - phase // 2
        j = step % 4
        i = j ^ 2

        @pl.when(j == 0)
        def _():
            @pl.when(b == 0)
            def _():
                for copy in moves():
                    copy.wait()
                gf[...] = moved[...]

            xhat, _ = normalized(mid_ref[0])
            nth[...], ntl[...] = split((xhat * g2_ref[pl.ds(b, 1), :] + b2_ref[pl.ds(b, 1), :]).T)
            gh[...], gl[...] = split(gf[...])
            acc[...] = jnp.zeros_like(acc)

        @pl.when(j > 0)
        def _():
            packed(b, j - 1, False).wait()

        slot = j % 2
        grad = (gh[...], gl[...])
        dws = mm3(split(hid_ref[0].T), grad, NN)
        for q in range(4):
            gbuf[slot, 2048 + q * 512 : 2560 + q * 512, :] = dws[:, q * 128 : (q + 1) * 128]
        dpre = mm3(grad, split(ws_ref[0, 0].reshape(512, C)), NT) * slope_ref[0]
        tsh[i, pl.ds(b, 1), :] = colsum(dpre)
        midway()
        pair_ = split(dpre)
        dwe = mm3((nth[...], ntl[...]), pair_, NN)
        for q in range(4):
            gbuf[slot, q * 512 : (q + 1) * 512, :] = dwe[:, q * 128 : (q + 1) * 128]
        acc[...] += mm3(pair_, split(we_ref[0, 0].reshape(C, 512)), NT)

        packed(b, j, False).start()

        @pl.when(j == 3)
        def _():
            grad_x, dgain, dshift = norm_back(mid_ref[0], g2_ref[pl.ds(b, 1), :], acc[...])
            ta[0, pl.ds(22 + 3 * b, 1), :] = dgain
            ta[0, pl.ds(23 + 3 * b, 1), :] = dshift
            ta[0, pl.ds(24 + 3 * b, 1), :] = colsum(gf[...])
            gf[...] = gf[...] + grad_x
            packed(b, 3, False).wait()

    @pl.when((phase == 1) | (phase == 3))
    def _():
        b = 1 - phase // 2
        j = step % 4
        i = j ^ 2

        @pl.when(j == 0)
        def _():
            xhat, _ = normalized(field_ref[0])
            nth[...], ntl[...] = split((xhat * g1_ref[pl.ds(b, 1), :] + b1_ref[pl.ds(b, 1), :]).T)
            gh[...], gl[...] = split(gf[...])
            acc[...] = jnp.zeros_like(acc)

        @pl.when(j > 0)
        def _():
            packed(b, j - 1, True).wait()

        slot = j % 2
        grad = (gh[...], gl[...])
        dwo = mm3(split(att_ref[0].T), grad, NN)
        for q in range(4):
            gbuf[slot, 1536 + q * 128 : 1664 + q * 128, :] = dwo[:, q * 128 : (q + 1) * 128]
        dout = mm3(grad, split(wo_ref[0, 0, 0]), NT)
        masks = head_masks(bf16)
        dbias = jnp.zeros((GROUP * WT, WT), f32)
        for w in range(NW):
            rows = slice(w * WT, (w + 1) * WT)
            seen = qkv_ref[0, pl.ds(w * WT, WT), :]
            q4 = stacked(split(seen[:, :128]), masks)
            k4 = stacked(split(seen[:, 128:256]), masks)
            v = split(seen[:, 256:])
            p = p_ref[0, w]
            do4 = stacked(split(dout[rows]), masks)
            dp = mm3(do4, v, NT)
            ds = p * (dp - jnp.sum(p * dp, axis=-1, keepdims=True))
            dbias = dbias + ds
            dpair = split(ds)
            dqkv[pl.ds(w * WT, WT), 0:128] = mm3(side_by_side(dpair), k4, NN) * HD ** (-0.5)
            dqkv[pl.ds(w * WT, WT), 128:256] = mm3(dpair, q4, TN)
            dqkv[pl.ds(w * WT, WT), 256:384] = mm3(split(p), do4, TN)
            if w == 1:
                midway()
        line = table_line(dbias, pick_ref[...], pile_ref[...])
        for q in range(3):
            tsh[i, pl.ds(4 + 3 * b + q, 1), :] = line[:, q * 512 : (q + 1) * 512]
        grads = dqkv[...]
        tsh[i, pl.ds(2 + b, 1), 0:384] = colsum(grads)
        pair_ = split(grads)
        dw = mm3((nth[...], ntl[...]), pair_, NN)
        for q in range(3):
            gbuf[slot, q * 512 : (q + 1) * 512, :] = dw[:, q * 128 : (q + 1) * 128]
        w = jnp.concatenate([wqkv_ref[0, 0, q] for q in range(3)], axis=1)
        acc[...] += mm3(pair_, split(w), NT)

        packed(b, j, True).start()

        @pl.when(j == 3)
        def _():
            grad_x, dgain, dshift = norm_back(field_ref[0], g1_ref[pl.ds(b, 1), :], acc[...])
            ta[0, pl.ds(16 + 3 * b, 1), :] = dgain
            ta[0, pl.ds(17 + 3 * b, 1), :] = dshift
            ta[0, pl.ds(18 + 3 * b, 1), :] = colsum(gf[...])
            acc[...] = gf[...] + grad_x

            @pl.when(b == 1)
            def _():
                for copy in moves():
                    copy.start()
                kept()

            packed(b, 3, True).wait()

    @pl.when(step == AG_STEP)
    def _():
        m2 = jnp.sum(acc[...] * (field_ref[0] - vec_ref[1:2, :]), axis=-1, keepdims=True)
        pick = placing()
        gdense[...] = selected(pick, acc[...], TN)
        lane = lax.broadcasted_iota(jnp.int32, (DENSE, 128), 1)
        tall = selected(pick, jnp.broadcast_to(m2, (TOK, 128)), TN)
        ext[...] = upright(jnp.where(lane == 2, tall, stat_ref[...]))
        for k in range(2):
            for copy in ag_copies(k):
                copy.start()

    @pl.when(step < STEPS - 1)
    def _():
        @pl.loop(begun(step) + 1, begun(step + 1))
        def _(p):
            turn(p)

    @pl.when(step == STEPS - 1)
    def _():
        @pl.loop(begun(step), begun(step + 1))
        def _(p):
            turn(p, True)

    @pl.when(step == STEPS - 1)
    def _():
        out_own().wait()
        for k in range(2):
            for i in range(4):
                if k + i > 0:
                    out_copy(k, i).wait_send()
                    out_in(k, i).wait_recv()
        tout_ref[...] = ta[3 + bits]


def backward(n, args, ident):
    m = n // 2
    ROWS, FULL_CH, CHUNKS, _ = chunk_plan(n)
    HALF = ROWS // 2
    bits = m.bit_length() - 1
    dma = pltpu.SemaphoreType.DMA

    def fixed(shape):
        return pl.BlockSpec(shape, lambda s: (0,) * len(shape), pipeline_mode=pl.Buffered(1))

    def mlp_at(s):
        return jnp.where(s < 4, 4 + (s ^ 2), jnp.where(s < 8, 2, jnp.where(s < 12, (s - 8) ^ 2, 1)))

    def att_at(s):
        return jnp.where(s < 4, 6, jnp.where(s < 8, 4 + ((s - 4) ^ 2), jnp.where(
            s < 12, 2, jnp.where(s < 16, (s - 12) ^ 2, 1))))

    def by(index, shape, mode=None):
        zeros = (0,) * len(shape)
        return pl.BlockSpec((1,) + shape, lambda s: (index(s),) + zeros, pipeline_mode=mode)

    def spot(index, shape, k):
        return pl.BlockSpec((1, 1) + shape, lambda s: (index(s) % 4, index(s) // 4, k, 0, 0))

    one = pl.Buffered(1)
    lanes = (CHUNKS, ROWS, 128)
    in_specs = [
        fixed((4, 2, 192, 128)), by(lambda s: jnp.where(s < 4, 1, 0), (TOK, C), one),
        by(lambda s: jnp.where(s < 8, 1, 0), (TOK, C), one),
        fixed((2, C)), fixed((2, C)), fixed((2, C)), fixed((2, C)),
        spot(mlp_at, (4, 128, 512), 0), spot(mlp_at, (4, 128, 512), 1), spot(att_at, (3, C, 128), 0),
        spot(att_at, (1, 128, C), 8),
        by(mlp_at, (TOK, 512)), by(mlp_at, (TOK, 512)), by(att_at, (TOK, 384)),
        by(att_at, (NW, GROUP * WT, WT)), by(att_at, (TOK, 128)),
        fixed((8, C)), ANY, fixed((256, C)), fixed((8, C)), fixed((8, 256)), fixed((DENSE, 128)), ANY,
        fixed((WT, 384)), fixed((160, WT)),
    ]
    return pl.pallas_call(
        functools.partial(bwd_kernel, n),
        grid=(STEPS,),
        in_specs=in_specs,
        out_specs=[ANY, ANY, ANY, ANY, ANY, ANY, fixed((TINY, C))],
        out_shape=[
            sds(4, FULL_CH * ROWS, 128), sds(4, DENSE, C), sds(4, 8, TOK), sds(2, 24, SUB, 128), sds(CHUNKS * ROWS, 128),
            sds(4, DENSE, 256), sds(TINY, C),
        ],
        scratch_shapes=[
            pltpu.VMEM((C, TOK), bf16), pltpu.VMEM((C, TOK), bf16), pltpu.VMEM((TOK, C), bf16),
            pltpu.VMEM((TOK, C), bf16), pltpu.VMEM((TOK, C), f32), pltpu.VMEM((TOK, 384), f32),
            pltpu.VMEM((TOK, C), f32), pltpu.VMEM((2, MLP_ROWS, 128), f32), pltpu.VMEM((TOK, C), f32),
            pltpu.VMEM((8, TOK), f32), pltpu.VMEM((8, TOK), f32), pltpu.VMEM((DENSE, 256), f32),
            pltpu.VMEM((DENSE, C), f32),
            pltpu.VMEM((4, 2, ROWS, 128), f32), pltpu.VMEM((CHUNKS, 2, ROWS, 128), f32),
            pltpu.VMEM((CHUNKS, HALF, 128), f32), pltpu.VMEM((CHUNKS, m, HALF // m, 128), f32),
            pltpu.VMEM(lanes, f32), pltpu.VMEM((4 + bits, TINY, C), f32),
            pltpu.VMEM((3 + bits, TINY, C), f32), pltpu.VMEM((4, 16, C), f32), pltpu.VMEM((2, 16, C), f32),
            dma((2,)), dma((7,)), dma((7,)), dma((2, 3)), dma((2, 3)), dma((2,)), dma((4,)),
            dma((5, CHUNKS)), dma((5, CHUNKS)), dma((4, m)), dma((CHUNKS, m)), dma((4, m)),
            dma((CHUNKS, m)), dma((4, 2)), dma((CHUNKS,)),
            dma((2, 4)), dma((2, 4)), dma((1,)), dma((3 + bits, 3)), dma((3 + bits, 3)),
        ],
        compiler_params=pltpu.CompilerParams(
            collective_id=ident, has_side_effects=True, vmem_limit_bytes=60 << 20,
            dimension_semantics=("arbitrary",),
        ),
        name="backward",
    )(*args)


def unpack_kernel(
    pack_ref, merge_ref, tiny_ref,
    we_ref, ws_ref, qkv_ref, wo_ref, mw_ref, mg_ref, ms_ref, g1_ref, b1_ref, bias_ref, tab_ref, bo_ref, g2_ref,
    b2_ref, be_ref, bs_ref, rms_ref,
):
    for q in range(4):
        lanes = slice(q * 128, (q + 1) * 128)
        we_ref[0, :, lanes] = pack_ref[q]
        ws_ref[0, :, lanes] = pack_ref[4 + q]
        wo_ref[0, :, lanes] = pack_ref[11, q * 128 : (q + 1) * 128, :]
    for j in range(3):
        qkv_ref[0, j] = pack_ref[8 + j]

    @pl.when(pl.program_id(0) == 0)
    def _():
        for i in range(2):
            for j in range(2):
                k, low = 2 * j + i, (2 * i + j) * 64
                for q in range(4):
                    mw_ref[k, :, q * 128 : (q + 1) * 128] = merge_ref[q, low : low + 64, :]
                mg_ref[k : k + 1, :] = tiny_ref[10:11, low : low + 64]
                ms_ref[k : k + 1, :] = tiny_ref[10:11, 256 + low : 320 + low]
        be_ref[...] = tiny_ref[0:2, :]
        for b in range(2):
            bias_ref[b, 0:1, :] = tiny_ref[2 + b : 3 + b, 0:128]
            bias_ref[b, 1:2, :] = tiny_ref[2 + b : 3 + b, 256:384]
            line = jnp.concatenate([tiny_ref[4 + 3 * b + q : 5 + 3 * b + q, :] for q in range(3)], axis=1)
            for h in range(4):
                tab_ref[b, h : h + 1, :] = line[:, h * 384 : h * 384 + 361]
            for k, ref in enumerate((g1_ref, b1_ref, bo_ref)):
                ref[b : b + 1, :] = tiny_ref[16 + 3 * b + k : 17 + 3 * b + k, :]
            for k, ref in enumerate((g2_ref, b2_ref, bs_ref)):
                ref[b : b + 1, :] = tiny_ref[22 + 3 * b + k : 23 + 3 * b + k, :]
        sums = jnp.sum(tiny_ref[28:36, :], axis=1, keepdims=True)
        rms_ref[...] = jnp.broadcast_to(jnp.sqrt(sums / (sums[5:6] * C)), (8, 128))


def unpack(packed, tiny):
    blocks = packed.reshape(-1, 512, 128)
    merged = packed.reshape(-1, 256, 128)
    whole = lambda *shape: pl.BlockSpec(shape, lambda b: (0,) * len(shape))
    layer = lambda *shape: pl.BlockSpec((1,) + shape, lambda b: (b,) + (0,) * len(shape))
    row = (2, C)
    return pl.pallas_call(
        unpack_kernel,
        grid=(2,),
        in_specs=[
            pl.BlockSpec((12, 512, 128), lambda b: (1 - b, 0, 0)),
            pl.BlockSpec((4, 256, 128), lambda b: (12, 0, 0)),
            whole(TINY, C),
        ],
        out_specs=[
            layer(512, 512), layer(512, 512), layer(3, 512, 128), layer(128, 512), whole(4, 64, C), whole(4, 64),
            whole(4, 64), whole(*row), whole(*row), whole(2, 2, 128), whole(2, 4, 361), whole(*row), whole(*row),
            whole(*row), whole(*row), whole(*row), whole(8, 128),
        ],
        out_shape=[
            sds(2, 512, 512), sds(2, 512, 512), sds(2, 3, 512, 128), sds(2, 128, 512), sds(4, 64, C), sds(4, 64),
            sds(4, 64), sds(*row), sds(*row), sds(2, 2, 128), sds(2, 4, 361), sds(*row), sds(*row), sds(*row),
            sds(*row), sds(*row), sds(8, 128),
        ],
        compiler_params=pltpu.CompilerParams(vmem_limit_bytes=48 << 20),
        name="unpack",
    )(blocks, merged, tiny)


def column_pick():
    pick = np.zeros((19, WIN, WIN), np.float32)
    for a in range(WIN):
        for b in range(WIN):
            pick[a - b + WIN - 1, a, b] = 1.0
    return pick


def row_pick():
    pick = np.zeros((19, WIN, WIN, WIN, 2, 2, SUB), np.float32)
    for pr in range(WIN):
        for qr in range(WIN):
            for qc in range(WIN):
                pick[pr - qr + WIN - 1, qc, pr, 0, qr // 5, qc // 5, (qr % 5) * 5 + qc % 5] = 1.0
    return pick[:, :, :, 0].reshape(190, WIN * WT)


def bias_of(table):
    heads = table.shape[0]
    grid = table.reshape(heads, 19, 19)
    columns = jnp.einsum("hrd,dab->harb", grid, jnp.asarray(column_pick()), precision="highest")
    rows = jnp.dot(columns.reshape(heads * WIN, 190), jnp.asarray(row_pick()), precision="highest")
    rows = rows.reshape(heads, 2, 5, 2, 5, WT).transpose(0, 3, 1, 4, 2, 5)
    rows = rows.reshape(heads, 4, REAL, WT)
    return jnp.pad(rows, ((0, 0), (0, 0), (0, SUB - REAL), (0, 0))).reshape(heads, WT, WT)


def shards(
    patches, merge_gain, merge_shift, merge_weight, first_gain, first_shift, input_weight,
    input_bias, position_table, output_weight, output_bias, second_gain, second_shift,
    expand_weight, expand_bias, shrink_weight, shrink_bias, page_map, valid_flags, cotangent,
):
    sp_count = lax.axis_size("sp")
    tp = lax.axis_index("tp")

    tables = position_table.transpose(0, 2, 1).reshape(8, 361)
    bias = bias_of(tables).reshape(2, 512, 128)
    pairs = jnp.concatenate([input_bias, jnp.zeros_like(input_bias)], axis=2).reshape(2, 512)
    small = jnp.concatenate([expand_bias, pairs, jnp.zeros((4, 512), f32)], axis=0)

    valid = valid_flags.astype(f32).reshape(2, 5, 24, 5).transpose(0, 2, 1, 3).reshape(2, 24, REAL)
    valid = jnp.pad(valid, ((0, 0), (0, 0), (0, 128 - REAL)))

    gain = merge_gain.reshape(2, 2, 64).transpose(1, 0, 2).reshape(1, 256)
    offset = merge_shift.reshape(2, 2, 64).transpose(1, 0, 2).reshape(1, 256)
    mgain = jnp.concatenate([gain, offset, jnp.zeros((6, 256), f32)], axis=0)
    weight = merge_weight.reshape(2, 2, 64, C).transpose(1, 0, 2, 3).reshape(256, C)
    quads = patches.reshape(2, 5, 2, 4, NW, 2, 5, 128).transpose(3, 4, 0, 5, 1, 6, 2, 7).reshape(4, 300, 256)
    quads = jnp.pad(quads, ((0, 0), (0, DENSE - 300), (0, 0)))
    cot = jnp.roll(cotangent.reshape(2, 5, 24, 5, 128), -1, axis=2).transpose(0, 2, 1, 3, 4).reshape(2, 24, REAL, 128)
    cot = jnp.pad(cot, ((0, 0), (0, 0), (0, SUB - REAL), (0, 0)))

    nall, wall, cot, fields, middles, qkv, p, att, hid, slope, stat, vecs, squares, out = forward(
        sp_count,
        (
            quads, weight, mgain, input_weight.transpose(0, 2, 1, 3), bias, output_weight.reshape(2, 1, 128, C),
            expand_weight.reshape(2, 4, 128, 512), shrink_weight.reshape(2, 4, 128, C), small,
            first_gain, first_shift, output_bias, second_gain, second_shift,
            shrink_bias, page_map, valid, cot,
        ),
        1,
    )
    _, _, _, output, packed, gquads, tiny = backward(
        sp_count,
        (
            cot.reshape(4, 2, 192, 128), middles, fields, first_gain, first_shift,
            second_gain, second_shift, wall, wall, nall, wall, hid, slope, qkv, p, att,
            squares, quads, weight, vecs, mgain, stat, out.reshape(4, 2, 6, SUB, 128),
            *table_picks(),
        ),
        2,
    )
    output = jnp.roll(output[:, :, :REAL], 1, axis=1).reshape(2, 24, 5, 5, 128)
    output = output.transpose(0, 2, 1, 3, 4).reshape(10, 120, 128)
    gquads = gquads[:, :300].reshape(4, NW, 2, 2, 5, 5, 2, 128)
    patches_grad = gquads.transpose(2, 4, 6, 0, 1, 3, 5, 7).reshape(20, 240, 64)
    we, ws, qkv, wo, dmw, dmg, dms, dg1, db1, dbias, table, dbo, dg2, db2, dbe, dbs, rms = unpack(packed, tiny)
    return (
        output, patches_grad, dmg, dms, dmw, dg1, db1, qkv.transpose(0, 2, 1, 3), dbias, table.transpose(0, 2, 1),
        wo, dbo, dg2, db2, we, dbe, ws, dbs, rms[:5, 0],
    )


def solution(mesh):
    placed = (
        P("sp", None, "tp"), P(None, "tp"), P(None, "tp"), P(None, "tp", None), P(), P(),
        P(None, None, None, "tp"), P(None, None, "tp"), P(None, None, "tp"), P(None, "tp", None),
        P(), P(), P(), P(None, None, "tp"), P(None, "tp"), P(None, "tp", None), P(), P(),
        P("sp", None), P("sp", None, "tp"),
    )
    results = (
        P("sp", None, "tp"), P("sp", None, "tp"), P(None, "tp"), P(None, "tp"), P(None, "tp", None),
        P(), P(), P(None, None, None, "tp"), P(None, None, "tp"), P(None, None, "tp"),
        P(None, "tp", None), P(), P(), P(), P(None, None, "tp"), P(None, "tp"), P(None, "tp", None),
        P(), P(),
    )
    return jax.shard_map(shards, mesh=mesh, in_specs=placed, out_specs=results, check_vma=False)
```
